32 devices in a mesh: seq: 8 (over z, x), head: 4 (over y, core).
Axes of the slice: x: 2, y: 2, z: 4, core: 2. Of those that a mesh axis runs over, the one named last changes fastest.
Arguments:
- tokens: bfloat16 [2, 2048, 1024], P(None, 'seq', 'head'), may hold values from -6 to 6
- cotangent: bfloat16 [2, 2048, 1024], P(None, 'seq', 'head'), may hold values from -6 to 6
- w_qkv: bfloat16 [1024, 3, 1024], P('seq', None, 'head'), may hold values from -0.1875 to 0.1875
- w_out_t: bfloat16 [1024, 1024], P('seq', 'head'), may hold values from -0.75 to 0.75
- w_up: bfloat16 [1024, 4096], P('seq', 'head'), may hold values from -0.1875 to 0.1875
- w_down_t: bfloat16 [1024, 4096], P('seq', 'head'), may hold values from -0.09375 to 0.09375
- gains: bfloat16 [2, 1024], P(None, 'seq'), may hold values from 0.099609375 to 1.8984375
- biases: bfloat16 [3, 1024], P(None, 'seq'), may hold values from -3 to 3
- up_bias: bfloat16 [4, 1024], P('head', 'seq'), may hold values from -3 to 3
- lengths: int32 [2, 16], replicated, may hold values from 1 to 512, 2048 in all within a row
- pixel_mask: int32 [2, 2048], P(None, 'seq'), may hold values 0 or 1
Outputs:
- activations: float32 [2, 2048, 1024], P(None, 'seq', 'head')
- input_grad: float32 [2, 2048, 1024], P(None, 'seq', 'head')
- grad_qkv: float32 [1024, 3, 1024], P('seq', None, 'head')
- grad_out_t: float32 [1024, 1024], P('seq', 'head')
- grad_up: float32 [1024, 4096], P('seq', 'head')
- grad_down_t: float32 [1024, 4096], P('seq', 'head')
- grad_gains: float32 [2, 1024], P(None, 'seq')
- grad_biases: float32 [3, 1024], P(None, 'seq')
- grad_up_bias: float32 [4, 1024], P('head', 'seq')
The draws below stay inside these ranges and needn't reach their ends.
Inputs may be any that keep to these rules, and one draw needn't show every extreme that they name: `lengths`: row b lists the 16 crops of micro-batch b in order of their place; each row sums to 2048 and its longest crop has 512 tokens.
All inputs are finite; a program needn't handle non-finite values. No bound on the sum of `pixel_mask` on one device may be relied on, other than what follows from the above.
Results may differ from the reference program's by a relative error of at most 0.017.
Values may be sent and summed in bfloat16 or wider, within the bound.
A program may use at most 128 MiB of HBM per device.

```python
import math
import jax
import jax.numpy as jnp
import numpy as np
from jax import lax

D = 1024
HEADS = 16
DH = 64
FF = 4096
MB = 2
ITEMS = 16
TOKENS = 2048
LONGEST = 512


def set_ends(entries, own_key, smallest, top_value):
    extent = entries.shape
    index_at = [jax.random.randint(jax.random.fold_in(own_key, axis), (), 0, extent[axis]) for axis in range(len(extent))]
    entries = entries.at[tuple(index_at)].set(smallest)
    longest = extent.index(max(extent))
    index_at[longest] = (index_at[longest] + 1) % extent[longest]
    return entries.at[tuple(index_at)].set(top_value)


def levels(key, extent, split, smallest, high):
    factor_of = 1.0
    for dim, parts in split:
        heights = jax.random.uniform(jax.random.fold_in(jax.random.fold_in(key, 6), dim), (parts,), jnp.float32, smallest / len(split), high / len(split))
        factor_of = factor_of * jnp.repeat(jnp.exp(heights), extent[dim] // parts).reshape((-1,) + (1,) * (len(extent) - 1 - dim))
    return factor_of


def split_up(amount, total, bound, skew):
    loads = [(1 << 20) // math.isqrt(rank ** skew) + 1 for rank in range(2, amount + 1)]
    spare, holding = total - bound - (amount - 1), [1] * (amount - 1)
    while spare > 0:
        movable = [i for i in range(amount - 1) if holding[i] < bound]
        mass, remaining = sum([loads[i] for i in movable]), spare
        for i in movable:
            more = min(bound - holding[i], max(1, remaining * loads[i] // mass), spare)
            holding[i] = holding[i] + more
            spare = spare - more
    return np.array([bound] + holding)


def ragged(rng, count, total, limit, lean):
    if count == 2:
        one = jax.random.randint(rng, (), max(1, total - limit), min(limit, total - 1) + 1)
        return jnp.stack([one, total - one])
    sizes = jnp.asarray(split_up(count, total, limit, lean), jnp.int32)
    pairs = (count - 1) // 2
    source_of, taker = sizes[1:1 + 2 * pairs:2], sizes[2:2 + 2 * pairs:2]
    slack = jnp.minimum(source_of - 1, limit - taker)
    moved = jax.random.randint(jax.random.fold_in(rng, 1), (pairs,), 0, 1 << 20) % (slack + 1)
    sizes = sizes.at[1:1 + 2 * pairs:2].set(source_of - moved).at[2:2 + 2 * pairs:2].set(taker + moved)
    return sizes[jax.random.permutation(jax.random.fold_in(rng, 2), count)]


def centred(own_key, shape, deviation, bound, cuts=(), kind=jnp.bfloat16):
    gain = levels(own_key, shape, cuts, -0.22, 0.18) if cuts else 1.0
    entries = jax.random.normal(own_key, shape, jnp.float32) * deviation * gain
    return jnp.minimum(jnp.maximum(entries, -bound), bound).astype(kind)


def setup_inputs(seed: int = 0) -> dict:
    seeds = jax.random.split(jax.random.key(seed), 12)
    tokens = centred(seeds[0], (MB, TOKENS, D), 1.0, 6.0, ((1, 8), (2, 4)))
    cotangent = centred(seeds[1], (MB, TOKENS, D), 1.0, 6.0, ((1, 8), (2, 4)))
    w_qkv = centred(seeds[2], (D, 3, D), D ** -0.5, 0.1875, ((0, 8), (2, 4)))
    w_out_t = centred(seeds[3], (D, D), DH ** -0.5, 0.75, ((0, 8), (1, 4)))
    w_up = centred(seeds[4], (D, FF), D ** -0.5, 0.1875, ((0, 8), (1, 4)))
    w_down_t = centred(seeds[5], (D, FF), FF ** -0.5, 0.09375, ((0, 8), (1, 4)))
    gains = jnp.clip(1.0 + 0.18 * jax.random.normal(seeds[6], (2, D), jnp.float32), 0.099609375, 1.8984375).astype(jnp.bfloat16)
    biases = centred(seeds[7], (3, D), 0.3, 3.0, ((1, 8),))
    up_bias = centred(seeds[8], (FF // D, D), 0.3, 3.0, ((0, 4), (1, 8)))
    lengths = jax.vmap(lambda own: ragged(own, ITEMS, TOKENS, LONGEST, 2))(jax.random.split(seeds[9], MB)).reshape((MB, ITEMS)).astype(jnp.int32)
    pixel_mask = set_ends((jax.random.randint(seeds[10], (MB, TOKENS), 0, 8) < 7).astype(jnp.int32), jax.random.fold_in(seeds[10], 1), 0, 1)
    return {"tokens": tokens, "cotangent": cotangent, "w_qkv": w_qkv, "w_out_t": w_out_t, "w_up": w_up, "w_down_t": w_down_t, "gains": gains, "biases": biases, "up_bias": up_bias, "lengths": lengths, "pixel_mask": pixel_mask}


@jax.custom_vjp
def low(v):
    return lax.optimization_barrier(v.astype(jnp.bfloat16)).astype(jnp.float32)

@jax.custom_vjp
def low_back(v):
    return v

def low_keep(v):
    return (low(v), None)

def low_pass(kept, grad):
    return (grad,)

def back_keep(v):
    return (v, None)

def back_low(kept, grad):
    return (low(grad),)
low.defvjp(low_keep, low_pass)
low_back.defvjp(back_keep, back_low)
highest = lax.Precision.HIGHEST

def layer_norm(values, gain_vec, shift_vec):
    mean_val = lax.optimization_barrier(jnp.mean(values, axis=-1, keepdims=True))
    centered = values - mean_val
    variance = lax.optimization_barrier(jnp.mean(centered * centered, axis=-1, keepdims=True))
    return centered * lax.rsqrt(variance + 1e-05) * gain_vec + shift_vec

def features(values):
    return jax.nn.elu(values) + 1.0

def item_numbers(lengths_row, first_place, number):
    offsets = (jnp.cumsum(lengths_row) - lengths_row).astype(jnp.int32)
    places = (first_place + jnp.arange(number, dtype=jnp.int32)).astype(jnp.int32)
    return (lax.optimization_barrier(jnp.sum((offsets[None, :] <= places[:, None]).astype(jnp.int32), axis=1)) - 1).astype(jnp.int32)

def attend_block(carry_in, block_data):
    state_sum, total_sum, last_item = carry_in
    query_feat, key_feat, value_feat, item_of = block_data
    block_len = item_of.shape[0]
    position = jnp.arange(block_len, dtype=jnp.int32)
    same_item = ((item_of[:, None] == item_of[None, :]) & (position[:, None] >= position[None, :])).astype(jnp.float32)
    carried = (item_of == last_item).astype(jnp.float32)
    scores = low_back(jnp.einsum('thd,jhd->htj', query_feat, key_feat, precision=highest) * same_item[None])
    scores_low = low(scores)
    numerator = jnp.einsum('htj,jhe->the', scores_low, value_feat, precision=highest) + carried[:, None, None] * jnp.einsum('thd,hde->the', query_feat, state_sum, precision=highest)
    numerator = low_back(numerator)
    denominator = lax.optimization_barrier(jnp.sum(scores, axis=2)).T + carried[:, None] * jnp.einsum('thd,hd->th', query_feat, total_sum, precision=highest)
    output = numerator / jnp.maximum(denominator, 1.0)[:, :, None]
    final_item = item_of[block_len - 1]
    keep_flag = (final_item == last_item).astype(jnp.float32)
    tail_key = key_feat * (item_of == final_item).astype(jnp.float32)[:, None, None]
    state_sum = keep_flag * state_sum + jnp.einsum('jhd,jhe->hde', tail_key, value_feat, precision=highest)
    total_sum = keep_flag * total_sum + lax.optimization_barrier(jnp.sum(tail_key, axis=0))
    return ((state_sum, total_sum, final_item), output)

def forward(inputs32, w_qkv, w_out_t, w_up, w_down_t, gains, biases, up_bias, keep_mask, item_of):
    row_count = inputs32.shape[0]
    block_len = math.gcd(row_count, 512)
    blocks = row_count // block_len
    normed = low(layer_norm(inputs32, gains[0], biases[0]))
    projected = low_back(jnp.einsum('td,dsf->tsf', normed, w_qkv, precision=highest))
    query_feat = low(features(projected[:, 0])).reshape(blocks, block_len, HEADS, DH)
    key_feat = (low(features(projected[:, 1])) * keep_mask[:, None]).reshape(blocks, block_len, HEADS, DH)
    value_feat = low(projected[:, 2]).reshape(blocks, block_len, HEADS, DH)
    initial = (jnp.zeros((HEADS, DH, DH), jnp.float32), jnp.zeros((HEADS, DH), jnp.float32), jnp.array(-1, jnp.int32))
    ignored, output = lax.scan(jax.checkpoint(attend_block), initial, (query_feat, key_feat, value_feat, item_of.reshape(blocks, block_len)))
    mixed_out = low(output.reshape(row_count, D))
    attended = low_back(jnp.dot(mixed_out, w_out_t.T, precision=highest))
    middle = inputs32 + attended
    normed_two = low(layer_norm(middle, gains[1], biases[1]))
    hidden = low_back(jnp.dot(normed_two, w_up, precision=highest) + up_bias.reshape(FF))
    activated = low(jax.nn.gelu(hidden))
    branch = low_back(jnp.dot(activated, w_down_t.T, precision=highest))
    return middle + branch + biases[2]

def reference(tokens, cotangent, w_qkv, w_out_t, w_up, w_down_t, gains, biases, up_bias, lengths, pixel_mask):
    weights32 = (w_qkv.astype(jnp.float32), w_out_t.astype(jnp.float32), w_up.astype(jnp.float32), w_down_t.astype(jnp.float32), gains.astype(jnp.float32), biases.astype(jnp.float32), up_bias.astype(jnp.float32))
    results = []
    input_grads = []
    totals = None
    for batch_index in range(MB):
        item_of = item_numbers(lengths[batch_index], 0, TOKENS)
        keep_mask = pixel_mask[batch_index].astype(jnp.float32)

        def layer_fn(inputs32, wq, wo, wu, wd, gn, bs, ub):
            return forward(inputs32, wq, wo, wu, wd, gn, bs, ub, keep_mask, item_of)
        result, pullback = jax.vjp(layer_fn, tokens[batch_index].astype(jnp.float32), *weights32)
        grad_list = pullback(cotangent[batch_index].astype(jnp.float32))
        results.append(result)
        input_grads.append(grad_list[0])
        if totals is None:
            totals = grad_list[1:]
        else:
            totals = tuple((first_part + second_part for first_part, second_part in zip(totals, grad_list[1:])))
    return (jnp.stack(results), jnp.stack(input_grads), totals[0], totals[1], totals[2], totals[3], totals[4], totals[5], totals[6])
```

```python
import functools

import jax
import jax.numpy as jnp
from jax import lax
from jax.experimental import pallas as pl
from jax.experimental.pallas import tpu as pltpu
from jax.sharding import PartitionSpec as P

DH = 64


highest = lax.Precision.HIGHEST
epsilon = 1e-05


def entering(array, axis, join, neutral):
    place = lax.axis_index(axis)
    gathered = jax.tree.map(
        lambda a, kind: lax.all_gather(a.astype(kind), axis),
        array,
        (jnp.bfloat16, jnp.bfloat16, jnp.bfloat16),
    )
    state = jax.tree.map(lambda a, e: jnp.zeros_like(a) + jnp.asarray(e, a.dtype), array, neutral)

    def one(hop, state):
        return join(
            state,
            jax.tree.map(
                lambda a, own: lax.dynamic_index_in_dim(a, hop, 0, False).astype(own.dtype),
                gathered,
                array,
            ),
        )

    return lax.fori_loop(0, place, one, state)


def entering_2(array, axis, combine, identity):
    length, place = (lax.axis_size(axis), lax.axis_index(axis))
    everything = jax.tree.map(
        lambda part, kind: lax.all_gather(part.astype(kind), axis),
        array,
        jax.tree.map(lambda a: jnp.bfloat16 if a.dtype == jnp.float32 else a.dtype, array),
    )
    start = jax.tree.map(
        lambda part, zero: jnp.broadcast_to(jnp.asarray(zero, part.dtype), part.shape),
        array,
        identity,
    )

    def hop(k, before):
        at = length - 1 - k
        reached = at > place
        new = combine(
            before, jax.tree.map(lambda part, own: part[at].astype(own.dtype), everything, array)
        )
        return jax.tree.map(lambda a, b: jnp.where(reached, a, b), new, before)

    return lax.fori_loop(0, length, hop, start)


def normalize(values, gain_vec, shift_vec):
    mean_val = jnp.mean(values, axis=-1, keepdims=True)
    centered = values - mean_val
    inverse = lax.rsqrt(jnp.mean(centered * centered, axis=-1, keepdims=True) + epsilon)
    unit_val = centered * inverse
    return (unit_val * gain_vec + shift_vec, unit_val, inverse)


def norm_back(grad_in, unit_val, inverse, gain_vec):
    scaled = grad_in * gain_vec
    centered = scaled - jnp.mean(scaled, axis=-1, keepdims=True)
    return inverse * (centered - unit_val * jnp.mean(scaled * unit_val, axis=-1, keepdims=True))


def features(values):
    return jax.nn.elu(values) + 1.0


def finish(numerator, denominator):
    return numerator / jnp.maximum(denominator, 1.0)[:, :, None]


def compose(earlier, later):
    return (
        later[0] + later[2] * earlier[0],
        later[1] + later[2] * earlier[1],
        later[2] * earlier[2],
    )


def item_numbers(lengths_row, first_place, number):
    offsets = jnp.cumsum(lengths_row) - lengths_row
    places = first_place + jnp.arange(number, dtype=jnp.int32)
    return jnp.sum((offsets[None, :] <= places[:, None]).astype(jnp.int32), axis=1) - 1


def on_device(
    tokens, cotangent, w_qkv, w_out_t, w_up, w_down_t, gains, biases, up_bias, lengths, pixel_mask
):
    batches, local_rows, columns = tokens.shape
    local_width = w_qkv.shape[2]
    heads_here = local_width // DH
    seq_index = lax.axis_index("seq")
    head_index = lax.axis_index("head")
    first_token = seq_index * local_rows
    position = jnp.arange(local_rows, dtype=jnp.int32)
    before = position[:, None] >= position[None, :]

    def own_columns(matrix):
        return lax.dynamic_slice_in_dim(matrix, head_index * columns, columns, 1)

    results = []
    input_grads = []
    shard_sums = None
    for batch_index in range(batches):
        full_qkv, full_out, full_up, full_down, full_gains, full_biases, full_upb = (
            lax.all_gather(w_qkv, "seq", axis=0, tiled=True),
            lax.all_gather(w_out_t, "seq", axis=0, tiled=True),
            lax.all_gather(w_up, "seq", axis=0, tiled=True),
            lax.all_gather(w_down_t, "seq", axis=0, tiled=True),
            lax.all_gather(gains, "seq", axis=1, tiled=True),
            lax.all_gather(biases, "seq", axis=1, tiled=True),
            lax.all_gather(up_bias, "seq", axis=1, tiled=True),
        )
        input_rows, grad_rows16 = (
            lax.all_gather(tokens[batch_index], "head", axis=1, tiled=True),
            lax.all_gather(cotangent[batch_index], "head", axis=1, tiled=True),
        )
        gains32 = full_gains.astype(jnp.float32)
        biases32 = full_biases.astype(jnp.float32)
        upb32 = full_upb.astype(jnp.float32).reshape(-1)
        inputs32 = input_rows.astype(jnp.float32)
        place_items = item_numbers(lengths[batch_index], first_token - 1, local_rows + 1)
        item_of = place_items[1:]
        carried = (item_of == place_items[0]).astype(jnp.float32)
        tail_mask = (item_of == item_of[local_rows - 1]).astype(jnp.float32)
        through = carried[local_rows - 1]
        same_item = ((item_of[:, None] == item_of[None, :]) & before).astype(jnp.float32)
        keep_half = pixel_mask[batch_index].astype(jnp.bfloat16)
        keep32 = pixel_mask[batch_index].astype(jnp.float32)
        lifted, unit_one, inverse_one = normalize(inputs32, gains32[0], biases32[0])
        normed = lifted.astype(jnp.bfloat16)
        projected = jnp.einsum("td,dsf->tsf", normed, full_qkv, preferred_element_type=jnp.float32)
        query_feat = (
            features(projected[:, 0]).astype(jnp.bfloat16).reshape(local_rows, heads_here, DH)
        )
        key_feat = (features(projected[:, 1]).astype(jnp.bfloat16) * keep_half[:, None]).reshape(
            local_rows, heads_here, DH
        )
        value_feat = projected[:, 2].astype(jnp.bfloat16).reshape(local_rows, heads_here, DH)
        tail_key = key_feat * tail_mask.astype(jnp.bfloat16)[:, None, None]
        state_loc = jnp.einsum(
            "jhd,jhe->hde", tail_key, value_feat, preferred_element_type=jnp.float32
        )
        total_loc = jnp.sum(tail_key.astype(jnp.float32), axis=0)
        identity = (jnp.zeros_like(state_loc), jnp.zeros_like(total_loc), jnp.ones((), jnp.float32))
        state_in, total_in, passed = entering(
            (state_loc, total_loc, through), "seq", compose, identity
        )
        query32 = query_feat.astype(jnp.float32)
        scores = (
            jnp.einsum("thd,jhd->htj", query_feat, key_feat, preferred_element_type=jnp.float32)
            * same_item[None]
        )
        scores_low = scores.astype(jnp.bfloat16)
        numerator = jnp.einsum(
            "htj,jhe->the", scores_low, value_feat, preferred_element_type=jnp.float32
        ) + carried[:, None, None] * jnp.einsum(
            "thd,hde->the", query32, state_in, precision=highest
        )
        denominator = jnp.sum(scores, axis=2).T + carried[:, None] * jnp.einsum(
            "thd,hd->th", query32, total_in, precision=highest
        )
        output, finish_back = jax.vjp(finish, numerator, denominator)
        mixed_out = output.reshape(local_rows, local_width).astype(jnp.bfloat16)
        attended = lax.psum(
            jnp.einsum("tf,df->td", mixed_out, full_out, preferred_element_type=jnp.float32).astype(
                jnp.bfloat16
            ),
            "head",
        ).astype(jnp.float32)
        middle = inputs32 + attended
        lifted_two, unit_two, inverse_two = normalize(middle, gains32[1], biases32[1])
        normed_two = lifted_two.astype(jnp.bfloat16)
        hidden = jnp.dot(normed_two, full_up, preferred_element_type=jnp.float32) + upb32
        activated32, gelu_back = jax.vjp(jax.nn.gelu, hidden)
        activated = activated32.astype(jnp.bfloat16)
        branch = lax.psum_scatter(
            jnp.einsum(
                "tf,df->td", activated, full_down, preferred_element_type=jnp.float32
            ).astype(jnp.bfloat16),
            "head",
            scatter_dimension=1,
            tiled=True,
        ).astype(jnp.float32)
        results.append(own_columns(middle) + branch + own_columns(biases32[2][None]))
        grad_out = grad_rows16.astype(jnp.float32)
        grad_down = jnp.einsum(
            "td,tf->df", grad_rows16, activated, preferred_element_type=jnp.float32
        )
        grad_act = jnp.einsum(
            "td,df->tf", grad_rows16, full_down, preferred_element_type=jnp.float32
        )
        grad_hidden = gelu_back(grad_act)[0].astype(jnp.bfloat16)
        grad_up = jnp.einsum(
            "td,tf->df", normed_two, grad_hidden, preferred_element_type=jnp.float32
        )
        grad_upb = jnp.sum(grad_hidden.astype(jnp.float32), axis=0).reshape(full_upb.shape)
        grad_two = lax.psum(
            jnp.einsum(
                "tf,df->td", grad_hidden, full_up, preferred_element_type=jnp.float32
            ).astype(jnp.bfloat16),
            "head",
        ).astype(jnp.float32)
        grad_middle = grad_out + norm_back(grad_two, unit_two, inverse_two, gains32[1])
        grad_attended = grad_middle.astype(jnp.bfloat16)
        grad_out_t = jnp.einsum(
            "td,tf->df", grad_attended, mixed_out, preferred_element_type=jnp.float32
        )
        grad_mixed = jnp.einsum(
            "td,df->tf", grad_attended, full_out, preferred_element_type=jnp.float32
        ).reshape(local_rows, heads_here, DH)
        grad_numer32, grad_denom = finish_back(grad_mixed)
        grad_numer = grad_numer32.astype(jnp.bfloat16)
        grad_numer_wide = grad_numer.astype(jnp.float32)
        grad_scores = (
            (
                jnp.einsum(
                    "the,jhe->htj", grad_numer, value_feat, preferred_element_type=jnp.float32
                )
                + grad_denom.T[:, :, None]
            )
            * same_item[None]
        ).astype(jnp.bfloat16)
        carried_query = query32 * carried[:, None, None]
        grad_query = jnp.einsum(
            "htj,jhd->thd", grad_scores, key_feat, preferred_element_type=jnp.float32
        ) + carried[:, None, None] * (
            jnp.einsum("hde,the->thd", state_in, grad_numer_wide, precision=highest)
            + grad_denom[:, :, None] * total_in[None]
        )
        grad_key = jnp.einsum(
            "htj,thd->jhd", grad_scores, query_feat, preferred_element_type=jnp.float32
        )
        grad_value = jnp.einsum(
            "htj,the->jhe", scores_low, grad_numer, preferred_element_type=jnp.float32
        )
        grad_state_in = jnp.einsum(
            "thd,the->hde", carried_query, grad_numer_wide, precision=highest
        )
        grad_total_in = jnp.einsum("thd,th->hd", carried_query, grad_denom, precision=highest)
        grad_state_loc, grad_total_loc, passed_back = entering_2(
            (grad_state_in, grad_total_in, through), "seq", compose, identity
        )
        tail_three = tail_mask[:, None, None]
        value_wide = value_feat.astype(jnp.float32)
        key_wide = key_feat.astype(jnp.float32)
        grad_key = grad_key + tail_three * (
            jnp.einsum("hde,jhe->jhd", grad_state_loc, value_wide, precision=highest)
            + grad_total_loc[None]
        )
        grad_value = grad_value + tail_three * jnp.einsum(
            "jhd,hde->jhe", key_wide, grad_state_loc, precision=highest
        )
        ignored, feature_back = jax.vjp(features, projected[:, :2])
        grad_features = jnp.stack(
            [
                grad_query.reshape(local_rows, local_width),
                grad_key.reshape(local_rows, local_width) * keep32[:, None],
            ],
            axis=1,
        )
        grad_pair = feature_back(grad_features)[0]
        grad_projected = jnp.concatenate(
            [grad_pair, grad_value.reshape(local_rows, 1, local_width)], axis=1
        ).astype(jnp.bfloat16)
        grad_qkv = jnp.einsum(
            "td,tsf->dsf", normed, grad_projected, preferred_element_type=jnp.float32
        )
        grad_one = lax.psum(
            jnp.einsum(
                "tsf,dsf->td", grad_projected, full_qkv, preferred_element_type=jnp.float32
            ).astype(jnp.bfloat16),
            "head",
        ).astype(jnp.float32)
        grad_inputs = grad_middle + norm_back(grad_one, unit_one, inverse_one, gains32[0])
        input_grads.append(own_columns(grad_inputs))
        grad_gains = jnp.stack(
            [jnp.sum(grad_one * unit_one, axis=0), jnp.sum(grad_two * unit_two, axis=0)]
        )
        grad_biases = jnp.stack(
            [jnp.sum(grad_one, axis=0), jnp.sum(grad_two, axis=0), jnp.sum(grad_out, axis=0)]
        )
        pieces = (
            lax.psum_scatter(grad_qkv, "seq", scatter_dimension=0, tiled=True),
            lax.psum_scatter(grad_out_t, "seq", scatter_dimension=0, tiled=True),
            lax.psum_scatter(grad_up, "seq", scatter_dimension=0, tiled=True),
            lax.psum_scatter(grad_down, "seq", scatter_dimension=0, tiled=True),
            lax.psum_scatter(grad_gains, "seq", scatter_dimension=1, tiled=True),
            lax.psum_scatter(grad_biases, "seq", scatter_dimension=1, tiled=True),
            lax.psum_scatter(grad_upb, "seq", scatter_dimension=1, tiled=True),
        )
        shard_sums = pieces if shard_sums is None else jax.tree.map(jnp.add, shard_sums, pieces)
    return (
        jnp.stack(results),
        jnp.stack(input_grads),
        shard_sums[0],
        shard_sums[1],
        shard_sums[2],
        shard_sums[3],
        shard_sums[4],
        shard_sums[5],
        shard_sums[6],
    )


MESH = pl.DeviceIdType.MESH
BF = jnp.bfloat16
F32 = jnp.float32
QKV, OUT, UP, DOWN = range(4)


def dot_nn(a, b):
    return lax.dot_general(a, b, (((1,), (0,)), ((), ())), preferred_element_type=F32)


def dot_nt(a, b):
    return lax.dot_general(a, b, (((1,), (1,)), ((), ())), preferred_element_type=F32)


def dot_tn(a, b):
    return lax.dot_general(a, b, (((0,), (0,)), ((), ())), preferred_element_type=F32)


def ds(start, size):
    return pl.ds(pl.multiple_of(start, size), size)


def loop(count, body):
    def step(i, carry):
        body(i)
        return carry

    lax.fori_loop(0, count, step, 0)


def layout(n, m, batches, rows, width, local, hidden):
    tokens = batches * rows
    block = width // n
    own = tokens // m
    hops = n // 2
    heads = local // DH
    vm = {
        "xg": ((batches, rows, width), BF),
        "cg": ((batches, rows, width), BF),
        "wq": ((3, width, local), BF),
        "wo": ((width, local), BF),
        "wu": ((width, hidden), BF),
        "wd": ((width, hidden), BF),
        "small": ((8, block), F32),
        "smallg": ((8, width), F32),
        "normed": ((tokens, width), BF),
        "phi_d": ((2, tokens, local), F32),
        "qf": ((tokens, local), BF),
        "kf": ((tokens, local), BF),
        "vf": ((tokens, local), BF),
        "mask": ((batches, rows, rows), F32),
        "car": ((batches, rows, local), F32),
        "tail": ((batches, rows, local), F32),
        "pmc": ((batches, rows, local), F32),
        "low": ((batches, rows, heads * rows), BF),
        "numer": ((tokens, local), F32),
        "denom": ((tokens, local), F32),
        "mixed": ((tokens, local), BF),
        "st_send": ((batches, DH + 16, local), BF),
        "st_recv": ((2, batches, DH + 16, local), BF),
        "gs_send": ((batches, DH + 16, local), BF),
        "gs_recv": ((2, batches, DH + 16, local), BF),
        "middle": ((own, width), F32),
        "ntwo": ((tokens, width), BF),
        "gelu_d": ((tokens, hidden), F32),
        "activ": ((tokens, hidden), BF),
        "g_hid": ((tokens, hidden), BF),
        "branch": ((own, width), F32),
        "total": ((own, width), F32),
        "g_mid": ((own, width), F32),
        "gatt": ((tokens, width), BF),
        "g_attn": ((tokens, local), F32),
        "g_num": ((tokens, local), BF),
        "g_den": ((tokens, local), F32),
        "gq": ((tokens, local), F32),
        "gk": ((tokens, local), F32),
        "gv": ((tokens, local), F32),
        "gproj": ((3, tokens, local), BF),
        "h_s1": ((4, 2, own, width), BF),
        "h_r1": ((4, 2, own, width), BF),
        "h_acc": ((4, 2, own, width), F32),
        "h_s2": ((4, own, width), BF),
        "h_r2": ((4, own, width), BF),
        "rq_s": ((2, 2, hops, 3, block, local // 2), BF),
        "rq_r": ((2, 2, hops, 3, block, local // 2), BF),
        "ro_s": ((2, 2, hops, block, local // 2), BF),
        "ro_r": ((2, 2, hops, block, local // 2), BF),
        "ru_s": ((2, 2, hops, block, hidden // 2), BF),
        "ru_r": ((2, 2, hops, block, hidden // 2), BF),
        "rd_s": ((2, 2, hops, block, hidden // 2), BF),
        "rd_r": ((2, 2, hops, block, hidden // 2), BF),
        "fq": ((3, block, local), F32),
        "fo": ((block, local), F32),
        "fu": ((block, hidden), F32),
        "fd": ((block, hidden), F32),
        "hs_recv": ((m, 8, width), F32),
        "hs_send": ((8, width), F32),
        "upb": ((1, hidden), F32),
        "sg": ((8, width), F32),
        "ss_recv": ((n, 8, block), F32),
        "a_rows": ((own, width), F32),
        "i_rows": ((own, width), F32),
    }
    sems = {
        "ag_s": (4, 2, 2, hops),
        "ag_r": (4, 2, 2, hops),
        "rs_s": (4, 2, 2, hops),
        "rs_r": (4, 2, 2, hops),
        "hg_s": (4, 3),
        "hg_r": (4, 3),
        "hr_s": (4, 2),
        "hr_r": (4, 2),
        "st_s": (2, 2),
        "st_r": (2, 2),
        "sm_s": (n,),
        "sm_r": (n,),
        "aa_s": (2, m),
        "aa_r": (2, m),
        "hs_s": (m,),
        "hs_r": (m,),
        "ss_s": (n,),
        "ss_r": (n,),
        "lc": (12,),
    }
    return vm, sems


class Refs:
    pass


def body(n, m, names, *refs):
    r = Refs()
    for name, ref in zip(names, refs):
        setattr(r, name, ref)
    batches, rows, width = r.xg.shape
    tokens = batches * rows
    own = tokens // m
    block = width // n
    local = r.wo.shape[1]
    hidden = r.wu.shape[1]
    heads = local // DH
    hops = n // 2
    s = lax.axis_index("seq")
    h = lax.axis_index("head")
    odd = lax.rem(s, 2)
    p = (1 - odd) * lax.div(s, 2) + odd * (n - 1 - lax.div(s, 2))
    lo, hi = lax.rem(h, 2), lax.div(h, 2)
    pair = h + 1 - 2 * lo
    cross = lax.rem(h + 2, m)

    def at(place):
        place = lax.rem(place + 2 * n, n)
        far = lax.div(place, hops)
        return (1 - far) * 2 * place + far * (2 * (n - 1 - place) + 1)

    ring = (at(p + 1), at(p - 1))
    sign = (1, -1)

    def remote(src, dst, send, recv, seq, head):
        return pltpu.make_async_remote_copy(
            src_ref=src,
            dst_ref=dst,
            send_sem=send,
            recv_sem=recv,
            device_id=(seq, head),
            device_id_type=MESH,
        )

    sent = []

    def launch(copy):
        copy.start()
        sent.append(copy)

    r.small[...] = jnp.zeros_like(r.small)
    r.small[0:2, :] = r.gains[...].astype(F32)
    r.small[2:5, :] = r.biases[...].astype(F32)
    r.small[5:6, :] = r.up_bias[...].astype(F32)

    barrier = pltpu.get_barrier_semaphore()
    for i in range(1, n):
        pl.semaphore_signal(
            barrier, inc=1, device_id=(lax.rem(s + i, n), h), device_id_type=MESH
        )
    for i in range(1, m):
        pl.semaphore_signal(
            barrier, inc=1, device_id=(s, lax.rem(h + i, m)), device_id_type=MESH
        )
    pl.semaphore_wait(barrier, n - 1 + m - 1)

    shards = (r.w_qkv, r.w_out, r.w_up, r.w_down)
    gathered = (r.wq, r.wo, r.wu, r.wd)

    def shard_piece(w, piece):
        half = shards[w].shape[-1] // 2
        cols = pl.ds(piece * half, half)
        return shards[w].at[:, :, cols] if w == QKV else shards[w].at[:, cols]

    def full_piece(w, owner, piece):
        half = gathered[w].shape[-1] // 2
        cols = pl.ds(piece * half, half)
        if w == QKV:
            return gathered[w].at[:, ds(owner * block, block), cols]
        return gathered[w].at[ds(owner * block, block), cols]

    def lanes():
        return [(piece, d) for piece in (0, 1) for d in (0, 1)]

    def reach(piece, d):
        return hops if piece == d else hops - 1

    def ag_send(w, j):
        for piece, d in lanes():
            if j < reach(piece, d):
                owner = at(p - sign[d] * j)
                src = shard_piece(w, piece) if j == 0 else full_piece(w, owner, piece)
                launch(
                    remote(
                        src,
                        full_piece(w, owner, piece),
                        r.ag_s.at[w, piece, d, j],
                        r.ag_r.at[w, piece, d, j],
                        ring[d],
                        h,
                    )
                )

    def ag_wait(w, j):
        for piece, d in lanes():
            if j < reach(piece, d):
                view = full_piece(w, at(p - sign[d] * (j + 1)), piece)
                remote(
                    view, view, r.ag_s.at[w, piece, d, j], r.ag_r.at[w, piece, d, j], ring[d], h
                ).wait_recv()

    def ag_pass(w, j):
        ag_wait(w, j)
        ag_send(w, j + 1)

    def hg_view(k, who):
        if k < 2:
            return (r.xg, r.cg)[k].at[:, :, ds(who * local, local)]
        return (r.ntwo, r.gatt)[k - 2].at[ds(who * own, own), :]

    def hg_copy(k, i, src, who, to):
        return remote(src, hg_view(k, who), r.hg_s.at[k, i], r.hg_r.at[k, i], s, to)

    def hg_start(k, src):
        launch(hg_copy(k, 1, src, h, cross))
        launch(hg_copy(k, 0, src, h, pair))

    def hg_forward(k):
        view = hg_view(k, cross)
        hg_copy(k, 1, view, cross, cross).wait_recv()
        launch(hg_copy(k, 2, view, cross, pair))

    def hg_finish(k):
        view = hg_view(k, pair)
        hg_copy(k, 0, view, pair, pair).wait_recv()
        across = lax.rem(pair + 2, m)
        view = hg_view(k, across)
        hg_copy(k, 2, view, across, pair).wait_recv()

    def hr_rows(who):
        return ds(who * own, own)

    def hr_first(k, term):
        for q in (0, 1):
            who = 2 * q + 1 - lo
            term(hr_rows(who), lambda cols, v, q=q: put(r.h_s1.at[k, q], cols, v))
        launch(remote(r.h_s1.at[k], r.h_r1.at[k], r.hr_s.at[k, 0], r.hr_r.at[k, 0], s, pair))
        for q in (0, 1):
            who = 2 * q + lo
            term(hr_rows(who), lambda cols, v, q=q: put(r.h_acc.at[k, q], cols, v))

    def put(ref, cols, value):
        ref[:, cols] = value.astype(ref.dtype)

    def hr_second(k):
        remote(
            r.h_s1.at[k], r.h_r1.at[k], r.hr_s.at[k, 0], r.hr_r.at[k, 0], s, pair
        ).wait_recv()
        tile = 32

        def away(i):
            rw = ds(i * tile, tile)
            r.h_s2[k, rw, :] = (
                r.h_acc[k, 1 - hi, rw, :] + r.h_r1[k, 1 - hi, rw, :].astype(F32)
            ).astype(BF)

        loop(own // tile, away)
        launch(remote(r.h_s2.at[k], r.h_r2.at[k], r.hr_s.at[k, 1], r.hr_r.at[k, 1], s, cross))

    def hr_wait(k):
        remote(
            r.h_s2.at[k], r.h_r2.at[k], r.hr_s.at[k, 1], r.hr_r.at[k, 1], s, cross
        ).wait_recv()

    def hr_value(k, rw):
        return (
            r.h_acc[k, hi, rw, :]
            + r.h_r1[k, hi, rw, :].astype(F32)
            + r.h_r2[k, rw, :].astype(F32)
        )

    def rs_term(w, owner, piece):
        cols = ds(owner * block, block)
        if w == DOWN:
            left = r.cg[:, :, cols].reshape(tokens, block)
            half = hidden // 2
            return [dot_tn(left, r.activ[:, pl.ds(piece * half, half)])]
        if w == UP:
            half = hidden // 2
            return [dot_tn(r.ntwo[:, cols], r.g_hid[:, pl.ds(piece * half, half)])]
        half = local // 2
        if w == OUT:
            return [dot_tn(r.gatt[:, cols], r.mixed[:, pl.ds(piece * half, half)])]
        left = r.normed[:, cols]
        return [dot_tn(left, r.gproj[i, :, pl.ds(piece * half, half)]) for i in range(3)]

    rs_send = (r.rq_s, r.ro_s, r.ru_s, r.rd_s)
    rs_recv = (r.rq_r, r.ro_r, r.ru_r, r.rd_r)

    def rs_copy(w, piece, d, j):
        return remote(
            rs_send[w].at[piece, d, j],
            rs_recv[w].at[piece, d, j],
            r.rs_s.at[w, piece, d, j],
            r.rs_r.at[w, piece, d, j],
            ring[d],
            h,
        )

    def rs_round(w, step):
        waiting = None
        for piece, d in lanes():
            far = reach(piece, d)
            j = step - (hops - far)
            if j < 0:
                continue
            terms = rs_term(w, at(p + sign[d] * (far - j)), piece)
            if j > 0:
                rs_copy(w, piece, d, j - 1).wait_recv()
            for i, v in enumerate(terms):
                where = (piece, d, j, i) if w == QKV else (piece, d, j)
                before = (piece, d, j - 1, i) if w == QKV else (piece, d, j - 1)
                if j > 0:
                    v = v + rs_recv[w][before].astype(F32)
                rs_send[w][where] = v.astype(BF)
            if waiting is not None:
                launch(waiting)
            waiting = rs_copy(w, piece, d, j)
        launch(waiting)

    finals = (r.fq, r.fo, r.fu, r.fd)
    results = (r.gq_o, r.go_o, r.gu_o, r.gd_o)
    local_copies = []

    def rs_final(w):
        for piece in (0, 1):
            terms = rs_term(w, s, piece)
            for d in (0, 1):
                rs_copy(w, piece, d, reach(piece, d) - 1).wait_recv()
            half = finals[w].shape[-1] // 2
            cols = pl.ds(piece * half, half)
            for i, v in enumerate(terms):
                for d in (0, 1):
                    j = reach(piece, d) - 1
                    where = (piece, d, j, i) if w == QKV else (piece, d, j)
                    v = v + rs_recv[w][where].astype(F32)
                if w == QKV:
                    finals[w][i, :, cols] = v
                else:
                    finals[w][:, cols] = v
        copy = pltpu.make_async_copy(finals[w], results[w], r.lc.at[w])
        copy.start()
        local_copies.append(copy)

    def turn(k, src, dst):
        where = (hi, ds(lo * own, own))
        for i in range(1, m):
            to = lax.rem(h + i, m)
            launch(
                remote(
                    src.at[:, ds(to * local, local)],
                    dst.at[where[0], where[1], :],
                    r.aa_s.at[k, i],
                    r.aa_r.at[k, i],
                    s,
                    to,
                )
            )
        copy = pltpu.make_async_copy(
            src.at[:, ds(h * local, local)], dst.at[where[0], where[1], :], r.lc.at[4 + k]
        )
        copy.start()
        local_copies.append(copy)

    def turn_wait(k, src, dst):
        for i in range(1, m):
            who = lax.rem(h + m - i, m)
            remote(
                src.at[:, ds(h * local, local)],
                dst.at[lax.div(who, 2), ds(lax.rem(who, 2) * own, own), :],
                r.aa_s.at[k, i],
                r.aa_r.at[k, i],
                s,
                who,
            ).wait_recv()

    ag_send(QKV, 0)
    ag_send(OUT, 0)
    hg_start(0, r.tok)
    for i in range(1, n):
        to = lax.rem(s + i, n)
        launch(
            remote(
                r.small,
                r.smallg.at[:, ds(s * block, block)],
                r.sm_s.at[i],
                r.sm_r.at[i],
                to,
                h,
            )
        )
    own_copies = [
        pltpu.make_async_copy(r.tok, hg_view(0, h), r.lc.at[6]),
        pltpu.make_async_copy(r.cot, hg_view(1, h), r.lc.at[7]),
        pltpu.make_async_copy(r.w_qkv, r.wq.at[:, ds(s * block, block), :], r.lc.at[8]),
        pltpu.make_async_copy(r.w_out, r.wo.at[ds(s * block, block), :], r.lc.at[9]),
        pltpu.make_async_copy(r.w_up, r.wu.at[ds(s * block, block), :], r.lc.at[10]),
        pltpu.make_async_copy(r.w_down, r.wd.at[ds(s * block, block), :], r.lc.at[11]),
    ]
    for copy in own_copies:
        copy.start()
    hg_start(1, r.cot)

    first = s * rows
    row_at = lax.broadcasted_iota(jnp.int32, (rows, local), 0)
    lane_at = lax.broadcasted_iota(jnp.int32, (rows, rows), 1)
    square = lax.broadcasted_iota(jnp.int32, (local, local), 0)
    square_lane = lax.broadcasted_iota(jnp.int32, (local, local), 1)
    same_head = (square // DH) == (square_lane // DH)
    diagonal = square == square_lane
    ones = jnp.ones((rows, local), BF)
    lane_head = lax.broadcasted_iota(jnp.int32, (rows, local), 1) // DH
    before_thr, after_thr = [], []

    def begin(offsets, place):
        value = 0
        for off in offsets:
            value = jnp.where(off <= place, off, value)
        return value

    def through(offsets, which):
        return jnp.where(
            begin(offsets, which * rows + rows - 1) < which * rows, 1.0, 0.0
        ).astype(F32)

    for b in range(batches):
        offsets, running = [], 0
        for i in range(r.lengths.shape[1]):
            offsets.append(running)
            running = running + r.lengths[b, i]
        start = jnp.zeros((rows, local), jnp.int32)
        for off in offsets:
            start = jnp.where(off <= row_at + first, off, start)
        last = begin(offsets, first + rows - 1)
        r.mask[b] = jnp.where(
            (lane_at + first >= start) & (lane_at <= row_at), 1.0, 0.0
        ).astype(F32)
        r.car[b] = jnp.where(start < first, 1.0, 0.0).astype(F32)
        r.tail[b] = jnp.where(start == last, 1.0, 0.0).astype(F32)
        before_thr.append(through(offsets, lax.rem(s + n - 1, n)))
        after_thr.append(through(offsets, lax.rem(s + 1, n)))
        keep = r.pixel[b : b + 1, :].astype(F32)
        r.pmc[b] = dot_nn(jnp.where(diagonal, keep, 0.0).astype(BF), ones)

    ag_pass(QKV, 0)
    ag_pass(OUT, 0)
    hg_forward(0)

    for i in range(1, n):
        who = lax.rem(s + n - i, n)
        remote(
            r.small,
            r.smallg.at[:, ds(who * block, block)],
            r.sm_s.at[i],
            r.sm_r.at[i],
            who,
            h,
        ).wait_recv()
    r.smallg[:, ds(s * block, block)] = r.small[...]
    for copy in own_copies:
        copy.wait()
    hg_finish(0)
    gain_one, gain_two = r.smallg[0:1, :], r.smallg[1:2, :]
    shift_one, shift_two, shift_out = r.smallg[2:3, :], r.smallg[3:4, :], r.smallg[4:5, :]
    up_shift = r.smallg[5:6, :]

    def unit(values):
        mean = jnp.mean(values, axis=1, keepdims=True)
        centered = values - mean
        inverse = lax.rsqrt(jnp.mean(centered * centered, axis=1, keepdims=True) + epsilon)
        return centered * inverse, inverse

    tile = 32

    def norm_one(i):
        b = lax.div(i, rows // tile)
        rw = ds(lax.rem(i, rows // tile) * tile, tile)
        u, _ = unit(r.xg[b, rw, :].astype(F32))
        r.normed[ds(i * tile, tile), :] = (u * gain_one + shift_one).astype(BF)

    ag_pass(QKV, 1)
    ag_pass(OUT, 1)
    loop(tokens // tile, norm_one)
    hg_forward(1)
    ag_pass(QKV, 2)
    ag_pass(OUT, 2)
    ag_send(UP, 0)
    ag_send(DOWN, 0)
    hg_finish(1)
    ag_wait(QKV, 3)
    ag_wait(OUT, 3)

    tm = 128

    def project(i):
        rw = ds(i * tm, tm)
        b = lax.div(i, rows // tm)
        rb = ds(lax.rem(i, rows // tm) * tm, tm)
        left = r.normed[rw, :]
        for kind in (0, 1):
            v = dot_nn(left, r.wq[kind])
            low = jnp.exp(jnp.minimum(v, 0.0))
            f = jnp.where(v > 0.0, v + 1.0, low).astype(BF)
            r.phi_d[kind, rw, :] = low
            if kind == 0:
                r.qf[rw, :] = f
            else:
                r.kf[rw, :] = (f.astype(F32) * r.pmc[b, rb, :]).astype(BF)
        r.vf[rw, :] = dot_nn(left, r.wq[2]).astype(BF)

    loop(tokens // tm, project)

    def fold(matrix, total):
        kept = jnp.where(same_head, matrix, 0.0)
        acc = kept[0:DH]
        for i in range(1, heads):
            acc = acc + kept[i * DH : (i + 1) * DH]
        top = lax.broadcasted_iota(jnp.int32, (16, local), 0) == 0
        return acc.astype(BF), jnp.where(top, total, 0.0).astype(BF)

    def unfold(ref):
        acc = ref[0:DH, :].astype(F32)
        wide = jnp.concatenate([acc] * heads, axis=0)
        return jnp.where(same_head, wide, 0.0).astype(BF)

    def state_send(k, ref, dest, step):
        for i in (0, 1):
            to = lax.rem(s + n + step * (i + 1), n)
            launch(remote(ref, dest.at[i], r.st_s.at[k, i], r.st_r.at[k, i], to, h))

    def state_wait(k, ref, dest, step):
        for i in (0, 1):
            to = lax.rem(s + n + step * (i + 1), n)
            remote(ref, dest.at[i], r.st_s.at[k, i], r.st_r.at[k, i], to, h).wait_recv()

    def rows_of(b):
        return pl.ds(b * rows, rows)

    def by_head(value):
        return jnp.concatenate(
            [jnp.where(lane_head == hd, value.astype(F32), 0.0).astype(BF) for hd in range(heads)],
            axis=0,
        )

    for b in range(batches):
        k = r.kf[rows_of(b), :].astype(F32) * r.tail[b]
        moved = dot_tn(k.astype(BF), r.vf[rows_of(b), :])
        a, t = fold(moved, jnp.sum(k, axis=0, keepdims=True))
        r.st_send[b, 0:DH, :] = a
        r.st_send[b, DH:, :] = t
    state_send(0, r.st_send, r.st_recv, 1)

    for b in range(batches):
        q, k = r.qf[rows_of(b), :], r.kf[rows_of(b), :]
        acc = jnp.zeros((rows, local), F32)
        for hd in range(heads):
            sc = dot_nt(jnp.where(lane_head == hd, q.astype(F32), 0.0).astype(BF), k) * r.mask[b]
            r.low[b, :, hd * rows : (hd + 1) * rows] = sc.astype(BF)
            acc = acc + jnp.where(lane_head == hd, jnp.sum(sc, axis=1, keepdims=True), 0.0)
        r.denom[rows_of(b), :] = acc
        r.numer[rows_of(b), :] = dot_nn(r.low[b], by_head(r.vf[rows_of(b), :]))

    ag_pass(UP, 0)
    ag_pass(DOWN, 0)
    state_wait(0, r.st_send, r.st_recv, 1)

    def both(b, value, thr):
        one = value.astype(F32) * r.car[b]
        return jnp.concatenate([one.astype(BF), (one * thr).astype(BF)], axis=1)

    for b in range(batches):
        left = both(b, r.qf[rows_of(b), :], before_thr[b])
        states = jnp.concatenate([unfold(r.st_recv.at[i, b]) for i in (0, 1)], axis=0)
        sums = jnp.concatenate(
            [
                jnp.where(
                    same_head,
                    dot_tn(r.st_recv[i, b, DH:, :], jnp.ones((16, local), BF)),
                    0.0,
                ).astype(BF)
                for i in (0, 1)
            ],
            axis=0,
        )
        top = r.numer[rows_of(b), :] + dot_nn(left, states)
        bottom = r.denom[rows_of(b), :] + dot_nn(left, sums)
        attn = top / jnp.maximum(bottom, 1.0)
        r.numer[rows_of(b), :] = attn
        r.denom[rows_of(b), :] = bottom
        r.mixed[rows_of(b), :] = attn.astype(BF)

    tn = 256

    def product_nt(left_ref, right_ref):
        def term(rw, store):
            def part(i):
                cols = ds(i * tn, tn)
                store(cols, dot_nt(left_ref[rw, :], right_ref[cols, :]))

            loop(width // tn, part)

        return term

    hr_first(0, product_nt(r.mixed, r.wo))
    hr_second(0)
    ag_pass(UP, 1)
    ag_pass(DOWN, 1)
    hr_wait(0)
    mine = h * own

    def x_rows(i):
        return r.xg[hi, ds(lo * own + i * tile, tile), :].astype(F32)

    def c_rows(i):
        return r.cg[hi, ds(lo * own + i * tile, tile), :].astype(F32)

    def norm_two(i):
        rw = ds(i * tile, tile)
        v = x_rows(i) + hr_value(0, rw)
        r.middle[rw, :] = v
        u, _ = unit(v)
        r.ntwo[ds(mine + i * tile, tile), :] = (u * gain_two + shift_two).astype(BF)

    loop(own // tile, norm_two)
    hg_start(2, hg_view(2, h))
    ag_pass(UP, 2)
    ag_pass(DOWN, 2)
    hg_forward(2)
    hg_finish(2)
    ag_wait(UP, 3)

    ft = 256

    def up(i):
        rw = ds(lax.div(i, hidden // ft) * tm, tm)
        cols = ds(lax.rem(i, hidden // ft) * ft, ft)
        v = dot_nn(r.ntwo[rw, :], r.wu[:, cols]) + r.smallg[5:6, cols]
        cube = 0.7978845608028654 * (v + 0.044715 * (v * v * v))
        t = jnp.tanh(cube)
        r.activ[rw, cols] = (0.5 * v * (1.0 + t)).astype(BF)
        r.gelu_d[rw, cols] = 0.5 * (1.0 + t) + 0.5 * v * (1.0 - t * t) * (
            0.7978845608028654 * (1.0 + 3.0 * 0.044715 * (v * v))
        )

    loop((tokens // tm) * (hidden // ft), up)
    rs_round(DOWN, 0)
    ag_wait(DOWN, 3)

    def back(i):
        rw = ds(lax.div(i, hidden // ft) * tm, tm)
        cols = ds(lax.rem(i, hidden // ft) * ft, ft)
        b = lax.div(lax.div(i, hidden // ft), rows // tm)
        rb = ds(lax.rem(lax.div(i, hidden // ft), rows // tm) * tm, tm)
        g = dot_nn(r.cg[b, rb, :], r.wd[:, cols])
        r.g_hid[rw, cols] = (g * r.gelu_d[rw, cols]).astype(BF)

    loop((tokens // tm) * (hidden // ft), back)
    hr_first(2, product_nt(r.g_hid, r.wu))
    hr_second(2)
    rs_round(UP, 0)
    rs_round(DOWN, 1)
    hr_wait(2)

    r.hs_send[...] = jnp.zeros_like(r.hs_send)

    def back_norm(g, u, inverse, gain):
        scaled = g * gain
        centered = scaled - jnp.mean(scaled, axis=1, keepdims=True)
        return inverse * (centered - u * jnp.mean(scaled * u, axis=1, keepdims=True))

    def norm_two_back(i):
        rw = ds(i * tile, tile)
        g = hr_value(2, rw)
        u, inverse = unit(r.middle[rw, :])
        out = c_rows(i)
        v = out + back_norm(g, u, inverse, gain_two)
        r.g_mid[rw, :] = v
        r.gatt[ds(mine + i * tile, tile), :] = v.astype(BF)
        r.hs_send[1:2, :] += jnp.sum(g * u, axis=0, keepdims=True)
        r.hs_send[3:4, :] += jnp.sum(g, axis=0, keepdims=True)
        r.hs_send[4:5, :] += jnp.sum(out, axis=0, keepdims=True)

    loop(own // tile, norm_two_back)
    hg_start(3, hg_view(3, h))
    hr_first(1, product_nt(r.activ, r.wd))
    rs_round(UP, 1)
    hg_forward(3)
    hr_second(1)
    rs_round(DOWN, 2)
    hg_finish(3)

    def mixed_back(i):
        rw = ds(i * tm, tm)
        g = dot_nn(r.gatt[rw, :], r.wo[...])
        attn, bottom = r.numer[rw, :], r.denom[rw, :]
        r.g_num[rw, :] = (g / jnp.maximum(bottom, 1.0)).astype(BF)
        prod = g * attn
        lh = lane_head[:tm]
        acc = jnp.zeros((tm, local), F32)
        for hd in range(heads):
            acc = acc + jnp.where(
                lh == hd,
                jnp.sum(jnp.where(lh == hd, prod, 0.0), axis=1, keepdims=True),
                0.0,
            )
        r.g_den[rw, :] = jnp.where(bottom > 1.0, -acc / jnp.maximum(bottom, 1.0), 0.0)

    loop(tokens // tm, mixed_back)

    for b in range(batches):
        q = r.qf[rows_of(b), :].astype(F32) * r.car[b]
        moved = dot_tn(q.astype(BF), r.g_num[rows_of(b), :])
        a, t = fold(moved, jnp.sum(q * r.g_den[rows_of(b), :], axis=0, keepdims=True))
        r.gs_send[b, 0:DH, :] = a
        r.gs_send[b, DH:, :] = t
    state_send(1, r.gs_send, r.gs_recv, -1)
    rs_round(OUT, 0)

    def head_lanes(hd, value):
        return jnp.where(lane_head == hd, value.astype(F32), 0.0).astype(BF)

    for b in range(batches):
        rw = rows_of(b)
        gk = jnp.zeros((rows, local), F32)
        gv = jnp.zeros((rows, local), F32)
        gq = jnp.zeros((rows, local), F32)
        for hd in range(heads):
            gn = head_lanes(hd, r.g_num[rw, :])
            g = dot_nt(gn, r.vf[rw, :]) + r.g_den[rw, hd * DH : hd * DH + 1]
            g = (g * r.mask[b]).astype(BF)
            gq = gq + dot_nn(g, head_lanes(hd, r.kf[rw, :]))
            gk = gk + dot_tn(g, head_lanes(hd, r.qf[rw, :]))
            gv = gv + dot_tn(r.low[b, :, hd * rows : (hd + 1) * rows], gn)
        left = both(b, r.g_num[rw, :], before_thr[b])
        states = jnp.concatenate([unfold(r.st_recv.at[i, b]) for i in (0, 1)], axis=1)
        totals = (
            r.st_recv[0, b, DH : DH + 16, :].astype(F32)[0:1]
            + before_thr[b] * r.st_recv[1, b, DH : DH + 16, :].astype(F32)[0:1]
        )
        gq = gq + dot_nt(left, states) + r.car[b] * r.g_den[rw, :] * totals
        r.gproj[0, rw, :] = (gq * r.phi_d[0, rw, :]).astype(BF)
        r.gk[rw, :] = gk
        r.gv[rw, :] = gv

    rs_round(OUT, 1)
    rs_round(UP, 2)
    state_wait(1, r.gs_send, r.gs_recv, -1)
    for b in range(batches):
        rw = rows_of(b)
        thr = after_thr[b]
        states = [unfold(r.gs_recv.at[i, b]) for i in (0, 1)]
        totals = (
            r.gs_recv[0, b, DH : DH + 16, :].astype(F32)[0:1]
            + thr * r.gs_recv[1, b, DH : DH + 16, :].astype(F32)[0:1]
        )
        k = r.kf[rw, :].astype(F32) * r.tail[b]
        v = r.vf[rw, :].astype(F32) * r.tail[b]
        k2 = jnp.concatenate([k.astype(BF), (k * thr).astype(BF)], axis=1)
        v2 = jnp.concatenate([v.astype(BF), (v * thr).astype(BF)], axis=1)
        gk = r.gk[rw, :] + dot_nt(v2, jnp.concatenate(states, axis=1)) + r.tail[b] * totals
        gv = r.gv[rw, :] + dot_nn(k2, jnp.concatenate(states, axis=0))
        r.gproj[1, rw, :] = (gk * r.pmc[b] * r.phi_d[1, rw, :]).astype(BF)
        r.gproj[2, rw, :] = gv.astype(BF)

    def first_term(rw, store):
        def part(i):
            cols = ds(i * tn, tn)
            v = dot_nt(r.gproj[0, rw, :], r.wq[0, cols, :])
            for kind in (1, 2):
                v = v + dot_nt(r.gproj[kind, rw, :], r.wq[kind, cols, :])
            store(cols, v)

        loop(width // tn, part)

    hr_first(3, first_term)
    hr_second(3)
    rs_round(QKV, 0)
    rs_round(DOWN, 3)
    rs_round(OUT, 2)
    rs_round(UP, 3)
    rs_round(QKV, 1)

    hr_wait(1)

    def finish_rows(i):
        rw = ds(i * tile, tile)
        r.a_rows[rw, :] = r.middle[rw, :] + hr_value(1, rw) + shift_out

    loop(own // tile, finish_rows)
    turn(0, r.a_rows, r.act_o)

    hr_wait(3)

    def norm_one_back(i):
        rw = ds(i * tile, tile)
        g = hr_value(3, rw)
        u, inverse = unit(x_rows(i))
        r.i_rows[rw, :] = r.g_mid[rw, :] + back_norm(g, u, inverse, gain_one)
        r.hs_send[0:1, :] += jnp.sum(g * u, axis=0, keepdims=True)
        r.hs_send[2:3, :] += jnp.sum(g, axis=0, keepdims=True)

    loop(own // tile, norm_one_back)
    turn(1, r.i_rows, r.ing_o)

    r.hs_recv[h] = r.hs_send[...]
    for i in range(1, m):
        launch(
            remote(r.hs_send, r.hs_recv.at[h], r.hs_s.at[i], r.hs_r.at[i], s, lax.rem(h + i, m))
        )
    r.upb[...] = jnp.zeros_like(r.upb)

    def column_sums(i):
        r.upb[...] += jnp.sum(r.g_hid[ds(i * tile, tile), :].astype(F32), axis=0, keepdims=True)

    loop(tokens // tile, column_sums)
    rs_round(OUT, 3)
    rs_round(QKV, 2)
    for i in range(1, m):
        who = lax.rem(h + m - i, m)
        remote(r.hs_send, r.hs_recv.at[who], r.hs_s.at[i], r.hs_r.at[i], s, who).wait_recv()
    acc = r.hs_recv[0]
    for i in range(1, m):
        acc = acc + r.hs_recv[i]
    r.sg[...] = acc
    r.sg[5:6, :] = r.upb[...]
    r.ss_recv[s] = r.sg[:, ds(s * block, block)]
    rs_final(DOWN)
    for i in range(1, n):
        to = lax.rem(s + i, n)
        launch(
            remote(
                r.sg.at[:, ds(to * block, block)],
                r.ss_recv.at[s],
                r.ss_s.at[i],
                r.ss_r.at[i],
                to,
                h,
            )
        )
    rs_round(QKV, 3)
    rs_final(UP)
    rs_final(OUT)
    for i in range(1, n):
        who = lax.rem(s + n - i, n)
        remote(
            r.sg.at[:, ds(s * block, block)],
            r.ss_recv.at[who],
            r.ss_s.at[i],
            r.ss_r.at[i],
            who,
            h,
        ).wait_recv()
    acc = r.ss_recv[0]
    for i in range(1, n):
        acc = acc + r.ss_recv[i]
    r.gg_o[...] = acc[0:2]
    r.gb_o[...] = acc[2:5]
    r.gup_o[...] = acc[5:6]
    rs_final(QKV)
    turn_wait(0, r.a_rows, r.act_o)
    turn_wait(1, r.i_rows, r.ing_o)
    for copy in local_copies:
        copy.wait()
    for copy in sent:
        copy.wait_send()


def whole_layer(n, m):
    def on_each(
        tokens, cotangent, w_qkv, w_out_t, w_up, w_down_t, gains, biases, up_bias, lengths, pixel_mask
    ):
        batches, rows, local = tokens.shape
        width = w_qkv.shape[0] * n
        hidden = w_up.shape[1]
        block = width // n
        vm, sems = layout(n, m, batches, rows, width, local, hidden)
        ins = ["tok", "cot", "w_qkv", "w_out", "w_up", "w_down", "gains", "biases", "up_bias", "lengths", "pixel"]
        outs = ["act_o", "ing_o", "gq_o", "go_o", "gu_o", "gd_o", "gg_o", "gb_o", "gup_o"]
        anywhere = pl.BlockSpec(memory_space=pl.ANY)
        in_vmem = pl.BlockSpec(memory_space=pltpu.VMEM)
        in_smem = pl.BlockSpec(memory_space=pltpu.SMEM)

        def wide(*shape):
            return jax.ShapeDtypeStruct(shape, F32)

        result = pl.pallas_call(
            functools.partial(body, n, m, ins + outs + list(vm) + list(sems)),
            name="layer",
            out_shape=(
                wide(batches, rows, local),
                wide(batches, rows, local),
                wide(3, block, local),
                wide(block, local),
                wide(block, hidden),
                wide(block, hidden),
                wide(2, block),
                wide(3, block),
                wide(1, block),
            ),
            in_specs=[anywhere] * 6 + [in_vmem] * 3 + [in_smem, in_vmem],
            out_specs=[anywhere] * 6 + [in_vmem] * 3,
            scratch_shapes=[pltpu.VMEM(shape, kind) for shape, kind in vm.values()]
            + [pltpu.SemaphoreType.DMA(shape) for shape in sems.values()],
            compiler_params=pltpu.CompilerParams(
                collective_id=0, has_side_effects=True, vmem_limit_bytes=66_000_000
            ),
        )(
            tokens,
            cotangent,
            jnp.transpose(w_qkv, (1, 0, 2)),
            w_out_t,
            w_up,
            w_down_t,
            gains,
            biases,
            up_bias,
            lengths,
            pixel_mask,
        )
        return result[:2] + (jnp.transpose(result[2], (1, 0, 2)),) + result[3:]

    return on_each


def solution(mesh):
    in_specs = (
        P(None, "seq", "head"),
        P(None, "seq", "head"),
        P("seq", None, "head"),
        P("seq", "head"),
        P("seq", "head"),
        P("seq", "head"),
        P(None, "seq"),
        P(None, "seq"),
        P("head", "seq"),
        P(),
        P(None, "seq"),
    )
    out_specs = (
        P(None, "seq", "head"),
        P(None, "seq", "head"),
        P("seq", None, "head"),
        P("seq", "head"),
        P("seq", "head"),
        P("seq", "head"),
        P(None, "seq"),
        P(None, "seq"),
        P("head", "seq"),
    )
    n, m = mesh.shape["seq"], mesh.shape["head"]
    fits = (n, m) == (8, 4)
    return jax.shard_map(
        whole_layer(n, m) if fits else on_device, mesh=mesh, in_specs=in_specs, out_specs=out_specs, check_vma=False
    )
```

```python
import functools

import jax
import jax.numpy as jnp
from jax import lax
from jax.experimental import pallas as pl
from jax.experimental.pallas import tpu as pltpu
from jax.sharding import PartitionSpec as P

DH = 64


highest = lax.Precision.HIGHEST
epsilon = 1e-05


def entering(array, axis, join, neutral):
    place = lax.axis_index(axis)
    gathered = jax.tree.map(
        lambda a, kind: lax.all_gather(a.astype(kind), axis),
        array,
        (jnp.bfloat16, jnp.bfloat16, jnp.bfloat16),
    )
    state = jax.tree.map(lambda a, e: jnp.zeros_like(a) + jnp.asarray(e, a.dtype), array, neutral)

    def one(hop, state):
        return join(
            state,
            jax.tree.map(
                lambda a, own: lax.dynamic_index_in_dim(a, hop, 0, False).astype(own.dtype),
                gathered,
                array,
            ),
        )

    return lax.fori_loop(0, place, one, state)


def entering_2(array, axis, combine, identity):
    length, place = (lax.axis_size(axis), lax.axis_index(axis))
    everything = jax.tree.map(
        lambda part, kind: lax.all_gather(part.astype(kind), axis),
        array,
        jax.tree.map(lambda a: jnp.bfloat16 if a.dtype == jnp.float32 else a.dtype, array),
    )
    start = jax.tree.map(
        lambda part, zero: jnp.broadcast_to(jnp.asarray(zero, part.dtype), part.shape),
        array,
        identity,
    )

    def hop(k, before):
        at = length - 1 - k
        reached = at > place
        new = combine(
            before, jax.tree.map(lambda part, own: part[at].astype(own.dtype), everything, array)
        )
        return jax.tree.map(lambda a, b: jnp.where(reached, a, b), new, before)

    return lax.fori_loop(0, length, hop, start)


def normalize(values, gain_vec, shift_vec):
    mean_val = jnp.mean(values, axis=-1, keepdims=True)
    centered = values - mean_val
    inverse = lax.rsqrt(jnp.mean(centered * centered, axis=-1, keepdims=True) + epsilon)
    unit_val = centered * inverse
    return (unit_val * gain_vec + shift_vec, unit_val, inverse)


def norm_back(grad_in, unit_val, inverse, gain_vec):
    scaled = grad_in * gain_vec
    centered = scaled - jnp.mean(scaled, axis=-1, keepdims=True)
    return inverse * (centered - unit_val * jnp.mean(scaled * unit_val, axis=-1, keepdims=True))


def features(values):
    return jax.nn.elu(values) + 1.0


def finish(numerator, denominator):
    return numerator / jnp.maximum(denominator, 1.0)[:, :, None]


def compose(earlier, later):
    return (
        later[0] + later[2] * earlier[0],
        later[1] + later[2] * earlier[1],
        later[2] * earlier[2],
    )


def item_numbers(lengths_row, first_place, number):
    offsets = jnp.cumsum(lengths_row) - lengths_row
    places = first_place + jnp.arange(number, dtype=jnp.int32)
    return jnp.sum((offsets[None, :] <= places[:, None]).astype(jnp.int32), axis=1) - 1


def on_device(
    tokens, cotangent, w_qkv, w_out_t, w_up, w_down_t, gains, biases, up_bias, lengths, pixel_mask
):
    batches, local_rows, columns = tokens.shape
    local_width = w_qkv.shape[2]
    heads_here = local_width // DH
    seq_index = lax.axis_index("seq")
    head_index = lax.axis_index("head")
    first_token = seq_index * local_rows
    position = jnp.arange(local_rows, dtype=jnp.int32)
    before = position[:, None] >= position[None, :]

    def own_columns(matrix):
        return lax.dynamic_slice_in_dim(matrix, head_index * columns, columns, 1)

    results = []
    input_grads = []
    shard_sums = None
    for batch_index in range(batches):
        full_qkv, full_out, full_up, full_down, full_gains, full_biases, full_upb = (
            lax.all_gather(w_qkv, "seq", axis=0, tiled=True),
            lax.all_gather(w_out_t, "seq", axis=0, tiled=True),
            lax.all_gather(w_up, "seq", axis=0, tiled=True),
            lax.all_gather(w_down_t, "seq", axis=0, tiled=True),
            lax.all_gather(gains, "seq", axis=1, tiled=True),
            lax.all_gather(biases, "seq", axis=1, tiled=True),
            lax.all_gather(up_bias, "seq", axis=1, tiled=True),
        )
        input_rows, grad_rows16 = (
            lax.all_gather(tokens[batch_index], "head", axis=1, tiled=True),
            lax.all_gather(cotangent[batch_index], "head", axis=1, tiled=True),
        )
        gains32 = full_gains.astype(jnp.float32)
        biases32 = full_biases.astype(jnp.float32)
        upb32 = full_upb.astype(jnp.float32).reshape(-1)
        inputs32 = input_rows.astype(jnp.float32)
        place_items = item_numbers(lengths[batch_index], first_token - 1, local_rows + 1)
        item_of = place_items[1:]
        carried = (item_of == place_items[0]).astype(jnp.float32)
        tail_mask = (item_of == item_of[local_rows - 1]).astype(jnp.float32)
        through = carried[local_rows - 1]
        same_item = ((item_of[:, None] == item_of[None, :]) & before).astype(jnp.float32)
        keep_half = pixel_mask[batch_index].astype(jnp.bfloat16)
        keep32 = pixel_mask[batch_index].astype(jnp.float32)
        lifted, unit_one, inverse_one = normalize(inputs32, gains32[0], biases32[0])
        normed = lifted.astype(jnp.bfloat16)
        projected = jnp.einsum("td,dsf->tsf", normed, full_qkv, preferred_element_type=jnp.float32)
        query_feat = (
            features(projected[:, 0]).astype(jnp.bfloat16).reshape(local_rows, heads_here, DH)
        )
        key_feat = (features(projected[:, 1]).astype(jnp.bfloat16) * keep_half[:, None]).reshape(
            local_rows, heads_here, DH
        )
        value_feat = projected[:, 2].astype(jnp.bfloat16).reshape(local_rows, heads_here, DH)
        tail_key = key_feat * tail_mask.astype(jnp.bfloat16)[:, None, None]
        state_loc = jnp.einsum(
            "jhd,jhe->hde", tail_key, value_feat, preferred_element_type=jnp.float32
        )
        total_loc = jnp.sum(tail_key.astype(jnp.float32), axis=0)
        identity = (jnp.zeros_like(state_loc), jnp.zeros_like(total_loc), jnp.ones((), jnp.float32))
        state_in, total_in, passed = entering(
            (state_loc, total_loc, through), "seq", compose, identity
        )
        query32 = query_feat.astype(jnp.float32)
        scores = (
            jnp.einsum("thd,jhd->htj", query_feat, key_feat, preferred_element_type=jnp.float32)
            * same_item[None]
        )
        scores_low = scores.astype(jnp.bfloat16)
        numerator = jnp.einsum(
            "htj,jhe->the", scores_low, value_feat, preferred_element_type=jnp.float32
        ) + carried[:, None, None] * jnp.einsum(
            "thd,hde->the", query32, state_in, precision=highest
        )
        denominator = jnp.sum(scores, axis=2).T + carried[:, None] * jnp.einsum(
            "thd,hd->th", query32, total_in, precision=highest
        )
        output, finish_back = jax.vjp(finish, numerator, denominator)
        mixed_out = output.reshape(local_rows, local_width).astype(jnp.bfloat16)
        attended = lax.psum(
            jnp.einsum("tf,df->td", mixed_out, full_out, preferred_element_type=jnp.float32).astype(
                jnp.bfloat16
            ),
            "head",
        ).astype(jnp.float32)
        middle = inputs32 + attended
        lifted_two, unit_two, inverse_two = normalize(middle, gains32[1], biases32[1])
        normed_two = lifted_two.astype(jnp.bfloat16)
        hidden = jnp.dot(normed_two, full_up, preferred_element_type=jnp.float32) + upb32
        activated32, gelu_back = jax.vjp(jax.nn.gelu, hidden)
        activated = activated32.astype(jnp.bfloat16)
        branch = lax.psum_scatter(
            jnp.einsum(
                "tf,df->td", activated, full_down, preferred_element_type=jnp.float32
            ).astype(jnp.bfloat16),
            "head",
            scatter_dimension=1,
            tiled=True,
        ).astype(jnp.float32)
        results.append(own_columns(middle) + branch + own_columns(biases32[2][None]))
        grad_out = grad_rows16.astype(jnp.float32)
        grad_down = jnp.einsum(
            "td,tf->df", grad_rows16, activated, preferred_element_type=jnp.float32
        )
        grad_act = jnp.einsum(
            "td,df->tf", grad_rows16, full_down, preferred_element_type=jnp.float32
        )
        grad_hidden = gelu_back(grad_act)[0].astype(jnp.bfloat16)
        grad_up = jnp.einsum(
            "td,tf->df", normed_two, grad_hidden, preferred_element_type=jnp.float32
        )
        grad_upb = jnp.sum(grad_hidden.astype(jnp.float32), axis=0).reshape(full_upb.shape)
        grad_two = lax.psum(
            jnp.einsum(
                "tf,df->td", grad_hidden, full_up, preferred_element_type=jnp.float32
            ).astype(jnp.bfloat16),
            "head",
        ).astype(jnp.float32)
        grad_middle = grad_out + norm_back(grad_two, unit_two, inverse_two, gains32[1])
        grad_attended = grad_middle.astype(jnp.bfloat16)
        grad_out_t = jnp.einsum(
            "td,tf->df", grad_attended, mixed_out, preferred_element_type=jnp.float32
        )
        grad_mixed = jnp.einsum(
            "td,df->tf", grad_attended, full_out, preferred_element_type=jnp.float32
        ).reshape(local_rows, heads_here, DH)
        grad_numer32, grad_denom = finish_back(grad_mixed)
        grad_numer = grad_numer32.astype(jnp.bfloat16)
        grad_numer_wide = grad_numer.astype(jnp.float32)
        grad_scores = (
            (
                jnp.einsum(
                    "the,jhe->htj", grad_numer, value_feat, preferred_element_type=jnp.float32
                )
                + grad_denom.T[:, :, None]
            )
            * same_item[None]
        ).astype(jnp.bfloat16)
        carried_query = query32 * carried[:, None, None]
        grad_query = jnp.einsum(
            "htj,jhd->thd", grad_scores, key_feat, preferred_element_type=jnp.float32
        ) + carried[:, None, None] * (
            jnp.einsum("hde,the->thd", state_in, grad_numer_wide, precision=highest)
            + grad_denom[:, :, None] * total_in[None]
        )
        grad_key = jnp.einsum(
            "htj,thd->jhd", grad_scores, query_feat, preferred_element_type=jnp.float32
        )
        grad_value = jnp.einsum(
            "htj,the->jhe", scores_low, grad_numer, preferred_element_type=jnp.float32
        )
        grad_state_in = jnp.einsum(
            "thd,the->hde", carried_query, grad_numer_wide, precision=highest
        )
        grad_total_in = jnp.einsum("thd,th->hd", carried_query, grad_denom, precision=highest)
        grad_state_loc, grad_total_loc, passed_back = entering_2(
            (grad_state_in, grad_total_in, through), "seq", compose, identity
        )
        tail_three = tail_mask[:, None, None]
        value_wide = value_feat.astype(jnp.float32)
        key_wide = key_feat.astype(jnp.float32)
        grad_key = grad_key + tail_three * (
            jnp.einsum("hde,jhe->jhd", grad_state_loc, value_wide, precision=highest)
            + grad_total_loc[None]
        )
        grad_value = grad_value + tail_three * jnp.einsum(
            "jhd,hde->jhe", key_wide, grad_state_loc, precision=highest
        )
        ignored, feature_back = jax.vjp(features, projected[:, :2])
        grad_features = jnp.stack(
            [
                grad_query.reshape(local_rows, local_width),
                grad_key.reshape(local_rows, local_width) * keep32[:, None],
            ],
            axis=1,
        )
        grad_pair = feature_back(grad_features)[0]
        grad_projected = jnp.concatenate(
            [grad_pair, grad_value.reshape(local_rows, 1, local_width)], axis=1
        ).astype(jnp.bfloat16)
        grad_qkv = jnp.einsum(
            "td,tsf->dsf", normed, grad_projected, preferred_element_type=jnp.float32
        )
        grad_one = lax.psum(
            jnp.einsum(
                "tsf,dsf->td", grad_projected, full_qkv, preferred_element_type=jnp.float32
            ).astype(jnp.bfloat16),
            "head",
        ).astype(jnp.float32)
        grad_inputs = grad_middle + norm_back(grad_one, unit_one, inverse_one, gains32[0])
        input_grads.append(own_columns(grad_inputs))
        grad_gains = jnp.stack(
            [jnp.sum(grad_one * unit_one, axis=0), jnp.sum(grad_two * unit_two, axis=0)]
        )
        grad_biases = jnp.stack(
            [jnp.sum(grad_one, axis=0), jnp.sum(grad_two, axis=0), jnp.sum(grad_out, axis=0)]
        )
        pieces = (
            lax.psum_scatter(grad_qkv, "seq", scatter_dimension=0, tiled=True),
            lax.psum_scatter(grad_out_t, "seq", scatter_dimension=0, tiled=True),
            lax.psum_scatter(grad_up, "seq", scatter_dimension=0, tiled=True),
            lax.psum_scatter(grad_down, "seq", scatter_dimension=0, tiled=True),
            lax.psum_scatter(grad_gains, "seq", scatter_dimension=1, tiled=True),
            lax.psum_scatter(grad_biases, "seq", scatter_dimension=1, tiled=True),
            lax.psum_scatter(grad_upb, "seq", scatter_dimension=1, tiled=True),
        )
        shard_sums = pieces if shard_sums is None else jax.tree.map(jnp.add, shard_sums, pieces)
    return (
        jnp.stack(results),
        jnp.stack(input_grads),
        shard_sums[0],
        shard_sums[1],
        shard_sums[2],
        shard_sums[3],
        shard_sums[4],
        shard_sums[5],
        shard_sums[6],
    )


MESH = pl.DeviceIdType.MESH
BF = jnp.bfloat16
F32 = jnp.float32
QKV, OUT, UP, DOWN, SMALL = range(5)


def dot_nn(a, b):
    return lax.dot_general(a, b, (((1,), (0,)), ((), ())), preferred_element_type=F32)


def dot_nt(a, b):
    return lax.dot_general(a, b, (((1,), (1,)), ((), ())), preferred_element_type=F32)


def dot_tn(a, b):
    return lax.dot_general(a, b, (((0,), (0,)), ((), ())), preferred_element_type=F32)


def ds(start, size):
    return pl.ds(pl.multiple_of(start, size), size)


def loop(count, body):
    def step(i, carry):
        body(i)
        return carry

    lax.fori_loop(0, count, step, 0)


def layout(n, m, batches, rows, width, local, hidden):
    tokens = batches * rows
    block = width // n
    own = tokens // m
    hops = n // 2
    heads = local // DH
    vm = {
        "xg": ((batches, rows, width), BF),
        "cg": ((batches, rows, width), BF),
        "wq": ((3, width, local), BF),
        "wo": ((width, local), BF),
        "wu": ((width, hidden), BF),
        "wd": ((width, hidden), BF),
        "small": ((8, block), F32),
        "smallg": ((8, width), F32),
        "normed": ((tokens, width), BF),
        "phi_d": ((2, tokens, local), F32),
        "qf": ((tokens, local), BF),
        "kf": ((tokens, local), BF),
        "vf": ((tokens, local), BF),
        "mask": ((batches, rows, rows), F32),
        "car": ((batches, rows, 128), F32),
        "tail": ((batches, rows, 128), F32),
        "pmc": ((batches, rows, 128), F32),
        "low": ((batches, rows, heads * rows), BF),
        "numer": ((tokens, local), F32),
        "denom": ((tokens, local), F32),
        "mixed": ((tokens, local), BF),
        "st_send": ((batches, DH + 16, local), BF),
        "st_recv": ((2, batches, DH + 16, local), BF),
        "gs_send": ((batches, DH + 16, local), BF),
        "gs_recv": ((2, batches, DH + 16, local), BF),
        "middle": ((own, width), F32),
        "ntwo": ((tokens, width), BF),
        "gelu_d": ((tokens, hidden), F32),
        "activ": ((tokens, hidden), BF),
        "g_hid": ((tokens, hidden), BF),
        "branch": ((own, width), F32),
        "total": ((own, width), F32),
        "g_mid": ((own, width), F32),
        "gatt": ((tokens, width), BF),
        "g_attn": ((tokens, local), F32),
        "g_num": ((tokens, local), BF),
        "g_den": ((tokens, local), F32),
        "gq": ((tokens, local), F32),
        "gk": ((tokens, local), F32),
        "gv": ((tokens, local), F32),
        "gproj": ((3, tokens, local), BF),
        "h_s1": ((4, 2, 2, own // 2, width), BF),
        "h_r1": ((4, 2, 2, own // 2, width), BF),
        "h_acc": ((4, 2, 2, own // 2, width), F32),
        "h_s2": ((4, 2, own // 2, width), BF),
        "h_r2": ((4, 2, own // 2, width), BF),
        "rq_s": ((n, 3, block, local), BF),
        "rq_r": ((n, 3, block, local), BF),
        "ro_s": ((n, block, local), BF),
        "ro_r": ((n, block, local), BF),
        "ru_s": ((n, block, hidden), BF),
        "ru_r": ((n, block, hidden), BF),
        "rd_s": ((n, block, hidden), BF),
        "rd_r": ((n, block, hidden), BF),
        "fq": ((3, block, local), F32),
        "fo": ((block, local), F32),
        "fu": ((block, hidden), F32),
        "fd": ((block, hidden), F32),
        "hs_recv": ((m, 8, width), F32),
        "hs_send": ((8, width), F32),
        "upb": ((1, hidden), F32),
        "sg": ((8, width), F32),
        "ss_recv": ((n, 8, block), F32),
        "a_rows": ((own, width), F32),
        "i_rows": ((own, width), F32),
    }
    sems = {
        "ag_s": (5,),
        "ag_r": (5, 2, hops),
        "rs_s": (4,),
        "rs_r": (4, 2, hops),
        "hg_s": (4,),
        "hg_r": (4, 2, 3),
        "hr_s": (4, 2),
        "hr_r": (4, 2, 2),
        "st_s": (2,),
        "st_r": (2,),
        "aa_s": (2,),
        "aa_r": (2,),
        "hs_s": (1,),
        "hs_r": (1,),
        "ss_s": (1,),
        "ss_r": (1,),
        "lc": (12,),
    }
    return vm, sems


class Refs:
    pass


def body(n, m, names, *refs):
    r = Refs()
    for name, ref in zip(names, refs):
        setattr(r, name, ref)
    batches, rows, width = r.xg.shape
    tokens = batches * rows
    own = tokens // m
    block = width // n
    local = r.wo.shape[1]
    hidden = r.wu.shape[1]
    heads = local // DH
    hops = n // 2
    s = lax.axis_index("seq")
    h = lax.axis_index("head")
    odd = lax.rem(s, 2)
    p = (1 - odd) * lax.div(s, 2) + odd * (n - 1 - lax.div(s, 2))
    lo, hi = lax.rem(h, 2), lax.div(h, 2)
    pair = h + 1 - 2 * lo
    cross = lax.rem(h + 2, m)

    def at(place):
        place = lax.rem(place + 2 * n, n)
        far = lax.div(place, hops)
        return (1 - far) * 2 * place + far * (2 * (n - 1 - place) + 1)

    ring = (at(p + 1), at(p - 1))
    sign = (1, -1)

    def remote(src, dst, send, recv, seq, head):
        return pltpu.make_async_remote_copy(
            src_ref=src,
            dst_ref=dst,
            send_sem=send,
            recv_sem=recv,
            device_id=(seq, head),
            device_id_type=MESH,
        )

    def drained(view, sem):
        remote(view, view, sem, sem, ring[0], h).wait_send()

    def landed(view, sem):
        remote(view, view, sem, sem, ring[0], h).wait_recv()

    r.small[...] = jnp.zeros_like(r.small)
    r.small[0:2, :] = r.gains[...].astype(F32)
    r.small[2:5, :] = r.biases[...].astype(F32)
    r.small[5:6, :] = r.up_bias[...].astype(F32)

    barrier = pltpu.get_barrier_semaphore()
    for peer in ((ring[0], h), (ring[1], h), (s, pair), (s, cross)):
        pl.semaphore_signal(barrier, inc=1, device_id=peer, device_id_type=MESH)
    pl.semaphore_wait(barrier, 4)

    shards = (r.w_qkv, r.w_out, r.w_up, r.w_down, r.small)
    gathered = (r.wq, r.wo, r.wu, r.wd, r.smallg)

    def part_of(w, d, j):
        wide_part = r.wq.shape[2] if w == QKV else shards[w].shape[1]
        if j < hops - 1 or w == SMALL:
            return pl.ds(0, wide_part)
        return pl.ds(d * (wide_part // 2), wide_part // 2)

    def ag_shard(w, d, j):
        cols = part_of(w, d, j)
        if w == SMALL:
            return r.small
        return shards[w].at[:, :, cols] if w == QKV else shards[w].at[:, cols]

    def ag_full(w, owner, d, j):
        cols = part_of(w, d, j)
        if w == SMALL:
            return r.smallg.at[:, ds(owner * block, block)]
        if w == QKV:
            return r.wq.at[:, ds(owner * block, block), cols]
        return gathered[w].at[ds(owner * block, block), cols]

    def ways(w, j):
        return (0,) if w == SMALL and j == hops - 1 else (0, 1)

    def ag_send(w, j):
        for d in ways(w, j):
            owner = at(p - sign[d] * j)
            src = ag_shard(w, d, j) if j == 0 else ag_full(w, owner, d, j)
            remote(
                src, ag_full(w, owner, d, j), r.ag_s.at[w], r.ag_r.at[w, d, j], ring[d], h
            ).start()

    def ag_wait(w, j):
        for d in ways(w, j):
            landed(ag_full(w, at(p - sign[d] * (j + 1)), d, j), r.ag_r.at[w, d, j])

    def ag_pass(w, j):
        ag_wait(w, j)
        ag_send(w, j + 1)

    part_rows = own // 2

    def hg_view(k, c, who):
        if k < 2:
            return (r.xg, r.cg)[k].at[c, :, ds(who * local, local)]
        return (r.ntwo, r.gatt)[k - 2].at[ds(who * own + c * part_rows, part_rows), :]

    def hg_copy(k, c, i, src, who, to):
        return remote(src, hg_view(k, c, who), r.hg_s.at[k], r.hg_r.at[k, c, i], s, to)

    def hg_start(k, c):
        src = (r.tok, r.cot)[k].at[c] if k < 2 else hg_view(k, c, h)
        hg_copy(k, c, 1, src, h, cross).start()
        hg_copy(k, c, 0, src, h, pair).start()

    def hg_forward(k, c):
        view = hg_view(k, c, cross)
        hg_copy(k, c, 1, view, cross, cross).wait_recv()
        hg_copy(k, c, 2, view, cross, pair).start()

    def hg_finish(k, c):
        view = hg_view(k, c, pair)
        hg_copy(k, c, 0, view, pair, pair).wait_recv()
        across = lax.rem(pair + 2, m)
        view = hg_view(k, c, across)
        hg_copy(k, c, 2, view, across, pair).wait_recv()

    tn = 256

    def hr_first(k, c, left, product):
        blocks = [2 * i + 1 - lo for i in (0, 1)] + [2 * i + lo for i in (0, 1)]
        where = [ds(who * own + c * part_rows, part_rows) for who in blocks]

        def some(i):
            cols = ds(i * tn, tn)
            v = product(left(where), cols)
            for q in (0, 1):
                r.h_s1[k, c, q, :, cols] = v[q * part_rows : (q + 1) * part_rows].astype(BF)
                r.h_acc[k, c, q, :, cols] = v[(q + 2) * part_rows : (q + 3) * part_rows]

        loop(width // tn, some)
        hr_copy(k, c, 0).start()

    def hr_copy(k, c, stage):
        if stage == 0:
            src, dst, to = r.h_s1.at[k, c], r.h_r1.at[k, c], pair
        else:
            src, dst, to = r.h_s2.at[k, c], r.h_r2.at[k, c], cross
        return remote(src, dst, r.hr_s.at[k, stage], r.hr_r.at[k, c, stage], s, to)

    def hr_second(k, c):
        hr_copy(k, c, 0).wait_recv()

        def away(i):
            rw = ds(i * 32, 32)
            r.h_s2[k, c, rw, :] = (
                r.h_acc[k, c, 1 - hi, rw, :] + r.h_r1[k, c, 1 - hi, rw, :].astype(F32)
            ).astype(BF)

        loop(part_rows // 32, away)
        hr_copy(k, c, 1).start()

    def hr_wait(k, c):
        hr_copy(k, c, 1).wait_recv()

    def hr_value(k, c, rw):
        return (
            r.h_acc[k, c, hi, rw, :]
            + r.h_r1[k, c, hi, rw, :].astype(F32)
            + r.h_r2[k, c, rw, :].astype(F32)
        )

    def pick(ref):
        return lambda where: jnp.concatenate([ref[rw, :] for rw in where], axis=0)

    def product_nt(right):
        return lambda left, cols: dot_nt(left, right[cols, :])

    def rs_term(w, owner, piece):
        cols = ds(owner * block, block)
        if w == DOWN:
            left = r.cg[:, :, cols].reshape(tokens, block)
            half = hidden // 2
            return [dot_tn(left, r.activ[:, pl.ds(piece * half, half)])]
        if w == UP:
            half = hidden // 2
            return [dot_tn(r.ntwo[:, cols], r.g_hid[:, pl.ds(piece * half, half)])]
        half = local // 2
        if w == OUT:
            return [dot_tn(r.gatt[:, cols], r.mixed[:, pl.ds(piece * half, half)])]
        left = r.normed[:, cols]
        return [dot_tn(left, r.gproj[i, :, pl.ds(piece * half, half)]) for i in range(3)]

    rs_send = (r.rq_s, r.ro_s, r.ru_s, r.rd_s)
    rs_recv = (r.rq_r, r.ro_r, r.ru_r, r.rd_r)

    def rs_half(w, piece):
        half = rs_send[w].shape[-1] // 2
        return pl.ds(piece * half, half)

    def rs_view(ref, w, d, step):
        if step > 0:
            return ref.at[d * hops + step]
        if w == QKV:
            return ref.at[d * hops, :, :, rs_half(w, d)]
        return ref.at[d * hops, :, rs_half(w, d)]

    def rs_arrived(w, d, step):
        landed(rs_view(rs_recv[w], w, d, step), r.rs_r.at[w, d, step])

    def rs_round(w, step):
        for d in (0, 1):
            slot = d * hops + step
            if step > 0:
                rs_arrived(w, d, step - 1)
            for piece in (0, 1):
                if step == 0 and piece != d:
                    continue
                terms = rs_term(w, at(p + sign[d] * (hops - step)), piece)
                cols = rs_half(w, piece)
                for i, v in enumerate(terms):
                    lead = (i,) if w == QKV else ()
                    if step > 1 or (step == 1 and piece == d):
                        v = v + rs_recv[w][(slot - 1, *lead, slice(None), cols)].astype(F32)
                    rs_send[w][(slot, *lead, slice(None), cols)] = v.astype(BF)
            remote(
                rs_view(rs_send[w], w, d, step),
                rs_view(rs_recv[w], w, d, step),
                r.rs_s.at[w],
                r.rs_r.at[w, d, step],
                ring[d],
                h,
            ).start()

    finals = (r.fq, r.fo, r.fu, r.fd)
    results = (r.gq_o, r.go_o, r.gu_o, r.gd_o)
    local_copies = []

    def rs_final(w):
        terms = [rs_term(w, s, piece) for piece in (0, 1)]
        for d in (0, 1):
            rs_arrived(w, d, hops - 1)
        for piece in (0, 1):
            cols = rs_half(w, piece)
            for i, v in enumerate(terms[piece]):
                lead = (i,) if w == QKV else ()
                for d in (0, 1):
                    v = v + rs_recv[w][(d * hops + hops - 1, *lead, slice(None), cols)].astype(F32)
                finals[w][(*lead, slice(None), cols)] = v
        copy = pltpu.make_async_copy(finals[w], results[w], r.lc.at[w])
        copy.start()
        local_copies.append(copy)

    def turn(k, src, dst):
        where = (hi, ds(lo * own, own))
        for i in range(1, m):
            to = lax.rem(h + i, m)
            remote(
                src.at[:, ds(to * local, local)],
                dst.at[where[0], where[1], :],
                r.aa_s.at[k],
                r.aa_r.at[k],
                s,
                to,
            ).start()
        copy = pltpu.make_async_copy(
            src.at[:, ds(h * local, local)], dst.at[where[0], where[1], :], r.lc.at[4 + k]
        )
        copy.start()
        local_copies.append(copy)

    def turn_wait(k, src):
        landed(src.at[:, pl.ds(0, (m - 1) * local)], r.aa_r.at[k])

    ag_send(SMALL, 0)
    ag_send(QKV, 0)
    ag_send(OUT, 0)
    hg_start(0, 0)
    hg_start(0, 1)
    own_copies = [
        pltpu.make_async_copy(r.w_qkv, r.wq.at[:, ds(s * block, block), :], r.lc.at[8]),
        pltpu.make_async_copy(r.w_out, r.wo.at[ds(s * block, block), :], r.lc.at[9]),
        pltpu.make_async_copy(r.w_up, r.wu.at[ds(s * block, block), :], r.lc.at[10]),
        pltpu.make_async_copy(r.w_down, r.wd.at[ds(s * block, block), :], r.lc.at[11]),
        pltpu.make_async_copy(r.tok, r.xg.at[:, :, ds(h * local, local)], r.lc.at[6]),
        pltpu.make_async_copy(r.cot, r.cg.at[:, :, ds(h * local, local)], r.lc.at[7]),
    ]
    for copy in own_copies:
        copy.start()
    hg_start(1, 0)
    hg_start(1, 1)

    first = s * rows
    row_at = lax.broadcasted_iota(jnp.int32, (rows, 128), 0)
    lane_at = lax.broadcasted_iota(jnp.int32, (rows, rows), 1)
    square = lax.broadcasted_iota(jnp.int32, (local, local), 0)
    square_lane = lax.broadcasted_iota(jnp.int32, (local, local), 1)
    same_head = (square // DH) == (square_lane // DH)
    diagonal = square == square_lane
    lane_head = lax.broadcasted_iota(jnp.int32, (rows, local), 1) // DH
    before_thr, after_thr = [], []

    def wide(value):
        return jnp.concatenate([value] * (local // 128), axis=1)

    def begin(offsets, place):
        value = 0
        for off in offsets:
            value = jnp.where(off <= place, off, value)
        return value

    def through(offsets, which):
        return jnp.where(
            begin(offsets, which * rows + rows - 1) < which * rows, 1.0, 0.0
        ).astype(F32)

    def crops(b):
        offsets, running = [], 0
        for i in range(r.lengths.shape[1]):
            offsets.append(running)
            running = running + r.lengths[b, i]
        start = jnp.zeros((rows, 128), jnp.int32)
        for off in offsets:
            start = jnp.where(off <= row_at + first, off, start)
        last = begin(offsets, first + rows - 1)
        r.mask[b] = jnp.where(
            (lane_at + first >= wide(start)) & (lane_at <= wide(row_at)), 1.0, 0.0
        ).astype(F32)
        r.car[b] = jnp.where(start < first, 1.0, 0.0).astype(F32)
        r.tail[b] = jnp.where(start == last, 1.0, 0.0).astype(F32)
        before_thr.append(through(offsets, lax.rem(s + n - 1, n)))
        after_thr.append(through(offsets, lax.rem(s + 1, n)))
        keep = r.pixel[b : b + 1, :].astype(F32)
        r.pmc[b] = dot_nn(
            jnp.where(diagonal, keep, 0.0).astype(BF), jnp.ones((rows, 128), BF)
        )

    def ag_step(j):
        ag_pass(SMALL, j)
        ag_pass(QKV, j)
        ag_pass(OUT, j)

    crops(0)
    for c in (0, 1):
        hg_forward(0, c)
    ag_step(0)
    for copy in own_copies:
        copy.wait()
    r.smallg[:, ds(s * block, block)] = r.small[...]

    def unit(values):
        mean = jnp.mean(values, axis=1, keepdims=True)
        centered = values - mean
        inverse = lax.rsqrt(jnp.mean(centered * centered, axis=1, keepdims=True) + epsilon)
        return centered * inverse, inverse

    tile = 32

    def unit_one(b):
        def some(i):
            u, _ = unit(r.xg[b, ds(i * tile, tile), :].astype(F32))
            r.gelu_d[ds(b * rows + i * tile, tile), :] = u

        loop(rows // tile, some)

    def norm_one(i):
        rw = ds(i * tile, tile)
        r.normed[rw, :] = (r.gelu_d[rw, :] * gain_one + shift_one).astype(BF)

    for c in (0, 1):
        hg_finish(0, c)
    unit_one(0)
    ag_step(1)
    unit_one(1)
    crops(1)
    ag_step(2)
    ag_send(UP, 0)
    for c in (0, 1):
        hg_forward(1, c)
    ag_wait(SMALL, 3)
    gain_one, gain_two = r.smallg[0:1, :], r.smallg[1:2, :]
    shift_one, shift_two, shift_out = r.smallg[2:3, :], r.smallg[3:4, :], r.smallg[4:5, :]
    loop(tokens // tile, norm_one)
    ag_wait(QKV, 3)
    ag_wait(OUT, 3)

    tm = 128

    def project(i):
        rw = ds(i * tm, tm)
        b = lax.div(i, rows // tm)
        rb = ds(lax.rem(i, rows // tm) * tm, tm)
        left = r.normed[rw, :]
        for kind in (0, 1):
            v = dot_nn(left, r.wq[kind])
            low = jnp.exp(jnp.minimum(v, 0.0))
            f = jnp.where(v > 0.0, v + 1.0, low).astype(BF)
            r.phi_d[kind, rw, :] = low
            if kind == 0:
                r.qf[rw, :] = f
            else:
                r.kf[rw, :] = (f.astype(F32) * wide(r.pmc[b, rb, :])).astype(BF)
        r.vf[rw, :] = dot_nn(left, r.wq[2]).astype(BF)

    loop(tokens // tm, project)

    def fold(matrix, total):
        kept = jnp.where(same_head, matrix, 0.0)
        acc = kept[0:DH]
        for i in range(1, heads):
            acc = acc + kept[i * DH : (i + 1) * DH]
        top = lax.broadcasted_iota(jnp.int32, (16, local), 0) == 0
        return acc.astype(BF), jnp.where(top, total, 0.0).astype(BF)

    def unfold(ref):
        acc = ref[0:DH, :].astype(F32)
        wide = jnp.concatenate([acc] * heads, axis=0)
        return jnp.where(same_head, wide, 0.0).astype(BF)

    def state_send(k, ref, dest, step):
        for i in (0, 1):
            to = lax.rem(s + n + step * (i + 1), n)
            remote(ref, dest.at[i], r.st_s.at[k], r.st_r.at[k], to, h).start()

    def state_wait(k, dest):
        landed(dest, r.st_r.at[k])

    def rows_of(b):
        return pl.ds(b * rows, rows)

    def by_head(value):
        return jnp.concatenate(
            [jnp.where(lane_head == hd, value.astype(F32), 0.0).astype(BF) for hd in range(heads)],
            axis=0,
        )

    for b in range(batches):
        k = r.kf[rows_of(b), :].astype(F32) * wide(r.tail[b])
        moved = dot_tn(k.astype(BF), r.vf[rows_of(b), :])
        a, t = fold(moved, jnp.sum(k, axis=0, keepdims=True))
        r.st_send[b, 0:DH, :] = a
        r.st_send[b, DH:, :] = t
    state_send(0, r.st_send, r.st_recv, 1)

    for b in range(batches):
        q, k = r.qf[rows_of(b), :], r.kf[rows_of(b), :]
        acc = jnp.zeros((rows, local), F32)
        for hd in range(heads):
            sc = dot_nt(jnp.where(lane_head == hd, q.astype(F32), 0.0).astype(BF), k) * r.mask[b]
            r.low[b, :, hd * rows : (hd + 1) * rows] = sc.astype(BF)
            acc = acc + jnp.where(lane_head == hd, jnp.sum(sc, axis=1, keepdims=True), 0.0)
        r.denom[rows_of(b), :] = acc
        r.numer[rows_of(b), :] = dot_nn(r.low[b], by_head(r.vf[rows_of(b), :]))

    for c in (0, 1):
        hg_finish(1, c)
    ag_pass(UP, 0)
    ag_send(DOWN, 0)
    state_wait(0, r.st_recv)

    def both(b, value, thr):
        one = value.astype(F32) * wide(r.car[b])
        return jnp.concatenate([one.astype(BF), (one * thr).astype(BF)], axis=1)

    for b in range(batches):
        left = both(b, r.qf[rows_of(b), :], before_thr[b])
        states = jnp.concatenate([unfold(r.st_recv.at[i, b]) for i in (0, 1)], axis=0)
        sums = jnp.concatenate(
            [
                jnp.where(
                    same_head,
                    dot_tn(r.st_recv[i, b, DH:, :], jnp.ones((16, local), BF)),
                    0.0,
                ).astype(BF)
                for i in (0, 1)
            ],
            axis=0,
        )
        top = r.numer[rows_of(b), :] + dot_nn(left, states)
        bottom = r.denom[rows_of(b), :] + dot_nn(left, sums)
        attn = top / jnp.maximum(bottom, 1.0)
        r.numer[rows_of(b), :] = attn
        r.denom[rows_of(b), :] = bottom
        r.mixed[rows_of(b), :] = attn.astype(BF)

    hr_first(0, 0, pick(r.mixed), product_nt(r.wo))
    hr_first(0, 1, pick(r.mixed), product_nt(r.wo))
    hr_second(0, 0)
    hr_second(0, 1)
    ag_pass(UP, 1)
    mine = h * own

    def x_rows(at_row):
        return r.xg[hi, ds(lo * own + at_row, tile), :].astype(F32)

    def c_rows(at_row):
        return r.cg[hi, ds(lo * own + at_row, tile), :].astype(F32)

    def norm_two(c):
        def some(i):
            at_row = c * part_rows + i * tile
            v = x_rows(at_row) + hr_value(0, c, ds(i * tile, tile))
            r.middle[ds(at_row, tile), :] = v
            u, _ = unit(v)
            r.ntwo[ds(mine + at_row, tile), :] = (u * gain_two + shift_two).astype(BF)

        loop(part_rows // tile, some)

    for c in (0, 1):
        hr_wait(0, c)
        norm_two(c)
        hg_start(2, c)
    ag_pass(DOWN, 0)
    hg_forward(2, 0)
    hg_forward(2, 1)
    ag_pass(UP, 2)
    hg_finish(2, 0)
    hg_finish(2, 1)
    ag_pass(DOWN, 1)
    ag_wait(UP, 3)

    tu = 256

    def up(i):
        rw = ds(lax.div(i, hidden // tn) * tu, tu)
        cols = ds(lax.rem(i, hidden // tn) * tn, tn)
        v = dot_nn(r.ntwo[rw, :], r.wu[:, cols]) + r.smallg[5:6, cols]
        square_of = v * v
        t = jnp.tanh(0.7978845608028654 * (v + 0.044715 * (square_of * v)))
        half = 0.5 * (1.0 + t)
        r.activ[rw, cols] = (v * half).astype(BF)
        r.gelu_d[rw, cols] = half + (0.5 * v) * (1.0 - t * t) * (
            0.7978845608028654 + (3.0 * 0.044715 * 0.7978845608028654) * square_of
        )

    loop((tokens // tu) * (hidden // tn), up)
    rs_round(DOWN, 0)
    ag_pass(DOWN, 2)
    ag_wait(DOWN, 3)

    def back(i):
        cols = ds(i * tn, tn)
        for b in range(batches):
            g = dot_nn(r.cg[b], r.wd[:, cols])
            r.g_hid[rows_of(b), cols] = (g * r.gelu_d[rows_of(b), cols]).astype(BF)

    loop(hidden // tn, back)
    rs_round(UP, 0)
    hr_first(2, 0, pick(r.g_hid), product_nt(r.wu))
    hr_first(2, 1, pick(r.g_hid), product_nt(r.wu))
    rs_round(DOWN, 1)
    hr_second(2, 0)
    hr_second(2, 1)
    rs_round(UP, 1)

    r.hs_send[...] = jnp.zeros_like(r.hs_send)

    def back_norm(g, u, inverse, gain):
        scaled = g * gain
        centered = scaled - jnp.mean(scaled, axis=1, keepdims=True)
        return inverse * (centered - u * jnp.mean(scaled * u, axis=1, keepdims=True))

    def norm_two_back(c):
        def some(i):
            at_row = c * part_rows + i * tile
            rw = ds(at_row, tile)
            g = hr_value(2, c, ds(i * tile, tile))
            u, inverse = unit(r.middle[rw, :])
            out = c_rows(at_row)
            v = out + back_norm(g, u, inverse, gain_two)
            r.g_mid[rw, :] = v
            r.gatt[ds(mine + at_row, tile), :] = v.astype(BF)
            r.hs_send[1:2, :] += jnp.sum(g * u, axis=0, keepdims=True)
            r.hs_send[3:4, :] += jnp.sum(g, axis=0, keepdims=True)
            r.hs_send[4:5, :] += jnp.sum(out, axis=0, keepdims=True)

        loop(part_rows // tile, some)

    for c in (0, 1):
        hr_wait(2, c)
        norm_two_back(c)
        hg_start(3, c)
    rs_round(DOWN, 2)
    for c in (0, 1):
        hg_forward(3, c)
    for c in (0, 1):
        hg_finish(3, c)

    def mixed_back(i):
        rw = ds(i * tm, tm)
        g = dot_nn(r.gatt[rw, :], r.wo[...])
        attn, bottom = r.numer[rw, :], r.denom[rw, :]
        r.g_num[rw, :] = (g / jnp.maximum(bottom, 1.0)).astype(BF)
        prod = g * attn
        lh = lane_head[:tm]
        acc = jnp.zeros((tm, local), F32)
        for hd in range(heads):
            acc = acc + jnp.where(
                lh == hd,
                jnp.sum(jnp.where(lh == hd, prod, 0.0), axis=1, keepdims=True),
                0.0,
            )
        r.g_den[rw, :] = jnp.where(bottom > 1.0, -acc / jnp.maximum(bottom, 1.0), 0.0)

    loop(tokens // tm, mixed_back)

    for b in range(batches):
        q = r.qf[rows_of(b), :].astype(F32) * wide(r.car[b])
        moved = dot_tn(q.astype(BF), r.g_num[rows_of(b), :])
        a, t = fold(moved, jnp.sum(q * r.g_den[rows_of(b), :], axis=0, keepdims=True))
        r.gs_send[b, 0:DH, :] = a
        r.gs_send[b, DH:, :] = t
    state_send(1, r.gs_send, r.gs_recv, -1)
    rs_round(UP, 2)

    def head_lanes(hd, value):
        return jnp.where(lane_head == hd, value.astype(F32), 0.0).astype(BF)

    for b in range(batches):
        rw = rows_of(b)
        gk = jnp.zeros((rows, local), F32)
        gv = jnp.zeros((rows, local), F32)
        gq = jnp.zeros((rows, local), F32)
        for hd in range(heads):
            gn = head_lanes(hd, r.g_num[rw, :])
            g = dot_nt(gn, r.vf[rw, :]) + r.g_den[rw, hd * DH : hd * DH + 1]
            g = (g * r.mask[b]).astype(BF)
            gq = gq + dot_nn(g, head_lanes(hd, r.kf[rw, :]))
            gk = gk + dot_tn(g, head_lanes(hd, r.qf[rw, :]))
            gv = gv + dot_tn(r.low[b, :, hd * rows : (hd + 1) * rows], gn)
        left = both(b, r.g_num[rw, :], before_thr[b])
        states = jnp.concatenate([unfold(r.st_recv.at[i, b]) for i in (0, 1)], axis=1)
        totals = (
            r.st_recv[0, b, DH : DH + 16, :].astype(F32)[0:1]
            + before_thr[b] * r.st_recv[1, b, DH : DH + 16, :].astype(F32)[0:1]
        )
        gq = gq + dot_nt(left, states) + wide(r.car[b]) * r.g_den[rw, :] * totals
        r.gproj[0, rw, :] = (gq * r.phi_d[0, rw, :]).astype(BF)
        r.gk[rw, :] = gk
        r.gv[rw, :] = gv

    rs_round(OUT, 0)
    state_wait(1, r.gs_recv)
    for b in range(batches):
        rw = rows_of(b)
        thr = after_thr[b]
        states = [unfold(r.gs_recv.at[i, b]) for i in (0, 1)]
        totals = (
            r.gs_recv[0, b, DH : DH + 16, :].astype(F32)[0:1]
            + thr * r.gs_recv[1, b, DH : DH + 16, :].astype(F32)[0:1]
        )
        k = r.kf[rw, :].astype(F32) * wide(r.tail[b])
        v = r.vf[rw, :].astype(F32) * wide(r.tail[b])
        k2 = jnp.concatenate([k.astype(BF), (k * thr).astype(BF)], axis=1)
        v2 = jnp.concatenate([v.astype(BF), (v * thr).astype(BF)], axis=1)
        gk = r.gk[rw, :] + dot_nt(v2, jnp.concatenate(states, axis=1)) + wide(r.tail[b]) * totals
        gv = r.gv[rw, :] + dot_nn(k2, jnp.concatenate(states, axis=0))
        r.gproj[1, rw, :] = (gk * wide(r.pmc[b]) * r.phi_d[1, rw, :]).astype(BF)
        r.gproj[2, rw, :] = gv.astype(BF)

    rs_round(QKV, 0)
    rs_round(DOWN, 3)

    def picks(where):
        return [
            jnp.concatenate([r.gproj[kind, rw, :] for rw in where], axis=0) for kind in range(3)
        ]

    def first_term(left, cols):
        v = dot_nt(left[0], r.wq[0, cols, :])
        for kind in (1, 2):
            v = v + dot_nt(left[kind], r.wq[kind, cols, :])
        return v

    hr_first(3, 0, picks, first_term)
    hr_first(3, 1, picks, first_term)
    hr_second(3, 0)
    hr_second(3, 1)
    rs_round(QKV, 1)
    rs_round(OUT, 1)
    rs_round(UP, 3)
    hr_first(1, 0, pick(r.activ), product_nt(r.wd))
    hr_first(1, 1, pick(r.activ), product_nt(r.wd))
    hr_second(1, 0)
    hr_second(1, 1)

    def norm_one_back(c):
        def some(i):
            at_row = c * part_rows + i * tile
            rw = ds(at_row, tile)
            g = hr_value(3, c, ds(i * tile, tile))
            u, inverse = unit(x_rows(at_row))
            r.i_rows[rw, :] = r.g_mid[rw, :] + back_norm(g, u, inverse, gain_one)
            r.hs_send[0:1, :] += jnp.sum(g * u, axis=0, keepdims=True)
            r.hs_send[2:3, :] += jnp.sum(g, axis=0, keepdims=True)

        loop(part_rows // tile, some)

    for c in (0, 1):
        hr_wait(3, c)
        norm_one_back(c)
    turn(1, r.i_rows, r.ing_o)
    rs_round(OUT, 2)
    rs_round(QKV, 2)

    def finish_rows(c):
        def some(i):
            rw = ds(c * part_rows + i * tile, tile)
            r.a_rows[rw, :] = r.middle[rw, :] + hr_value(1, c, ds(i * tile, tile)) + shift_out

        loop(part_rows // tile, some)

    for c in (0, 1):
        hr_wait(1, c)
        finish_rows(c)
    turn(0, r.a_rows, r.act_o)

    r.hs_recv[h] = r.hs_send[...]
    for i in range(1, m):
        remote(
            r.hs_send, r.hs_recv.at[h], r.hs_s.at[0], r.hs_r.at[0], s, lax.rem(h + i, m)
        ).start()
    r.upb[...] = jnp.zeros_like(r.upb)

    def column_sums(i):
        r.upb[...] += jnp.sum(r.g_hid[ds(i * tile, tile), :].astype(F32), axis=0, keepdims=True)

    loop(tokens // tile, column_sums)
    rs_round(OUT, 3)
    rs_final(DOWN)
    landed(r.hs_recv.at[pl.ds(0, m - 1)], r.hs_r.at[0])
    acc = r.hs_recv[0]
    for i in range(1, m):
        acc = acc + r.hs_recv[i]
    r.sg[...] = acc
    r.sg[5:6, :] = r.upb[...]
    r.ss_recv[s] = r.sg[:, ds(s * block, block)]
    for i in range(1, n):
        to = lax.rem(s + i, n)
        remote(
            r.sg.at[:, ds(to * block, block)],
            r.ss_recv.at[s],
            r.ss_s.at[0],
            r.ss_r.at[0],
            to,
            h,
        ).start()
    rs_final(UP)
    rs_round(QKV, 3)
    rs_final(OUT)
    landed(r.ss_recv.at[pl.ds(0, n - 1)], r.ss_r.at[0])
    acc = r.ss_recv[0]
    for i in range(1, n):
        acc = acc + r.ss_recv[i]
    r.gg_o[...] = acc[0:2]
    r.gb_o[...] = acc[2:5]
    r.gup_o[...] = acc[5:6]
    turn_wait(0, r.a_rows)
    turn_wait(1, r.i_rows)

    far = pl.ds(0, (n - 1) * block)
    for w in range(5):
        views = (r.wq.at[:, far, :], r.wo.at[far], r.wu.at[far], r.wd.at[far], r.smallg.at[:, far])
        drained(views[w], r.ag_s.at[w])
    others = pl.ds(0, (m - 1) * local)
    rest = pl.ds(0, (m - 1) * own)
    for k in range(4):
        view = (r.xg, r.cg)[k].at[:, :, others] if k < 2 else (r.ntwo, r.gatt)[k - 2].at[rest]
        drained(view, r.hg_s.at[k])
        drained(r.h_s1.at[k], r.hr_s.at[k, 0])
        drained(r.h_s2.at[k], r.hr_s.at[k, 1])
    for k, dest in enumerate((r.st_recv, r.gs_recv)):
        drained(dest, r.st_s.at[k])
    drained(r.a_rows.at[:, others], r.aa_s.at[0])
    drained(r.i_rows.at[:, others], r.aa_s.at[1])
    drained(r.hs_recv.at[pl.ds(0, m - 1)], r.hs_s.at[0])
    drained(r.ss_recv.at[pl.ds(0, n - 1)], r.ss_s.at[0])
    rs_final(QKV)
    for w in range(4):
        drained(rs_send[w].at[pl.ds(0, n - 1)], r.rs_s.at[w])
    for copy in local_copies:
        copy.wait()


def settle(*refs):
    count = (len(refs) - 1) // 3
    src, dst, mid, sems = refs[:count], refs[count : 2 * count], refs[2 * count : -1], refs[-1]
    into = [pltpu.make_async_copy(src[i], mid[i], sems.at[0, i]) for i in range(count)]
    out = [pltpu.make_async_copy(mid[i], dst[i], sems.at[1, i]) for i in range(count)]
    for copy in into:
        copy.start()
    for i in range(count):
        into[i].wait()
        out[i].start()
    for copy in out:
        copy.wait()


def whole_layer(n, m):
    def on_each(
        tokens, cotangent, w_qkv, w_out_t, w_up, w_down_t, gains, biases, up_bias, lengths, pixel_mask
    ):
        batches, rows, local = tokens.shape
        width = w_qkv.shape[0] * n
        hidden = w_up.shape[1]
        block = width // n
        vm, sems = layout(n, m, batches, rows, width, local, hidden)
        ins = ["tok", "cot", "w_qkv", "w_out", "w_up", "w_down", "gains", "biases", "up_bias", "lengths", "pixel"]
        outs = ["act_o", "ing_o", "gq_o", "go_o", "gu_o", "gd_o", "gg_o", "gb_o", "gup_o"]
        anywhere = pl.BlockSpec(memory_space=pl.ANY)
        in_vmem = pl.BlockSpec(memory_space=pltpu.VMEM)
        in_smem = pl.BlockSpec(memory_space=pltpu.SMEM)

        def wide(*shape):
            return jax.ShapeDtypeStruct(shape, F32)

        result = pl.pallas_call(
            functools.partial(body, n, m, ins + outs + list(vm) + list(sems)),
            name="layer",
            out_shape=(
                wide(batches, rows, local),
                wide(batches, rows, local),
                wide(3, block, local),
                wide(block, local),
                wide(block, hidden),
                wide(block, hidden),
                wide(2, block),
                wide(3, block),
                wide(1, block),
            ),
            in_specs=[anywhere] * 6 + [in_vmem] * 3 + [in_smem, in_vmem],
            out_specs=[anywhere] * 6 + [in_vmem] * 3,
            scratch_shapes=[pltpu.VMEM(shape, kind) for shape, kind in vm.values()]
            + [pltpu.SemaphoreType.DMA(shape) for shape in sems.values()],
            compiler_params=pltpu.CompilerParams(
                collective_id=0, has_side_effects=True, vmem_limit_bytes=66_000_000
            ),
        )(
            tokens,
            cotangent,
            jnp.transpose(w_qkv, (1, 0, 2)),
            w_out_t,
            w_up,
            w_down_t,
            gains,
            biases,
            up_bias,
            lengths,
            pixel_mask,
        )
        result = pl.pallas_call(
            settle,
            name="settle",
            out_shape=[jax.ShapeDtypeStruct(a.shape, a.dtype) for a in result],
            in_specs=[anywhere] * len(result),
            out_specs=[anywhere] * len(result),
            scratch_shapes=[pltpu.VMEM(a.shape, a.dtype) for a in result]
            + [pltpu.SemaphoreType.DMA((2, len(result)))],
        )(*result)
        return (*result[:2], jnp.transpose(result[2], (1, 0, 2)), *result[3:])

    return on_each


def solution(mesh):
    in_specs = (
        P(None, "seq", "head"),
        P(None, "seq", "head"),
        P("seq", None, "head"),
        P("seq", "head"),
        P("seq", "head"),
        P("seq", "head"),
        P(None, "seq"),
        P(None, "seq"),
        P("head", "seq"),
        P(),
        P(None, "seq"),
    )
    out_specs = (
        P(None, "seq", "head"),
        P(None, "seq", "head"),
        P("seq", None, "head"),
        P("seq", "head"),
        P("seq", "head"),
        P("seq", "head"),
        P(None, "seq"),
        P(None, "seq"),
        P("head", "seq"),
    )
    n, m = mesh.shape["seq"], mesh.shape["head"]
    fits = (n, m) == (8, 4)
    return jax.shard_map(
        whole_layer(n, m) if fits else on_device, mesh=mesh, in_specs=in_specs, out_specs=out_specs, check_vma=False
    )
```

```python
import functools

import jax
import jax.numpy as jnp
from jax import lax
from jax.experimental import pallas as pl
from jax.experimental.pallas import tpu as pltpu
from jax.sharding import PartitionSpec as P

DH = 64


highest = lax.Precision.HIGHEST
epsilon = 1e-05


def entering(array, axis, join, neutral):
    place = lax.axis_index(axis)
    gathered = jax.tree.map(
        lambda a, kind: lax.all_gather(a.astype(kind), axis),
        array,
        (jnp.bfloat16, jnp.bfloat16, jnp.bfloat16),
    )
    state = jax.tree.map(lambda a, e: jnp.zeros_like(a) + jnp.asarray(e, a.dtype), array, neutral)

    def one(hop, state):
        return join(
            state,
            jax.tree.map(
                lambda a, own: lax.dynamic_index_in_dim(a, hop, 0, False).astype(own.dtype),
                gathered,
                array,
            ),
        )

    return lax.fori_loop(0, place, one, state)


def entering_2(array, axis, combine, identity):
    length, place = (lax.axis_size(axis), lax.axis_index(axis))
    everything = jax.tree.map(
        lambda part, kind: lax.all_gather(part.astype(kind), axis),
        array,
        jax.tree.map(lambda a: jnp.bfloat16 if a.dtype == jnp.float32 else a.dtype, array),
    )
    start = jax.tree.map(
        lambda part, zero: jnp.broadcast_to(jnp.asarray(zero, part.dtype), part.shape),
        array,
        identity,
    )

    def hop(k, before):
        at = length - 1 - k
        reached = at > place
        new = combine(
            before, jax.tree.map(lambda part, own: part[at].astype(own.dtype), everything, array)
        )
        return jax.tree.map(lambda a, b: jnp.where(reached, a, b), new, before)

    return lax.fori_loop(0, length, hop, start)


def normalize(values, gain_vec, shift_vec):
    mean_val = jnp.mean(values, axis=-1, keepdims=True)
    centered = values - mean_val
    inverse = lax.rsqrt(jnp.mean(centered * centered, axis=-1, keepdims=True) + epsilon)
    unit_val = centered * inverse
    return (unit_val * gain_vec + shift_vec, unit_val, inverse)


def norm_back(grad_in, unit_val, inverse, gain_vec):
    scaled = grad_in * gain_vec
    centered = scaled - jnp.mean(scaled, axis=-1, keepdims=True)
    return inverse * (centered - unit_val * jnp.mean(scaled * unit_val, axis=-1, keepdims=True))


def features(values):
    return jax.nn.elu(values) + 1.0


def finish(numerator, denominator):
    return numerator / jnp.maximum(denominator, 1.0)[:, :, None]


def compose(earlier, later):
    return (
        later[0] + later[2] * earlier[0],
        later[1] + later[2] * earlier[1],
        later[2] * earlier[2],
    )


def item_numbers(lengths_row, first_place, number):
    offsets = jnp.cumsum(lengths_row) - lengths_row
    places = first_place + jnp.arange(number, dtype=jnp.int32)
    return jnp.sum((offsets[None, :] <= places[:, None]).astype(jnp.int32), axis=1) - 1


def on_device(
    tokens, cotangent, w_qkv, w_out_t, w_up, w_down_t, gains, biases, up_bias, lengths, pixel_mask
):
    batches, local_rows, columns = tokens.shape
    local_width = w_qkv.shape[2]
    heads_here = local_width // DH
    seq_index = lax.axis_index("seq")
    head_index = lax.axis_index("head")
    first_token = seq_index * local_rows
    position = jnp.arange(local_rows, dtype=jnp.int32)
    before = position[:, None] >= position[None, :]

    def own_columns(matrix):
        return lax.dynamic_slice_in_dim(matrix, head_index * columns, columns, 1)

    results = []
    input_grads = []
    shard_sums = None
    for batch_index in range(batches):
        full_qkv, full_out, full_up, full_down, full_gains, full_biases, full_upb = (
            lax.all_gather(w_qkv, "seq", axis=0, tiled=True),
            lax.all_gather(w_out_t, "seq", axis=0, tiled=True),
            lax.all_gather(w_up, "seq", axis=0, tiled=True),
            lax.all_gather(w_down_t, "seq", axis=0, tiled=True),
            lax.all_gather(gains, "seq", axis=1, tiled=True),
            lax.all_gather(biases, "seq", axis=1, tiled=True),
            lax.all_gather(up_bias, "seq", axis=1, tiled=True),
        )
        input_rows, grad_rows16 = (
            lax.all_gather(tokens[batch_index], "head", axis=1, tiled=True),
            lax.all_gather(cotangent[batch_index], "head", axis=1, tiled=True),
        )
        gains32 = full_gains.astype(jnp.float32)
        biases32 = full_biases.astype(jnp.float32)
        upb32 = full_upb.astype(jnp.float32).reshape(-1)
        inputs32 = input_rows.astype(jnp.float32)
        place_items = item_numbers(lengths[batch_index], first_token - 1, local_rows + 1)
        item_of = place_items[1:]
        carried = (item_of == place_items[0]).astype(jnp.float32)
        tail_mask = (item_of == item_of[local_rows - 1]).astype(jnp.float32)
        through = carried[local_rows - 1]
        same_item = ((item_of[:, None] == item_of[None, :]) & before).astype(jnp.float32)
        keep_half = pixel_mask[batch_index].astype(jnp.bfloat16)
        keep32 = pixel_mask[batch_index].astype(jnp.float32)
        lifted, unit_one, inverse_one = normalize(inputs32, gains32[0], biases32[0])
        normed = lifted.astype(jnp.bfloat16)
        projected = jnp.einsum("td,dsf->tsf", normed, full_qkv, preferred_element_type=jnp.float32)
        query_feat = (
            features(projected[:, 0]).astype(jnp.bfloat16).reshape(local_rows, heads_here, DH)
        )
        key_feat = (features(projected[:, 1]).astype(jnp.bfloat16) * keep_half[:, None]).reshape(
            local_rows, heads_here, DH
        )
        value_feat = projected[:, 2].astype(jnp.bfloat16).reshape(local_rows, heads_here, DH)
        tail_key = key_feat * tail_mask.astype(jnp.bfloat16)[:, None, None]
        state_loc = jnp.einsum(
            "jhd,jhe->hde", tail_key, value_feat, preferred_element_type=jnp.float32
        )
        total_loc = jnp.sum(tail_key.astype(jnp.float32), axis=0)
        identity = (jnp.zeros_like(state_loc), jnp.zeros_like(total_loc), jnp.ones((), jnp.float32))
        state_in, total_in, passed = entering(
            (state_loc, total_loc, through), "seq", compose, identity
        )
        query32 = query_feat.astype(jnp.float32)
        scores = (
            jnp.einsum("thd,jhd->htj", query_feat, key_feat, preferred_element_type=jnp.float32)
            * same_item[None]
        )
        scores_low = scores.astype(jnp.bfloat16)
        numerator = jnp.einsum(
            "htj,jhe->the", scores_low, value_feat, preferred_element_type=jnp.float32
        ) + carried[:, None, None] * jnp.einsum(
            "thd,hde->the", query32, state_in, precision=highest
        )
        denominator = jnp.sum(scores, axis=2).T + carried[:, None] * jnp.einsum(
            "thd,hd->th", query32, total_in, precision=highest
        )
        output, finish_back = jax.vjp(finish, numerator, denominator)
        mixed_out = output.reshape(local_rows, local_width).astype(jnp.bfloat16)
        attended = lax.psum(
            jnp.einsum("tf,df->td", mixed_out, full_out, preferred_element_type=jnp.float32).astype(
                jnp.bfloat16
            ),
            "head",
        ).astype(jnp.float32)
        middle = inputs32 + attended
        lifted_two, unit_two, inverse_two = normalize(middle, gains32[1], biases32[1])
        normed_two = lifted_two.astype(jnp.bfloat16)
        hidden = jnp.dot(normed_two, full_up, preferred_element_type=jnp.float32) + upb32
        activated32, gelu_back = jax.vjp(jax.nn.gelu, hidden)
        activated = activated32.astype(jnp.bfloat16)
        branch = lax.psum_scatter(
            jnp.einsum(
                "tf,df->td", activated, full_down, preferred_element_type=jnp.float32
            ).astype(jnp.bfloat16),
            "head",
            scatter_dimension=1,
            tiled=True,
        ).astype(jnp.float32)
        results.append(own_columns(middle) + branch + own_columns(biases32[2][None]))
        grad_out = grad_rows16.astype(jnp.float32)
        grad_down = jnp.einsum(
            "td,tf->df", grad_rows16, activated, preferred_element_type=jnp.float32
        )
        grad_act = jnp.einsum(
            "td,df->tf", grad_rows16, full_down, preferred_element_type=jnp.float32
        )
        grad_hidden = gelu_back(grad_act)[0].astype(jnp.bfloat16)
        grad_up = jnp.einsum(
            "td,tf->df", normed_two, grad_hidden, preferred_element_type=jnp.float32
        )
        grad_upb = jnp.sum(grad_hidden.astype(jnp.float32), axis=0).reshape(full_upb.shape)
        grad_two = lax.psum(
            jnp.einsum(
                "tf,df->td", grad_hidden, full_up, preferred_element_type=jnp.float32
            ).astype(jnp.bfloat16),
            "head",
        ).astype(jnp.float32)
        grad_middle = grad_out + norm_back(grad_two, unit_two, inverse_two, gains32[1])
        grad_attended = grad_middle.astype(jnp.bfloat16)
        grad_out_t = jnp.einsum(
            "td,tf->df", grad_attended, mixed_out, preferred_element_type=jnp.float32
        )
        grad_mixed = jnp.einsum(
            "td,df->tf", grad_attended, full_out, preferred_element_type=jnp.float32
        ).reshape(local_rows, heads_here, DH)
        grad_numer32, grad_denom = finish_back(grad_mixed)
        grad_numer = grad_numer32.astype(jnp.bfloat16)
        grad_numer_wide = grad_numer.astype(jnp.float32)
        grad_scores = (
            (
                jnp.einsum(
                    "the,jhe->htj", grad_numer, value_feat, preferred_element_type=jnp.float32
                )
                + grad_denom.T[:, :, None]
            )
            * same_item[None]
        ).astype(jnp.bfloat16)
        carried_query = query32 * carried[:, None, None]
        grad_query = jnp.einsum(
            "htj,jhd->thd", grad_scores, key_feat, preferred_element_type=jnp.float32
        ) + carried[:, None, None] * (
            jnp.einsum("hde,the->thd", state_in, grad_numer_wide, precision=highest)
            + grad_denom[:, :, None] * total_in[None]
        )
        grad_key = jnp.einsum(
            "htj,thd->jhd", grad_scores, query_feat, preferred_element_type=jnp.float32
        )
        grad_value = jnp.einsum(
            "htj,the->jhe", scores_low, grad_numer, preferred_element_type=jnp.float32
        )
        grad_state_in = jnp.einsum(
            "thd,the->hde", carried_query, grad_numer_wide, precision=highest
        )
        grad_total_in = jnp.einsum("thd,th->hd", carried_query, grad_denom, precision=highest)
        grad_state_loc, grad_total_loc, passed_back = entering_2(
            (grad_state_in, grad_total_in, through), "seq", compose, identity
        )
        tail_three = tail_mask[:, None, None]
        value_wide = value_feat.astype(jnp.float32)
        key_wide = key_feat.astype(jnp.float32)
        grad_key = grad_key + tail_three * (
            jnp.einsum("hde,jhe->jhd", grad_state_loc, value_wide, precision=highest)
            + grad_total_loc[None]
        )
        grad_value = grad_value + tail_three * jnp.einsum(
            "jhd,hde->jhe", key_wide, grad_state_loc, precision=highest
        )
        ignored, feature_back = jax.vjp(features, projected[:, :2])
        grad_features = jnp.stack(
            [
                grad_query.reshape(local_rows, local_width),
                grad_key.reshape(local_rows, local_width) * keep32[:, None],
            ],
            axis=1,
        )
        grad_pair = feature_back(grad_features)[0]
        grad_projected = jnp.concatenate(
            [grad_pair, grad_value.reshape(local_rows, 1, local_width)], axis=1
        ).astype(jnp.bfloat16)
        grad_qkv = jnp.einsum(
            "td,tsf->dsf", normed, grad_projected, preferred_element_type=jnp.float32
        )
        grad_one = lax.psum(
            jnp.einsum(
                "tsf,dsf->td", grad_projected, full_qkv, preferred_element_type=jnp.float32
            ).astype(jnp.bfloat16),
            "head",
        ).astype(jnp.float32)
        grad_inputs = grad_middle + norm_back(grad_one, unit_one, inverse_one, gains32[0])
        input_grads.append(own_columns(grad_inputs))
        grad_gains = jnp.stack(
            [jnp.sum(grad_one * unit_one, axis=0), jnp.sum(grad_two * unit_two, axis=0)]
        )
        grad_biases = jnp.stack(
            [jnp.sum(grad_one, axis=0), jnp.sum(grad_two, axis=0), jnp.sum(grad_out, axis=0)]
        )
        pieces = (
            lax.psum_scatter(grad_qkv, "seq", scatter_dimension=0, tiled=True),
            lax.psum_scatter(grad_out_t, "seq", scatter_dimension=0, tiled=True),
            lax.psum_scatter(grad_up, "seq", scatter_dimension=0, tiled=True),
            lax.psum_scatter(grad_down, "seq", scatter_dimension=0, tiled=True),
            lax.psum_scatter(grad_gains, "seq", scatter_dimension=1, tiled=True),
            lax.psum_scatter(grad_biases, "seq", scatter_dimension=1, tiled=True),
            lax.psum_scatter(grad_upb, "seq", scatter_dimension=1, tiled=True),
        )
        shard_sums = pieces if shard_sums is None else jax.tree.map(jnp.add, shard_sums, pieces)
    return (
        jnp.stack(results),
        jnp.stack(input_grads),
        shard_sums[0],
        shard_sums[1],
        shard_sums[2],
        shard_sums[3],
        shard_sums[4],
        shard_sums[5],
        shard_sums[6],
    )


MESH = pl.DeviceIdType.MESH
BF = jnp.bfloat16
F32 = jnp.float32
QKV, OUT, UP, DOWN, SMALL = range(5)


def dot_nn(a, b):
    return lax.dot_general(a, b, (((1,), (0,)), ((), ())), preferred_element_type=F32)


def dot_nt(a, b):
    return lax.dot_general(a, b, (((1,), (1,)), ((), ())), preferred_element_type=F32)


def dot_tn(a, b):
    return lax.dot_general(a, b, (((0,), (0,)), ((), ())), preferred_element_type=F32)


def ds(start, size):
    return pl.ds(pl.multiple_of(start, size), size)


def loop(count, body):
    def step(i, carry):
        body(i)
        return carry

    lax.fori_loop(0, count, step, 0)


def layout(n, m, batches, rows, width, local, hidden):
    tokens = batches * rows
    block = width // n
    own = tokens // m
    hops = n // 2
    heads = local // DH
    vm = {
        "xg": ((batches, rows, width), BF),
        "cg": ((batches, rows, width), BF),
        "wq": ((3, width, local), BF),
        "wo": ((width, local), BF),
        "wu": ((width, hidden), BF),
        "wd": ((width, hidden), BF),
        "small": ((8, block), F32),
        "smallg": ((8, width), F32),
        "normed": ((tokens, width), BF),
        "phi_d": ((2, tokens, local), F32),
        "qf": ((tokens, local), BF),
        "kf": ((tokens, local), BF),
        "vf": ((tokens, local), BF),
        "mask": ((batches, rows, rows), F32),
        "car": ((batches, rows, 128), F32),
        "tail": ((batches, rows, 128), F32),
        "pmc": ((batches, rows, 128), F32),
        "low": ((batches, rows, heads * rows), BF),
        "numer": ((tokens, local), F32),
        "denom": ((tokens, local), F32),
        "mixed": ((tokens, local), BF),
        "st_send": ((batches * DH + 16, local), BF),
        "st_recv": ((2, batches * DH + 16, local), BF),
        "gs_send": ((batches * DH + 16, local), BF),
        "gs_recv": ((2, batches * DH + 16, local), BF),
        "middle": ((own, width), F32),
        "ntwo": ((tokens, width), BF),
        "gelu_d": ((tokens, hidden), F32),
        "activ": ((tokens, hidden), BF),
        "g_hid": ((tokens, hidden), BF),
        "branch": ((own, width), F32),
        "total": ((own, width), F32),
        "g_mid": ((own, width), F32),
        "gatt": ((tokens, width), BF),
        "g_attn": ((tokens, local), F32),
        "g_num": ((tokens, local), BF),
        "g_den": ((tokens, local), F32),
        "gq": ((tokens, local), F32),
        "gk": ((tokens, local), F32),
        "gv": ((tokens, local), F32),
        "gproj": ((3, tokens, local), BF),
        "h_s1": ((4, 2, 2, own // 2, width), BF),
        "h_r1": ((4, 2, 2, own // 2, width), BF),
        "h_acc": ((4, 2, 2, own // 2, width), F32),
        "h_s2": ((4, 2, own // 2, width), BF),
        "h_r2": ((4, 2, own // 2, width), BF),
        "rq_s": ((n, 3, block, local), BF),
        "rq_r": ((n, 3, block, local), BF),
        "ro_s": ((n, block, local), BF),
        "ro_r": ((n, block, local), BF),
        "ru_s": ((n, block, hidden), BF),
        "ru_r": ((n, block, hidden), BF),
        "rd_s": ((n, block, hidden), BF),
        "rd_r": ((n, block, hidden), BF),
        "hs_recv": ((m, 8, width), F32),
        "hs_send": ((8, width), F32),
        "upb": ((1, hidden), F32),
        "sg": ((8, width), F32),
        "ss_recv": ((n, 8, block), F32),
        "a_rows": ((own, width), F32),
        "i_rows": ((own, width), F32),
    }
    sems = {
        "ag_s": (5,),
        "ag_r": (5, 2, hops),
        "rs_s": (4,),
        "rs_r": (4, 2, hops),
        "hg_s": (4,),
        "hg_r": (4, 2, 3),
        "hr_s": (4, 2),
        "hr_r": (4, 2, 2),
        "st_s": (2,),
        "st_r": (2,),
        "aa_s": (2,),
        "aa_r": (2,),
        "hs_s": (1,),
        "hs_r": (1,),
        "ss_s": (1,),
        "ss_r": (1,),
        "lc": (12,),
    }
    return vm, sems


class Refs:
    pass


def body(n, m, names, *refs):
    r = Refs()
    for name, ref in zip(names, refs):
        setattr(r, name, ref)
    batches, rows, width = r.xg.shape
    tokens = batches * rows
    own = tokens // m
    block = width // n
    local = r.wo.shape[1]
    hidden = r.wu.shape[1]
    heads = local // DH
    hops = n // 2
    s = lax.axis_index("seq")
    h = lax.axis_index("head")
    odd = lax.rem(s, 2)
    p = (1 - odd) * lax.div(s, 2) + odd * (n - 1 - lax.div(s, 2))
    lo, hi = lax.rem(h, 2), lax.div(h, 2)
    pair = h + 1 - 2 * lo
    cross = lax.rem(h + 2, m)

    def at(place):
        place = lax.rem(place + 2 * n, n)
        far = lax.div(place, hops)
        return (1 - far) * 2 * place + far * (2 * (n - 1 - place) + 1)

    ring = (at(p + 1), at(p - 1))
    sign = (1, -1)

    def remote(src, dst, send, recv, seq, head):
        return pltpu.make_async_remote_copy(
            src_ref=src,
            dst_ref=dst,
            send_sem=send,
            recv_sem=recv,
            device_id=(seq, head),
            device_id_type=MESH,
        )

    def drained(view, sem):
        remote(view, view, sem, sem, ring[0], h).wait_send()

    def landed(view, sem):
        remote(view, view, sem, sem, ring[0], h).wait_recv()

    r.small[...] = jnp.zeros_like(r.small)
    r.small[0:2, :] = r.gains[...].astype(F32)
    r.small[2:5, :] = r.biases[...].astype(F32)
    r.small[5:6, :] = r.up_bias[...].astype(F32)

    barrier = pltpu.get_barrier_semaphore()
    for peer in ((ring[0], h), (ring[1], h), (s, pair), (s, cross)):
        pl.semaphore_signal(barrier, inc=1, device_id=peer, device_id_type=MESH)
    pl.semaphore_wait(barrier, 4)

    shards = (r.w_qkv, r.w_out, r.w_up, r.w_down, r.small)
    gathered = (r.wq, r.wo, r.wu, r.wd, r.smallg)

    def part_of(w, d, j):
        wide_part = r.wq.shape[2] if w == QKV else shards[w].shape[1]
        if j < hops - 1 or w == SMALL:
            return pl.ds(0, wide_part)
        return pl.ds(d * (wide_part // 2), wide_part // 2)

    def ag_shard(w, d, j):
        cols = part_of(w, d, j)
        if w == SMALL:
            return r.small
        return shards[w].at[:, :, cols] if w == QKV else shards[w].at[:, cols]

    def ag_full(w, owner, d, j):
        cols = part_of(w, d, j)
        if w == SMALL:
            return r.smallg.at[:, ds(owner * block, block)]
        if w == QKV:
            return r.wq.at[:, ds(owner * block, block), cols]
        return gathered[w].at[ds(owner * block, block), cols]

    def ways(w, j):
        return (0,) if w == SMALL and j == hops - 1 else (0, 1)

    def ag_send(w, j):
        for d in ways(w, j):
            owner = at(p - sign[d] * j)
            src = ag_shard(w, d, j) if j == 0 else ag_full(w, owner, d, j)
            remote(
                src, ag_full(w, owner, d, j), r.ag_s.at[w], r.ag_r.at[w, d, j], ring[d], h
            ).start()

    def ag_wait(w, j):
        for d in ways(w, j):
            landed(ag_full(w, at(p - sign[d] * (j + 1)), d, j), r.ag_r.at[w, d, j])

    def ag_pass(w, j):
        ag_wait(w, j)
        ag_send(w, j + 1)

    part_rows = own // 2

    def hg_view(k, c, who):
        if k < 2:
            return (r.xg, r.cg)[k].at[c, :, ds(who * local, local)]
        return (r.ntwo, r.gatt)[k - 2].at[ds(who * own + c * part_rows, part_rows), :]

    def hg_copy(k, c, i, src, who, to):
        return remote(src, hg_view(k, c, who), r.hg_s.at[k], r.hg_r.at[k, c, i], s, to)

    def hg_start(k, c):
        src = (r.tok, r.cot)[k].at[c] if k < 2 else hg_view(k, c, h)
        hg_copy(k, c, 1, src, h, cross).start()
        hg_copy(k, c, 0, src, h, pair).start()

    def hg_forward(k, c):
        view = hg_view(k, c, cross)
        hg_copy(k, c, 1, view, cross, cross).wait_recv()
        hg_copy(k, c, 2, view, cross, pair).start()

    def hg_finish(k, c):
        view = hg_view(k, c, pair)
        hg_copy(k, c, 0, view, pair, pair).wait_recv()
        across = lax.rem(pair + 2, m)
        view = hg_view(k, c, across)
        hg_copy(k, c, 2, view, across, pair).wait_recv()

    tn = 256

    def hr_first(k, c, left, product):
        blocks = [2 * i + 1 - lo for i in (0, 1)] + [2 * i + lo for i in (0, 1)]
        where = [ds(who * own + c * part_rows, part_rows) for who in blocks]

        def some(i):
            cols = ds(i * tn, tn)
            v = product(left(where), cols)
            for q in (0, 1):
                r.h_s1[k, c, q, :, cols] = v[q * part_rows : (q + 1) * part_rows].astype(BF)
                r.h_acc[k, c, q, :, cols] = v[(q + 2) * part_rows : (q + 3) * part_rows]

        loop(width // tn, some)
        hr_copy(k, c, 0).start()

    def hr_copy(k, c, stage):
        if stage == 0:
            src, dst, to = r.h_s1.at[k, c], r.h_r1.at[k, c], pair
        else:
            src, dst, to = r.h_s2.at[k, c], r.h_r2.at[k, c], cross
        return remote(src, dst, r.hr_s.at[k, stage], r.hr_r.at[k, c, stage], s, to)

    def hr_second(k, c):
        hr_copy(k, c, 0).wait_recv()

        def away(i):
            rw = ds(i * 32, 32)
            r.h_s2[k, c, rw, :] = (
                r.h_acc[k, c, 1 - hi, rw, :] + r.h_r1[k, c, 1 - hi, rw, :].astype(F32)
            ).astype(BF)

        loop(part_rows // 32, away)
        hr_copy(k, c, 1).start()

    def hr_wait(k, c):
        hr_copy(k, c, 1).wait_recv()

    def hr_value(k, c, rw):
        return (
            r.h_acc[k, c, hi, rw, :]
            + r.h_r1[k, c, hi, rw, :].astype(F32)
            + r.h_r2[k, c, rw, :].astype(F32)
        )

    def pick(ref):
        return lambda where: jnp.concatenate([ref[rw, :] for rw in where], axis=0)

    def product_nt(right):
        return lambda left, cols: dot_nt(left, right[cols, :])

    def rs_term(w, owner, piece):
        cols = ds(owner * block, block)
        if w == DOWN:
            left = r.cg[:, :, cols].reshape(tokens, block)
            half = hidden // 2
            return [dot_tn(left, r.activ[:, pl.ds(piece * half, half)])]
        if w == UP:
            half = hidden // 2
            return [dot_tn(r.ntwo[:, cols], r.g_hid[:, pl.ds(piece * half, half)])]
        half = local // 2
        if w == OUT:
            return [dot_tn(r.gatt[:, cols], r.mixed[:, pl.ds(piece * half, half)])]
        left = r.normed[:, cols]
        return [dot_tn(left, r.gproj[i, :, pl.ds(piece * half, half)]) for i in range(3)]

    rs_send = (r.rq_s, r.ro_s, r.ru_s, r.rd_s)
    rs_recv = (r.rq_r, r.ro_r, r.ru_r, r.rd_r)

    def rs_half(w, piece):
        half = rs_send[w].shape[-1] // 2
        return pl.ds(piece * half, half)

    def rs_view(ref, w, d, step):
        if step > 0:
            return ref.at[d * hops + step]
        if w == QKV:
            return ref.at[d * hops, :, :, rs_half(w, d)]
        return ref.at[d * hops, :, rs_half(w, d)]

    def rs_arrived(w, d, step):
        landed(rs_view(rs_recv[w], w, d, step), r.rs_r.at[w, d, step])

    def rs_round(w, step):
        for d in (0, 1):
            slot = d * hops + step
            if step > 0:
                rs_arrived(w, d, step - 1)
            for piece in (0, 1):
                if step == 0 and piece != d:
                    continue
                terms = rs_term(w, at(p + sign[d] * (hops - step)), piece)
                cols = rs_half(w, piece)
                for i, v in enumerate(terms):
                    lead = (i,) if w == QKV else ()
                    if step > 1 or (step == 1 and piece == d):
                        v = v + rs_recv[w][(slot - 1, *lead, slice(None), cols)].astype(F32)
                    rs_send[w][(slot, *lead, slice(None), cols)] = v.astype(BF)
            remote(
                rs_view(rs_send[w], w, d, step),
                rs_view(rs_recv[w], w, d, step),
                r.rs_s.at[w],
                r.rs_r.at[w, d, step],
                ring[d],
                h,
            ).start()

    finals = (r.gq_o, r.go_o, r.gu_o, r.gd_o)
    local_copies = []

    def rs_final(w):
        terms = [rs_term(w, s, piece) for piece in (0, 1)]
        for d in (0, 1):
            rs_arrived(w, d, hops - 1)
        for piece in (0, 1):
            cols = rs_half(w, piece)
            for i, v in enumerate(terms[piece]):
                lead = (i,) if w == QKV else ()
                for d in (0, 1):
                    v = v + rs_recv[w][(d * hops + hops - 1, *lead, slice(None), cols)].astype(F32)
                finals[w][(*lead, slice(None), cols)] = v
    def turn(k, src, dst):
        where = (hi, ds(lo * own, own))
        for i in range(1, m):
            to = lax.rem(h + i, m)
            remote(
                src.at[:, ds(to * local, local)],
                dst.at[where[0], where[1], :],
                r.aa_s.at[k],
                r.aa_r.at[k],
                s,
                to,
            ).start()
        copy = pltpu.make_async_copy(
            src.at[:, ds(h * local, local)], dst.at[where[0], where[1], :], r.lc.at[4 + k]
        )
        copy.start()
        local_copies.append(copy)

    def turn_wait(k, src):
        landed(src.at[:, pl.ds(0, (m - 1) * local)], r.aa_r.at[k])

    ag_send(SMALL, 0)
    ag_send(QKV, 0)
    ag_send(OUT, 0)
    hg_start(0, 0)
    hg_start(0, 1)
    own_copies = [
        pltpu.make_async_copy(r.w_qkv, r.wq.at[:, ds(s * block, block), :], r.lc.at[8]),
        pltpu.make_async_copy(r.w_out, r.wo.at[ds(s * block, block), :], r.lc.at[9]),
        pltpu.make_async_copy(r.w_up, r.wu.at[ds(s * block, block), :], r.lc.at[10]),
        pltpu.make_async_copy(r.w_down, r.wd.at[ds(s * block, block), :], r.lc.at[11]),
        pltpu.make_async_copy(r.tok, r.xg.at[:, :, ds(h * local, local)], r.lc.at[6]),
        pltpu.make_async_copy(r.cot, r.cg.at[:, :, ds(h * local, local)], r.lc.at[7]),
    ]
    for copy in own_copies:
        copy.start()
    hg_start(1, 0)
    hg_start(1, 1)

    first = s * rows
    row_at = lax.broadcasted_iota(jnp.int32, (rows, 128), 0)
    lane_at = lax.broadcasted_iota(jnp.int32, (rows, rows), 1)
    square = lax.broadcasted_iota(jnp.int32, (local, local), 0)
    square_lane = lax.broadcasted_iota(jnp.int32, (local, local), 1)
    same_head = (square // DH) == (square_lane // DH)
    diagonal = square == square_lane
    lane_head = lax.broadcasted_iota(jnp.int32, (rows, local), 1) // DH
    before_thr, after_thr = [], []

    def wide(value):
        return jnp.concatenate([value] * (local // 128), axis=1)

    def begin(offsets, place):
        value = 0
        for off in offsets:
            value = jnp.where(off <= place, off, value)
        return value

    def through(offsets, which):
        return jnp.where(
            begin(offsets, which * rows + rows - 1) < which * rows, 1.0, 0.0
        ).astype(F32)

    def crops(b):
        offsets, running = [], 0
        for i in range(r.lengths.shape[1]):
            offsets.append(running)
            running = running + r.lengths[b, i]
        start = jnp.zeros((rows, 128), jnp.int32)
        for off in offsets:
            start = jnp.where(off <= row_at + first, off, start)
        last = begin(offsets, first + rows - 1)
        r.mask[b] = jnp.where(
            (lane_at + first >= wide(start)) & (lane_at <= wide(row_at)), 1.0, 0.0
        ).astype(F32)
        r.car[b] = jnp.where(start < first, 1.0, 0.0).astype(F32)
        r.tail[b] = jnp.where(start == last, 1.0, 0.0).astype(F32)
        before_thr.append(through(offsets, lax.rem(s + n - 1, n)))
        after_thr.append(through(offsets, lax.rem(s + 1, n)))
        keep = r.pixel[b : b + 1, :].astype(F32)
        r.pmc[b] = dot_nn(
            jnp.where(diagonal, keep, 0.0).astype(BF), jnp.ones((rows, 128), BF)
        )

    def ag_step(j):
        ag_pass(SMALL, j)
        ag_pass(QKV, j)
        ag_pass(OUT, j)

    crops(0)
    hg_forward(0, 0)
    ag_step(0)
    hg_forward(0, 1)
    for copy in own_copies:
        copy.wait()
    r.smallg[:, ds(s * block, block)] = r.small[...]

    def unit(values):
        mean = jnp.mean(values, axis=1, keepdims=True)
        centered = values - mean
        inverse = lax.rsqrt(jnp.mean(centered * centered, axis=1, keepdims=True) + epsilon)
        return centered * inverse, inverse

    tile = 32

    def unit_one(b):
        def some(i):
            u, _ = unit(r.xg[b, ds(i * tile, tile), :].astype(F32))
            r.gelu_d[ds(b * rows + i * tile, tile), :] = u

        loop(rows // tile, some)

    def norm_one(i):
        rw = ds(i * tile, tile)
        r.normed[rw, :] = (r.gelu_d[rw, :] * gain_one + shift_one).astype(BF)

    for c in (0, 1):
        hg_finish(0, c)
    unit_one(0)
    ag_step(1)
    unit_one(1)
    crops(1)
    ag_step(2)
    ag_send(UP, 0)
    for c in (0, 1):
        hg_forward(1, c)
    ag_wait(SMALL, 3)
    gain_one, gain_two = r.smallg[0:1, :], r.smallg[1:2, :]
    shift_one, shift_two, shift_out = r.smallg[2:3, :], r.smallg[3:4, :], r.smallg[4:5, :]
    loop(tokens // tile, norm_one)
    ag_wait(QKV, 3)
    ag_wait(OUT, 3)

    tm = 128

    def project(i):
        rw = ds(i * tm, tm)
        b = lax.div(i, rows // tm)
        rb = ds(lax.rem(i, rows // tm) * tm, tm)
        left = r.normed[rw, :]
        for kind in (0, 1):
            v = dot_nn(left, r.wq[kind])
            low = jnp.exp(jnp.minimum(v, 0.0))
            f = jnp.where(v > 0.0, v + 1.0, low).astype(BF)
            r.phi_d[kind, rw, :] = low
            if kind == 0:
                r.qf[rw, :] = f
            else:
                r.kf[rw, :] = (f.astype(F32) * wide(r.pmc[b, rb, :])).astype(BF)
        r.vf[rw, :] = dot_nn(left, r.wq[2]).astype(BF)

    loop(tokens // tm, project)

    def fold(ref, parts):
        row = lax.broadcasted_iota(jnp.int32, (16, local), 0)
        sums = jnp.zeros((16, local), F32)
        for b, (matrix, total) in enumerate(parts):
            kept = jnp.where(same_head, matrix, 0.0)
            acc = kept[0:DH]
            for i in range(1, heads):
                acc = acc + kept[i * DH : (i + 1) * DH]
            ref[b * DH : (b + 1) * DH, :] = acc.astype(BF)
            sums = jnp.where(row == b, total, sums)
        ref[batches * DH :, :] = sums.astype(BF)

    def unfold(ref, i, b):
        acc = ref[i, b * DH : (b + 1) * DH, :].astype(F32)
        return jnp.where(same_head, jnp.concatenate([acc] * heads, axis=0), 0.0).astype(BF)

    def unfold_sum(ref, i, b):
        return ref[i, batches * DH :, :].astype(F32)[b : b + 1]

    def state_send(k, ref, dest, step):
        for i in (0, 1):
            to = lax.rem(s + n + step * (i + 1), n)
            remote(ref, dest.at[i], r.st_s.at[k], r.st_r.at[k], to, h).start()

    def state_wait(k, dest):
        landed(dest, r.st_r.at[k])

    def rows_of(b):
        return pl.ds(b * rows, rows)

    def by_head(value):
        return jnp.concatenate(
            [jnp.where(lane_head == hd, value.astype(F32), 0.0).astype(BF) for hd in range(heads)],
            axis=0,
        )

    parts = []
    for b in range(batches):
        k = r.kf[rows_of(b), :].astype(F32) * wide(r.tail[b])
        parts.append(
            (dot_tn(k.astype(BF), r.vf[rows_of(b), :]), jnp.sum(k, axis=0, keepdims=True))
        )
    fold(r.st_send, parts)
    state_send(0, r.st_send, r.st_recv, 1)

    for b in range(batches):
        q, k = r.qf[rows_of(b), :], r.kf[rows_of(b), :]
        acc = jnp.zeros((rows, local), F32)
        for hd in range(heads):
            sc = dot_nt(jnp.where(lane_head == hd, q.astype(F32), 0.0).astype(BF), k) * r.mask[b]
            r.low[b, :, hd * rows : (hd + 1) * rows] = sc.astype(BF)
            acc = acc + jnp.where(lane_head == hd, jnp.sum(sc, axis=1, keepdims=True), 0.0)
        r.denom[rows_of(b), :] = acc
        r.numer[rows_of(b), :] = dot_nn(r.low[b], by_head(r.vf[rows_of(b), :]))

    for c in (0, 1):
        hg_finish(1, c)
    ag_pass(UP, 0)
    ag_send(DOWN, 0)
    state_wait(0, r.st_recv)

    def both(b, value, thr):
        one = value.astype(F32) * wide(r.car[b])
        return jnp.concatenate([one.astype(BF), (one * thr).astype(BF)], axis=1)

    for b in range(batches):
        left = both(b, r.qf[rows_of(b), :], before_thr[b])
        states = jnp.concatenate([unfold(r.st_recv, i, b) for i in (0, 1)], axis=0)
        only = lax.broadcasted_iota(jnp.int32, (16, local), 0)
        sums = jnp.concatenate(
            [
                jnp.where(
                    same_head,
                    dot_tn(
                        jnp.where(
                            only == b, r.st_recv[i, batches * DH :, :].astype(F32), 0.0
                        ).astype(BF),
                        jnp.ones((16, local), BF),
                    ),
                    0.0,
                ).astype(BF)
                for i in (0, 1)
            ],
            axis=0,
        )
        top = r.numer[rows_of(b), :] + dot_nn(left, states)
        bottom = r.denom[rows_of(b), :] + dot_nn(left, sums)
        attn = top / jnp.maximum(bottom, 1.0)
        r.numer[rows_of(b), :] = attn
        r.denom[rows_of(b), :] = bottom
        r.mixed[rows_of(b), :] = attn.astype(BF)

    hr_first(0, 0, pick(r.mixed), product_nt(r.wo))
    hr_first(0, 1, pick(r.mixed), product_nt(r.wo))
    hr_second(0, 0)
    hr_second(0, 1)
    ag_pass(UP, 1)
    mine = h * own

    def x_rows(at_row):
        return r.xg[hi, ds(lo * own + at_row, tile), :].astype(F32)

    def c_rows(at_row):
        return r.cg[hi, ds(lo * own + at_row, tile), :].astype(F32)

    def norm_two(c):
        def some(i):
            at_row = c * part_rows + i * tile
            v = x_rows(at_row) + hr_value(0, c, ds(i * tile, tile))
            r.middle[ds(at_row, tile), :] = v
            u, _ = unit(v)
            r.ntwo[ds(mine + at_row, tile), :] = (u * gain_two + shift_two).astype(BF)

        loop(part_rows // tile, some)

    for c in (0, 1):
        hr_wait(0, c)
        norm_two(c)
        hg_start(2, c)
    ag_pass(DOWN, 0)
    hg_forward(2, 0)
    hg_forward(2, 1)
    ag_pass(UP, 2)
    hg_finish(2, 0)
    hg_finish(2, 1)
    ag_pass(DOWN, 1)
    ag_wait(UP, 3)

    tu = 256

    def up(i):
        rw = ds(lax.div(i, hidden // tn) * tu, tu)
        cols = ds(lax.rem(i, hidden // tn) * tn, tn)
        v = dot_nn(r.ntwo[rw, :], r.wu[:, cols]) + r.smallg[5:6, cols]
        square_of = v * v
        t = jnp.tanh(0.7978845608028654 * (v + 0.044715 * (square_of * v)))
        half = 0.5 * (1.0 + t)
        r.activ[rw, cols] = (v * half).astype(BF)
        r.gelu_d[rw, cols] = half + (0.5 * v) * (1.0 - t * t) * (
            0.7978845608028654 + (3.0 * 0.044715 * 0.7978845608028654) * square_of
        )

    loop((tokens // tu) * (hidden // tn), up)
    rs_round(DOWN, 0)
    ag_pass(DOWN, 2)
    rs_round(DOWN, 1)
    ag_wait(DOWN, 3)

    def back(i):
        cols = ds(i * tn, tn)
        for b in range(batches):
            g = dot_nn(r.cg[b], r.wd[:, cols])
            r.g_hid[rows_of(b), cols] = (g * r.gelu_d[rows_of(b), cols]).astype(BF)

    loop(hidden // tn, back)
    rs_round(UP, 0)
    hr_first(2, 0, pick(r.g_hid), product_nt(r.wu))
    hr_first(2, 1, pick(r.g_hid), product_nt(r.wu))
    hr_second(2, 0)
    hr_second(2, 1)
    rs_round(DOWN, 2)

    r.hs_send[...] = jnp.zeros_like(r.hs_send)

    def back_norm(g, u, inverse, gain):
        scaled = g * gain
        centered = scaled - jnp.mean(scaled, axis=1, keepdims=True)
        return inverse * (centered - u * jnp.mean(scaled * u, axis=1, keepdims=True))

    def norm_two_back(c):
        def some(i):
            at_row = c * part_rows + i * tile
            rw = ds(at_row, tile)
            g = hr_value(2, c, ds(i * tile, tile))
            u, inverse = unit(r.middle[rw, :])
            out = c_rows(at_row)
            v = out + back_norm(g, u, inverse, gain_two)
            r.g_mid[rw, :] = v
            r.gatt[ds(mine + at_row, tile), :] = v.astype(BF)
            r.hs_send[1:2, :] += jnp.sum(g * u, axis=0, keepdims=True)
            r.hs_send[3:4, :] += jnp.sum(g, axis=0, keepdims=True)
            r.hs_send[4:5, :] += jnp.sum(out, axis=0, keepdims=True)

        loop(part_rows // tile, some)

    hr_wait(2, 0)
    norm_two_back(0)
    hg_start(3, 0)
    rs_round(UP, 1)
    hr_wait(2, 1)
    norm_two_back(1)
    hg_start(3, 1)
    hr_first(1, 0, pick(r.activ), product_nt(r.wd))
    hr_first(1, 1, pick(r.activ), product_nt(r.wd))
    rs_round(DOWN, 3)
    for c in (0, 1):
        hg_forward(3, c)
    for c in (0, 1):
        hr_second(1, c)
    for c in (0, 1):
        hg_finish(3, c)

    def mixed_back(i):
        rw = ds(i * tm, tm)
        g = dot_nn(r.gatt[rw, :], r.wo[...])
        attn, bottom = r.numer[rw, :], r.denom[rw, :]
        r.g_num[rw, :] = (g / jnp.maximum(bottom, 1.0)).astype(BF)
        prod = g * attn
        lh = lane_head[:tm]
        acc = jnp.zeros((tm, local), F32)
        for hd in range(heads):
            acc = acc + jnp.where(
                lh == hd,
                jnp.sum(jnp.where(lh == hd, prod, 0.0), axis=1, keepdims=True),
                0.0,
            )
        r.g_den[rw, :] = jnp.where(bottom > 1.0, -acc / jnp.maximum(bottom, 1.0), 0.0)

    loop(tokens // tm, mixed_back)

    parts = []
    for b in range(batches):
        q = r.qf[rows_of(b), :].astype(F32) * wide(r.car[b])
        parts.append(
            (
                dot_tn(q.astype(BF), r.g_num[rows_of(b), :]),
                jnp.sum(q * r.g_den[rows_of(b), :], axis=0, keepdims=True),
            )
        )
    fold(r.gs_send, parts)
    state_send(1, r.gs_send, r.gs_recv, -1)
    rs_round(UP, 2)

    def head_lanes(hd, value):
        return jnp.where(lane_head == hd, value.astype(F32), 0.0).astype(BF)

    for b in range(batches):
        rw = rows_of(b)
        gk = jnp.zeros((rows, local), F32)
        gv = jnp.zeros((rows, local), F32)
        gq = jnp.zeros((rows, local), F32)
        for hd in range(heads):
            gn = head_lanes(hd, r.g_num[rw, :])
            g = dot_nt(gn, r.vf[rw, :]) + r.g_den[rw, hd * DH : hd * DH + 1]
            g = (g * r.mask[b]).astype(BF)
            gq = gq + dot_nn(g, head_lanes(hd, r.kf[rw, :]))
            gk = gk + dot_tn(g, head_lanes(hd, r.qf[rw, :]))
            gv = gv + dot_tn(r.low[b, :, hd * rows : (hd + 1) * rows], gn)
        left = both(b, r.g_num[rw, :], before_thr[b])
        states = jnp.concatenate([unfold(r.st_recv, i, b) for i in (0, 1)], axis=1)
        totals = unfold_sum(r.st_recv, 0, b) + before_thr[b] * unfold_sum(r.st_recv, 1, b)
        gq = gq + dot_nt(left, states) + wide(r.car[b]) * r.g_den[rw, :] * totals
        r.gproj[0, rw, :] = (gq * r.phi_d[0, rw, :]).astype(BF)
        r.gk[rw, :] = gk
        r.gv[rw, :] = gv

    rs_round(OUT, 0)
    state_wait(1, r.gs_recv)
    for b in range(batches):
        rw = rows_of(b)
        thr = after_thr[b]
        states = [unfold(r.gs_recv, i, b) for i in (0, 1)]
        totals = unfold_sum(r.gs_recv, 0, b) + thr * unfold_sum(r.gs_recv, 1, b)
        k = r.kf[rw, :].astype(F32) * wide(r.tail[b])
        v = r.vf[rw, :].astype(F32) * wide(r.tail[b])
        k2 = jnp.concatenate([k.astype(BF), (k * thr).astype(BF)], axis=1)
        v2 = jnp.concatenate([v.astype(BF), (v * thr).astype(BF)], axis=1)
        gk = r.gk[rw, :] + dot_nt(v2, jnp.concatenate(states, axis=1)) + wide(r.tail[b]) * totals
        gv = r.gv[rw, :] + dot_nn(k2, jnp.concatenate(states, axis=0))
        r.gproj[1, rw, :] = (gk * wide(r.pmc[b]) * r.phi_d[1, rw, :]).astype(BF)
        r.gproj[2, rw, :] = gv.astype(BF)

    rs_round(QKV, 0)

    def picks(where):
        return [
            jnp.concatenate([r.gproj[kind, rw, :] for rw in where], axis=0) for kind in range(3)
        ]

    def first_term(left, cols):
        v = dot_nt(left[0], r.wq[0, cols, :])
        for kind in (1, 2):
            v = v + dot_nt(left[kind], r.wq[kind, cols, :])
        return v

    hr_first(3, 0, picks, first_term)
    hr_first(3, 1, picks, first_term)
    hr_second(3, 0)
    hr_second(3, 1)
    rs_round(OUT, 1)
    rs_round(QKV, 1)
    rs_round(UP, 3)

    def norm_one_back(c):
        def some(i):
            at_row = c * part_rows + i * tile
            rw = ds(at_row, tile)
            g = hr_value(3, c, ds(i * tile, tile))
            u, inverse = unit(x_rows(at_row))
            r.i_rows[rw, :] = r.g_mid[rw, :] + back_norm(g, u, inverse, gain_one)
            r.hs_send[0:1, :] += jnp.sum(g * u, axis=0, keepdims=True)
            r.hs_send[2:3, :] += jnp.sum(g, axis=0, keepdims=True)

        loop(part_rows // tile, some)

    for c in (0, 1):
        hr_wait(3, c)
        norm_one_back(c)
    turn(1, r.i_rows, r.ing_o)
    rs_round(OUT, 2)
    rs_round(QKV, 2)

    def finish_rows(c):
        def some(i):
            rw = ds(c * part_rows + i * tile, tile)
            r.a_rows[rw, :] = r.middle[rw, :] + hr_value(1, c, ds(i * tile, tile)) + shift_out

        loop(part_rows // tile, some)

    for c in (0, 1):
        hr_wait(1, c)
        finish_rows(c)
    turn(0, r.a_rows, r.act_o)

    r.hs_recv[h] = r.hs_send[...]
    for i in range(1, m):
        remote(
            r.hs_send, r.hs_recv.at[h], r.hs_s.at[0], r.hs_r.at[0], s, lax.rem(h + i, m)
        ).start()
    r.upb[...] = jnp.zeros_like(r.upb)

    def column_sums(i):
        r.upb[...] += jnp.sum(r.g_hid[ds(i * tile, tile), :].astype(F32), axis=0, keepdims=True)

    loop(tokens // tile, column_sums)
    rs_round(OUT, 3)
    rs_final(DOWN)
    rs_round(QKV, 3)
    landed(r.hs_recv.at[pl.ds(0, m - 1)], r.hs_r.at[0])
    acc = r.hs_recv[0]
    for i in range(1, m):
        acc = acc + r.hs_recv[i]
    r.sg[...] = acc
    r.sg[5:6, :] = r.upb[...]
    r.ss_recv[s] = r.sg[:, ds(s * block, block)]
    for i in range(1, n):
        to = lax.rem(s + i, n)
        remote(
            r.sg.at[:, ds(to * block, block)],
            r.ss_recv.at[s],
            r.ss_s.at[0],
            r.ss_r.at[0],
            to,
            h,
        ).start()
    rs_final(UP)
    rs_final(OUT)
    landed(r.ss_recv.at[pl.ds(0, n - 1)], r.ss_r.at[0])
    acc = r.ss_recv[0]
    for i in range(1, n):
        acc = acc + r.ss_recv[i]
    r.gg_o[...] = acc[0:2]
    r.gb_o[...] = acc[2:5]
    r.gup_o[...] = acc[5:6]
    turn_wait(0, r.a_rows)
    turn_wait(1, r.i_rows)

    far = pl.ds(0, (n - 1) * block)
    for w in range(5):
        views = (r.wq.at[:, far, :], r.wo.at[far], r.wu.at[far], r.wd.at[far], r.smallg.at[:, far])
        drained(views[w], r.ag_s.at[w])
    others = pl.ds(0, (m - 1) * local)
    rest = pl.ds(0, (m - 1) * own)
    for k in range(4):
        view = (r.xg, r.cg)[k].at[:, :, others] if k < 2 else (r.ntwo, r.gatt)[k - 2].at[rest]
        drained(view, r.hg_s.at[k])
        drained(r.h_s1.at[k], r.hr_s.at[k, 0])
        drained(r.h_s2.at[k], r.hr_s.at[k, 1])
    for k, dest in enumerate((r.st_recv, r.gs_recv)):
        drained(dest, r.st_s.at[k])
    drained(r.a_rows.at[:, others], r.aa_s.at[0])
    drained(r.i_rows.at[:, others], r.aa_s.at[1])
    drained(r.hs_recv.at[pl.ds(0, m - 1)], r.hs_s.at[0])
    drained(r.ss_recv.at[pl.ds(0, n - 1)], r.ss_s.at[0])
    rs_final(QKV)
    for w in range(4):
        drained(rs_send[w].at[pl.ds(0, n - 1)], r.rs_s.at[w])
    for copy in local_copies:
        copy.wait()


def settle(*refs):
    count = len(refs) // 2
    copies = [
        pltpu.make_async_copy(refs[i], refs[count + i], refs[-1].at[i]) for i in range(count)
    ]
    for copy in copies:
        copy.start()
    for copy in copies:
        copy.wait()


def whole_layer(n, m):
    def on_each(
        tokens, cotangent, w_qkv, w_out_t, w_up, w_down_t, gains, biases, up_bias, lengths, pixel_mask
    ):
        batches, rows, local = tokens.shape
        width = w_qkv.shape[0] * n
        hidden = w_up.shape[1]
        block = width // n
        vm, sems = layout(n, m, batches, rows, width, local, hidden)
        ins = ["tok", "cot", "w_qkv", "w_out", "w_up", "w_down", "gains", "biases", "up_bias", "lengths", "pixel"]
        outs = ["act_o", "ing_o", "gq_o", "go_o", "gu_o", "gd_o", "gg_o", "gb_o", "gup_o"]
        anywhere = pl.BlockSpec(memory_space=pl.ANY)
        in_vmem = pl.BlockSpec(memory_space=pltpu.VMEM)
        in_smem = pl.BlockSpec(memory_space=pltpu.SMEM)

        result = pl.pallas_call(
            functools.partial(body, n, m, ins + outs + list(vm) + list(sems)),
            name="layer",
            out_shape=(
                pltpu.VMEM((batches, rows, local), F32),
                pltpu.VMEM((batches, rows, local), F32),
                pltpu.VMEM((3, block, local), F32),
                pltpu.VMEM((block, local), F32),
                pltpu.VMEM((block, hidden), F32),
                pltpu.VMEM((block, hidden), F32),
                pltpu.VMEM((2, block), F32),
                pltpu.VMEM((3, block), F32),
                pltpu.VMEM((1, block), F32),
            ),
            in_specs=[anywhere] * 6 + [in_vmem] * 3 + [in_smem, in_vmem],
            out_specs=[in_vmem] * 9,
            scratch_shapes=[pltpu.VMEM(shape, kind) for shape, kind in vm.values()]
            + [pltpu.SemaphoreType.DMA(shape) for shape in sems.values()],
            compiler_params=pltpu.CompilerParams(
                collective_id=0, has_side_effects=True, vmem_limit_bytes=60_000_000
            ),
        )(
            tokens,
            cotangent,
            jnp.transpose(w_qkv, (1, 0, 2)),
            w_out_t,
            w_up,
            w_down_t,
            gains,
            biases,
            up_bias,
            lengths,
            pixel_mask,
        )
        result = pl.pallas_call(
            settle,
            name="settle",
            out_shape=[jax.ShapeDtypeStruct(a.shape, a.dtype) for a in result],
            in_specs=[in_vmem] * len(result),
            out_specs=[anywhere] * len(result),
            scratch_shapes=[pltpu.SemaphoreType.DMA((len(result),))],
        )(*[pltpu.with_memory_space_constraint(a, pltpu.VMEM) for a in result])
        return (*result[:2], jnp.transpose(result[2], (1, 0, 2)), *result[3:])

    return on_each


def solution(mesh):
    in_specs = (
        P(None, "seq", "head"),
        P(None, "seq", "head"),
        P("seq", None, "head"),
        P("seq", "head"),
        P("seq", "head"),
        P("seq", "head"),
        P(None, "seq"),
        P(None, "seq"),
        P("head", "seq"),
        P(),
        P(None, "seq"),
    )
    out_specs = (
        P(None, "seq", "head"),
        P(None, "seq", "head"),
        P("seq", None, "head"),
        P("seq", "head"),
        P("seq", "head"),
        P("seq", "head"),
        P(None, "seq"),
        P(None, "seq"),
        P("head", "seq"),
    )
    n, m = mesh.shape["seq"], mesh.shape["head"]
    fits = (n, m) == (8, 4)
    return jax.shard_map(
        whole_layer(n, m) if fits else on_device, mesh=mesh, in_specs=in_specs, out_specs=out_specs, check_vma=False
    )
```

```python
import functools

import jax
import jax.numpy as jnp
from jax import lax
from jax.experimental import pallas as pl
from jax.experimental.pallas import tpu as pltpu
from jax.sharding import PartitionSpec as P

DH = 64


highest = lax.Precision.HIGHEST
epsilon = 1e-05


def entering(array, axis, join, neutral):
    place = lax.axis_index(axis)
    gathered = jax.tree.map(
        lambda a, kind: lax.all_gather(a.astype(kind), axis),
        array,
        (jnp.bfloat16, jnp.bfloat16, jnp.bfloat16),
    )
    state = jax.tree.map(lambda a, e: jnp.zeros_like(a) + jnp.asarray(e, a.dtype), array, neutral)

    def one(hop, state):
        return join(
            state,
            jax.tree.map(
                lambda a, own: lax.dynamic_index_in_dim(a, hop, 0, False).astype(own.dtype),
                gathered,
                array,
            ),
        )

    return lax.fori_loop(0, place, one, state)


def entering_2(array, axis, combine, identity):
    length, place = (lax.axis_size(axis), lax.axis_index(axis))
    everything = jax.tree.map(
        lambda part, kind: lax.all_gather(part.astype(kind), axis),
        array,
        jax.tree.map(lambda a: jnp.bfloat16 if a.dtype == jnp.float32 else a.dtype, array),
    )
    start = jax.tree.map(
        lambda part, zero: jnp.broadcast_to(jnp.asarray(zero, part.dtype), part.shape),
        array,
        identity,
    )

    def hop(k, before):
        at = length - 1 - k
        reached = at > place
        new = combine(
            before, jax.tree.map(lambda part, own: part[at].astype(own.dtype), everything, array)
        )
        return jax.tree.map(lambda a, b: jnp.where(reached, a, b), new, before)

    return lax.fori_loop(0, length, hop, start)


def normalize(values, gain_vec, shift_vec):
    mean_val = jnp.mean(values, axis=-1, keepdims=True)
    centered = values - mean_val
    inverse = lax.rsqrt(jnp.mean(centered * centered, axis=-1, keepdims=True) + epsilon)
    unit_val = centered * inverse
    return (unit_val * gain_vec + shift_vec, unit_val, inverse)


def norm_back(grad_in, unit_val, inverse, gain_vec):
    scaled = grad_in * gain_vec
    centered = scaled - jnp.mean(scaled, axis=-1, keepdims=True)
    return inverse * (centered - unit_val * jnp.mean(scaled * unit_val, axis=-1, keepdims=True))


def features(values):
    return jax.nn.elu(values) + 1.0


def finish(numerator, denominator):
    return numerator / jnp.maximum(denominator, 1.0)[:, :, None]


def compose(earlier, later):
    return (
        later[0] + later[2] * earlier[0],
        later[1] + later[2] * earlier[1],
        later[2] * earlier[2],
    )


def item_numbers(lengths_row, first_place, number):
    offsets = jnp.cumsum(lengths_row) - lengths_row
    places = first_place + jnp.arange(number, dtype=jnp.int32)
    return jnp.sum((offsets[None, :] <= places[:, None]).astype(jnp.int32), axis=1) - 1


def on_device(
    tokens, cotangent, w_qkv, w_out_t, w_up, w_down_t, gains, biases, up_bias, lengths, pixel_mask
):
    batches, local_rows, columns = tokens.shape
    local_width = w_qkv.shape[2]
    heads_here = local_width // DH
    seq_index = lax.axis_index("seq")
    head_index = lax.axis_index("head")
    first_token = seq_index * local_rows
    position = jnp.arange(local_rows, dtype=jnp.int32)
    before = position[:, None] >= position[None, :]

    def own_columns(matrix):
        return lax.dynamic_slice_in_dim(matrix, head_index * columns, columns, 1)

    results = []
    input_grads = []
    shard_sums = None
    for batch_index in range(batches):
        full_qkv, full_out, full_up, full_down, full_gains, full_biases, full_upb = (
            lax.all_gather(w_qkv, "seq", axis=0, tiled=True),
            lax.all_gather(w_out_t, "seq", axis=0, tiled=True),
            lax.all_gather(w_up, "seq", axis=0, tiled=True),
            lax.all_gather(w_down_t, "seq", axis=0, tiled=True),
            lax.all_gather(gains, "seq", axis=1, tiled=True),
            lax.all_gather(biases, "seq", axis=1, tiled=True),
            lax.all_gather(up_bias, "seq", axis=1, tiled=True),
        )
        input_rows, grad_rows16 = (
            lax.all_gather(tokens[batch_index], "head", axis=1, tiled=True),
            lax.all_gather(cotangent[batch_index], "head", axis=1, tiled=True),
        )
        gains32 = full_gains.astype(jnp.float32)
        biases32 = full_biases.astype(jnp.float32)
        upb32 = full_upb.astype(jnp.float32).reshape(-1)
        inputs32 = input_rows.astype(jnp.float32)
        place_items = item_numbers(lengths[batch_index], first_token - 1, local_rows + 1)
        item_of = place_items[1:]
        carried = (item_of == place_items[0]).astype(jnp.float32)
        tail_mask = (item_of == item_of[local_rows - 1]).astype(jnp.float32)
        through = carried[local_rows - 1]
        same_item = ((item_of[:, None] == item_of[None, :]) & before).astype(jnp.float32)
        keep_half = pixel_mask[batch_index].astype(jnp.bfloat16)
        keep32 = pixel_mask[batch_index].astype(jnp.float32)
        lifted, unit_one, inverse_one = normalize(inputs32, gains32[0], biases32[0])
        normed = lifted.astype(jnp.bfloat16)
        projected = jnp.einsum("td,dsf->tsf", normed, full_qkv, preferred_element_type=jnp.float32)
        query_feat = (
            features(projected[:, 0]).astype(jnp.bfloat16).reshape(local_rows, heads_here, DH)
        )
        key_feat = (features(projected[:, 1]).astype(jnp.bfloat16) * keep_half[:, None]).reshape(
            local_rows, heads_here, DH
        )
        value_feat = projected[:, 2].astype(jnp.bfloat16).reshape(local_rows, heads_here, DH)
        tail_key = key_feat * tail_mask.astype(jnp.bfloat16)[:, None, None]
        state_loc = jnp.einsum(
            "jhd,jhe->hde", tail_key, value_feat, preferred_element_type=jnp.float32
        )
        total_loc = jnp.sum(tail_key.astype(jnp.float32), axis=0)
        identity = (jnp.zeros_like(state_loc), jnp.zeros_like(total_loc), jnp.ones((), jnp.float32))
        state_in, total_in, passed = entering(
            (state_loc, total_loc, through), "seq", compose, identity
        )
        query32 = query_feat.astype(jnp.float32)
        scores = (
            jnp.einsum("thd,jhd->htj", query_feat, key_feat, preferred_element_type=jnp.float32)
            * same_item[None]
        )
        scores_low = scores.astype(jnp.bfloat16)
        numerator = jnp.einsum(
            "htj,jhe->the", scores_low, value_feat, preferred_element_type=jnp.float32
        ) + carried[:, None, None] * jnp.einsum(
            "thd,hde->the", query32, state_in, precision=highest
        )
        denominator = jnp.sum(scores, axis=2).T + carried[:, None] * jnp.einsum(
            "thd,hd->th", query32, total_in, precision=highest
        )
        output, finish_back = jax.vjp(finish, numerator, denominator)
        mixed_out = output.reshape(local_rows, local_width).astype(jnp.bfloat16)
        attended = lax.psum(
            jnp.einsum("tf,df->td", mixed_out, full_out, preferred_element_type=jnp.float32).astype(
                jnp.bfloat16
            ),
            "head",
        ).astype(jnp.float32)
        middle = inputs32 + attended
        lifted_two, unit_two, inverse_two = normalize(middle, gains32[1], biases32[1])
        normed_two = lifted_two.astype(jnp.bfloat16)
        hidden = jnp.dot(normed_two, full_up, preferred_element_type=jnp.float32) + upb32
        activated32, gelu_back = jax.vjp(jax.nn.gelu, hidden)
        activated = activated32.astype(jnp.bfloat16)
        branch = lax.psum_scatter(
            jnp.einsum(
                "tf,df->td", activated, full_down, preferred_element_type=jnp.float32
            ).astype(jnp.bfloat16),
            "head",
            scatter_dimension=1,
            tiled=True,
        ).astype(jnp.float32)
        results.append(own_columns(middle) + branch + own_columns(biases32[2][None]))
        grad_out = grad_rows16.astype(jnp.float32)
        grad_down = jnp.einsum(
            "td,tf->df", grad_rows16, activated, preferred_element_type=jnp.float32
        )
        grad_act = jnp.einsum(
            "td,df->tf", grad_rows16, full_down, preferred_element_type=jnp.float32
        )
        grad_hidden = gelu_back(grad_act)[0].astype(jnp.bfloat16)
        grad_up = jnp.einsum(
            "td,tf->df", normed_two, grad_hidden, preferred_element_type=jnp.float32
        )
        grad_upb = jnp.sum(grad_hidden.astype(jnp.float32), axis=0).reshape(full_upb.shape)
        grad_two = lax.psum(
            jnp.einsum(
                "tf,df->td", grad_hidden, full_up, preferred_element_type=jnp.float32
            ).astype(jnp.bfloat16),
            "head",
        ).astype(jnp.float32)
        grad_middle = grad_out + norm_back(grad_two, unit_two, inverse_two, gains32[1])
        grad_attended = grad_middle.astype(jnp.bfloat16)
        grad_out_t = jnp.einsum(
            "td,tf->df", grad_attended, mixed_out, preferred_element_type=jnp.float32
        )
        grad_mixed = jnp.einsum(
            "td,df->tf", grad_attended, full_out, preferred_element_type=jnp.float32
        ).reshape(local_rows, heads_here, DH)
        grad_numer32, grad_denom = finish_back(grad_mixed)
        grad_numer = grad_numer32.astype(jnp.bfloat16)
        grad_numer_wide = grad_numer.astype(jnp.float32)
        grad_scores = (
            (
                jnp.einsum(
                    "the,jhe->htj", grad_numer, value_feat, preferred_element_type=jnp.float32
                )
                + grad_denom.T[:, :, None]
            )
            * same_item[None]
        ).astype(jnp.bfloat16)
        carried_query = query32 * carried[:, None, None]
        grad_query = jnp.einsum(
            "htj,jhd->thd", grad_scores, key_feat, preferred_element_type=jnp.float32
        ) + carried[:, None, None] * (
            jnp.einsum("hde,the->thd", state_in, grad_numer_wide, precision=highest)
            + grad_denom[:, :, None] * total_in[None]
        )
        grad_key = jnp.einsum(
            "htj,thd->jhd", grad_scores, query_feat, preferred_element_type=jnp.float32
        )
        grad_value = jnp.einsum(
            "htj,the->jhe", scores_low, grad_numer, preferred_element_type=jnp.float32
        )
        grad_state_in = jnp.einsum(
            "thd,the->hde", carried_query, grad_numer_wide, precision=highest
        )
        grad_total_in = jnp.einsum("thd,th->hd", carried_query, grad_denom, precision=highest)
        grad_state_loc, grad_total_loc, passed_back = entering_2(
            (grad_state_in, grad_total_in, through), "seq", compose, identity
        )
        tail_three = tail_mask[:, None, None]
        value_wide = value_feat.astype(jnp.float32)
        key_wide = key_feat.astype(jnp.float32)
        grad_key = grad_key + tail_three * (
            jnp.einsum("hde,jhe->jhd", grad_state_loc, value_wide, precision=highest)
            + grad_total_loc[None]
        )
        grad_value = grad_value + tail_three * jnp.einsum(
            "jhd,hde->jhe", key_wide, grad_state_loc, precision=highest
        )
        ignored, feature_back = jax.vjp(features, projected[:, :2])
        grad_features = jnp.stack(
            [
                grad_query.reshape(local_rows, local_width),
                grad_key.reshape(local_rows, local_width) * keep32[:, None],
            ],
            axis=1,
        )
        grad_pair = feature_back(grad_features)[0]
        grad_projected = jnp.concatenate(
            [grad_pair, grad_value.reshape(local_rows, 1, local_width)], axis=1
        ).astype(jnp.bfloat16)
        grad_qkv = jnp.einsum(
            "td,tsf->dsf", normed, grad_projected, preferred_element_type=jnp.float32
        )
        grad_one = lax.psum(
            jnp.einsum(
                "tsf,dsf->td", grad_projected, full_qkv, preferred_element_type=jnp.float32
            ).astype(jnp.bfloat16),
            "head",
        ).astype(jnp.float32)
        grad_inputs = grad_middle + norm_back(grad_one, unit_one, inverse_one, gains32[0])
        input_grads.append(own_columns(grad_inputs))
        grad_gains = jnp.stack(
            [jnp.sum(grad_one * unit_one, axis=0), jnp.sum(grad_two * unit_two, axis=0)]
        )
        grad_biases = jnp.stack(
            [jnp.sum(grad_one, axis=0), jnp.sum(grad_two, axis=0), jnp.sum(grad_out, axis=0)]
        )
        pieces = (
            lax.psum_scatter(grad_qkv, "seq", scatter_dimension=0, tiled=True),
            lax.psum_scatter(grad_out_t, "seq", scatter_dimension=0, tiled=True),
            lax.psum_scatter(grad_up, "seq", scatter_dimension=0, tiled=True),
            lax.psum_scatter(grad_down, "seq", scatter_dimension=0, tiled=True),
            lax.psum_scatter(grad_gains, "seq", scatter_dimension=1, tiled=True),
            lax.psum_scatter(grad_biases, "seq", scatter_dimension=1, tiled=True),
            lax.psum_scatter(grad_upb, "seq", scatter_dimension=1, tiled=True),
        )
        shard_sums = pieces if shard_sums is None else jax.tree.map(jnp.add, shard_sums, pieces)
    return (
        jnp.stack(results),
        jnp.stack(input_grads),
        shard_sums[0],
        shard_sums[1],
        shard_sums[2],
        shard_sums[3],
        shard_sums[4],
        shard_sums[5],
        shard_sums[6],
    )


MESH = pl.DeviceIdType.MESH
BF = jnp.bfloat16
F32 = jnp.float32
QKV, OUT, UP, DOWN, SMALL = range(5)


def dot_nn(a, b):
    return lax.dot_general(a, b, (((1,), (0,)), ((), ())), preferred_element_type=F32)


def dot_nt(a, b):
    return lax.dot_general(a, b, (((1,), (1,)), ((), ())), preferred_element_type=F32)


def dot_tn(a, b):
    return lax.dot_general(a, b, (((0,), (0,)), ((), ())), preferred_element_type=F32)


def ds(start, size):
    return pl.ds(pl.multiple_of(start, size), size)


def loop(count, body):
    def step(i, carry):
        body(i)
        return carry

    lax.fori_loop(0, count, step, 0)


def layout(n, m, batches, rows, width, local, hidden):
    tokens = batches * rows
    block = width // n
    own = tokens // m
    hops = n // 2
    heads = local // DH
    vm = {
        "xg": ((batches, rows, width), BF),
        "cg": ((batches, rows, width), BF),
        "wq": ((3, width, local), BF),
        "wo": ((width, local), BF),
        "wu": ((width, hidden), BF),
        "wd": ((width, hidden), BF),
        "small": ((8, block), F32),
        "smallg": ((8, width), F32),
        "normed": ((tokens, width), BF),
        "phi_d": ((2, tokens, local), F32),
        "qf": ((tokens, local), BF),
        "kf": ((tokens, local), BF),
        "vf": ((tokens, local), BF),
        "mask": ((batches, rows, rows), F32),
        "car": ((batches, rows, 128), F32),
        "tail": ((batches, rows, 128), F32),
        "pmc": ((batches, rows, 128), F32),
        "low": ((batches, rows, heads * rows), BF),
        "numer": ((tokens, local), F32),
        "denom": ((tokens, local), F32),
        "mixed": ((tokens, local), BF),
        "st_send": ((batches * DH + 16, local), BF),
        "st_recv": ((2, batches * DH + 16, local), BF),
        "gs_send": ((batches * DH + 16, local), BF),
        "gs_recv": ((2, batches * DH + 16, local), BF),
        "middle": ((own, width), F32),
        "ntwo": ((tokens, width), BF),
        "gelu_d": ((tokens, hidden), F32),
        "activ": ((tokens, hidden), BF),
        "g_hid": ((tokens, hidden), BF),
        "branch": ((own, width), F32),
        "total": ((own, width), F32),
        "g_mid": ((own, width), F32),
        "gatt": ((tokens, width), BF),
        "g_attn": ((tokens, local), F32),
        "g_num": ((tokens, local), BF),
        "g_den": ((tokens, local), F32),
        "gq": ((tokens, local), F32),
        "gk": ((tokens, local), F32),
        "gv": ((tokens, local), F32),
        "gproj": ((3, tokens, local), BF),
        "h_s1": ((4, 2, 2, own // 2, width), BF),
        "h_r1": ((4, 2, 2, own // 2, width), BF),
        "h_acc": ((4, 2, 2, own // 2, width), F32),
        "h_s2": ((4, 2, own // 2, width), BF),
        "h_r2": ((4, 2, own // 2, width), BF),
        "rq_s": ((n, 3, block, local), BF),
        "rq_r": ((n, 3, block, local), BF),
        "ro_s": ((n, block, local), BF),
        "ro_r": ((n, block, local), BF),
        "ru_s": ((n, block, hidden), BF),
        "ru_r": ((n, block, hidden), BF),
        "rd_s": ((n, block, hidden), BF),
        "rd_r": ((n, block, hidden), BF),
        "hs_recv": ((m, 8, width), F32),
        "hs_send": ((8, width), F32),
        "upb": ((1, hidden), F32),
        "sg": ((8, width), F32),
        "ss_recv": ((n, 8, block), F32),
        "a_rows": ((own, width), F32),
        "i_rows": ((own, width), F32),
    }
    sems = {
        "ag_s": (5,),
        "ag_r": (5, 2, hops),
        "rs_s": (4,),
        "rs_r": (4, 2, hops),
        "hg_s": (4,),
        "hg_r": (4, 2, 3),
        "hr_s": (4, 2),
        "hr_r": (4, 2, 2),
        "st_s": (2,),
        "st_r": (2,),
        "aa_s": (2,),
        "aa_r": (2,),
        "hs_s": (1,),
        "hs_r": (1,),
        "ss_s": (1,),
        "ss_r": (1,),
        "lc": (8,),
    }
    return vm, sems


class Refs:
    pass


def body(n, m, names, *refs):
    r = Refs()
    for name, ref in zip(names, refs):
        setattr(r, name, ref)
    batches, rows, width = r.xg.shape
    tokens = batches * rows
    own = tokens // m
    block = width // n
    local = r.wo.shape[1]
    hidden = r.wu.shape[1]
    heads = local // DH
    hops = n // 2
    s = lax.axis_index("seq")
    h = lax.axis_index("head")
    odd = lax.rem(s, 2)
    p = (1 - odd) * lax.div(s, 2) + odd * (n - 1 - lax.div(s, 2))
    lo, hi = lax.rem(h, 2), lax.div(h, 2)
    pair = h + 1 - 2 * lo
    cross = lax.rem(h + 2, m)

    def at(place):
        place = lax.rem(place + 2 * n, n)
        far = lax.div(place, hops)
        return (1 - far) * 2 * place + far * (2 * (n - 1 - place) + 1)

    ring = (at(p + 1), at(p - 1))
    sign = (1, -1)

    def remote(src, dst, send, recv, seq, head):
        return pltpu.make_async_remote_copy(
            src_ref=src,
            dst_ref=dst,
            send_sem=send,
            recv_sem=recv,
            device_id=(seq, head),
            device_id_type=MESH,
        )

    def drained(view, sem):
        remote(view, view, sem, sem, ring[0], h).wait_send()

    def landed(view, sem):
        remote(view, view, sem, sem, ring[0], h).wait_recv()

    r.small[...] = jnp.zeros_like(r.small)
    r.small[0:2, :] = r.gains[...].astype(F32)
    r.small[2:5, :] = r.biases[...].astype(F32)
    r.small[5:6, :] = r.up_bias[...].astype(F32)

    barrier = pltpu.get_barrier_semaphore()
    for peer in ((ring[0], h), (ring[1], h), (s, pair), (s, cross)):
        pl.semaphore_signal(barrier, inc=1, device_id=peer, device_id_type=MESH)
    pl.semaphore_wait(barrier, 4)

    shards = (r.w_qkv, r.w_out, r.w_up, r.w_down, r.small)
    gathered = (r.wq, r.wo, r.wu, r.wd, r.smallg)

    def part_of(w, d, j):
        wide_part = r.wq.shape[2] if w == QKV else shards[w].shape[1]
        if j < hops - 1 or w == SMALL:
            return pl.ds(0, wide_part)
        return pl.ds(d * (wide_part // 2), wide_part // 2)

    def ag_shard(w, d, j):
        cols = part_of(w, d, j)
        if w == SMALL:
            return r.small
        return shards[w].at[:, :, cols] if w == QKV else shards[w].at[:, cols]

    def ag_full(w, owner, d, j):
        cols = part_of(w, d, j)
        if w == SMALL:
            return r.smallg.at[:, ds(owner * block, block)]
        if w == QKV:
            return r.wq.at[:, ds(owner * block, block), cols]
        return gathered[w].at[ds(owner * block, block), cols]

    def ways(w, j):
        return (0,) if w == SMALL and j == hops - 1 else (0, 1)

    def ag_send(w, j):
        for d in ways(w, j):
            owner = at(p - sign[d] * j)
            src = ag_shard(w, d, j) if j == 0 else ag_full(w, owner, d, j)
            remote(
                src, ag_full(w, owner, d, j), r.ag_s.at[w], r.ag_r.at[w, d, j], ring[d], h
            ).start()

    def ag_wait(w, j):
        for d in ways(w, j):
            landed(ag_full(w, at(p - sign[d] * (j + 1)), d, j), r.ag_r.at[w, d, j])

    def ag_pass(w, j):
        ag_wait(w, j)
        ag_send(w, j + 1)

    part_rows = own // 2

    def hg_view(k, c, who):
        if k < 2:
            return (r.xg, r.cg)[k].at[c, :, ds(who * local, local)]
        return (r.ntwo, r.gatt)[k - 2].at[ds(who * own + c * part_rows, part_rows), :]

    def hg_copy(k, c, i, src, who, to):
        return remote(src, hg_view(k, c, who), r.hg_s.at[k], r.hg_r.at[k, c, i], s, to)

    def hg_start(k, c):
        src = (r.tok, r.cot)[k].at[c] if k < 2 else hg_view(k, c, h)
        hg_copy(k, c, 1, src, h, cross).start()
        hg_copy(k, c, 0, src, h, pair).start()

    def hg_forward(k, c):
        view = hg_view(k, c, cross)
        hg_copy(k, c, 1, view, cross, cross).wait_recv()
        hg_copy(k, c, 2, view, cross, pair).start()

    def hg_finish(k, c):
        view = hg_view(k, c, pair)
        hg_copy(k, c, 0, view, pair, pair).wait_recv()
        across = lax.rem(pair + 2, m)
        view = hg_view(k, c, across)
        hg_copy(k, c, 2, view, across, pair).wait_recv()

    tn = 256

    def hr_first(k, c, left, product):
        blocks = [2 * i + 1 - lo for i in (0, 1)] + [2 * i + lo for i in (0, 1)]
        where = [ds(who * own + c * part_rows, part_rows) for who in blocks]

        def some(i):
            cols = ds(i * tn, tn)
            v = product(left(where), cols)
            for q in (0, 1):
                r.h_s1[k, c, q, :, cols] = v[q * part_rows : (q + 1) * part_rows].astype(BF)
                r.h_acc[k, c, q, :, cols] = v[(q + 2) * part_rows : (q + 3) * part_rows]

        loop(width // tn, some)
        hr_copy(k, c, 0).start()

    def hr_copy(k, c, stage):
        if stage == 0:
            src, dst, to = r.h_s1.at[k, c], r.h_r1.at[k, c], pair
        else:
            src, dst, to = r.h_s2.at[k, c], r.h_r2.at[k, c], cross
        return remote(src, dst, r.hr_s.at[k, stage], r.hr_r.at[k, c, stage], s, to)

    def hr_second(k, c):
        hr_copy(k, c, 0).wait_recv()

        def away(i):
            rw = ds(i * 32, 32)
            r.h_s2[k, c, rw, :] = (
                r.h_acc[k, c, 1 - hi, rw, :] + r.h_r1[k, c, 1 - hi, rw, :].astype(F32)
            ).astype(BF)

        loop(part_rows // 32, away)
        hr_copy(k, c, 1).start()

    def hr_wait(k, c):
        hr_copy(k, c, 1).wait_recv()

    def hr_value(k, c, rw):
        return (
            r.h_acc[k, c, hi, rw, :]
            + r.h_r1[k, c, hi, rw, :].astype(F32)
            + r.h_r2[k, c, rw, :].astype(F32)
        )

    def pick(ref):
        return lambda where: jnp.concatenate([ref[rw, :] for rw in where], axis=0)

    def product_nt(right):
        return lambda left, cols: dot_nt(left, right[cols, :])

    def rs_term(w, owner, piece):
        cols = ds(owner * block, block)
        if w == DOWN:
            left = r.cg[:, :, cols].reshape(tokens, block)
            half = hidden // 2
            return [dot_tn(left, r.activ[:, pl.ds(piece * half, half)])]
        if w == UP:
            half = hidden // 2
            return [dot_tn(r.ntwo[:, cols], r.g_hid[:, pl.ds(piece * half, half)])]
        half = local // 2
        if w == OUT:
            return [dot_tn(r.gatt[:, cols], r.mixed[:, pl.ds(piece * half, half)])]
        left = r.normed[:, cols]
        return [dot_tn(left, r.gproj[i, :, pl.ds(piece * half, half)]) for i in range(3)]

    rs_send = (r.rq_s, r.ro_s, r.ru_s, r.rd_s)
    rs_recv = (r.rq_r, r.ro_r, r.ru_r, r.rd_r)

    def rs_half(w, piece):
        half = rs_send[w].shape[-1] // 2
        return pl.ds(piece * half, half)

    def rs_view(ref, w, d, step):
        if step > 0:
            return ref.at[d * hops + step]
        if w == QKV:
            return ref.at[d * hops, :, :, rs_half(w, d)]
        return ref.at[d * hops, :, rs_half(w, d)]

    def rs_arrived(w, d, step):
        landed(rs_view(rs_recv[w], w, d, step), r.rs_r.at[w, d, step])

    def rs_round(w, step):
        for d in (0, 1):
            slot = d * hops + step
            owner = at(p + sign[d] * (hops - step))
            pieces = (0, 1) if step > 0 else (d,)
            terms = [rs_term(w, owner, piece) for piece in pieces]
            if step > 0:
                rs_arrived(w, d, step - 1)
            for piece, parts in zip(pieces, terms):
                cols = rs_half(w, piece)
                for i, v in enumerate(parts):
                    lead = (i,) if w == QKV else ()
                    if step > 1 or (step == 1 and piece == d):
                        v = v + rs_recv[w][(slot - 1, *lead, slice(None), cols)].astype(F32)
                    rs_send[w][(slot, *lead, slice(None), cols)] = v.astype(BF)
            remote(
                rs_view(rs_send[w], w, d, step),
                rs_view(rs_recv[w], w, d, step),
                r.rs_s.at[w],
                r.rs_r.at[w, d, step],
                ring[d],
                h,
            ).start()

    finals = (r.gq_o, r.go_o, r.gu_o, r.gd_o)
    local_copies = []

    def rs_final(w):
        terms = [rs_term(w, s, piece) for piece in (0, 1)]
        for d in (0, 1):
            rs_arrived(w, d, hops - 1)
        for piece in (0, 1):
            cols = rs_half(w, piece)
            for i, v in enumerate(terms[piece]):
                lead = (i,) if w == QKV else ()
                for d in (0, 1):
                    v = v + rs_recv[w][(d * hops + hops - 1, *lead, slice(None), cols)].astype(F32)
                finals[w][(*lead, slice(None), cols)] = v
    def turn(k, src, dst):
        where = (hi, ds(lo * own, own))
        for i in range(1, m):
            to = lax.rem(h + i, m)
            remote(
                src.at[:, ds(to * local, local)],
                dst.at[where[0], where[1], :],
                r.aa_s.at[k],
                r.aa_r.at[k],
                s,
                to,
            ).start()
        copy = pltpu.make_async_copy(
            src.at[:, ds(h * local, local)], dst.at[where[0], where[1], :], r.lc.at[k]
        )
        copy.start()
        local_copies.append(copy)

    def turn_wait(k, src):
        landed(src.at[:, pl.ds(0, (m - 1) * local)], r.aa_r.at[k])

    ag_send(SMALL, 0)
    ag_send(QKV, 0)
    ag_send(OUT, 0)
    hg_start(0, 0)
    hg_start(0, 1)
    own_copies = [
        pltpu.make_async_copy(r.w_qkv, r.wq.at[:, ds(s * block, block), :], r.lc.at[4]),
        pltpu.make_async_copy(r.w_out, r.wo.at[ds(s * block, block), :], r.lc.at[5]),
        pltpu.make_async_copy(r.w_up, r.wu.at[ds(s * block, block), :], r.lc.at[6]),
        pltpu.make_async_copy(r.w_down, r.wd.at[ds(s * block, block), :], r.lc.at[7]),
        pltpu.make_async_copy(r.tok, r.xg.at[:, :, ds(h * local, local)], r.lc.at[2]),
        pltpu.make_async_copy(r.cot, r.cg.at[:, :, ds(h * local, local)], r.lc.at[3]),
    ]
    for copy in own_copies:
        copy.start()
    hg_start(1, 0)
    hg_start(1, 1)

    first = s * rows
    row_at = lax.broadcasted_iota(jnp.int32, (rows, 128), 0)
    lane_at = lax.broadcasted_iota(jnp.int32, (rows, rows), 1)
    square = lax.broadcasted_iota(jnp.int32, (local, local), 0)
    square_lane = lax.broadcasted_iota(jnp.int32, (local, local), 1)
    same_head = (square // DH) == (square_lane // DH)
    diagonal = square == square_lane
    lane_head = lax.broadcasted_iota(jnp.int32, (rows, local), 1) // DH
    before_thr, after_thr = [], []

    def wide(value):
        return jnp.concatenate([value] * (local // 128), axis=1)

    def begin(offsets, place):
        value = 0
        for off in offsets:
            value = jnp.where(off <= place, off, value)
        return value

    def through(offsets, which):
        return jnp.where(
            begin(offsets, which * rows + rows - 1) < which * rows, 1.0, 0.0
        ).astype(F32)

    def crops(b):
        offsets, running = [], 0
        for i in range(r.lengths.shape[1]):
            offsets.append(running)
            running = running + r.lengths[b, i]
        start = jnp.zeros((rows, 128), jnp.int32)
        for off in offsets:
            start = jnp.where(off <= row_at + first, off, start)
        last = begin(offsets, first + rows - 1)
        r.mask[b] = jnp.where(
            (lane_at + first >= wide(start)) & (lane_at <= wide(row_at)), 1.0, 0.0
        ).astype(F32)
        r.car[b] = jnp.where(start < first, 1.0, 0.0).astype(F32)
        r.tail[b] = jnp.where(start == last, 1.0, 0.0).astype(F32)
        before_thr.append(through(offsets, lax.rem(s + n - 1, n)))
        after_thr.append(through(offsets, lax.rem(s + 1, n)))
        keep = r.pixel[b : b + 1, :].astype(F32)
        r.pmc[b] = dot_nn(
            jnp.where(diagonal, keep, 0.0).astype(BF), jnp.ones((rows, 128), BF)
        )

    def ag_step(j):
        ag_pass(SMALL, j)
        ag_pass(QKV, j)
        ag_pass(OUT, j)

    crops(0)
    hg_forward(0, 0)
    ag_step(0)
    hg_forward(0, 1)
    for copy in own_copies:
        copy.wait()
    r.smallg[:, ds(s * block, block)] = r.small[...]

    def unit(values):
        mean = jnp.mean(values, axis=1, keepdims=True)
        centered = values - mean
        inverse = lax.rsqrt(jnp.mean(centered * centered, axis=1, keepdims=True) + epsilon)
        return centered * inverse, inverse

    tile = 32

    def unit_one(b):
        def some(i):
            u, _ = unit(r.xg[b, ds(i * tile, tile), :].astype(F32))
            r.gelu_d[ds(b * rows + i * tile, tile), :] = u

        loop(rows // tile, some)

    def norm_one(i):
        rw = ds(i * tile, tile)
        r.normed[rw, :] = (r.gelu_d[rw, :] * gain_one + shift_one).astype(BF)

    for c in (0, 1):
        hg_finish(0, c)
    unit_one(0)
    ag_step(1)
    unit_one(1)
    crops(1)
    ag_step(2)
    ag_send(UP, 0)
    for c in (0, 1):
        hg_forward(1, c)
    ag_wait(SMALL, 3)
    gain_one, gain_two = r.smallg[0:1, :], r.smallg[1:2, :]
    shift_one, shift_two, shift_out = r.smallg[2:3, :], r.smallg[3:4, :], r.smallg[4:5, :]
    loop(tokens // tile, norm_one)
    ag_wait(QKV, 3)
    ag_wait(OUT, 3)

    tm = 128

    def project(i):
        rw = ds(i * tm, tm)
        b = lax.div(i, rows // tm)
        rb = ds(lax.rem(i, rows // tm) * tm, tm)
        left = r.normed[rw, :]
        for kind in (0, 1):
            v = dot_nn(left, r.wq[kind])
            low = jnp.exp(jnp.minimum(v, 0.0))
            f = jnp.where(v > 0.0, v + 1.0, low).astype(BF)
            r.phi_d[kind, rw, :] = low
            if kind == 0:
                r.qf[rw, :] = f
            else:
                r.kf[rw, :] = (f.astype(F32) * wide(r.pmc[b, rb, :])).astype(BF)
        r.vf[rw, :] = dot_nn(left, r.wq[2]).astype(BF)

    loop(tokens // tm, project)

    def fold(ref, parts):
        row = lax.broadcasted_iota(jnp.int32, (16, local), 0)
        sums = jnp.zeros((16, local), F32)
        for b, (matrix, total) in enumerate(parts):
            kept = jnp.where(same_head, matrix, 0.0)
            acc = kept[0:DH]
            for i in range(1, heads):
                acc = acc + kept[i * DH : (i + 1) * DH]
            ref[b * DH : (b + 1) * DH, :] = acc.astype(BF)
            sums = jnp.where(row == b, total, sums)
        ref[batches * DH :, :] = sums.astype(BF)

    def unfold(ref, i, b):
        acc = ref[i, b * DH : (b + 1) * DH, :].astype(F32)
        return jnp.where(same_head, jnp.concatenate([acc] * heads, axis=0), 0.0).astype(BF)

    def unfold_sum(ref, i, b):
        return ref[i, batches * DH :, :].astype(F32)[b : b + 1]

    def state_send(k, ref, dest, step):
        for i in (0, 1):
            to = lax.rem(s + n + step * (i + 1), n)
            remote(ref, dest.at[i], r.st_s.at[k], r.st_r.at[k], to, h).start()

    def state_wait(k, dest):
        landed(dest, r.st_r.at[k])

    def rows_of(b):
        return pl.ds(b * rows, rows)

    def by_head(value):
        return jnp.concatenate(
            [jnp.where(lane_head == hd, value.astype(F32), 0.0).astype(BF) for hd in range(heads)],
            axis=0,
        )

    parts = []
    for b in range(batches):
        k = r.kf[rows_of(b), :].astype(F32) * wide(r.tail[b])
        parts.append(
            (dot_tn(k.astype(BF), r.vf[rows_of(b), :]), jnp.sum(k, axis=0, keepdims=True))
        )
    fold(r.st_send, parts)
    state_send(0, r.st_send, r.st_recv, 1)

    for b in range(batches):
        q, k = r.qf[rows_of(b), :], r.kf[rows_of(b), :]
        acc = jnp.zeros((rows, local), F32)
        for hd in range(heads):
            sc = dot_nt(jnp.where(lane_head == hd, q.astype(F32), 0.0).astype(BF), k) * r.mask[b]
            r.low[b, :, hd * rows : (hd + 1) * rows] = sc.astype(BF)
            acc = acc + jnp.where(lane_head == hd, jnp.sum(sc, axis=1, keepdims=True), 0.0)
        r.denom[rows_of(b), :] = acc
        r.numer[rows_of(b), :] = dot_nn(r.low[b], by_head(r.vf[rows_of(b), :]))

    for c in (0, 1):
        hg_finish(1, c)
    ag_pass(UP, 0)
    ag_send(DOWN, 0)
    state_wait(0, r.st_recv)

    def both(b, value, thr):
        one = value.astype(F32) * wide(r.car[b])
        return jnp.concatenate([one.astype(BF), (one * thr).astype(BF)], axis=1)

    for b in range(batches):
        left = both(b, r.qf[rows_of(b), :], before_thr[b])
        states = jnp.concatenate([unfold(r.st_recv, i, b) for i in (0, 1)], axis=0)
        only = lax.broadcasted_iota(jnp.int32, (16, local), 0)
        sums = jnp.concatenate(
            [
                jnp.where(
                    same_head,
                    dot_tn(
                        jnp.where(
                            only == b, r.st_recv[i, batches * DH :, :].astype(F32), 0.0
                        ).astype(BF),
                        jnp.ones((16, local), BF),
                    ),
                    0.0,
                ).astype(BF)
                for i in (0, 1)
            ],
            axis=0,
        )
        top = r.numer[rows_of(b), :] + dot_nn(left, states)
        bottom = r.denom[rows_of(b), :] + dot_nn(left, sums)
        attn = top / jnp.maximum(bottom, 1.0)
        r.numer[rows_of(b), :] = attn
        r.denom[rows_of(b), :] = bottom
        r.mixed[rows_of(b), :] = attn.astype(BF)

    hr_first(0, 0, pick(r.mixed), product_nt(r.wo))
    hr_first(0, 1, pick(r.mixed), product_nt(r.wo))
    hr_second(0, 0)
    hr_second(0, 1)
    ag_pass(UP, 1)
    mine = h * own

    def x_rows(at_row):
        return r.xg[hi, ds(lo * own + at_row, tile), :].astype(F32)

    def c_rows(at_row):
        return r.cg[hi, ds(lo * own + at_row, tile), :].astype(F32)

    def norm_two(c):
        def some(i):
            at_row = c * part_rows + i * tile
            v = x_rows(at_row) + hr_value(0, c, ds(i * tile, tile))
            r.middle[ds(at_row, tile), :] = v
            u, _ = unit(v)
            r.ntwo[ds(mine + at_row, tile), :] = (u * gain_two + shift_two).astype(BF)

        loop(part_rows // tile, some)

    for c in (0, 1):
        hr_wait(0, c)
        norm_two(c)
        hg_start(2, c)
    ag_pass(DOWN, 0)
    hg_forward(2, 0)
    hg_forward(2, 1)
    ag_pass(UP, 2)
    hg_finish(2, 0)
    hg_finish(2, 1)
    ag_pass(DOWN, 1)
    ag_wait(UP, 3)

    tu = 256

    def up(i):
        rw = ds(lax.div(i, hidden // tn) * tu, tu)
        cols = ds(lax.rem(i, hidden // tn) * tn, tn)
        v = dot_nn(r.ntwo[rw, :], r.wu[:, cols]) + r.smallg[5:6, cols]
        square_of = v * v
        t = jnp.tanh(0.7978845608028654 * (v + 0.044715 * (square_of * v)))
        half = 0.5 * (1.0 + t)
        r.activ[rw, cols] = (v * half).astype(BF)
        r.gelu_d[rw, cols] = half + (0.5 * v) * (1.0 - t * t) * (
            0.7978845608028654 + (3.0 * 0.044715 * 0.7978845608028654) * square_of
        )

    loop((tokens // tu) * (hidden // tn), up)
    rs_round(DOWN, 0)
    ag_pass(DOWN, 2)
    rs_round(DOWN, 1)
    ag_wait(DOWN, 3)

    def back(i):
        cols = ds(i * tn, tn)
        for b in range(batches):
            g = dot_nn(r.cg[b], r.wd[:, cols])
            r.g_hid[rows_of(b), cols] = (g * r.gelu_d[rows_of(b), cols]).astype(BF)

    loop(hidden // tn, back)
    rs_round(UP, 0)
    hr_first(2, 0, pick(r.g_hid), product_nt(r.wu))
    hr_first(2, 1, pick(r.g_hid), product_nt(r.wu))
    hr_second(2, 0)
    rs_round(DOWN, 2)
    hr_second(2, 1)

    r.hs_send[...] = jnp.zeros_like(r.hs_send)

    def back_norm(g, u, inverse, gain):
        scaled = g * gain
        centered = scaled - jnp.mean(scaled, axis=1, keepdims=True)
        return inverse * (centered - u * jnp.mean(scaled * u, axis=1, keepdims=True))

    def norm_two_back(c):
        def some(i):
            at_row = c * part_rows + i * tile
            rw = ds(at_row, tile)
            g = hr_value(2, c, ds(i * tile, tile))
            u, inverse = unit(r.middle[rw, :])
            out = c_rows(at_row)
            v = out + back_norm(g, u, inverse, gain_two)
            r.g_mid[rw, :] = v
            r.gatt[ds(mine + at_row, tile), :] = v.astype(BF)
            r.hs_send[1:2, :] += jnp.sum(g * u, axis=0, keepdims=True)
            r.hs_send[3:4, :] += jnp.sum(g, axis=0, keepdims=True)
            r.hs_send[4:5, :] += jnp.sum(out, axis=0, keepdims=True)

        loop(part_rows // tile, some)

    hr_wait(2, 0)
    norm_two_back(0)
    hg_start(3, 0)
    rs_round(UP, 1)
    hr_wait(2, 1)
    norm_two_back(1)
    hg_start(3, 1)
    hr_first(1, 0, pick(r.activ), product_nt(r.wd))
    hr_first(1, 1, pick(r.activ), product_nt(r.wd))
    rs_round(DOWN, 3)
    for c in (0, 1):
        hg_forward(3, c)
    for c in (0, 1):
        hr_second(1, c)
    for c in (0, 1):
        hg_finish(3, c)

    def mixed_back(i):
        rw = ds(i * tm, tm)
        g = dot_nn(r.gatt[rw, :], r.wo[...])
        attn, bottom = r.numer[rw, :], r.denom[rw, :]
        r.g_num[rw, :] = (g / jnp.maximum(bottom, 1.0)).astype(BF)
        prod = g * attn
        lh = lane_head[:tm]
        acc = jnp.zeros((tm, local), F32)
        for hd in range(heads):
            acc = acc + jnp.where(
                lh == hd,
                jnp.sum(jnp.where(lh == hd, prod, 0.0), axis=1, keepdims=True),
                0.0,
            )
        r.g_den[rw, :] = jnp.where(bottom > 1.0, -acc / jnp.maximum(bottom, 1.0), 0.0)

    loop(tokens // tm, mixed_back)

    parts = []
    for b in range(batches):
        q = r.qf[rows_of(b), :].astype(F32) * wide(r.car[b])
        parts.append(
            (
                dot_tn(q.astype(BF), r.g_num[rows_of(b), :]),
                jnp.sum(q * r.g_den[rows_of(b), :], axis=0, keepdims=True),
            )
        )
    fold(r.gs_send, parts)
    state_send(1, r.gs_send, r.gs_recv, -1)
    rs_round(UP, 2)

    def head_lanes(hd, value):
        return jnp.where(lane_head == hd, value.astype(F32), 0.0).astype(BF)

    for b in range(batches):
        rw = rows_of(b)
        gk = jnp.zeros((rows, local), F32)
        gv = jnp.zeros((rows, local), F32)
        gq = jnp.zeros((rows, local), F32)
        for hd in range(heads):
            gn = head_lanes(hd, r.g_num[rw, :])
            g = dot_nt(gn, r.vf[rw, :]) + r.g_den[rw, hd * DH : hd * DH + 1]
            g = (g * r.mask[b]).astype(BF)
            gq = gq + dot_nn(g, head_lanes(hd, r.kf[rw, :]))
            gk = gk + dot_tn(g, head_lanes(hd, r.qf[rw, :]))
            gv = gv + dot_tn(r.low[b, :, hd * rows : (hd + 1) * rows], gn)
        left = both(b, r.g_num[rw, :], before_thr[b])
        states = jnp.concatenate([unfold(r.st_recv, i, b) for i in (0, 1)], axis=1)
        totals = unfold_sum(r.st_recv, 0, b) + before_thr[b] * unfold_sum(r.st_recv, 1, b)
        gq = gq + dot_nt(left, states) + wide(r.car[b]) * r.g_den[rw, :] * totals
        r.gproj[0, rw, :] = (gq * r.phi_d[0, rw, :]).astype(BF)
        r.gk[rw, :] = gk
        r.gv[rw, :] = gv

    rs_round(OUT, 0)
    state_wait(1, r.gs_recv)
    for b in range(batches):
        rw = rows_of(b)
        thr = after_thr[b]
        states = [unfold(r.gs_recv, i, b) for i in (0, 1)]
        totals = unfold_sum(r.gs_recv, 0, b) + thr * unfold_sum(r.gs_recv, 1, b)
        k = r.kf[rw, :].astype(F32) * wide(r.tail[b])
        v = r.vf[rw, :].astype(F32) * wide(r.tail[b])
        k2 = jnp.concatenate([k.astype(BF), (k * thr).astype(BF)], axis=1)
        v2 = jnp.concatenate([v.astype(BF), (v * thr).astype(BF)], axis=1)
        gk = r.gk[rw, :] + dot_nt(v2, jnp.concatenate(states, axis=1)) + wide(r.tail[b]) * totals
        gv = r.gv[rw, :] + dot_nn(k2, jnp.concatenate(states, axis=0))
        r.gproj[1, rw, :] = (gk * wide(r.pmc[b]) * r.phi_d[1, rw, :]).astype(BF)
        r.gproj[2, rw, :] = gv.astype(BF)

    rs_round(QKV, 0)

    def picks(where):
        return [
            jnp.concatenate([r.gproj[kind, rw, :] for rw in where], axis=0) for kind in range(3)
        ]

    def first_term(left, cols):
        v = dot_nt(left[0], r.wq[0, cols, :])
        for kind in (1, 2):
            v = v + dot_nt(left[kind], r.wq[kind, cols, :])
        return v

    hr_first(3, 0, picks, first_term)
    hr_first(3, 1, picks, first_term)
    hr_second(3, 0)
    hr_second(3, 1)
    rs_round(OUT, 1)
    rs_round(QKV, 1)
    rs_round(UP, 3)

    def norm_one_back(c):
        def some(i):
            at_row = c * part_rows + i * tile
            rw = ds(at_row, tile)
            g = hr_value(3, c, ds(i * tile, tile))
            u, inverse = unit(x_rows(at_row))
            r.i_rows[rw, :] = r.g_mid[rw, :] + back_norm(g, u, inverse, gain_one)
            r.hs_send[0:1, :] += jnp.sum(g * u, axis=0, keepdims=True)
            r.hs_send[2:3, :] += jnp.sum(g, axis=0, keepdims=True)

        loop(part_rows // tile, some)

    for c in (0, 1):
        hr_wait(3, c)
        norm_one_back(c)
    turn(1, r.i_rows, r.ing_o)
    rs_round(OUT, 2)
    rs_round(QKV, 2)

    def finish_rows(c):
        def some(i):
            rw = ds(c * part_rows + i * tile, tile)
            r.a_rows[rw, :] = r.middle[rw, :] + hr_value(1, c, ds(i * tile, tile)) + shift_out

        loop(part_rows // tile, some)

    for c in (0, 1):
        hr_wait(1, c)
        finish_rows(c)
    turn(0, r.a_rows, r.act_o)

    r.hs_recv[h] = r.hs_send[...]
    for i in range(1, m):
        remote(
            r.hs_send, r.hs_recv.at[h], r.hs_s.at[0], r.hs_r.at[0], s, lax.rem(h + i, m)
        ).start()
    r.upb[...] = jnp.zeros_like(r.upb)

    def column_sums(i):
        r.upb[...] += jnp.sum(r.g_hid[ds(i * tile, tile), :].astype(F32), axis=0, keepdims=True)

    loop(tokens // tile, column_sums)
    rs_round(OUT, 3)
    rs_final(DOWN)
    rs_round(QKV, 3)
    landed(r.hs_recv.at[pl.ds(0, m - 1)], r.hs_r.at[0])
    acc = r.hs_recv[0]
    for i in range(1, m):
        acc = acc + r.hs_recv[i]
    r.sg[...] = acc
    r.sg[5:6, :] = r.upb[...]
    r.ss_recv[s] = r.sg[:, ds(s * block, block)]
    for i in range(1, n):
        to = lax.rem(s + i, n)
        remote(
            r.sg.at[:, ds(to * block, block)],
            r.ss_recv.at[s],
            r.ss_s.at[0],
            r.ss_r.at[0],
            to,
            h,
        ).start()
    rs_final(UP)
    rs_final(OUT)
    landed(r.ss_recv.at[pl.ds(0, n - 1)], r.ss_r.at[0])
    acc = r.ss_recv[0]
    for i in range(1, n):
        acc = acc + r.ss_recv[i]
    r.gg_o[...] = acc[0:2]
    r.gb_o[...] = acc[2:5]
    r.gup_o[...] = acc[5:6]
    turn_wait(0, r.a_rows)
    turn_wait(1, r.i_rows)

    far = pl.ds(0, (n - 1) * block)
    for w in range(5):
        views = (r.wq.at[:, far, :], r.wo.at[far], r.wu.at[far], r.wd.at[far], r.smallg.at[:, far])
        drained(views[w], r.ag_s.at[w])
    others = pl.ds(0, (m - 1) * local)
    rest = pl.ds(0, (m - 1) * own)
    for k in range(4):
        view = (r.xg, r.cg)[k].at[:, :, others] if k < 2 else (r.ntwo, r.gatt)[k - 2].at[rest]
        drained(view, r.hg_s.at[k])
        drained(r.h_s1.at[k], r.hr_s.at[k, 0])
        drained(r.h_s2.at[k], r.hr_s.at[k, 1])
    for k, dest in enumerate((r.st_recv, r.gs_recv)):
        drained(dest, r.st_s.at[k])
    drained(r.a_rows.at[:, others], r.aa_s.at[0])
    drained(r.i_rows.at[:, others], r.aa_s.at[1])
    drained(r.hs_recv.at[pl.ds(0, m - 1)], r.hs_s.at[0])
    drained(r.ss_recv.at[pl.ds(0, n - 1)], r.ss_s.at[0])
    rs_final(QKV)
    for w in range(4):
        drained(rs_send[w].at[pl.ds(0, n - 1)], r.rs_s.at[w])
    for copy in local_copies:
        copy.wait()


def settle(*refs):
    count = len(refs) // 2
    copies = [
        pltpu.make_async_copy(refs[i], refs[count + i], refs[-1].at[i]) for i in range(count)
    ]
    for copy in copies:
        copy.start()
    for copy in copies:
        copy.wait()


def whole_layer(n, m):
    def on_each(
        tokens, cotangent, w_qkv, w_out_t, w_up, w_down_t, gains, biases, up_bias, lengths, pixel_mask
    ):
        batches, rows, local = tokens.shape
        width = w_qkv.shape[0] * n
        hidden = w_up.shape[1]
        block = width // n
        vm, sems = layout(n, m, batches, rows, width, local, hidden)
        ins = ["tok", "cot", "w_qkv", "w_out", "w_up", "w_down", "gains", "biases", "up_bias", "lengths", "pixel"]
        outs = ["act_o", "ing_o", "gq_o", "go_o", "gu_o", "gd_o", "gg_o", "gb_o", "gup_o"]
        anywhere = pl.BlockSpec(memory_space=pl.ANY)
        in_vmem = pl.BlockSpec(memory_space=pltpu.VMEM)
        in_smem = pl.BlockSpec(memory_space=pltpu.SMEM)

        result = pl.pallas_call(
            functools.partial(body, n, m, ins + outs + list(vm) + list(sems)),
            name="layer",
            out_shape=(
                pltpu.VMEM((batches, rows, local), F32),
                pltpu.VMEM((batches, rows, local), F32),
                pltpu.VMEM((3, block, local), F32),
                pltpu.VMEM((block, local), F32),
                pltpu.VMEM((block, hidden), F32),
                pltpu.VMEM((block, hidden), F32),
                pltpu.VMEM((2, block), F32),
                pltpu.VMEM((3, block), F32),
                pltpu.VMEM((1, block), F32),
            ),
            in_specs=[anywhere] * 6 + [in_vmem] * 3 + [in_smem, in_vmem],
            out_specs=[in_vmem] * 9,
            scratch_shapes=[pltpu.VMEM(shape, kind) for shape, kind in vm.values()]
            + [pltpu.SemaphoreType.DMA(shape) for shape in sems.values()],
            compiler_params=pltpu.CompilerParams(
                collective_id=0, has_side_effects=True, vmem_limit_bytes=60_000_000
            ),
        )(
            tokens,
            cotangent,
            jnp.transpose(w_qkv, (1, 0, 2)),
            w_out_t,
            w_up,
            w_down_t,
            gains,
            biases,
            up_bias,
            lengths,
            pixel_mask,
        )
        result = pl.pallas_call(
            settle,
            name="settle",
            out_shape=[jax.ShapeDtypeStruct(a.shape, a.dtype) for a in result],
            in_specs=[in_vmem] * len(result),
            out_specs=[anywhere] * len(result),
            scratch_shapes=[pltpu.SemaphoreType.DMA((len(result),))],
        )(*[pltpu.with_memory_space_constraint(a, pltpu.VMEM) for a in result])
        return (*result[:2], jnp.transpose(result[2], (1, 0, 2)), *result[3:])

    return on_each


def solution(mesh):
    in_specs = (
        P(None, "seq", "head"),
        P(None, "seq", "head"),
        P("seq", None, "head"),
        P("seq", "head"),
        P("seq", "head"),
        P("seq", "head"),
        P(None, "seq"),
        P(None, "seq"),
        P("head", "seq"),
        P(),
        P(None, "seq"),
    )
    out_specs = (
        P(None, "seq", "head"),
        P(None, "seq", "head"),
        P("seq", None, "head"),
        P("seq", "head"),
        P("seq", "head"),
        P("seq", "head"),
        P(None, "seq"),
        P(None, "seq"),
        P("head", "seq"),
    )
    n, m = mesh.shape["seq"], mesh.shape["head"]
    fits = (n, m) == (8, 4)
    return jax.shard_map(
        whole_layer(n, m) if fits else on_device, mesh=mesh, in_specs=in_specs, out_specs=out_specs, check_vma=False
    )
```

```python
import functools

import jax
import jax.numpy as jnp
from jax import lax
from jax.experimental import pallas as pl
from jax.experimental.pallas import tpu as pltpu
from jax.sharding import PartitionSpec as P

DH = 64


highest = lax.Precision.HIGHEST
epsilon = 1e-05


def entering(array, axis, join, neutral):
    place = lax.axis_index(axis)
    gathered = jax.tree.map(
        lambda a, kind: lax.all_gather(a.astype(kind), axis),
        array,
        (jnp.bfloat16, jnp.bfloat16, jnp.bfloat16),
    )
    state = jax.tree.map(lambda a, e: jnp.zeros_like(a) + jnp.asarray(e, a.dtype), array, neutral)

    def one(hop, state):
        return join(
            state,
            jax.tree.map(
                lambda a, own: lax.dynamic_index_in_dim(a, hop, 0, False).astype(own.dtype),
                gathered,
                array,
            ),
        )

    return lax.fori_loop(0, place, one, state)


def entering_2(array, axis, combine, identity):
    length, place = (lax.axis_size(axis), lax.axis_index(axis))
    everything = jax.tree.map(
        lambda part, kind: lax.all_gather(part.astype(kind), axis),
        array,
        jax.tree.map(lambda a: jnp.bfloat16 if a.dtype == jnp.float32 else a.dtype, array),
    )
    start = jax.tree.map(
        lambda part, zero: jnp.broadcast_to(jnp.asarray(zero, part.dtype), part.shape),
        array,
        identity,
    )

    def hop(k, before):
        at = length - 1 - k
        reached = at > place
        new = combine(
            before, jax.tree.map(lambda part, own: part[at].astype(own.dtype), everything, array)
        )
        return jax.tree.map(lambda a, b: jnp.where(reached, a, b), new, before)

    return lax.fori_loop(0, length, hop, start)


def normalize(values, gain_vec, shift_vec):
    mean_val = jnp.mean(values, axis=-1, keepdims=True)
    centered = values - mean_val
    inverse = lax.rsqrt(jnp.mean(centered * centered, axis=-1, keepdims=True) + epsilon)
    unit_val = centered * inverse
    return (unit_val * gain_vec + shift_vec, unit_val, inverse)


def norm_back(grad_in, unit_val, inverse, gain_vec):
    scaled = grad_in * gain_vec
    centered = scaled - jnp.mean(scaled, axis=-1, keepdims=True)
    return inverse * (centered - unit_val * jnp.mean(scaled * unit_val, axis=-1, keepdims=True))


def features(values):
    return jax.nn.elu(values) + 1.0


def finish(numerator, denominator):
    return numerator / jnp.maximum(denominator, 1.0)[:, :, None]


def compose(earlier, later):
    return (
        later[0] + later[2] * earlier[0],
        later[1] + later[2] * earlier[1],
        later[2] * earlier[2],
    )


def item_numbers(lengths_row, first_place, number):
    offsets = jnp.cumsum(lengths_row) - lengths_row
    places = first_place + jnp.arange(number, dtype=jnp.int32)
    return jnp.sum((offsets[None, :] <= places[:, None]).astype(jnp.int32), axis=1) - 1


def on_device(
    tokens, cotangent, w_qkv, w_out_t, w_up, w_down_t, gains, biases, up_bias, lengths, pixel_mask
):
    batches, local_rows, columns = tokens.shape
    local_width = w_qkv.shape[2]
    heads_here = local_width // DH
    seq_index = lax.axis_index("seq")
    head_index = lax.axis_index("head")
    first_token = seq_index * local_rows
    position = jnp.arange(local_rows, dtype=jnp.int32)
    before = position[:, None] >= position[None, :]

    def own_columns(matrix):
        return lax.dynamic_slice_in_dim(matrix, head_index * columns, columns, 1)

    results = []
    input_grads = []
    shard_sums = None
    for batch_index in range(batches):
        full_qkv, full_out, full_up, full_down, full_gains, full_biases, full_upb = (
            lax.all_gather(w_qkv, "seq", axis=0, tiled=True),
            lax.all_gather(w_out_t, "seq", axis=0, tiled=True),
            lax.all_gather(w_up, "seq", axis=0, tiled=True),
            lax.all_gather(w_down_t, "seq", axis=0, tiled=True),
            lax.all_gather(gains, "seq", axis=1, tiled=True),
            lax.all_gather(biases, "seq", axis=1, tiled=True),
            lax.all_gather(up_bias, "seq", axis=1, tiled=True),
        )
        input_rows, grad_rows16 = (
            lax.all_gather(tokens[batch_index], "head", axis=1, tiled=True),
            lax.all_gather(cotangent[batch_index], "head", axis=1, tiled=True),
        )
        gains32 = full_gains.astype(jnp.float32)
        biases32 = full_biases.astype(jnp.float32)
        upb32 = full_upb.astype(jnp.float32).reshape(-1)
        inputs32 = input_rows.astype(jnp.float32)
        place_items = item_numbers(lengths[batch_index], first_token - 1, local_rows + 1)
        item_of = place_items[1:]
        carried = (item_of == place_items[0]).astype(jnp.float32)
        tail_mask = (item_of == item_of[local_rows - 1]).astype(jnp.float32)
        through = carried[local_rows - 1]
        same_item = ((item_of[:, None] == item_of[None, :]) & before).astype(jnp.float32)
        keep_half = pixel_mask[batch_index].astype(jnp.bfloat16)
        keep32 = pixel_mask[batch_index].astype(jnp.float32)
        lifted, unit_one, inverse_one = normalize(inputs32, gains32[0], biases32[0])
        normed = lifted.astype(jnp.bfloat16)
        projected = jnp.einsum("td,dsf->tsf", normed, full_qkv, preferred_element_type=jnp.float32)
        query_feat = (
            features(projected[:, 0]).astype(jnp.bfloat16).reshape(local_rows, heads_here, DH)
        )
        key_feat = (features(projected[:, 1]).astype(jnp.bfloat16) * keep_half[:, None]).reshape(
            local_rows, heads_here, DH
        )
        value_feat = projected[:, 2].astype(jnp.bfloat16).reshape(local_rows, heads_here, DH)
        tail_key = key_feat * tail_mask.astype(jnp.bfloat16)[:, None, None]
        state_loc = jnp.einsum(
            "jhd,jhe->hde", tail_key, value_feat, preferred_element_type=jnp.float32
        )
        total_loc = jnp.sum(tail_key.astype(jnp.float32), axis=0)
        identity = (jnp.zeros_like(state_loc), jnp.zeros_like(total_loc), jnp.ones((), jnp.float32))
        state_in, total_in, passed = entering(
            (state_loc, total_loc, through), "seq", compose, identity
        )
        query32 = query_feat.astype(jnp.float32)
        scores = (
            jnp.einsum("thd,jhd->htj", query_feat, key_feat, preferred_element_type=jnp.float32)
            * same_item[None]
        )
        scores_low = scores.astype(jnp.bfloat16)
        numerator = jnp.einsum(
            "htj,jhe->the", scores_low, value_feat, preferred_element_type=jnp.float32
        ) + carried[:, None, None] * jnp.einsum(
            "thd,hde->the", query32, state_in, precision=highest
        )
        denominator = jnp.sum(scores, axis=2).T + carried[:, None] * jnp.einsum(
            "thd,hd->th", query32, total_in, precision=highest
        )
        output, finish_back = jax.vjp(finish, numerator, denominator)
        mixed_out = output.reshape(local_rows, local_width).astype(jnp.bfloat16)
        attended = lax.psum(
            jnp.einsum("tf,df->td", mixed_out, full_out, preferred_element_type=jnp.float32).astype(
                jnp.bfloat16
            ),
            "head",
        ).astype(jnp.float32)
        middle = inputs32 + attended
        lifted_two, unit_two, inverse_two = normalize(middle, gains32[1], biases32[1])
        normed_two = lifted_two.astype(jnp.bfloat16)
        hidden = jnp.dot(normed_two, full_up, preferred_element_type=jnp.float32) + upb32
        activated32, gelu_back = jax.vjp(jax.nn.gelu, hidden)
        activated = activated32.astype(jnp.bfloat16)
        branch = lax.psum_scatter(
            jnp.einsum(
                "tf,df->td", activated, full_down, preferred_element_type=jnp.float32
            ).astype(jnp.bfloat16),
            "head",
            scatter_dimension=1,
            tiled=True,
        ).astype(jnp.float32)
        results.append(own_columns(middle) + branch + own_columns(biases32[2][None]))
        grad_out = grad_rows16.astype(jnp.float32)
        grad_down = jnp.einsum(
            "td,tf->df", grad_rows16, activated, preferred_element_type=jnp.float32
        )
        grad_act = jnp.einsum(
            "td,df->tf", grad_rows16, full_down, preferred_element_type=jnp.float32
        )
        grad_hidden = gelu_back(grad_act)[0].astype(jnp.bfloat16)
        grad_up = jnp.einsum(
            "td,tf->df", normed_two, grad_hidden, preferred_element_type=jnp.float32
        )
        grad_upb = jnp.sum(grad_hidden.astype(jnp.float32), axis=0).reshape(full_upb.shape)
        grad_two = lax.psum(
            jnp.einsum(
                "tf,df->td", grad_hidden, full_up, preferred_element_type=jnp.float32
            ).astype(jnp.bfloat16),
            "head",
        ).astype(jnp.float32)
        grad_middle = grad_out + norm_back(grad_two, unit_two, inverse_two, gains32[1])
        grad_attended = grad_middle.astype(jnp.bfloat16)
        grad_out_t = jnp.einsum(
            "td,tf->df", grad_attended, mixed_out, preferred_element_type=jnp.float32
        )
        grad_mixed = jnp.einsum(
            "td,df->tf", grad_attended, full_out, preferred_element_type=jnp.float32
        ).reshape(local_rows, heads_here, DH)
        grad_numer32, grad_denom = finish_back(grad_mixed)
        grad_numer = grad_numer32.astype(jnp.bfloat16)
        grad_numer_wide = grad_numer.astype(jnp.float32)
        grad_scores = (
            (
                jnp.einsum(
                    "the,jhe->htj", grad_numer, value_feat, preferred_element_type=jnp.float32
                )
                + grad_denom.T[:, :, None]
            )
            * same_item[None]
        ).astype(jnp.bfloat16)
        carried_query = query32 * carried[:, None, None]
        grad_query = jnp.einsum(
            "htj,jhd->thd", grad_scores, key_feat, preferred_element_type=jnp.float32
        ) + carried[:, None, None] * (
            jnp.einsum("hde,the->thd", state_in, grad_numer_wide, precision=highest)
            + grad_denom[:, :, None] * total_in[None]
        )
        grad_key = jnp.einsum(
            "htj,thd->jhd", grad_scores, query_feat, preferred_element_type=jnp.float32
        )
        grad_value = jnp.einsum(
            "htj,the->jhe", scores_low, grad_numer, preferred_element_type=jnp.float32
        )
        grad_state_in = jnp.einsum(
            "thd,the->hde", carried_query, grad_numer_wide, precision=highest
        )
        grad_total_in = jnp.einsum("thd,th->hd", carried_query, grad_denom, precision=highest)
        grad_state_loc, grad_total_loc, passed_back = entering_2(
            (grad_state_in, grad_total_in, through), "seq", compose, identity
        )
        tail_three = tail_mask[:, None, None]
        value_wide = value_feat.astype(jnp.float32)
        key_wide = key_feat.astype(jnp.float32)
        grad_key = grad_key + tail_three * (
            jnp.einsum("hde,jhe->jhd", grad_state_loc, value_wide, precision=highest)
            + grad_total_loc[None]
        )
        grad_value = grad_value + tail_three * jnp.einsum(
            "jhd,hde->jhe", key_wide, grad_state_loc, precision=highest
        )
        ignored, feature_back = jax.vjp(features, projected[:, :2])
        grad_features = jnp.stack(
            [
                grad_query.reshape(local_rows, local_width),
                grad_key.reshape(local_rows, local_width) * keep32[:, None],
            ],
            axis=1,
        )
        grad_pair = feature_back(grad_features)[0]
        grad_projected = jnp.concatenate(
            [grad_pair, grad_value.reshape(local_rows, 1, local_width)], axis=1
        ).astype(jnp.bfloat16)
        grad_qkv = jnp.einsum(
            "td,tsf->dsf", normed, grad_projected, preferred_element_type=jnp.float32
        )
        grad_one = lax.psum(
            jnp.einsum(
                "tsf,dsf->td", grad_projected, full_qkv, preferred_element_type=jnp.float32
            ).astype(jnp.bfloat16),
            "head",
        ).astype(jnp.float32)
        grad_inputs = grad_middle + norm_back(grad_one, unit_one, inverse_one, gains32[0])
        input_grads.append(own_columns(grad_inputs))
        grad_gains = jnp.stack(
            [jnp.sum(grad_one * unit_one, axis=0), jnp.sum(grad_two * unit_two, axis=0)]
        )
        grad_biases = jnp.stack(
            [jnp.sum(grad_one, axis=0), jnp.sum(grad_two, axis=0), jnp.sum(grad_out, axis=0)]
        )
        pieces = (
            lax.psum_scatter(grad_qkv, "seq", scatter_dimension=0, tiled=True),
            lax.psum_scatter(grad_out_t, "seq", scatter_dimension=0, tiled=True),
            lax.psum_scatter(grad_up, "seq", scatter_dimension=0, tiled=True),
            lax.psum_scatter(grad_down, "seq", scatter_dimension=0, tiled=True),
            lax.psum_scatter(grad_gains, "seq", scatter_dimension=1, tiled=True),
            lax.psum_scatter(grad_biases, "seq", scatter_dimension=1, tiled=True),
            lax.psum_scatter(grad_upb, "seq", scatter_dimension=1, tiled=True),
        )
        shard_sums = pieces if shard_sums is None else jax.tree.map(jnp.add, shard_sums, pieces)
    return (
        jnp.stack(results),
        jnp.stack(input_grads),
        shard_sums[0],
        shard_sums[1],
        shard_sums[2],
        shard_sums[3],
        shard_sums[4],
        shard_sums[5],
        shard_sums[6],
    )


MESH = pl.DeviceIdType.MESH
BF = jnp.bfloat16
F32 = jnp.float32
QKV, OUT, UP, DOWN, SMALL = range(5)
QUERY = 4


def dot_nn(a, b):
    return lax.dot_general(a, b, (((1,), (0,)), ((), ())), preferred_element_type=F32)


def dot_nt(a, b):
    return lax.dot_general(a, b, (((1,), (1,)), ((), ())), preferred_element_type=F32)


def dot_tn(a, b):
    return lax.dot_general(a, b, (((0,), (0,)), ((), ())), preferred_element_type=F32)


def ds(start, size):
    return pl.ds(pl.multiple_of(start, size), size)


def loop(count, body):
    def step(i, carry):
        body(i)
        return carry

    lax.fori_loop(0, count, step, 0)


def layout(n, m, batches, rows, width, local, hidden):
    tokens = batches * rows
    block = width // n
    own = tokens // m
    hops = n // 2
    heads = local // DH
    vm = {
        "xg": ((batches, rows, width), BF),
        "cg": ((batches, rows, width), BF),
        "wq": ((3, width, local), BF),
        "wo": ((width, local), BF),
        "wu": ((width, hidden), BF),
        "wd": ((width, hidden), BF),
        "small": ((8, block), F32),
        "smallg": ((8, width), F32),
        "normed": ((tokens, width), BF),
        "phi_d": ((2, tokens, local), F32),
        "qf": ((tokens, local), BF),
        "kf": ((tokens, local), BF),
        "vf": ((tokens, local), BF),
        "mask": ((batches, rows, rows), F32),
        "car": ((batches, rows, 128), F32),
        "tail": ((batches, rows, 128), F32),
        "pmc": ((batches, rows, 128), F32),
        "low": ((batches, rows, heads * rows), BF),
        "numer": ((tokens, local), F32),
        "denom": ((tokens, local), F32),
        "mixed": ((tokens, local), BF),
        "st_send": ((batches * DH + 16, local), BF),
        "st_recv": ((2, batches * DH + 16, local), BF),
        "gs_send": ((batches * DH + 16, local), BF),
        "gs_recv": ((2, batches * DH + 16, local), BF),
        "middle": ((own, width), F32),
        "ntwo": ((tokens, width), BF),
        "gelu_d": ((tokens, hidden), F32),
        "activ": ((tokens, hidden), BF),
        "g_hid": ((tokens, hidden), BF),
        "branch": ((own, width), F32),
        "total": ((own, width), F32),
        "g_mid": ((own, width), F32),
        "gatt": ((tokens, width), BF),
        "g_attn": ((tokens, local), F32),
        "g_num": ((tokens, local), BF),
        "g_den": ((tokens, local), F32),
        "gq": ((tokens, local), F32),
        "gk": ((tokens, local), F32),
        "gv": ((tokens, local), F32),
        "gproj": ((3, tokens, local), BF),
        "h_s1": ((4, 2, 2, own // 2, width), BF),
        "h_r1": ((4, 2, 2, own // 2, width), BF),
        "h_acc": ((4, 2, 2, own // 2, width), F32),
        "h_s2": ((4, 2, own // 2, width), BF),
        "h_r2": ((4, 2, own // 2, width), BF),
        "rq_s": ((n, 2, block, local), BF),
        "rq_r": ((n, 2, block, local), BF),
        "rx_s": ((n, block, local), BF),
        "rx_r": ((n, block, local), BF),
        "ro_s": ((n, block, local), BF),
        "ro_r": ((n, block, local), BF),
        "ru_s": ((n, block, hidden), BF),
        "ru_r": ((n, block, hidden), BF),
        "rd_s": ((n, block, hidden), BF),
        "rd_r": ((n, block, hidden), BF),
        "pq": ((2, 2, block, local), F32),
        "po": ((2, block, local), F32),
        "pu": ((2, block, hidden), F32),
        "pd": ((2, block, hidden), F32),
        "px": ((2, block, local), F32),
        "g_act": ((tokens, hidden), F32),
        "hs_recv": ((m, 8, width), F32),
        "hs_send": ((8, width), F32),
        "upb": ((1, hidden), F32),
        "sg": ((8, width), F32),
        "ss_recv": ((n, 8, block), F32),
        "a_rows": ((own, width), F32),
        "i_rows": ((own, width), F32),
    }
    sems = {
        "ag_s": (5,),
        "ag_r": (5, 2, hops),
        "rs_s": (5,),
        "rs_r": (5, 2, hops),
        "hg_s": (4,),
        "hg_r": (4, 2, 3),
        "hr_s": (4, 2),
        "hr_r": (4, 2, 2),
        "st_s": (2,),
        "st_r": (2,),
        "aa_s": (2,),
        "aa_r": (2,),
        "hs_s": (1,),
        "hs_r": (1,),
        "ss_s": (1,),
        "ss_r": (1,),
        "lc": (8,),
    }
    return vm, sems


class Refs:
    pass


def body(n, m, names, *refs):
    r = Refs()
    for name, ref in zip(names, refs):
        setattr(r, name, ref)
    batches, rows, width = r.xg.shape
    tokens = batches * rows
    own = tokens // m
    block = width // n
    local = r.wo.shape[1]
    hidden = r.wu.shape[1]
    heads = local // DH
    hops = n // 2
    s = lax.axis_index("seq")
    h = lax.axis_index("head")
    odd = lax.rem(s, 2)
    p = (1 - odd) * lax.div(s, 2) + odd * (n - 1 - lax.div(s, 2))
    lo, hi = lax.rem(h, 2), lax.div(h, 2)
    pair = h + 1 - 2 * lo
    cross = lax.rem(h + 2, m)

    def at(place):
        place = lax.rem(place + 2 * n, n)
        far = lax.div(place, hops)
        return (1 - far) * 2 * place + far * (2 * (n - 1 - place) + 1)

    ring = (at(p + 1), at(p - 1))
    sign = (1, -1)

    def remote(src, dst, send, recv, seq, head):
        return pltpu.make_async_remote_copy(
            src_ref=src,
            dst_ref=dst,
            send_sem=send,
            recv_sem=recv,
            device_id=(seq, head),
            device_id_type=MESH,
        )

    def drained(view, sem):
        remote(view, view, sem, sem, ring[0], h).wait_send()

    def landed(view, sem):
        remote(view, view, sem, sem, ring[0], h).wait_recv()

    r.small[...] = jnp.zeros_like(r.small)
    r.small[0:2, :] = r.gains[...].astype(F32)
    r.small[2:5, :] = r.biases[...].astype(F32)
    r.small[5:6, :] = r.up_bias[...].astype(F32)

    barrier = pltpu.get_barrier_semaphore()
    for peer in ((ring[0], h), (ring[1], h), (s, pair), (s, cross)):
        pl.semaphore_signal(barrier, inc=1, device_id=peer, device_id_type=MESH)
    pl.semaphore_wait(barrier, 4)

    shards = (r.w_qkv, r.w_out, r.w_up, r.w_down, r.small)
    gathered = (r.wq, r.wo, r.wu, r.wd, r.smallg)

    def part_of(w, d, j):
        wide_part = r.wq.shape[2] if w == QKV else shards[w].shape[1]
        if j < hops - 1 or w == SMALL:
            return pl.ds(0, wide_part)
        return pl.ds(d * (wide_part // 2), wide_part // 2)

    def ag_shard(w, d, j):
        cols = part_of(w, d, j)
        if w == SMALL:
            return r.small
        return shards[w].at[:, :, cols] if w == QKV else shards[w].at[:, cols]

    def ag_full(w, owner, d, j):
        cols = part_of(w, d, j)
        if w == SMALL:
            return r.smallg.at[:, ds(owner * block, block)]
        if w == QKV:
            return r.wq.at[:, ds(owner * block, block), cols]
        return gathered[w].at[ds(owner * block, block), cols]

    def ways(w, j):
        return (0,) if w == SMALL and j == hops - 1 else (0, 1)

    def ag_send(w, j):
        for d in ways(w, j):
            owner = at(p - sign[d] * j)
            src = ag_shard(w, d, j) if j == 0 else ag_full(w, owner, d, j)
            remote(
                src, ag_full(w, owner, d, j), r.ag_s.at[w], r.ag_r.at[w, d, j], ring[d], h
            ).start()

    def ag_wait(w, j):
        for d in ways(w, j):
            landed(ag_full(w, at(p - sign[d] * (j + 1)), d, j), r.ag_r.at[w, d, j])

    def ag_pass(w, j):
        ag_wait(w, j)
        ag_send(w, j + 1)

    part_rows = own // 2

    def hg_view(k, c, who):
        if k < 2:
            return (r.xg, r.cg)[k].at[c, :, ds(who * local, local)]
        return (r.ntwo, r.gatt)[k - 2].at[ds(who * own + c * part_rows, part_rows), :]

    def hg_copy(k, c, i, src, who, to):
        return remote(src, hg_view(k, c, who), r.hg_s.at[k], r.hg_r.at[k, c, i], s, to)

    def hg_start(k, c):
        src = (r.tok, r.cot)[k].at[c] if k < 2 else hg_view(k, c, h)
        hg_copy(k, c, 1, src, h, cross).start()
        hg_copy(k, c, 0, src, h, pair).start()

    def hg_forward(k, c):
        view = hg_view(k, c, cross)
        hg_copy(k, c, 1, view, cross, cross).wait_recv()
        hg_copy(k, c, 2, view, cross, pair).start()

    def hg_finish(k, c):
        view = hg_view(k, c, pair)
        hg_copy(k, c, 0, view, pair, pair).wait_recv()
        across = lax.rem(pair + 2, m)
        view = hg_view(k, c, across)
        hg_copy(k, c, 2, view, across, pair).wait_recv()

    tn = 256

    def hr_first(k, c, left, product):
        blocks = [2 * i + 1 - lo for i in (0, 1)] + [2 * i + lo for i in (0, 1)]
        where = [ds(who * own + c * part_rows, part_rows) for who in blocks]

        def some(i):
            cols = ds(i * tn, tn)
            v = product(left(where), cols)
            for q in (0, 1):
                r.h_s1[k, c, q, :, cols] = v[q * part_rows : (q + 1) * part_rows].astype(BF)
                r.h_acc[k, c, q, :, cols] = v[(q + 2) * part_rows : (q + 3) * part_rows]

        loop(width // tn, some)
        hr_copy(k, c, 0).start()

    def hr_copy(k, c, stage):
        if stage == 0:
            src, dst, to = r.h_s1.at[k, c], r.h_r1.at[k, c], pair
        else:
            src, dst, to = r.h_s2.at[k, c], r.h_r2.at[k, c], cross
        return remote(src, dst, r.hr_s.at[k, stage], r.hr_r.at[k, c, stage], s, to)

    def hr_second(k, c):
        hr_copy(k, c, 0).wait_recv()

        def away(i):
            rw = ds(i * 32, 32)
            r.h_s2[k, c, rw, :] = (
                r.h_acc[k, c, 1 - hi, rw, :] + r.h_r1[k, c, 1 - hi, rw, :].astype(F32)
            ).astype(BF)

        loop(part_rows // 32, away)
        hr_copy(k, c, 1).start()

    def hr_wait(k, c):
        hr_copy(k, c, 1).wait_recv()

    def hr_value(k, c, rw):
        return (
            r.h_acc[k, c, hi, rw, :]
            + r.h_r1[k, c, hi, rw, :].astype(F32)
            + r.h_r2[k, c, rw, :].astype(F32)
        )

    def pick(ref):
        return lambda where: jnp.concatenate([ref[rw, :] for rw in where], axis=0)

    def product_nt(right):
        return lambda left, cols: dot_nt(left, right[cols, :])

    def rs_term(w, owner, piece):
        cols = ds(owner * block, block)
        if w == DOWN:
            left = r.cg[:, :, cols].reshape(tokens, block)
            half = hidden // 2
            return [dot_tn(left, r.activ[:, pl.ds(piece * half, half)])]
        if w == UP:
            half = hidden // 2
            return [dot_tn(r.ntwo[:, cols], r.g_hid[:, pl.ds(piece * half, half)])]
        half = local // 2
        if w == OUT:
            return [dot_tn(r.gatt[:, cols], r.mixed[:, pl.ds(piece * half, half)])]
        left = r.normed[:, cols]
        kinds = (0,) if w == QUERY else (1, 2)
        return [dot_tn(left, r.gproj[i, :, pl.ds(piece * half, half)]) for i in kinds]

    rs_send = (r.rq_s, r.ro_s, r.ru_s, r.rd_s, r.rx_s)
    rs_recv = (r.rq_r, r.ro_r, r.ru_r, r.rd_r, r.rx_r)

    def rs_half(w, piece):
        half = rs_send[w].shape[-1] // 2
        return pl.ds(piece * half, half)

    def rs_view(ref, w, d, step):
        if step > 0:
            return ref.at[d * hops + step]
        if w == QKV:
            return ref.at[d * hops, :, :, rs_half(w, d)]
        return ref.at[d * hops, :, rs_half(w, d)]

    def rs_arrived(w, d, step):
        landed(rs_view(rs_recv[w], w, d, step), r.rs_r.at[w, d, step])

    ahead = (r.pq, r.po, r.pu, r.pd, r.px)

    def rs_prepare(w, step):
        for d in (0, 1) if step < hops else (0,):
            owner = at(p + sign[d] * (hops - step)) if step < hops else s
            for piece in (0, 1) if step > 0 else (d,):
                cols = rs_half(w, piece)
                for i, v in enumerate(rs_term(w, owner, piece)):
                    lead = (i,) if w == QKV else ()
                    ahead[w][(d, *lead, slice(None), cols)] = v

    def rs_round(w, step):
        if step == 0:
            rs_prepare(w, 0)
        for d in (0, 1):
            slot = d * hops + step
            if step > 0:
                rs_arrived(w, d, step - 1)
            for piece in (0, 1) if step > 0 else (d,):
                cols = rs_half(w, piece)
                for i in range(2 if w == QKV else 1):
                    lead = (i,) if w == QKV else ()
                    v = ahead[w][(d, *lead, slice(None), cols)]
                    if step > 1 or (step == 1 and piece == d):
                        v = v + rs_recv[w][(slot - 1, *lead, slice(None), cols)].astype(F32)
                    rs_send[w][(slot, *lead, slice(None), cols)] = v.astype(BF)
            remote(
                rs_view(rs_send[w], w, d, step),
                rs_view(rs_recv[w], w, d, step),
                r.rs_s.at[w],
                r.rs_r.at[w, d, step],
                ring[d],
                h,
            ).start()
        rs_prepare(w, step + 1)

    finals = (r.gq_o.at[pl.ds(1, 2)], r.go_o, r.gu_o, r.gd_o, r.gq_o.at[0])
    local_copies = []

    def rs_final(w):
        for d in (0, 1):
            rs_arrived(w, d, hops - 1)
        for piece in (0, 1):
            cols = rs_half(w, piece)
            for i in range(2 if w == QKV else 1):
                lead = (i,) if w == QKV else ()
                v = ahead[w][(0, *lead, slice(None), cols)]
                for d in (0, 1):
                    v = v + rs_recv[w][(d * hops + hops - 1, *lead, slice(None), cols)].astype(F32)
                finals[w][(*lead, slice(None), cols)] = v

    def turn(k, src, dst):
        where = (hi, ds(lo * own, own))
        for i in range(1, m):
            to = lax.rem(h + i, m)
            remote(
                src.at[:, ds(to * local, local)],
                dst.at[where[0], where[1], :],
                r.aa_s.at[k],
                r.aa_r.at[k],
                s,
                to,
            ).start()
        copy = pltpu.make_async_copy(
            src.at[:, ds(h * local, local)], dst.at[where[0], where[1], :], r.lc.at[k]
        )
        copy.start()
        local_copies.append(copy)

    def turn_wait(k, src):
        landed(src.at[:, pl.ds(0, (m - 1) * local)], r.aa_r.at[k])

    ag_send(SMALL, 0)
    ag_send(QKV, 0)
    ag_send(OUT, 0)
    hg_start(0, 0)
    hg_start(0, 1)
    own_copies = [
        pltpu.make_async_copy(r.w_qkv, r.wq.at[:, ds(s * block, block), :], r.lc.at[4]),
        pltpu.make_async_copy(r.w_out, r.wo.at[ds(s * block, block), :], r.lc.at[5]),
        pltpu.make_async_copy(r.w_up, r.wu.at[ds(s * block, block), :], r.lc.at[6]),
        pltpu.make_async_copy(r.w_down, r.wd.at[ds(s * block, block), :], r.lc.at[7]),
        pltpu.make_async_copy(r.tok, r.xg.at[:, :, ds(h * local, local)], r.lc.at[2]),
        pltpu.make_async_copy(r.cot, r.cg.at[:, :, ds(h * local, local)], r.lc.at[3]),
    ]
    for copy in own_copies:
        copy.start()
    hg_start(1, 0)
    hg_start(1, 1)

    first = s * rows
    row_at = lax.broadcasted_iota(jnp.int32, (rows, 128), 0)
    lane_at = lax.broadcasted_iota(jnp.int32, (rows, rows), 1)
    square = lax.broadcasted_iota(jnp.int32, (local, local), 0)
    square_lane = lax.broadcasted_iota(jnp.int32, (local, local), 1)
    same_head = (square // DH) == (square_lane // DH)
    diagonal = square == square_lane
    lane_head = lax.broadcasted_iota(jnp.int32, (rows, local), 1) // DH
    before_thr, after_thr = [], []

    def wide(value):
        return jnp.concatenate([value] * (local // 128), axis=1)

    def begin(offsets, place):
        value = 0
        for off in offsets:
            value = jnp.where(off <= place, off, value)
        return value

    def through(offsets, which):
        return jnp.where(
            begin(offsets, which * rows + rows - 1) < which * rows, 1.0, 0.0
        ).astype(F32)

    def crops(b):
        offsets, running = [], 0
        for i in range(r.lengths.shape[1]):
            offsets.append(running)
            running = running + r.lengths[b, i]
        start = jnp.zeros((rows, 128), jnp.int32)
        for off in offsets:
            start = jnp.where(off <= row_at + first, off, start)
        last = begin(offsets, first + rows - 1)
        r.mask[b] = jnp.where(
            (lane_at + first >= wide(start)) & (lane_at <= wide(row_at)), 1.0, 0.0
        ).astype(F32)
        r.car[b] = jnp.where(start < first, 1.0, 0.0).astype(F32)
        r.tail[b] = jnp.where(start == last, 1.0, 0.0).astype(F32)
        before_thr.append(through(offsets, lax.rem(s + n - 1, n)))
        after_thr.append(through(offsets, lax.rem(s + 1, n)))
        keep = r.pixel[b : b + 1, :].astype(F32)
        r.pmc[b] = dot_nn(
            jnp.where(diagonal, keep, 0.0).astype(BF), jnp.ones((rows, 128), BF)
        )

    def ag_step(j):
        ag_pass(SMALL, j)
        ag_pass(QKV, j)
        ag_pass(OUT, j)

    crops(0)
    hg_forward(0, 0)
    ag_step(0)
    hg_forward(0, 1)
    for copy in own_copies:
        copy.wait()
    r.smallg[:, ds(s * block, block)] = r.small[...]

    def unit(values):
        mean = jnp.mean(values, axis=1, keepdims=True)
        centered = values - mean
        inverse = lax.rsqrt(jnp.mean(centered * centered, axis=1, keepdims=True) + epsilon)
        return centered * inverse, inverse

    tile = 32

    def unit_one(b):
        def some(i):
            u, _ = unit(r.xg[b, ds(i * tile, tile), :].astype(F32))
            r.gelu_d[ds(b * rows + i * tile, tile), :] = u

        loop(rows // tile, some)

    def norm_one(i):
        rw = ds(i * tile, tile)
        r.normed[rw, :] = (r.gelu_d[rw, :] * gain_one + shift_one).astype(BF)

    for c in (0, 1):
        hg_finish(0, c)
    unit_one(0)
    ag_step(1)
    unit_one(1)
    crops(1)
    ag_step(2)
    ag_send(UP, 0)
    for c in (0, 1):
        hg_forward(1, c)
    ag_wait(SMALL, 3)
    gain_one, gain_two = r.smallg[0:1, :], r.smallg[1:2, :]
    shift_one, shift_two, shift_out = r.smallg[2:3, :], r.smallg[3:4, :], r.smallg[4:5, :]
    loop(tokens // tile, norm_one)
    ag_wait(QKV, 3)
    ag_wait(OUT, 3)

    tm = 128

    def project(i):
        rw = ds(i * tm, tm)
        b = lax.div(i, rows // tm)
        rb = ds(lax.rem(i, rows // tm) * tm, tm)
        left = r.normed[rw, :]
        for kind in (0, 1):
            v = dot_nn(left, r.wq[kind])
            low = jnp.exp(jnp.minimum(v, 0.0))
            f = jnp.where(v > 0.0, v + 1.0, low).astype(BF)
            r.phi_d[kind, rw, :] = low
            if kind == 0:
                r.qf[rw, :] = f
            else:
                r.kf[rw, :] = (f.astype(F32) * wide(r.pmc[b, rb, :])).astype(BF)
        r.vf[rw, :] = dot_nn(left, r.wq[2]).astype(BF)

    loop(tokens // tm, project)

    def fold(ref, parts):
        row = lax.broadcasted_iota(jnp.int32, (16, local), 0)
        sums = jnp.zeros((16, local), F32)
        for b, (matrix, total) in enumerate(parts):
            kept = jnp.where(same_head, matrix, 0.0)
            acc = kept[0:DH]
            for i in range(1, heads):
                acc = acc + kept[i * DH : (i + 1) * DH]
            ref[b * DH : (b + 1) * DH, :] = acc.astype(BF)
            sums = jnp.where(row == b, total, sums)
        ref[batches * DH :, :] = sums.astype(BF)

    def unfold(ref, i, b):
        acc = ref[i, b * DH : (b + 1) * DH, :].astype(F32)
        return jnp.where(same_head, jnp.concatenate([acc] * heads, axis=0), 0.0).astype(BF)

    def unfold_sum(ref, i, b):
        return ref[i, batches * DH :, :].astype(F32)[b : b + 1]

    def state_send(k, ref, dest, step):
        for i in (0, 1):
            to = lax.rem(s + n + step * (i + 1), n)
            remote(ref, dest.at[i], r.st_s.at[k], r.st_r.at[k], to, h).start()

    def state_wait(k, dest):
        landed(dest, r.st_r.at[k])

    def rows_of(b):
        return pl.ds(b * rows, rows)

    def by_head(value):
        return jnp.concatenate(
            [jnp.where(lane_head == hd, value.astype(F32), 0.0).astype(BF) for hd in range(heads)],
            axis=0,
        )

    parts = []
    for b in range(batches):
        k = r.kf[rows_of(b), :].astype(F32) * wide(r.tail[b])
        parts.append(
            (dot_tn(k.astype(BF), r.vf[rows_of(b), :]), jnp.sum(k, axis=0, keepdims=True))
        )
    fold(r.st_send, parts)
    state_send(0, r.st_send, r.st_recv, 1)

    for b in range(batches):
        q, k = r.qf[rows_of(b), :], r.kf[rows_of(b), :]
        acc = jnp.zeros((rows, local), F32)
        for hd in range(heads):
            sc = dot_nt(jnp.where(lane_head == hd, q.astype(F32), 0.0).astype(BF), k) * r.mask[b]
            r.low[b, :, hd * rows : (hd + 1) * rows] = sc.astype(BF)
            acc = acc + jnp.where(lane_head == hd, jnp.sum(sc, axis=1, keepdims=True), 0.0)
        r.denom[rows_of(b), :] = acc
        r.numer[rows_of(b), :] = dot_nn(r.low[b], by_head(r.vf[rows_of(b), :]))

    for c in (0, 1):
        hg_finish(1, c)
    ag_pass(UP, 0)
    ag_send(DOWN, 0)
    state_wait(0, r.st_recv)

    def both(b, value, thr):
        one = value.astype(F32) * wide(r.car[b])
        return jnp.concatenate([one.astype(BF), (one * thr).astype(BF)], axis=1)

    for b in range(batches):
        left = both(b, r.qf[rows_of(b), :], before_thr[b])
        states = jnp.concatenate([unfold(r.st_recv, i, b) for i in (0, 1)], axis=0)
        only = lax.broadcasted_iota(jnp.int32, (16, local), 0)
        sums = jnp.concatenate(
            [
                jnp.where(
                    same_head,
                    dot_tn(
                        jnp.where(
                            only == b, r.st_recv[i, batches * DH :, :].astype(F32), 0.0
                        ).astype(BF),
                        jnp.ones((16, local), BF),
                    ),
                    0.0,
                ).astype(BF)
                for i in (0, 1)
            ],
            axis=0,
        )
        top = r.numer[rows_of(b), :] + dot_nn(left, states)
        bottom = r.denom[rows_of(b), :] + dot_nn(left, sums)
        attn = top / jnp.maximum(bottom, 1.0)
        r.numer[rows_of(b), :] = attn
        r.denom[rows_of(b), :] = bottom
        r.mixed[rows_of(b), :] = attn.astype(BF)

    hr_first(0, 0, pick(r.mixed), product_nt(r.wo))
    hr_first(0, 1, pick(r.mixed), product_nt(r.wo))
    hr_second(0, 0)
    hr_second(0, 1)
    ag_pass(UP, 1)
    mine = h * own

    def x_rows(at_row):
        return r.xg[hi, ds(lo * own + at_row, tile), :].astype(F32)

    def c_rows(at_row):
        return r.cg[hi, ds(lo * own + at_row, tile), :].astype(F32)

    def norm_two(c):
        def some(i):
            at_row = c * part_rows + i * tile
            v = x_rows(at_row) + hr_value(0, c, ds(i * tile, tile))
            r.middle[ds(at_row, tile), :] = v
            u, _ = unit(v)
            r.ntwo[ds(mine + at_row, tile), :] = (u * gain_two + shift_two).astype(BF)

        loop(part_rows // tile, some)

    for c in (0, 1):
        hr_wait(0, c)
        norm_two(c)
        hg_start(2, c)
    ag_pass(DOWN, 0)
    hg_forward(2, 0)
    hg_forward(2, 1)
    ag_pass(UP, 2)
    hg_finish(2, 0)
    hg_finish(2, 1)
    ag_pass(DOWN, 1)
    ag_wait(UP, 3)

    tu = 256

    def up(i):
        rw = ds(lax.div(i, hidden // tn) * tu, tu)
        cols = ds(lax.rem(i, hidden // tn) * tn, tn)
        v = dot_nn(r.ntwo[rw, :], r.wu[:, cols]) + r.smallg[5:6, cols]
        square_of = v * v
        t = jnp.tanh(0.7978845608028654 * (v + 0.044715 * (square_of * v)))
        half = 0.5 * (1.0 + t)
        r.activ[rw, cols] = (v * half).astype(BF)
        r.gelu_d[rw, cols] = half + (0.5 * v) * (1.0 - t * t) * (
            0.7978845608028654 + (3.0 * 0.044715 * 0.7978845608028654) * square_of
        )

    loop((tokens // tu) * (hidden // tn), up)
    near = [ds(at(p + n + i) * block, block) for i in range(1 - hops, hops)]

    def back_near(i):
        cols = ds(i * tn, tn)
        right = jnp.concatenate([r.wd[rw, cols] for rw in near], axis=0)
        for b in range(batches):
            left = jnp.concatenate([r.cg[b, :, rw] for rw in near], axis=1)
            r.g_act[rows_of(b), cols] = dot_nn(left, right)

    rs_round(DOWN, 0)
    ag_pass(DOWN, 2)
    rs_round(DOWN, 1)
    loop(hidden // tn, back_near)
    ag_wait(DOWN, 3)

    far_block = ds(at(p + hops) * block, block)

    def back(i):
        cols = ds(i * tn, tn)
        for b in range(batches):
            rw = rows_of(b)
            g = r.g_act[rw, cols] + dot_nn(r.cg[b, :, far_block], r.wd[far_block, cols])
            r.g_hid[rw, cols] = (g * r.gelu_d[rw, cols]).astype(BF)

    loop(hidden // tn, back)
    rs_round(UP, 0)
    hr_first(2, 0, pick(r.g_hid), product_nt(r.wu))
    hr_first(2, 1, pick(r.g_hid), product_nt(r.wu))
    rs_round(DOWN, 2)
    hr_second(2, 0)
    hr_second(2, 1)

    r.hs_send[...] = jnp.zeros_like(r.hs_send)

    def back_norm(g, u, inverse, gain):
        scaled = g * gain
        centered = scaled - jnp.mean(scaled, axis=1, keepdims=True)
        return inverse * (centered - u * jnp.mean(scaled * u, axis=1, keepdims=True))

    def norm_two_back(c):
        def some(i):
            at_row = c * part_rows + i * tile
            rw = ds(at_row, tile)
            g = hr_value(2, c, ds(i * tile, tile))
            u, inverse = unit(r.middle[rw, :])
            out = c_rows(at_row)
            v = out + back_norm(g, u, inverse, gain_two)
            r.g_mid[rw, :] = v
            r.gatt[ds(mine + at_row, tile), :] = v.astype(BF)
            r.hs_send[1:2, :] += jnp.sum(g * u, axis=0, keepdims=True)
            r.hs_send[3:4, :] += jnp.sum(g, axis=0, keepdims=True)
            r.hs_send[4:5, :] += jnp.sum(out, axis=0, keepdims=True)

        loop(part_rows // tile, some)

    hr_wait(2, 0)
    norm_two_back(0)
    hg_start(3, 0)
    rs_round(UP, 1)
    hr_wait(2, 1)
    norm_two_back(1)
    hg_start(3, 1)
    hr_first(1, 0, pick(r.activ), product_nt(r.wd))
    hr_first(1, 1, pick(r.activ), product_nt(r.wd))
    rs_round(DOWN, 3)
    for c in (0, 1):
        hg_forward(3, c)
    for c in (0, 1):
        hr_second(1, c)
    for c in (0, 1):
        hg_finish(3, c)

    def mixed_back(i):
        rw = ds(i * tm, tm)
        g = dot_nn(r.gatt[rw, :], r.wo[...])
        attn, bottom = r.numer[rw, :], r.denom[rw, :]
        r.g_num[rw, :] = (g / jnp.maximum(bottom, 1.0)).astype(BF)
        prod = g * attn
        lh = lane_head[:tm]
        acc = jnp.zeros((tm, local), F32)
        for hd in range(heads):
            acc = acc + jnp.where(
                lh == hd,
                jnp.sum(jnp.where(lh == hd, prod, 0.0), axis=1, keepdims=True),
                0.0,
            )
        r.g_den[rw, :] = jnp.where(bottom > 1.0, -acc / jnp.maximum(bottom, 1.0), 0.0)

    loop(tokens // tm, mixed_back)

    parts = []
    for b in range(batches):
        q = r.qf[rows_of(b), :].astype(F32) * wide(r.car[b])
        parts.append(
            (
                dot_tn(q.astype(BF), r.g_num[rows_of(b), :]),
                jnp.sum(q * r.g_den[rows_of(b), :], axis=0, keepdims=True),
            )
        )
    fold(r.gs_send, parts)
    state_send(1, r.gs_send, r.gs_recv, -1)
    rs_round(UP, 2)

    def head_lanes(hd, value):
        return jnp.where(lane_head == hd, value.astype(F32), 0.0).astype(BF)

    for b in range(batches):
        rw = rows_of(b)
        gk = jnp.zeros((rows, local), F32)
        gv = jnp.zeros((rows, local), F32)
        gq = jnp.zeros((rows, local), F32)
        for hd in range(heads):
            gn = head_lanes(hd, r.g_num[rw, :])
            g = dot_nt(gn, r.vf[rw, :]) + r.g_den[rw, hd * DH : hd * DH + 1]
            g = (g * r.mask[b]).astype(BF)
            gq = gq + dot_nn(g, head_lanes(hd, r.kf[rw, :]))
            gk = gk + dot_tn(g, head_lanes(hd, r.qf[rw, :]))
            gv = gv + dot_tn(r.low[b, :, hd * rows : (hd + 1) * rows], gn)
        left = both(b, r.g_num[rw, :], before_thr[b])
        states = jnp.concatenate([unfold(r.st_recv, i, b) for i in (0, 1)], axis=1)
        totals = unfold_sum(r.st_recv, 0, b) + before_thr[b] * unfold_sum(r.st_recv, 1, b)
        gq = gq + dot_nt(left, states) + wide(r.car[b]) * r.g_den[rw, :] * totals
        r.gproj[0, rw, :] = (gq * r.phi_d[0, rw, :]).astype(BF)
        r.gk[rw, :] = gk
        r.gv[rw, :] = gv

    rs_round(OUT, 0)
    rs_round(QUERY, 0)
    state_wait(1, r.gs_recv)
    for b in range(batches):
        rw = rows_of(b)
        thr = after_thr[b]
        states = [unfold(r.gs_recv, i, b) for i in (0, 1)]
        totals = unfold_sum(r.gs_recv, 0, b) + thr * unfold_sum(r.gs_recv, 1, b)
        k = r.kf[rw, :].astype(F32) * wide(r.tail[b])
        v = r.vf[rw, :].astype(F32) * wide(r.tail[b])
        k2 = jnp.concatenate([k.astype(BF), (k * thr).astype(BF)], axis=1)
        v2 = jnp.concatenate([v.astype(BF), (v * thr).astype(BF)], axis=1)
        gk = r.gk[rw, :] + dot_nt(v2, jnp.concatenate(states, axis=1)) + wide(r.tail[b]) * totals
        gv = r.gv[rw, :] + dot_nn(k2, jnp.concatenate(states, axis=0))
        r.gproj[1, rw, :] = (gk * wide(r.pmc[b]) * r.phi_d[1, rw, :]).astype(BF)
        r.gproj[2, rw, :] = gv.astype(BF)

    rs_round(QKV, 0)

    def picks(where):
        return [
            jnp.concatenate([r.gproj[kind, rw, :] for rw in where], axis=0) for kind in range(3)
        ]

    def first_term(left, cols):
        v = dot_nt(left[0], r.wq[0, cols, :])
        for kind in (1, 2):
            v = v + dot_nt(left[kind], r.wq[kind, cols, :])
        return v

    hr_first(3, 0, picks, first_term)
    hr_first(3, 1, picks, first_term)
    hr_second(3, 0)
    hr_second(3, 1)
    rs_round(OUT, 1)
    rs_round(QUERY, 1)
    rs_round(QKV, 1)
    rs_round(UP, 3)

    def norm_one_back(c):
        def some(i):
            at_row = c * part_rows + i * tile
            rw = ds(at_row, tile)
            g = hr_value(3, c, ds(i * tile, tile))
            u, inverse = unit(x_rows(at_row))
            r.i_rows[rw, :] = r.g_mid[rw, :] + back_norm(g, u, inverse, gain_one)
            r.hs_send[0:1, :] += jnp.sum(g * u, axis=0, keepdims=True)
            r.hs_send[2:3, :] += jnp.sum(g, axis=0, keepdims=True)

        loop(part_rows // tile, some)

    for c in (0, 1):
        hr_wait(3, c)
        norm_one_back(c)
    turn(1, r.i_rows, r.ing_o)
    rs_round(OUT, 2)
    rs_round(QUERY, 2)
    rs_round(QKV, 2)

    def finish_rows(c):
        def some(i):
            rw = ds(c * part_rows + i * tile, tile)
            r.a_rows[rw, :] = r.middle[rw, :] + hr_value(1, c, ds(i * tile, tile)) + shift_out

        loop(part_rows // tile, some)

    for c in (0, 1):
        hr_wait(1, c)
        finish_rows(c)
    turn(0, r.a_rows, r.act_o)

    r.hs_recv[h] = r.hs_send[...]
    for i in range(1, m):
        remote(
            r.hs_send, r.hs_recv.at[h], r.hs_s.at[0], r.hs_r.at[0], s, lax.rem(h + i, m)
        ).start()
    r.upb[...] = jnp.zeros_like(r.upb)

    def column_sums(i):
        r.upb[...] += jnp.sum(r.g_hid[ds(i * tile, tile), :].astype(F32), axis=0, keepdims=True)

    loop(tokens // tile, column_sums)
    rs_round(OUT, 3)
    rs_round(QUERY, 3)
    rs_final(DOWN)
    rs_round(QKV, 3)
    landed(r.hs_recv.at[pl.ds(0, m - 1)], r.hs_r.at[0])
    acc = r.hs_recv[0]
    for i in range(1, m):
        acc = acc + r.hs_recv[i]
    r.sg[...] = acc
    r.sg[5:6, :] = r.upb[...]
    r.ss_recv[s] = r.sg[:, ds(s * block, block)]
    for i in range(1, n):
        to = lax.rem(s + i, n)
        remote(
            r.sg.at[:, ds(to * block, block)],
            r.ss_recv.at[s],
            r.ss_s.at[0],
            r.ss_r.at[0],
            to,
            h,
        ).start()
    rs_final(UP)
    rs_final(OUT)
    rs_final(QUERY)
    landed(r.ss_recv.at[pl.ds(0, n - 1)], r.ss_r.at[0])
    acc = r.ss_recv[0]
    for i in range(1, n):
        acc = acc + r.ss_recv[i]
    r.gg_o[...] = acc[0:2]
    r.gb_o[...] = acc[2:5]
    r.gup_o[...] = acc[5:6]
    turn_wait(0, r.a_rows)
    turn_wait(1, r.i_rows)

    far = pl.ds(0, (n - 1) * block)
    for w in range(5):
        views = (r.wq.at[:, far, :], r.wo.at[far], r.wu.at[far], r.wd.at[far], r.smallg.at[:, far])
        drained(views[w], r.ag_s.at[w])
    others = pl.ds(0, (m - 1) * local)
    rest = pl.ds(0, (m - 1) * own)
    for k in range(4):
        view = (r.xg, r.cg)[k].at[:, :, others] if k < 2 else (r.ntwo, r.gatt)[k - 2].at[rest]
        drained(view, r.hg_s.at[k])
        drained(r.h_s1.at[k], r.hr_s.at[k, 0])
        drained(r.h_s2.at[k], r.hr_s.at[k, 1])
    for k, dest in enumerate((r.st_recv, r.gs_recv)):
        drained(dest, r.st_s.at[k])
    drained(r.a_rows.at[:, others], r.aa_s.at[0])
    drained(r.i_rows.at[:, others], r.aa_s.at[1])
    drained(r.hs_recv.at[pl.ds(0, m - 1)], r.hs_s.at[0])
    drained(r.ss_recv.at[pl.ds(0, n - 1)], r.ss_s.at[0])
    rs_final(QKV)
    for w in range(5):
        drained(rs_send[w].at[pl.ds(0, n - 1)], r.rs_s.at[w])
    for copy in local_copies:
        copy.wait()


def settle(*refs):
    count = len(refs) // 2
    copies = [
        pltpu.make_async_copy(refs[i], refs[count + i], refs[-1].at[i]) for i in range(count)
    ]
    for copy in copies:
        copy.start()
    for copy in copies:
        copy.wait()


def whole_layer(n, m):
    def on_each(
        tokens, cotangent, w_qkv, w_out_t, w_up, w_down_t, gains, biases, up_bias, lengths, pixel_mask
    ):
        batches, rows, local = tokens.shape
        width = w_qkv.shape[0] * n
        hidden = w_up.shape[1]
        block = width // n
        vm, sems = layout(n, m, batches, rows, width, local, hidden)
        ins = ["tok", "cot", "w_qkv", "w_out", "w_up", "w_down", "gains", "biases", "up_bias", "lengths", "pixel"]
        outs = ["act_o", "ing_o", "gq_o", "go_o", "gu_o", "gd_o", "gg_o", "gb_o", "gup_o"]
        anywhere = pl.BlockSpec(memory_space=pl.ANY)
        in_vmem = pl.BlockSpec(memory_space=pltpu.VMEM)
        in_smem = pl.BlockSpec(memory_space=pltpu.SMEM)

        result = pl.pallas_call(
            functools.partial(body, n, m, ins + outs + list(vm) + list(sems)),
            name="layer",
            out_shape=(
                pltpu.VMEM((batches, rows, local), F32),
                pltpu.VMEM((batches, rows, local), F32),
                pltpu.VMEM((3, block, local), F32),
                pltpu.VMEM((block, local), F32),
                pltpu.VMEM((block, hidden), F32),
                pltpu.VMEM((block, hidden), F32),
                pltpu.VMEM((2, block), F32),
                pltpu.VMEM((3, block), F32),
                pltpu.VMEM((1, block), F32),
            ),
            in_specs=[anywhere] * 6 + [in_vmem] * 3 + [in_smem, in_vmem],
            out_specs=[in_vmem] * 9,
            scratch_shapes=[pltpu.VMEM(shape, kind) for shape, kind in vm.values()]
            + [pltpu.SemaphoreType.DMA(shape) for shape in sems.values()],
            compiler_params=pltpu.CompilerParams(
                collective_id=0, has_side_effects=True, vmem_limit_bytes=60_000_000
            ),
        )(
            tokens,
            cotangent,
            jnp.transpose(w_qkv, (1, 0, 2)),
            w_out_t,
            w_up,
            w_down_t,
            gains,
            biases,
            up_bias,
            lengths,
            pixel_mask,
        )
        result = pl.pallas_call(
            settle,
            name="settle",
            out_shape=[jax.ShapeDtypeStruct(a.shape, a.dtype) for a in result],
            in_specs=[in_vmem] * len(result),
            out_specs=[anywhere] * len(result),
            scratch_shapes=[pltpu.SemaphoreType.DMA((len(result),))],
        )(*[pltpu.with_memory_space_constraint(a, pltpu.VMEM) for a in result])
        return (*result[:2], jnp.transpose(result[2], (1, 0, 2)), *result[3:])

    return on_each


def solution(mesh):
    in_specs = (
        P(None, "seq", "head"),
        P(None, "seq", "head"),
        P("seq", None, "head"),
        P("seq", "head"),
        P("seq", "head"),
        P("seq", "head"),
        P(None, "seq"),
        P(None, "seq"),
        P("head", "seq"),
        P(),
        P(None, "seq"),
    )
    out_specs = (
        P(None, "seq", "head"),
        P(None, "seq", "head"),
        P("seq", None, "head"),
        P("seq", "head"),
        P("seq", "head"),
        P("seq", "head"),
        P(None, "seq"),
        P(None, "seq"),
        P("head", "seq"),
    )
    n, m = mesh.shape["seq"], mesh.shape["head"]
    fits = (n, m) == (8, 4)
    return jax.shard_map(
        whole_layer(n, m) if fits else on_device, mesh=mesh, in_specs=in_specs, out_specs=out_specs, check_vma=False
    )
```

```python
import functools

import jax
import jax.numpy as jnp
from jax import lax
from jax.experimental import pallas as pl
from jax.experimental.pallas import tpu as pltpu
from jax.sharding import PartitionSpec as P

DH = 64


highest = lax.Precision.HIGHEST
epsilon = 1e-05


def entering(array, axis, join, neutral):
    place = lax.axis_index(axis)
    gathered = jax.tree.map(
        lambda a, kind: lax.all_gather(a.astype(kind), axis),
        array,
        (jnp.bfloat16, jnp.bfloat16, jnp.bfloat16),
    )
    state = jax.tree.map(lambda a, e: jnp.zeros_like(a) + jnp.asarray(e, a.dtype), array, neutral)

    def one(hop, state):
        return join(
            state,
            jax.tree.map(
                lambda a, own: lax.dynamic_index_in_dim(a, hop, 0, False).astype(own.dtype),
                gathered,
                array,
            ),
        )

    return lax.fori_loop(0, place, one, state)


def entering_2(array, axis, combine, identity):
    length, place = (lax.axis_size(axis), lax.axis_index(axis))
    everything = jax.tree.map(
        lambda part, kind: lax.all_gather(part.astype(kind), axis),
        array,
        jax.tree.map(lambda a: jnp.bfloat16 if a.dtype == jnp.float32 else a.dtype, array),
    )
    start = jax.tree.map(
        lambda part, zero: jnp.broadcast_to(jnp.asarray(zero, part.dtype), part.shape),
        array,
        identity,
    )

    def hop(k, before):
        at = length - 1 - k
        reached = at > place
        new = combine(
            before, jax.tree.map(lambda part, own: part[at].astype(own.dtype), everything, array)
        )
        return jax.tree.map(lambda a, b: jnp.where(reached, a, b), new, before)

    return lax.fori_loop(0, length, hop, start)


def normalize(values, gain_vec, shift_vec):
    mean_val = jnp.mean(values, axis=-1, keepdims=True)
    centered = values - mean_val
    inverse = lax.rsqrt(jnp.mean(centered * centered, axis=-1, keepdims=True) + epsilon)
    unit_val = centered * inverse
    return (unit_val * gain_vec + shift_vec, unit_val, inverse)


def norm_back(grad_in, unit_val, inverse, gain_vec):
    scaled = grad_in * gain_vec
    centered = scaled - jnp.mean(scaled, axis=-1, keepdims=True)
    return inverse * (centered - unit_val * jnp.mean(scaled * unit_val, axis=-1, keepdims=True))


def features(values):
    return jax.nn.elu(values) + 1.0


def finish(numerator, denominator):
    return numerator / jnp.maximum(denominator, 1.0)[:, :, None]


def compose(earlier, later):
    return (
        later[0] + later[2] * earlier[0],
        later[1] + later[2] * earlier[1],
        later[2] * earlier[2],
    )


def item_numbers(lengths_row, first_place, number):
    offsets = jnp.cumsum(lengths_row) - lengths_row
    places = first_place + jnp.arange(number, dtype=jnp.int32)
    return jnp.sum((offsets[None, :] <= places[:, None]).astype(jnp.int32), axis=1) - 1


def on_device(
    tokens, cotangent, w_qkv, w_out_t, w_up, w_down_t, gains, biases, up_bias, lengths, pixel_mask
):
    batches, local_rows, columns = tokens.shape
    local_width = w_qkv.shape[2]
    heads_here = local_width // DH
    seq_index = lax.axis_index("seq")
    head_index = lax.axis_index("head")
    first_token = seq_index * local_rows
    position = jnp.arange(local_rows, dtype=jnp.int32)
    before = position[:, None] >= position[None, :]

    def own_columns(matrix):
        return lax.dynamic_slice_in_dim(matrix, head_index * columns, columns, 1)

    results = []
    input_grads = []
    shard_sums = None
    for batch_index in range(batches):
        full_qkv, full_out, full_up, full_down, full_gains, full_biases, full_upb = (
            lax.all_gather(w_qkv, "seq", axis=0, tiled=True),
            lax.all_gather(w_out_t, "seq", axis=0, tiled=True),
            lax.all_gather(w_up, "seq", axis=0, tiled=True),
            lax.all_gather(w_down_t, "seq", axis=0, tiled=True),
            lax.all_gather(gains, "seq", axis=1, tiled=True),
            lax.all_gather(biases, "seq", axis=1, tiled=True),
            lax.all_gather(up_bias, "seq", axis=1, tiled=True),
        )
        input_rows, grad_rows16 = (
            lax.all_gather(tokens[batch_index], "head", axis=1, tiled=True),
            lax.all_gather(cotangent[batch_index], "head", axis=1, tiled=True),
        )
        gains32 = full_gains.astype(jnp.float32)
        biases32 = full_biases.astype(jnp.float32)
        upb32 = full_upb.astype(jnp.float32).reshape(-1)
        inputs32 = input_rows.astype(jnp.float32)
        place_items = item_numbers(lengths[batch_index], first_token - 1, local_rows + 1)
        item_of = place_items[1:]
        carried = (item_of == place_items[0]).astype(jnp.float32)
        tail_mask = (item_of == item_of[local_rows - 1]).astype(jnp.float32)
        through = carried[local_rows - 1]
        same_item = ((item_of[:, None] == item_of[None, :]) & before).astype(jnp.float32)
        keep_half = pixel_mask[batch_index].astype(jnp.bfloat16)
        keep32 = pixel_mask[batch_index].astype(jnp.float32)
        lifted, unit_one, inverse_one = normalize(inputs32, gains32[0], biases32[0])
        normed = lifted.astype(jnp.bfloat16)
        projected = jnp.einsum("td,dsf->tsf", normed, full_qkv, preferred_element_type=jnp.float32)
        query_feat = (
            features(projected[:, 0]).astype(jnp.bfloat16).reshape(local_rows, heads_here, DH)
        )
        key_feat = (features(projected[:, 1]).astype(jnp.bfloat16) * keep_half[:, None]).reshape(
            local_rows, heads_here, DH
        )
        value_feat = projected[:, 2].astype(jnp.bfloat16).reshape(local_rows, heads_here, DH)
        tail_key = key_feat * tail_mask.astype(jnp.bfloat16)[:, None, None]
        state_loc = jnp.einsum(
            "jhd,jhe->hde", tail_key, value_feat, preferred_element_type=jnp.float32
        )
        total_loc = jnp.sum(tail_key.astype(jnp.float32), axis=0)
        identity = (jnp.zeros_like(state_loc), jnp.zeros_like(total_loc), jnp.ones((), jnp.float32))
        state_in, total_in, passed = entering(
            (state_loc, total_loc, through), "seq", compose, identity
        )
        query32 = query_feat.astype(jnp.float32)
        scores = (
            jnp.einsum("thd,jhd->htj", query_feat, key_feat, preferred_element_type=jnp.float32)
            * same_item[None]
        )
        scores_low = scores.astype(jnp.bfloat16)
        numerator = jnp.einsum(
            "htj,jhe->the", scores_low, value_feat, preferred_element_type=jnp.float32
        ) + carried[:, None, None] * jnp.einsum(
            "thd,hde->the", query32, state_in, precision=highest
        )
        denominator = jnp.sum(scores, axis=2).T + carried[:, None] * jnp.einsum(
            "thd,hd->th", query32, total_in, precision=highest
        )
        output, finish_back = jax.vjp(finish, numerator, denominator)
        mixed_out = output.reshape(local_rows, local_width).astype(jnp.bfloat16)
        attended = lax.psum(
            jnp.einsum("tf,df->td", mixed_out, full_out, preferred_element_type=jnp.float32).astype(
                jnp.bfloat16
            ),
            "head",
        ).astype(jnp.float32)
        middle = inputs32 + attended
        lifted_two, unit_two, inverse_two = normalize(middle, gains32[1], biases32[1])
        normed_two = lifted_two.astype(jnp.bfloat16)
        hidden = jnp.dot(normed_two, full_up, preferred_element_type=jnp.float32) + upb32
        activated32, gelu_back = jax.vjp(jax.nn.gelu, hidden)
        activated = activated32.astype(jnp.bfloat16)
        branch = lax.psum_scatter(
            jnp.einsum(
                "tf,df->td", activated, full_down, preferred_element_type=jnp.float32
            ).astype(jnp.bfloat16),
            "head",
            scatter_dimension=1,
            tiled=True,
        ).astype(jnp.float32)
        results.append(own_columns(middle) + branch + own_columns(biases32[2][None]))
        grad_out = grad_rows16.astype(jnp.float32)
        grad_down = jnp.einsum(
            "td,tf->df", grad_rows16, activated, preferred_element_type=jnp.float32
        )
        grad_act = jnp.einsum(
            "td,df->tf", grad_rows16, full_down, preferred_element_type=jnp.float32
        )
        grad_hidden = gelu_back(grad_act)[0].astype(jnp.bfloat16)
        grad_up = jnp.einsum(
            "td,tf->df", normed_two, grad_hidden, preferred_element_type=jnp.float32
        )
        grad_upb = jnp.sum(grad_hidden.astype(jnp.float32), axis=0).reshape(full_upb.shape)
        grad_two = lax.psum(
            jnp.einsum(
                "tf,df->td", grad_hidden, full_up, preferred_element_type=jnp.float32
            ).astype(jnp.bfloat16),
            "head",
        ).astype(jnp.float32)
        grad_middle = grad_out + norm_back(grad_two, unit_two, inverse_two, gains32[1])
        grad_attended = grad_middle.astype(jnp.bfloat16)
        grad_out_t = jnp.einsum(
            "td,tf->df", grad_attended, mixed_out, preferred_element_type=jnp.float32
        )
        grad_mixed = jnp.einsum(
            "td,df->tf", grad_attended, full_out, preferred_element_type=jnp.float32
        ).reshape(local_rows, heads_here, DH)
        grad_numer32, grad_denom = finish_back(grad_mixed)
        grad_numer = grad_numer32.astype(jnp.bfloat16)
        grad_numer_wide = grad_numer.astype(jnp.float32)
        grad_scores = (
            (
                jnp.einsum(
                    "the,jhe->htj", grad_numer, value_feat, preferred_element_type=jnp.float32
                )
                + grad_denom.T[:, :, None]
            )
            * same_item[None]
        ).astype(jnp.bfloat16)
        carried_query = query32 * carried[:, None, None]
        grad_query = jnp.einsum(
            "htj,jhd->thd", grad_scores, key_feat, preferred_element_type=jnp.float32
        ) + carried[:, None, None] * (
            jnp.einsum("hde,the->thd", state_in, grad_numer_wide, precision=highest)
            + grad_denom[:, :, None] * total_in[None]
        )
        grad_key = jnp.einsum(
            "htj,thd->jhd", grad_scores, query_feat, preferred_element_type=jnp.float32
        )
        grad_value = jnp.einsum(
            "htj,the->jhe", scores_low, grad_numer, preferred_element_type=jnp.float32
        )
        grad_state_in = jnp.einsum(
            "thd,the->hde", carried_query, grad_numer_wide, precision=highest
        )
        grad_total_in = jnp.einsum("thd,th->hd", carried_query, grad_denom, precision=highest)
        grad_state_loc, grad_total_loc, passed_back = entering_2(
            (grad_state_in, grad_total_in, through), "seq", compose, identity
        )
        tail_three = tail_mask[:, None, None]
        value_wide = value_feat.astype(jnp.float32)
        key_wide = key_feat.astype(jnp.float32)
        grad_key = grad_key + tail_three * (
            jnp.einsum("hde,jhe->jhd", grad_state_loc, value_wide, precision=highest)
            + grad_total_loc[None]
        )
        grad_value = grad_value + tail_three * jnp.einsum(
            "jhd,hde->jhe", key_wide, grad_state_loc, precision=highest
        )
        ignored, feature_back = jax.vjp(features, projected[:, :2])
        grad_features = jnp.stack(
            [
                grad_query.reshape(local_rows, local_width),
                grad_key.reshape(local_rows, local_width) * keep32[:, None],
            ],
            axis=1,
        )
        grad_pair = feature_back(grad_features)[0]
        grad_projected = jnp.concatenate(
            [grad_pair, grad_value.reshape(local_rows, 1, local_width)], axis=1
        ).astype(jnp.bfloat16)
        grad_qkv = jnp.einsum(
            "td,tsf->dsf", normed, grad_projected, preferred_element_type=jnp.float32
        )
        grad_one = lax.psum(
            jnp.einsum(
                "tsf,dsf->td", grad_projected, full_qkv, preferred_element_type=jnp.float32
            ).astype(jnp.bfloat16),
            "head",
        ).astype(jnp.float32)
        grad_inputs = grad_middle + norm_back(grad_one, unit_one, inverse_one, gains32[0])
        input_grads.append(own_columns(grad_inputs))
        grad_gains = jnp.stack(
            [jnp.sum(grad_one * unit_one, axis=0), jnp.sum(grad_two * unit_two, axis=0)]
        )
        grad_biases = jnp.stack(
            [jnp.sum(grad_one, axis=0), jnp.sum(grad_two, axis=0), jnp.sum(grad_out, axis=0)]
        )
        pieces = (
            lax.psum_scatter(grad_qkv, "seq", scatter_dimension=0, tiled=True),
            lax.psum_scatter(grad_out_t, "seq", scatter_dimension=0, tiled=True),
            lax.psum_scatter(grad_up, "seq", scatter_dimension=0, tiled=True),
            lax.psum_scatter(grad_down, "seq", scatter_dimension=0, tiled=True),
            lax.psum_scatter(grad_gains, "seq", scatter_dimension=1, tiled=True),
            lax.psum_scatter(grad_biases, "seq", scatter_dimension=1, tiled=True),
            lax.psum_scatter(grad_upb, "seq", scatter_dimension=1, tiled=True),
        )
        shard_sums = pieces if shard_sums is None else jax.tree.map(jnp.add, shard_sums, pieces)
    return (
        jnp.stack(results),
        jnp.stack(input_grads),
        shard_sums[0],
        shard_sums[1],
        shard_sums[2],
        shard_sums[3],
        shard_sums[4],
        shard_sums[5],
        shard_sums[6],
    )


MESH = pl.DeviceIdType.MESH
BF = jnp.bfloat16
F32 = jnp.float32
QKV, OUT, UP, DOWN, SMALL = range(5)
QUERY = 4


def dot_nn(a, b):
    return lax.dot_general(a, b, (((1,), (0,)), ((), ())), preferred_element_type=F32)


def dot_nt(a, b):
    return lax.dot_general(a, b, (((1,), (1,)), ((), ())), preferred_element_type=F32)


def dot_tn(a, b):
    return lax.dot_general(a, b, (((0,), (0,)), ((), ())), preferred_element_type=F32)


def ds(start, size):
    return pl.ds(pl.multiple_of(start, size), size)


def loop(count, body):
    def step(i, carry):
        body(i)
        return carry

    lax.fori_loop(0, count, step, 0)


def layout(n, m, batches, rows, width, local, hidden):
    tokens = batches * rows
    block = width // n
    own = tokens // m
    hops = n // 2
    heads = local // DH
    vm = {
        "xg": ((batches, rows, width), BF),
        "cg": ((batches, rows, width), BF),
        "wq": ((3, width, local), BF),
        "wo": ((width, local), BF),
        "wu": ((width, hidden), BF),
        "wd": ((width, hidden), BF),
        "small": ((8, block), F32),
        "smallg": ((8, width), F32),
        "normed": ((tokens, width), BF),
        "phi_d": ((2, tokens, local), F32),
        "qf": ((tokens, local), BF),
        "kf": ((tokens, local), BF),
        "vf": ((tokens, local), BF),
        "mask": ((batches, rows, rows), F32),
        "car": ((batches, rows, 128), F32),
        "tail": ((batches, rows, 128), F32),
        "pmc": ((batches, rows, 128), F32),
        "low": ((batches, rows, heads * rows), BF),
        "numer": ((tokens, local), F32),
        "denom": ((tokens, local), F32),
        "mixed": ((tokens, local), BF),
        "st_send": ((batches * DH + 16, local), BF),
        "st_recv": ((2, batches * DH + 16, local), BF),
        "gs_send": ((batches * DH + 16, local), BF),
        "gs_recv": ((2, batches * DH + 16, local), BF),
        "middle": ((own, width), F32),
        "ntwo": ((tokens, width), BF),
        "gelu_d": ((tokens, hidden), F32),
        "activ": ((tokens, hidden), BF),
        "g_hid": ((tokens, hidden), BF),
        "branch": ((own, width), F32),
        "total": ((own, width), F32),
        "g_mid": ((own, width), F32),
        "gatt": ((tokens, width), BF),
        "g_attn": ((tokens, local), F32),
        "g_num": ((tokens, local), BF),
        "g_den": ((tokens, local), F32),
        "gq": ((tokens, local), F32),
        "gk": ((tokens, local), F32),
        "gv": ((tokens, local), F32),
        "gproj": ((3, tokens, local), BF),
        "h_s1": ((4, 2, 2, own // 2, width), BF),
        "h_r1": ((4, 2, 2, own // 2, width), BF),
        "h_acc": ((4, 2, 2, own // 2, width), F32),
        "h_s2": ((4, 2, own // 2, width), BF),
        "h_r2": ((4, 2, own // 2, width), BF),
        "rq_s": ((n, 2, block, local), BF),
        "rq_r": ((n, 2, block, local), BF),
        "rx_s": ((n, block, local), BF),
        "rx_r": ((n, block, local), BF),
        "ro_s": ((n, block, local), BF),
        "ro_r": ((n, block, local), BF),
        "ru_s": ((n, block, hidden), BF),
        "ru_r": ((n, block, hidden), BF),
        "rd_s": ((n, block, hidden), BF),
        "rd_r": ((n, block, hidden), BF),
        "pq": ((2, 2, block, local), F32),
        "po": ((2, block, local), F32),
        "pu": ((2, block, hidden), F32),
        "pd": ((2, block, hidden), F32),
        "px": ((2, block, local), F32),
        "g_act": ((tokens, hidden), F32),
        "hs_recv": ((m, 8, width), F32),
        "hs_send": ((8, width), F32),
        "upb": ((1, hidden), F32),
        "sg": ((8, width), F32),
        "ss_recv": ((n, 8, block), F32),
        "a_rows": ((own, width), F32),
        "i_rows": ((own, width), F32),
    }
    sems = {
        "ag_s": (5,),
        "ag_r": (5, 2, hops),
        "rs_s": (5,),
        "hg_s": (4,),
        "hg_r": (2, 2, 3),
        "hr_s": (4, 2),
        "hr_r": (2, 2, 2),
        "st_s": (2,),
        "st_r": (2,),
        "aa_s": (2,),
        "aa_r": (2,),
        "hs_s": (1,),
        "hs_r": (1,),
        "ss_s": (1,),
        "ss_r": (1,),
        "lc": (8,),
    }
    return vm, sems


class Refs:
    pass


def body(n, m, names, *refs):
    r = Refs()
    for name, ref in zip(names, refs):
        setattr(r, name, ref)
    batches, rows, width = r.xg.shape
    tokens = batches * rows
    own = tokens // m
    block = width // n
    local = r.wo.shape[1]
    hidden = r.wu.shape[1]
    heads = local // DH
    hops = n // 2
    s = lax.axis_index("seq")
    h = lax.axis_index("head")
    odd = lax.rem(s, 2)
    p = (1 - odd) * lax.div(s, 2) + odd * (n - 1 - lax.div(s, 2))
    lo, hi = lax.rem(h, 2), lax.div(h, 2)
    pair = h + 1 - 2 * lo
    cross = lax.rem(h + 2, m)

    def at(place):
        place = lax.rem(place + 2 * n, n)
        far = lax.div(place, hops)
        return (1 - far) * 2 * place + far * (2 * (n - 1 - place) + 1)

    ring = (at(p + 1), at(p - 1))
    sign = (1, -1)

    def remote(src, dst, send, recv, seq, head):
        return pltpu.make_async_remote_copy(
            src_ref=src,
            dst_ref=dst,
            send_sem=send,
            recv_sem=recv,
            device_id=(seq, head),
            device_id_type=MESH,
        )

    def drained(view, sem):
        remote(view, view, sem, sem, ring[0], h).wait_send()

    def landed(view, sem):
        remote(view, view, sem, sem, ring[0], h).wait_recv()

    r.small[...] = jnp.zeros_like(r.small)
    r.small[0:2, :] = r.gains[...].astype(F32)
    r.small[2:5, :] = r.biases[...].astype(F32)
    r.small[5:6, :] = r.up_bias[...].astype(F32)

    barrier = pltpu.get_barrier_semaphore()
    for peer in ((ring[0], h), (ring[1], h), (s, pair), (s, cross)):
        pl.semaphore_signal(barrier, inc=1, device_id=peer, device_id_type=MESH)
    pl.semaphore_wait(barrier, 4)

    shards = (r.w_qkv, r.w_out, r.w_up, r.w_down, r.small)
    gathered = (r.wq, r.wo, r.wu, r.wd, r.smallg)

    def part_of(w, d, j):
        wide_part = r.wq.shape[2] if w == QKV else shards[w].shape[1]
        if j < hops - 1 or w == SMALL:
            return pl.ds(0, wide_part)
        return pl.ds(d * (wide_part // 2), wide_part // 2)

    def ag_shard(w, d, j):
        cols = part_of(w, d, j)
        if w == SMALL:
            return r.small
        return shards[w].at[:, :, cols] if w == QKV else shards[w].at[:, cols]

    def ag_full(w, owner, d, j):
        cols = part_of(w, d, j)
        if w == SMALL:
            return r.smallg.at[:, ds(owner * block, block)]
        if w == QKV:
            return r.wq.at[:, ds(owner * block, block), cols]
        return gathered[w].at[ds(owner * block, block), cols]

    def ways(w, j):
        return (0,) if w == SMALL and j == hops - 1 else (0, 1)

    def ag_send(w, j):
        for d in ways(w, j):
            owner = at(p - sign[d] * j)
            src = ag_shard(w, d, j) if j == 0 else ag_full(w, owner, d, j)
            remote(
                src, ag_full(w, owner, d, j), r.ag_s.at[w], r.ag_r.at[w, d, j], ring[d], h
            ).start()

    def ag_wait(w, j):
        for d in ways(w, j):
            landed(ag_full(w, at(p - sign[d] * (j + 1)), d, j), r.ag_r.at[w, d, j])

    def ag_pass(w, j):
        ag_wait(w, j)
        ag_send(w, j + 1)

    part_rows = own // 2

    def hg_view(k, c, who):
        if k < 2:
            return (r.xg, r.cg)[k].at[c, :, ds(who * local, local)]
        return (r.ntwo, r.gatt)[k - 2].at[ds(who * own + c * part_rows, part_rows), :]

    def hg_copy(k, c, i, src, who, to):
        return remote(src, hg_view(k, c, who), r.hg_s.at[k], r.hg_r.at[k % 2, c, i], s, to)

    def hg_start(k, c):
        src = (r.tok, r.cot)[k].at[c] if k < 2 else hg_view(k, c, h)
        hg_copy(k, c, 1, src, h, cross).start()
        hg_copy(k, c, 0, src, h, pair).start()

    def hg_forward(k, c):
        view = hg_view(k, c, cross)
        hg_copy(k, c, 1, view, cross, cross).wait_recv()
        hg_copy(k, c, 2, view, cross, pair).start()

    def hg_finish(k, c):
        view = hg_view(k, c, pair)
        hg_copy(k, c, 0, view, pair, pair).wait_recv()
        across = lax.rem(pair + 2, m)
        view = hg_view(k, c, across)
        hg_copy(k, c, 2, view, across, pair).wait_recv()

    tn = 256

    def hr_first(k, c, left, product):
        blocks = [2 * i + 1 - lo for i in (0, 1)] + [2 * i + lo for i in (0, 1)]
        where = [ds(who * own + c * part_rows, part_rows) for who in blocks]

        def some(i):
            cols = ds(i * tn, tn)
            v = product(left(where), cols)
            for q in (0, 1):
                r.h_s1[k, c, q, :, cols] = v[q * part_rows : (q + 1) * part_rows].astype(BF)
                r.h_acc[k, c, q, :, cols] = v[(q + 2) * part_rows : (q + 3) * part_rows]

        loop(width // tn, some)
        hr_copy(k, c, 0).start()

    def hr_copy(k, c, stage):
        if stage == 0:
            src, dst, to = r.h_s1.at[k, c], r.h_r1.at[k, c], pair
        else:
            src, dst, to = r.h_s2.at[k, c], r.h_r2.at[k, c], cross
        return remote(src, dst, r.hr_s.at[k, stage], r.hr_r.at[k // 2, c, stage], s, to)

    def hr_second(k, c):
        hr_copy(k, c, 0).wait_recv()

        def away(i):
            rw = ds(i * 32, 32)
            r.h_s2[k, c, rw, :] = (
                r.h_acc[k, c, 1 - hi, rw, :] + r.h_r1[k, c, 1 - hi, rw, :].astype(F32)
            ).astype(BF)

        loop(part_rows // 32, away)
        hr_copy(k, c, 1).start()

    def hr_wait(k, c):
        hr_copy(k, c, 1).wait_recv()

    def hr_value(k, c, rw):
        return (
            r.h_acc[k, c, hi, rw, :]
            + r.h_r1[k, c, hi, rw, :].astype(F32)
            + r.h_r2[k, c, rw, :].astype(F32)
        )

    def pick(ref):
        return lambda where: jnp.concatenate([ref[rw, :] for rw in where], axis=0)

    def product_nt(right):
        return lambda left, cols: dot_nt(left, right[cols, :])

    def rs_term(w, owner, piece):
        cols = ds(owner * block, block)
        if w == DOWN:
            left = r.cg[:, :, cols].reshape(tokens, block)
            half = hidden // 2
            return [dot_tn(left, r.activ[:, pl.ds(piece * half, half)])]
        if w == UP:
            half = hidden // 2
            return [dot_tn(r.ntwo[:, cols], r.g_hid[:, pl.ds(piece * half, half)])]
        half = local // 2
        if w == OUT:
            return [dot_tn(r.gatt[:, cols], r.mixed[:, pl.ds(piece * half, half)])]
        left = r.normed[:, cols]
        kinds = (0,) if w == QUERY else (1, 2)
        return [dot_tn(left, r.gproj[i, :, pl.ds(piece * half, half)]) for i in kinds]

    rs_send = (r.rq_s, r.ro_s, r.ru_s, r.rd_s, r.rx_s)
    rs_recv = (r.rq_r, r.ro_r, r.ru_r, r.rd_r, r.rx_r)

    def rs_half(w, piece):
        half = rs_send[w].shape[-1] // 2
        return pl.ds(piece * half, half)

    def rs_view(ref, w, d, step):
        if step > 0:
            return ref.at[d * hops + step]
        if w == QKV:
            return ref.at[d * hops, :, :, rs_half(w, d)]
        return ref.at[d * hops, :, rs_half(w, d)]

    def rs_arrived(w, d, step):
        landed(rs_view(rs_recv[w], w, d, step), r.ag_r.at[w, d, step])

    ahead = (r.pq, r.po, r.pu, r.pd, r.px)

    def rs_prepare(w, step):
        for d in (0, 1) if step < hops else (0,):
            owner = at(p + sign[d] * (hops - step)) if step < hops else s
            for piece in (0, 1) if step > 0 else (d,):
                cols = rs_half(w, piece)
                for i, v in enumerate(rs_term(w, owner, piece)):
                    lead = (i,) if w == QKV else ()
                    ahead[w][(d, *lead, slice(None), cols)] = v

    def rs_round(w, step):
        if step == 0:
            rs_prepare(w, 0)
        for d in (0, 1):
            slot = d * hops + step
            if step > 0:
                rs_arrived(w, d, step - 1)
            for piece in (0, 1) if step > 0 else (d,):
                cols = rs_half(w, piece)
                for i in range(2 if w == QKV else 1):
                    lead = (i,) if w == QKV else ()
                    v = ahead[w][(d, *lead, slice(None), cols)]
                    if step > 1 or (step == 1 and piece == d):
                        v = v + rs_recv[w][(slot - 1, *lead, slice(None), cols)].astype(F32)
                    rs_send[w][(slot, *lead, slice(None), cols)] = v.astype(BF)
            remote(
                rs_view(rs_send[w], w, d, step),
                rs_view(rs_recv[w], w, d, step),
                r.rs_s.at[w],
                r.ag_r.at[w, d, step],
                ring[d],
                h,
            ).start()
        rs_prepare(w, step + 1)

    finals = (r.gq_o.at[pl.ds(1, 2)], r.go_o, r.gu_o, r.gd_o, r.gq_o.at[0])
    local_copies = []

    def rs_final(w):
        for d in (0, 1):
            rs_arrived(w, d, hops - 1)
        for piece in (0, 1):
            cols = rs_half(w, piece)
            for i in range(2 if w == QKV else 1):
                lead = (i,) if w == QKV else ()
                v = ahead[w][(0, *lead, slice(None), cols)]
                for d in (0, 1):
                    v = v + rs_recv[w][(d * hops + hops - 1, *lead, slice(None), cols)].astype(F32)
                finals[w][(*lead, slice(None), cols)] = v

    def turn(k, src, dst):
        where = (hi, ds(lo * own, own))
        for i in range(1, m):
            to = lax.rem(h + i, m)
            remote(
                src.at[:, ds(to * local, local)],
                dst.at[where[0], where[1], :],
                r.aa_s.at[k],
                r.aa_r.at[k],
                s,
                to,
            ).start()
        copy = pltpu.make_async_copy(
            src.at[:, ds(h * local, local)], dst.at[where[0], where[1], :], r.lc.at[k]
        )
        copy.start()
        local_copies.append(copy)

    def turn_wait(k, src):
        landed(src.at[:, pl.ds(0, (m - 1) * local)], r.aa_r.at[k])

    ag_send(SMALL, 0)
    ag_send(QKV, 0)
    ag_send(OUT, 0)
    hg_start(0, 0)
    hg_start(0, 1)
    own_copies = [
        pltpu.make_async_copy(r.w_qkv, r.wq.at[:, ds(s * block, block), :], r.lc.at[4]),
        pltpu.make_async_copy(r.w_out, r.wo.at[ds(s * block, block), :], r.lc.at[5]),
        pltpu.make_async_copy(r.w_up, r.wu.at[ds(s * block, block), :], r.lc.at[6]),
        pltpu.make_async_copy(r.w_down, r.wd.at[ds(s * block, block), :], r.lc.at[7]),
        pltpu.make_async_copy(r.tok, r.xg.at[:, :, ds(h * local, local)], r.lc.at[2]),
        pltpu.make_async_copy(r.cot, r.cg.at[:, :, ds(h * local, local)], r.lc.at[3]),
    ]
    for copy in own_copies:
        copy.start()
    hg_start(1, 0)
    hg_start(1, 1)

    first = s * rows
    row_at = lax.broadcasted_iota(jnp.int32, (rows, 128), 0)
    lane_at = lax.broadcasted_iota(jnp.int32, (rows, rows), 1)
    square = lax.broadcasted_iota(jnp.int32, (local, local), 0)
    square_lane = lax.broadcasted_iota(jnp.int32, (local, local), 1)
    same_head = (square // DH) == (square_lane // DH)
    diagonal = square == square_lane
    lane_head = lax.broadcasted_iota(jnp.int32, (rows, local), 1) // DH
    before_thr, after_thr = [], []

    def wide(value):
        return jnp.concatenate([value] * (local // 128), axis=1)

    def begin(offsets, place):
        value = 0
        for off in offsets:
            value = jnp.where(off <= place, off, value)
        return value

    def through(offsets, which):
        return jnp.where(
            begin(offsets, which * rows + rows - 1) < which * rows, 1.0, 0.0
        ).astype(F32)

    def crops(b):
        offsets, running = [], 0
        for i in range(r.lengths.shape[1]):
            offsets.append(running)
            running = running + r.lengths[b, i]
        start = jnp.zeros((rows, 128), jnp.int32)
        for off in offsets:
            start = jnp.where(off <= row_at + first, off, start)
        last = begin(offsets, first + rows - 1)
        r.mask[b] = jnp.where(
            (lane_at + first >= wide(start)) & (lane_at <= wide(row_at)), 1.0, 0.0
        ).astype(F32)
        r.car[b] = jnp.where(start < first, 1.0, 0.0).astype(F32)
        r.tail[b] = jnp.where(start == last, 1.0, 0.0).astype(F32)
        before_thr.append(through(offsets, lax.rem(s + n - 1, n)))
        after_thr.append(through(offsets, lax.rem(s + 1, n)))
        keep = r.pixel[b : b + 1, :].astype(F32)
        r.pmc[b] = dot_nn(
            jnp.where(diagonal, keep, 0.0).astype(BF), jnp.ones((rows, 128), BF)
        )

    def ag_step(j):
        ag_pass(SMALL, j)
        ag_pass(QKV, j)
        ag_pass(OUT, j)

    crops(0)
    hg_forward(0, 0)
    ag_step(0)
    hg_forward(0, 1)
    for copy in own_copies:
        copy.wait()
    r.smallg[:, ds(s * block, block)] = r.small[...]

    def unit(values):
        mean = jnp.mean(values, axis=1, keepdims=True)
        centered = values - mean
        inverse = lax.rsqrt(jnp.mean(centered * centered, axis=1, keepdims=True) + epsilon)
        return centered * inverse, inverse

    tile = 32

    def unit_one(b):
        def some(i):
            u, _ = unit(r.xg[b, ds(i * tile, tile), :].astype(F32))
            r.gelu_d[ds(b * rows + i * tile, tile), :] = u

        loop(rows // tile, some)

    def norm_one(i):
        rw = ds(i * tile, tile)
        r.normed[rw, :] = (r.gelu_d[rw, :] * gain_one + shift_one).astype(BF)

    for c in (0, 1):
        hg_finish(0, c)
    unit_one(0)
    ag_step(1)
    unit_one(1)
    crops(1)
    ag_step(2)
    ag_send(UP, 0)
    for c in (0, 1):
        hg_forward(1, c)
    ag_wait(SMALL, 3)
    gain_one, gain_two = r.smallg[0:1, :], r.smallg[1:2, :]
    shift_one, shift_two, shift_out = r.smallg[2:3, :], r.smallg[3:4, :], r.smallg[4:5, :]
    loop(tokens // tile, norm_one)
    ag_wait(QKV, 3)
    ag_wait(OUT, 3)

    tm = 128

    def project(i):
        rw = ds(i * tm, tm)
        b = lax.div(i, rows // tm)
        rb = ds(lax.rem(i, rows // tm) * tm, tm)
        left = r.normed[rw, :]
        v = dot_nn(left, r.wq[1])
        low = jnp.exp(jnp.minimum(v, 0.0))
        f = jnp.where(v > 0.0, v + 1.0, low).astype(BF)
        r.phi_d[1, rw, :] = low
        r.kf[rw, :] = (f.astype(F32) * wide(r.pmc[b, rb, :])).astype(BF)
        r.vf[rw, :] = dot_nn(left, r.wq[2]).astype(BF)

    def project_query(i):
        rw = ds(i * tm, tm)
        v = dot_nn(r.normed[rw, :], r.wq[0])
        low = jnp.exp(jnp.minimum(v, 0.0))
        r.phi_d[0, rw, :] = low
        r.qf[rw, :] = jnp.where(v > 0.0, v + 1.0, low).astype(BF)

    loop(tokens // tm, project)

    def fold(ref, parts):
        row = lax.broadcasted_iota(jnp.int32, (16, local), 0)
        sums = jnp.zeros((16, local), F32)
        for b, (matrix, total) in enumerate(parts):
            kept = jnp.where(same_head, matrix, 0.0)
            acc = kept[0:DH]
            for i in range(1, heads):
                acc = acc + kept[i * DH : (i + 1) * DH]
            ref[b * DH : (b + 1) * DH, :] = acc.astype(BF)
            sums = jnp.where(row == b, total, sums)
        ref[batches * DH :, :] = sums.astype(BF)

    def unfold(ref, i, b):
        acc = ref[i, b * DH : (b + 1) * DH, :].astype(F32)
        return jnp.where(same_head, jnp.concatenate([acc] * heads, axis=0), 0.0).astype(BF)

    def unfold_sum(ref, i, b):
        return ref[i, batches * DH :, :].astype(F32)[b : b + 1]

    def state_send(k, ref, dest, step):
        for i in (0, 1):
            to = lax.rem(s + n + step * (i + 1), n)
            remote(ref, dest.at[i], r.st_s.at[k], r.st_r.at[k], to, h).start()

    def state_wait(k, dest):
        landed(dest, r.st_r.at[k])

    def rows_of(b):
        return pl.ds(b * rows, rows)

    def by_head(value):
        return jnp.concatenate(
            [jnp.where(lane_head == hd, value.astype(F32), 0.0).astype(BF) for hd in range(heads)],
            axis=0,
        )

    parts = []
    for b in range(batches):
        k = r.kf[rows_of(b), :].astype(F32) * wide(r.tail[b])
        parts.append(
            (dot_tn(k.astype(BF), r.vf[rows_of(b), :]), jnp.sum(k, axis=0, keepdims=True))
        )
    fold(r.st_send, parts)
    state_send(0, r.st_send, r.st_recv, 1)
    loop(tokens // tm, project_query)

    for b in range(batches):
        q, k = r.qf[rows_of(b), :], r.kf[rows_of(b), :]
        acc = jnp.zeros((rows, local), F32)
        for hd in range(heads):
            sc = dot_nt(jnp.where(lane_head == hd, q.astype(F32), 0.0).astype(BF), k) * r.mask[b]
            r.low[b, :, hd * rows : (hd + 1) * rows] = sc.astype(BF)
            acc = acc + jnp.where(lane_head == hd, jnp.sum(sc, axis=1, keepdims=True), 0.0)
        r.denom[rows_of(b), :] = acc
        r.numer[rows_of(b), :] = dot_nn(r.low[b], by_head(r.vf[rows_of(b), :]))

    for c in (0, 1):
        hg_finish(1, c)
    ag_pass(UP, 0)
    ag_send(DOWN, 0)
    state_wait(0, r.st_recv)

    def both(b, value, thr):
        one = value.astype(F32) * wide(r.car[b])
        return jnp.concatenate([one.astype(BF), (one * thr).astype(BF)], axis=1)

    for b in range(batches):
        left = both(b, r.qf[rows_of(b), :], before_thr[b])
        states = jnp.concatenate([unfold(r.st_recv, i, b) for i in (0, 1)], axis=0)
        only = lax.broadcasted_iota(jnp.int32, (16, local), 0)
        sums = jnp.concatenate(
            [
                jnp.where(
                    same_head,
                    dot_tn(
                        jnp.where(
                            only == b, r.st_recv[i, batches * DH :, :].astype(F32), 0.0
                        ).astype(BF),
                        jnp.ones((16, local), BF),
                    ),
                    0.0,
                ).astype(BF)
                for i in (0, 1)
            ],
            axis=0,
        )
        top = r.numer[rows_of(b), :] + dot_nn(left, states)
        bottom = r.denom[rows_of(b), :] + dot_nn(left, sums)
        attn = top / jnp.maximum(bottom, 1.0)
        r.numer[rows_of(b), :] = attn
        r.denom[rows_of(b), :] = bottom
        r.mixed[rows_of(b), :] = attn.astype(BF)

    hr_first(0, 0, pick(r.mixed), product_nt(r.wo))
    hr_first(0, 1, pick(r.mixed), product_nt(r.wo))
    hr_second(0, 0)
    hr_second(0, 1)
    ag_pass(UP, 1)
    mine = h * own

    def x_rows(at_row):
        return r.xg[hi, ds(lo * own + at_row, tile), :].astype(F32)

    def c_rows(at_row):
        return r.cg[hi, ds(lo * own + at_row, tile), :].astype(F32)

    def norm_two(c):
        def some(i):
            at_row = c * part_rows + i * tile
            v = x_rows(at_row) + hr_value(0, c, ds(i * tile, tile))
            r.middle[ds(at_row, tile), :] = v
            u, _ = unit(v)
            r.ntwo[ds(mine + at_row, tile), :] = (u * gain_two + shift_two).astype(BF)

        loop(part_rows // tile, some)

    for c in (0, 1):
        hr_wait(0, c)
        norm_two(c)
        hg_start(2, c)
    ag_pass(DOWN, 0)
    hg_forward(2, 0)
    hg_forward(2, 1)
    ag_pass(UP, 2)
    hg_finish(2, 0)
    hg_finish(2, 1)
    ag_pass(DOWN, 1)
    ag_wait(UP, 3)

    tu = 256

    def up(i):
        rw = ds(lax.div(i, hidden // tn) * tu, tu)
        cols = ds(lax.rem(i, hidden // tn) * tn, tn)
        v = dot_nn(r.ntwo[rw, :], r.wu[:, cols]) + r.smallg[5:6, cols]
        square_of = v * v
        t = jnp.tanh(0.7978845608028654 * (v + 0.044715 * (square_of * v)))
        half = 0.5 * (1.0 + t)
        r.activ[rw, cols] = (v * half).astype(BF)
        r.gelu_d[rw, cols] = half + (0.5 * v) * (1.0 - t * t) * (
            0.7978845608028654 + (3.0 * 0.044715 * 0.7978845608028654) * square_of
        )

    loop((tokens // tu) * (hidden // tn), up)
    near = [ds(at(p + n + i) * block, block) for i in range(1 - hops, hops)]

    def back_near(i):
        cols = ds(i * tn, tn)
        right = jnp.concatenate([r.wd[rw, cols] for rw in near], axis=0)
        for b in range(batches):
            left = jnp.concatenate([r.cg[b, :, rw] for rw in near], axis=1)
            r.g_act[rows_of(b), cols] = dot_nn(left, right)

    rs_round(DOWN, 0)
    ag_pass(DOWN, 2)
    rs_round(DOWN, 1)
    loop(hidden // tn, back_near)
    ag_wait(DOWN, 3)

    far_block = ds(at(p + hops) * block, block)

    def back(i):
        cols = ds(i * tn, tn)
        for b in range(batches):
            rw = rows_of(b)
            g = r.g_act[rw, cols] + dot_nn(r.cg[b, :, far_block], r.wd[far_block, cols])
            r.g_hid[rw, cols] = (g * r.gelu_d[rw, cols]).astype(BF)

    loop(hidden // tn, back)
    rs_round(UP, 0)
    hr_first(2, 0, pick(r.g_hid), product_nt(r.wu))
    hr_first(2, 1, pick(r.g_hid), product_nt(r.wu))
    rs_round(DOWN, 2)
    hr_second(2, 0)
    hr_second(2, 1)

    r.hs_send[...] = jnp.zeros_like(r.hs_send)

    def back_norm(g, u, inverse, gain):
        scaled = g * gain
        centered = scaled - jnp.mean(scaled, axis=1, keepdims=True)
        return inverse * (centered - u * jnp.mean(scaled * u, axis=1, keepdims=True))

    def norm_two_back(c):
        def some(i):
            at_row = c * part_rows + i * tile
            rw = ds(at_row, tile)
            g = hr_value(2, c, ds(i * tile, tile))
            u, inverse = unit(r.middle[rw, :])
            out = c_rows(at_row)
            v = out + back_norm(g, u, inverse, gain_two)
            r.g_mid[rw, :] = v
            r.gatt[ds(mine + at_row, tile), :] = v.astype(BF)
            r.hs_send[1:2, :] += jnp.sum(g * u, axis=0, keepdims=True)
            r.hs_send[3:4, :] += jnp.sum(g, axis=0, keepdims=True)
            r.hs_send[4:5, :] += jnp.sum(out, axis=0, keepdims=True)

        loop(part_rows // tile, some)

    hr_wait(2, 0)
    norm_two_back(0)
    hg_start(3, 0)
    rs_round(UP, 1)
    hr_wait(2, 1)
    norm_two_back(1)
    hg_start(3, 1)
    hr_first(1, 0, pick(r.activ), product_nt(r.wd))
    hr_first(1, 1, pick(r.activ), product_nt(r.wd))
    rs_round(DOWN, 3)
    for c in (0, 1):
        hg_forward(3, c)
    for c in (0, 1):
        hr_second(1, c)
    for c in (0, 1):
        hg_finish(3, c)

    def mixed_back(i):
        rw = ds(i * tm, tm)
        g = dot_nn(r.gatt[rw, :], r.wo[...])
        attn, bottom = r.numer[rw, :], r.denom[rw, :]
        r.g_num[rw, :] = (g / jnp.maximum(bottom, 1.0)).astype(BF)
        prod = g * attn
        lh = lane_head[:tm]
        acc = jnp.zeros((tm, local), F32)
        for hd in range(heads):
            acc = acc + jnp.where(
                lh == hd,
                jnp.sum(jnp.where(lh == hd, prod, 0.0), axis=1, keepdims=True),
                0.0,
            )
        r.g_den[rw, :] = jnp.where(bottom > 1.0, -acc / jnp.maximum(bottom, 1.0), 0.0)

    loop(tokens // tm, mixed_back)

    parts = []
    for b in range(batches):
        q = r.qf[rows_of(b), :].astype(F32) * wide(r.car[b])
        parts.append(
            (
                dot_tn(q.astype(BF), r.g_num[rows_of(b), :]),
                jnp.sum(q * r.g_den[rows_of(b), :], axis=0, keepdims=True),
            )
        )
    fold(r.gs_send, parts)
    state_send(1, r.gs_send, r.gs_recv, -1)
    rs_round(UP, 2)

    def head_lanes(hd, value):
        return jnp.where(lane_head == hd, value.astype(F32), 0.0).astype(BF)

    for b in range(batches):
        rw = rows_of(b)
        gk = jnp.zeros((rows, local), F32)
        gv = jnp.zeros((rows, local), F32)
        gq = jnp.zeros((rows, local), F32)
        for hd in range(heads):
            gn = head_lanes(hd, r.g_num[rw, :])
            g = dot_nt(gn, r.vf[rw, :]) + r.g_den[rw, hd * DH : hd * DH + 1]
            g = (g * r.mask[b]).astype(BF)
            gq = gq + dot_nn(g, head_lanes(hd, r.kf[rw, :]))
            gk = gk + dot_tn(g, head_lanes(hd, r.qf[rw, :]))
            gv = gv + dot_tn(r.low[b, :, hd * rows : (hd + 1) * rows], gn)
        left = both(b, r.g_num[rw, :], before_thr[b])
        states = jnp.concatenate([unfold(r.st_recv, i, b) for i in (0, 1)], axis=1)
        totals = unfold_sum(r.st_recv, 0, b) + before_thr[b] * unfold_sum(r.st_recv, 1, b)
        gq = gq + dot_nt(left, states) + wide(r.car[b]) * r.g_den[rw, :] * totals
        r.gproj[0, rw, :] = (gq * r.phi_d[0, rw, :]).astype(BF)
        r.gk[rw, :] = gk
        r.gv[rw, :] = gv

    rs_round(OUT, 0)
    rs_round(QUERY, 0)
    state_wait(1, r.gs_recv)
    for b in range(batches):
        rw = rows_of(b)
        thr = after_thr[b]
        states = [unfold(r.gs_recv, i, b) for i in (0, 1)]
        totals = unfold_sum(r.gs_recv, 0, b) + thr * unfold_sum(r.gs_recv, 1, b)
        k = r.kf[rw, :].astype(F32) * wide(r.tail[b])
        v = r.vf[rw, :].astype(F32) * wide(r.tail[b])
        k2 = jnp.concatenate([k.astype(BF), (k * thr).astype(BF)], axis=1)
        v2 = jnp.concatenate([v.astype(BF), (v * thr).astype(BF)], axis=1)
        gk = r.gk[rw, :] + dot_nt(v2, jnp.concatenate(states, axis=1)) + wide(r.tail[b]) * totals
        gv = r.gv[rw, :] + dot_nn(k2, jnp.concatenate(states, axis=0))
        r.gproj[1, rw, :] = (gk * wide(r.pmc[b]) * r.phi_d[1, rw, :]).astype(BF)
        r.gproj[2, rw, :] = gv.astype(BF)

    rs_round(QKV, 0)

    def picks(where):
        return [
            jnp.concatenate([r.gproj[kind, rw, :] for rw in where], axis=0) for kind in range(3)
        ]

    def first_term(left, cols):
        v = dot_nt(left[0], r.wq[0, cols, :])
        for kind in (1, 2):
            v = v + dot_nt(left[kind], r.wq[kind, cols, :])
        return v

    hr_first(3, 0, picks, first_term)
    hr_first(3, 1, picks, first_term)
    hr_second(3, 0)
    hr_second(3, 1)
    rs_round(OUT, 1)
    rs_round(QUERY, 1)
    rs_round(QKV, 1)
    rs_round(UP, 3)

    def norm_one_back(c):
        def some(i):
            at_row = c * part_rows + i * tile
            rw = ds(at_row, tile)
            g = hr_value(3, c, ds(i * tile, tile))
            u, inverse = unit(x_rows(at_row))
            r.i_rows[rw, :] = r.g_mid[rw, :] + back_norm(g, u, inverse, gain_one)
            r.hs_send[0:1, :] += jnp.sum(g * u, axis=0, keepdims=True)
            r.hs_send[2:3, :] += jnp.sum(g, axis=0, keepdims=True)

        loop(part_rows // tile, some)

    for c in (0, 1):
        hr_wait(3, c)
        norm_one_back(c)
    turn(1, r.i_rows, r.ing_o)
    rs_round(OUT, 2)
    rs_round(QUERY, 2)
    rs_round(QKV, 2)

    def finish_rows(c):
        def some(i):
            rw = ds(c * part_rows + i * tile, tile)
            r.a_rows[rw, :] = r.middle[rw, :] + hr_value(1, c, ds(i * tile, tile)) + shift_out

        loop(part_rows // tile, some)

    for c in (0, 1):
        hr_wait(1, c)
        finish_rows(c)
    turn(0, r.a_rows, r.act_o)

    r.hs_recv[h] = r.hs_send[...]
    for i in range(1, m):
        remote(
            r.hs_send, r.hs_recv.at[h], r.hs_s.at[0], r.hs_r.at[0], s, lax.rem(h + i, m)
        ).start()
    r.upb[...] = jnp.zeros_like(r.upb)

    def column_sums(i):
        r.upb[...] += jnp.sum(r.g_hid[ds(i * tile, tile), :].astype(F32), axis=0, keepdims=True)

    loop(tokens // tile, column_sums)
    rs_round(OUT, 3)
    rs_round(QUERY, 3)
    rs_final(DOWN)
    rs_round(QKV, 3)
    landed(r.hs_recv.at[pl.ds(0, m - 1)], r.hs_r.at[0])
    acc = r.hs_recv[0]
    for i in range(1, m):
        acc = acc + r.hs_recv[i]
    r.sg[...] = acc
    r.sg[5:6, :] = r.upb[...]
    r.ss_recv[s] = r.sg[:, ds(s * block, block)]
    for i in range(1, n):
        to = lax.rem(s + i, n)
        remote(
            r.sg.at[:, ds(to * block, block)],
            r.ss_recv.at[s],
            r.ss_s.at[0],
            r.ss_r.at[0],
            to,
            h,
        ).start()
    rs_final(UP)
    rs_final(OUT)
    rs_final(QUERY)
    landed(r.ss_recv.at[pl.ds(0, n - 1)], r.ss_r.at[0])
    acc = r.ss_recv[0]
    for i in range(1, n):
        acc = acc + r.ss_recv[i]
    r.gg_o[...] = acc[0:2]
    r.gb_o[...] = acc[2:5]
    r.gup_o[...] = acc[5:6]
    turn_wait(0, r.a_rows)
    turn_wait(1, r.i_rows)

    far = pl.ds(0, (n - 1) * block)
    for w in range(5):
        views = (r.wq.at[:, far, :], r.wo.at[far], r.wu.at[far], r.wd.at[far], r.smallg.at[:, far])
        drained(views[w], r.ag_s.at[w])
    others = pl.ds(0, (m - 1) * local)
    rest = pl.ds(0, (m - 1) * own)
    for k in range(4):
        view = (r.xg, r.cg)[k].at[:, :, others] if k < 2 else (r.ntwo, r.gatt)[k - 2].at[rest]
        drained(view, r.hg_s.at[k])
        drained(r.h_s1.at[k], r.hr_s.at[k, 0])
        drained(r.h_s2.at[k], r.hr_s.at[k, 1])
    for k, dest in enumerate((r.st_recv, r.gs_recv)):
        drained(dest, r.st_s.at[k])
    drained(r.a_rows.at[:, others], r.aa_s.at[0])
    drained(r.i_rows.at[:, others], r.aa_s.at[1])
    drained(r.hs_recv.at[pl.ds(0, m - 1)], r.hs_s.at[0])
    drained(r.ss_recv.at[pl.ds(0, n - 1)], r.ss_s.at[0])
    rs_final(QKV)
    for w in range(5):
        drained(rs_send[w].at[pl.ds(0, n - 1)], r.rs_s.at[w])
    for copy in local_copies:
        copy.wait()


def settle(*refs):
    count = len(refs) // 2
    copies = [
        pltpu.make_async_copy(refs[i], refs[count + i], refs[-1].at[i]) for i in range(count)
    ]
    for copy in copies:
        copy.start()
    for copy in copies:
        copy.wait()


def whole_layer(n, m):
    def on_each(
        tokens, cotangent, w_qkv, w_out_t, w_up, w_down_t, gains, biases, up_bias, lengths, pixel_mask
    ):
        batches, rows, local = tokens.shape
        width = w_qkv.shape[0] * n
        hidden = w_up.shape[1]
        block = width // n
        vm, sems = layout(n, m, batches, rows, width, local, hidden)
        ins = ["tok", "cot", "w_qkv", "w_out", "w_up", "w_down", "gains", "biases", "up_bias", "lengths", "pixel"]
        outs = ["act_o", "ing_o", "gq_o", "go_o", "gu_o", "gd_o", "gg_o", "gb_o", "gup_o"]
        anywhere = pl.BlockSpec(memory_space=pl.ANY)
        in_vmem = pl.BlockSpec(memory_space=pltpu.VMEM)
        in_smem = pl.BlockSpec(memory_space=pltpu.SMEM)

        result = pl.pallas_call(
            functools.partial(body, n, m, ins + outs + list(vm) + list(sems)),
            name="layer",
            out_shape=(
                pltpu.VMEM((batches, rows, local), F32),
                pltpu.VMEM((batches, rows, local), F32),
                pltpu.VMEM((3, block, local), F32),
                pltpu.VMEM((block, local), F32),
                pltpu.VMEM((block, hidden), F32),
                pltpu.VMEM((block, hidden), F32),
                pltpu.VMEM((2, block), F32),
                pltpu.VMEM((3, block), F32),
                pltpu.VMEM((1, block), F32),
            ),
            in_specs=[anywhere] * 6 + [in_vmem] * 3 + [in_smem, in_vmem],
            out_specs=[in_vmem] * 9,
            scratch_shapes=[pltpu.VMEM(shape, kind) for shape, kind in vm.values()]
            + [pltpu.SemaphoreType.DMA(shape) for shape in sems.values()],
            compiler_params=pltpu.CompilerParams(
                collective_id=0, has_side_effects=True, vmem_limit_bytes=60_000_000
            ),
        )(
            tokens,
            cotangent,
            jnp.transpose(w_qkv, (1, 0, 2)),
            w_out_t,
            w_up,
            w_down_t,
            gains,
            biases,
            up_bias,
            lengths,
            pixel_mask,
        )
        result = pl.pallas_call(
            settle,
            name="settle",
            out_shape=[jax.ShapeDtypeStruct(a.shape, a.dtype) for a in result],
            in_specs=[in_vmem] * len(result),
            out_specs=[anywhere] * len(result),
            scratch_shapes=[pltpu.SemaphoreType.DMA((len(result),))],
        )(*[pltpu.with_memory_space_constraint(a, pltpu.VMEM) for a in result])
        return (*result[:2], jnp.transpose(result[2], (1, 0, 2)), *result[3:])

    return on_each


def solution(mesh):
    in_specs = (
        P(None, "seq", "head"),
        P(None, "seq", "head"),
        P("seq", None, "head"),
        P("seq", "head"),
        P("seq", "head"),
        P("seq", "head"),
        P(None, "seq"),
        P(None, "seq"),
        P("head", "seq"),
        P(),
        P(None, "seq"),
    )
    out_specs = (
        P(None, "seq", "head"),
        P(None, "seq", "head"),
        P("seq", None, "head"),
        P("seq", "head"),
        P("seq", "head"),
        P("seq", "head"),
        P(None, "seq"),
        P(None, "seq"),
        P("head", "seq"),
    )
    n, m = mesh.shape["seq"], mesh.shape["head"]
    fits = (n, m) == (8, 4)
    return jax.shard_map(
        whole_layer(n, m) if fits else on_device, mesh=mesh, in_specs=in_specs, out_specs=out_specs, check_vma=False
    )
```

```python
import functools

import jax
import jax.numpy as jnp
from jax import lax
from jax.experimental import pallas as pl
from jax.experimental.pallas import tpu as pltpu
from jax.sharding import PartitionSpec as P

DH = 64


highest = lax.Precision.HIGHEST
epsilon = 1e-05


def entering(array, axis, join, neutral):
    place = lax.axis_index(axis)
    gathered = jax.tree.map(
        lambda a, kind: lax.all_gather(a.astype(kind), axis),
        array,
        (jnp.bfloat16, jnp.bfloat16, jnp.bfloat16),
    )
    state = jax.tree.map(lambda a, e: jnp.zeros_like(a) + jnp.asarray(e, a.dtype), array, neutral)

    def one(hop, state):
        return join(
            state,
            jax.tree.map(
                lambda a, own: lax.dynamic_index_in_dim(a, hop, 0, False).astype(own.dtype),
                gathered,
                array,
            ),
        )

    return lax.fori_loop(0, place, one, state)


def entering_2(array, axis, combine, identity):
    length, place = (lax.axis_size(axis), lax.axis_index(axis))
    everything = jax.tree.map(
        lambda part, kind: lax.all_gather(part.astype(kind), axis),
        array,
        jax.tree.map(lambda a: jnp.bfloat16 if a.dtype == jnp.float32 else a.dtype, array),
    )
    start = jax.tree.map(
        lambda part, zero: jnp.broadcast_to(jnp.asarray(zero, part.dtype), part.shape),
        array,
        identity,
    )

    def hop(k, before):
        at = length - 1 - k
        reached = at > place
        new = combine(
            before, jax.tree.map(lambda part, own: part[at].astype(own.dtype), everything, array)
        )
        return jax.tree.map(lambda a, b: jnp.where(reached, a, b), new, before)

    return lax.fori_loop(0, length, hop, start)


def normalize(values, gain_vec, shift_vec):
    mean_val = jnp.mean(values, axis=-1, keepdims=True)
    centered = values - mean_val
    inverse = lax.rsqrt(jnp.mean(centered * centered, axis=-1, keepdims=True) + epsilon)
    unit_val = centered * inverse
    return (unit_val * gain_vec + shift_vec, unit_val, inverse)


def norm_back(grad_in, unit_val, inverse, gain_vec):
    scaled = grad_in * gain_vec
    centered = scaled - jnp.mean(scaled, axis=-1, keepdims=True)
    return inverse * (centered - unit_val * jnp.mean(scaled * unit_val, axis=-1, keepdims=True))


def features(values):
    return jax.nn.elu(values) + 1.0


def finish(numerator, denominator):
    return numerator / jnp.maximum(denominator, 1.0)[:, :, None]


def compose(earlier, later):
    return (
        later[0] + later[2] * earlier[0],
        later[1] + later[2] * earlier[1],
        later[2] * earlier[2],
    )


def item_numbers(lengths_row, first_place, number):
    offsets = jnp.cumsum(lengths_row) - lengths_row
    places = first_place + jnp.arange(number, dtype=jnp.int32)
    return jnp.sum((offsets[None, :] <= places[:, None]).astype(jnp.int32), axis=1) - 1


def on_device(
    tokens, cotangent, w_qkv, w_out_t, w_up, w_down_t, gains, biases, up_bias, lengths, pixel_mask
):
    batches, local_rows, columns = tokens.shape
    local_width = w_qkv.shape[2]
    heads_here = local_width // DH
    seq_index = lax.axis_index("seq")
    head_index = lax.axis_index("head")
    first_token = seq_index * local_rows
    position = jnp.arange(local_rows, dtype=jnp.int32)
    before = position[:, None] >= position[None, :]

    def own_columns(matrix):
        return lax.dynamic_slice_in_dim(matrix, head_index * columns, columns, 1)

    results = []
    input_grads = []
    shard_sums = None
    for batch_index in range(batches):
        full_qkv, full_out, full_up, full_down, full_gains, full_biases, full_upb = (
            lax.all_gather(w_qkv, "seq", axis=0, tiled=True),
            lax.all_gather(w_out_t, "seq", axis=0, tiled=True),
            lax.all_gather(w_up, "seq", axis=0, tiled=True),
            lax.all_gather(w_down_t, "seq", axis=0, tiled=True),
            lax.all_gather(gains, "seq", axis=1, tiled=True),
            lax.all_gather(biases, "seq", axis=1, tiled=True),
            lax.all_gather(up_bias, "seq", axis=1, tiled=True),
        )
        input_rows, grad_rows16 = (
            lax.all_gather(tokens[batch_index], "head", axis=1, tiled=True),
            lax.all_gather(cotangent[batch_index], "head", axis=1, tiled=True),
        )
        gains32 = full_gains.astype(jnp.float32)
        biases32 = full_biases.astype(jnp.float32)
        upb32 = full_upb.astype(jnp.float32).reshape(-1)
        inputs32 = input_rows.astype(jnp.float32)
        place_items = item_numbers(lengths[batch_index], first_token - 1, local_rows + 1)
        item_of = place_items[1:]
        carried = (item_of == place_items[0]).astype(jnp.float32)
        tail_mask = (item_of == item_of[local_rows - 1]).astype(jnp.float32)
        through = carried[local_rows - 1]
        same_item = ((item_of[:, None] == item_of[None, :]) & before).astype(jnp.float32)
        keep_half = pixel_mask[batch_index].astype(jnp.bfloat16)
        keep32 = pixel_mask[batch_index].astype(jnp.float32)
        lifted, unit_one, inverse_one = normalize(inputs32, gains32[0], biases32[0])
        normed = lifted.astype(jnp.bfloat16)
        projected = jnp.einsum("td,dsf->tsf", normed, full_qkv, preferred_element_type=jnp.float32)
        query_feat = (
            features(projected[:, 0]).astype(jnp.bfloat16).reshape(local_rows, heads_here, DH)
        )
        key_feat = (features(projected[:, 1]).astype(jnp.bfloat16) * keep_half[:, None]).reshape(
            local_rows, heads_here, DH
        )
        value_feat = projected[:, 2].astype(jnp.bfloat16).reshape(local_rows, heads_here, DH)
        tail_key = key_feat * tail_mask.astype(jnp.bfloat16)[:, None, None]
        state_loc = jnp.einsum(
            "jhd,jhe->hde", tail_key, value_feat, preferred_element_type=jnp.float32
        )
        total_loc = jnp.sum(tail_key.astype(jnp.float32), axis=0)
        identity = (jnp.zeros_like(state_loc), jnp.zeros_like(total_loc), jnp.ones((), jnp.float32))
        state_in, total_in, passed = entering(
            (state_loc, total_loc, through), "seq", compose, identity
        )
        query32 = query_feat.astype(jnp.float32)
        scores = (
            jnp.einsum("thd,jhd->htj", query_feat, key_feat, preferred_element_type=jnp.float32)
            * same_item[None]
        )
        scores_low = scores.astype(jnp.bfloat16)
        numerator = jnp.einsum(
            "htj,jhe->the", scores_low, value_feat, preferred_element_type=jnp.float32
        ) + carried[:, None, None] * jnp.einsum(
            "thd,hde->the", query32, state_in, precision=highest
        )
        denominator = jnp.sum(scores, axis=2).T + carried[:, None] * jnp.einsum(
            "thd,hd->th", query32, total_in, precision=highest
        )
        output, finish_back = jax.vjp(finish, numerator, denominator)
        mixed_out = output.reshape(local_rows, local_width).astype(jnp.bfloat16)
        attended = lax.psum(
            jnp.einsum("tf,df->td", mixed_out, full_out, preferred_element_type=jnp.float32).astype(
                jnp.bfloat16
            ),
            "head",
        ).astype(jnp.float32)
        middle = inputs32 + attended
        lifted_two, unit_two, inverse_two = normalize(middle, gains32[1], biases32[1])
        normed_two = lifted_two.astype(jnp.bfloat16)
        hidden = jnp.dot(normed_two, full_up, preferred_element_type=jnp.float32) + upb32
        activated32, gelu_back = jax.vjp(jax.nn.gelu, hidden)
        activated = activated32.astype(jnp.bfloat16)
        branch = lax.psum_scatter(
            jnp.einsum(
                "tf,df->td", activated, full_down, preferred_element_type=jnp.float32
            ).astype(jnp.bfloat16),
            "head",
            scatter_dimension=1,
            tiled=True,
        ).astype(jnp.float32)
        results.append(own_columns(middle) + branch + own_columns(biases32[2][None]))
        grad_out = grad_rows16.astype(jnp.float32)
        grad_down = jnp.einsum(
            "td,tf->df", grad_rows16, activated, preferred_element_type=jnp.float32
        )
        grad_act = jnp.einsum(
            "td,df->tf", grad_rows16, full_down, preferred_element_type=jnp.float32
        )
        grad_hidden = gelu_back(grad_act)[0].astype(jnp.bfloat16)
        grad_up = jnp.einsum(
            "td,tf->df", normed_two, grad_hidden, preferred_element_type=jnp.float32
        )
        grad_upb = jnp.sum(grad_hidden.astype(jnp.float32), axis=0).reshape(full_upb.shape)
        grad_two = lax.psum(
            jnp.einsum(
                "tf,df->td", grad_hidden, full_up, preferred_element_type=jnp.float32
            ).astype(jnp.bfloat16),
            "head",
        ).astype(jnp.float32)
        grad_middle = grad_out + norm_back(grad_two, unit_two, inverse_two, gains32[1])
        grad_attended = grad_middle.astype(jnp.bfloat16)
        grad_out_t = jnp.einsum(
            "td,tf->df", grad_attended, mixed_out, preferred_element_type=jnp.float32
        )
        grad_mixed = jnp.einsum(
            "td,df->tf", grad_attended, full_out, preferred_element_type=jnp.float32
        ).reshape(local_rows, heads_here, DH)
        grad_numer32, grad_denom = finish_back(grad_mixed)
        grad_numer = grad_numer32.astype(jnp.bfloat16)
        grad_numer_wide = grad_numer.astype(jnp.float32)
        grad_scores = (
            (
                jnp.einsum(
                    "the,jhe->htj", grad_numer, value_feat, preferred_element_type=jnp.float32
                )
                + grad_denom.T[:, :, None]
            )
            * same_item[None]
        ).astype(jnp.bfloat16)
        carried_query = query32 * carried[:, None, None]
        grad_query = jnp.einsum(
            "htj,jhd->thd", grad_scores, key_feat, preferred_element_type=jnp.float32
        ) + carried[:, None, None] * (
            jnp.einsum("hde,the->thd", state_in, grad_numer_wide, precision=highest)
            + grad_denom[:, :, None] * total_in[None]
        )
        grad_key = jnp.einsum(
            "htj,thd->jhd", grad_scores, query_feat, preferred_element_type=jnp.float32
        )
        grad_value = jnp.einsum(
            "htj,the->jhe", scores_low, grad_numer, preferred_element_type=jnp.float32
        )
        grad_state_in = jnp.einsum(
            "thd,the->hde", carried_query, grad_numer_wide, precision=highest
        )
        grad_total_in = jnp.einsum("thd,th->hd", carried_query, grad_denom, precision=highest)
        grad_state_loc, grad_total_loc, passed_back = entering_2(
            (grad_state_in, grad_total_in, through), "seq", compose, identity
        )
        tail_three = tail_mask[:, None, None]
        value_wide = value_feat.astype(jnp.float32)
        key_wide = key_feat.astype(jnp.float32)
        grad_key = grad_key + tail_three * (
            jnp.einsum("hde,jhe->jhd", grad_state_loc, value_wide, precision=highest)
            + grad_total_loc[None]
        )
        grad_value = grad_value + tail_three * jnp.einsum(
            "jhd,hde->jhe", key_wide, grad_state_loc, precision=highest
        )
        ignored, feature_back = jax.vjp(features, projected[:, :2])
        grad_features = jnp.stack(
            [
                grad_query.reshape(local_rows, local_width),
                grad_key.reshape(local_rows, local_width) * keep32[:, None],
            ],
            axis=1,
        )
        grad_pair = feature_back(grad_features)[0]
        grad_projected = jnp.concatenate(
            [grad_pair, grad_value.reshape(local_rows, 1, local_width)], axis=1
        ).astype(jnp.bfloat16)
        grad_qkv = jnp.einsum(
            "td,tsf->dsf", normed, grad_projected, preferred_element_type=jnp.float32
        )
        grad_one = lax.psum(
            jnp.einsum(
                "tsf,dsf->td", grad_projected, full_qkv, preferred_element_type=jnp.float32
            ).astype(jnp.bfloat16),
            "head",
        ).astype(jnp.float32)
        grad_inputs = grad_middle + norm_back(grad_one, unit_one, inverse_one, gains32[0])
        input_grads.append(own_columns(grad_inputs))
        grad_gains = jnp.stack(
            [jnp.sum(grad_one * unit_one, axis=0), jnp.sum(grad_two * unit_two, axis=0)]
        )
        grad_biases = jnp.stack(
            [jnp.sum(grad_one, axis=0), jnp.sum(grad_two, axis=0), jnp.sum(grad_out, axis=0)]
        )
        pieces = (
            lax.psum_scatter(grad_qkv, "seq", scatter_dimension=0, tiled=True),
            lax.psum_scatter(grad_out_t, "seq", scatter_dimension=0, tiled=True),
            lax.psum_scatter(grad_up, "seq", scatter_dimension=0, tiled=True),
            lax.psum_scatter(grad_down, "seq", scatter_dimension=0, tiled=True),
            lax.psum_scatter(grad_gains, "seq", scatter_dimension=1, tiled=True),
            lax.psum_scatter(grad_biases, "seq", scatter_dimension=1, tiled=True),
            lax.psum_scatter(grad_upb, "seq", scatter_dimension=1, tiled=True),
        )
        shard_sums = pieces if shard_sums is None else jax.tree.map(jnp.add, shard_sums, pieces)
    return (
        jnp.stack(results),
        jnp.stack(input_grads),
        shard_sums[0],
        shard_sums[1],
        shard_sums[2],
        shard_sums[3],
        shard_sums[4],
        shard_sums[5],
        shard_sums[6],
    )


MESH = pl.DeviceIdType.MESH
BF = jnp.bfloat16
F32 = jnp.float32
QKV, OUT, UP, DOWN, SMALL = range(5)
QUERY = 4


def dot_nn(a, b):
    return lax.dot_general(a, b, (((1,), (0,)), ((), ())), preferred_element_type=F32)


def dot_nt(a, b):
    return lax.dot_general(a, b, (((1,), (1,)), ((), ())), preferred_element_type=F32)


def dot_tn(a, b):
    return lax.dot_general(a, b, (((0,), (0,)), ((), ())), preferred_element_type=F32)


def ds(start, size):
    return pl.ds(pl.multiple_of(start, size), size)


def loop(count, body):
    def step(i, carry):
        body(i)
        return carry

    lax.fori_loop(0, count, step, 0)


def layout(n, m, batches, rows, width, local, hidden):
    tokens = batches * rows
    block = width // n
    own = tokens // m
    hops = n // 2
    heads = local // DH
    vm = {
        "xg": ((batches, rows, width), BF),
        "cg": ((batches, rows, width), BF),
        "wq": ((3, width, local), BF),
        "wo": ((width, local), BF),
        "wu": ((width, hidden), BF),
        "wd": ((width, hidden), BF),
        "small": ((8, block), F32),
        "smallg": ((8, width), F32),
        "normed": ((tokens, width), BF),
        "phi_d": ((2, tokens, local), F32),
        "qf": ((tokens, local), BF),
        "kf": ((tokens, local), BF),
        "vf": ((tokens, local), BF),
        "mask": ((batches, rows, rows), F32),
        "car": ((batches, rows, 128), F32),
        "tail": ((batches, rows, 128), F32),
        "pmc": ((batches, rows, 128), F32),
        "low": ((batches, rows, heads * rows), BF),
        "numer": ((tokens, local), F32),
        "denom": ((tokens, local), F32),
        "mixed": ((tokens, local), BF),
        "st_send": ((batches * DH + 16, local), BF),
        "st_recv": ((2, batches * DH + 16, local), BF),
        "gs_send": ((batches * DH + 16, local), BF),
        "gs_recv": ((2, batches * DH + 16, local), BF),
        "middle": ((own, width), F32),
        "ntwo": ((tokens, width), BF),
        "gelu_d": ((tokens, hidden), F32),
        "activ": ((tokens, hidden), BF),
        "g_hid": ((tokens, hidden), BF),
        "branch": ((own, width), F32),
        "total": ((own, width), F32),
        "g_mid": ((own, width), F32),
        "gatt": ((tokens, width), BF),
        "g_attn": ((tokens, local), F32),
        "g_num": ((tokens, local), BF),
        "g_den": ((tokens, local), F32),
        "gq": ((tokens, local), F32),
        "gk": ((tokens, local), F32),
        "gv": ((tokens, local), F32),
        "gproj": ((3, tokens, local), BF),
        "h_s1": ((4, 2, 2, own // 2, width), BF),
        "h_r1": ((4, 2, 2, own // 2, width), BF),
        "h_acc": ((4, 2, 2, own // 2, width), F32),
        "h_s2": ((4, 2, own // 2, width), BF),
        "h_r2": ((4, 2, own // 2, width), BF),
        "rq_s": ((n, 2, block, local), BF),
        "rq_r": ((n, 2, block, local), BF),
        "rx_s": ((n, block, local), BF),
        "rx_r": ((n, block, local), BF),
        "ro_s": ((n, block, local), BF),
        "ro_r": ((n, block, local), BF),
        "ru_s": ((n, block, hidden), BF),
        "ru_r": ((n, block, hidden), BF),
        "rd_s": ((n, block, hidden), BF),
        "rd_r": ((n, block, hidden), BF),
        "pq": ((2, 2, block, local), F32),
        "po": ((2, block, local), F32),
        "pu": ((2, block, hidden), F32),
        "pd": ((2, block, hidden), F32),
        "px": ((2, block, local), F32),
        "g_act": ((tokens, hidden), F32),
        "hs_recv": ((m, 8, width), F32),
        "hs_send": ((8, width), F32),
        "upb": ((1, hidden), F32),
        "sg": ((8, width), F32),
        "ss_recv": ((n, 8, block), F32),
        "a_rows": ((own, width), F32),
        "i_rows": ((own, width), F32),
    }
    sems = {
        "ag_s": (5,),
        "ag_r": (5, 2, hops),
        "rs_s": (5,),
        "hg_s": (4,),
        "hg_r": (2, 2, 3),
        "hr_s": (4, 2),
        "hr_r": (2, 2, 2),
        "st_s": (2,),
        "st_r": (2,),
        "aa_s": (2,),
        "aa_r": (2,),
        "hs_s": (1,),
        "hs_r": (1,),
        "ss_s": (1,),
        "ss_r": (1,),
        "lc": (8,),
    }
    return vm, sems


class Refs:
    pass


def body(n, m, names, *refs):
    r = Refs()
    for name, ref in zip(names, refs):
        setattr(r, name, ref)
    batches, rows, width = r.xg.shape
    tokens = batches * rows
    own = tokens // m
    block = width // n
    local = r.wo.shape[1]
    hidden = r.wu.shape[1]
    heads = local // DH
    hops = n // 2
    s = lax.axis_index("seq")
    h = lax.axis_index("head")
    odd = lax.rem(s, 2)
    p = (1 - odd) * lax.div(s, 2) + odd * (n - 1 - lax.div(s, 2))
    lo, hi = lax.rem(h, 2), lax.div(h, 2)
    pair = h + 1 - 2 * lo
    cross = lax.rem(h + 2, m)

    def at(place):
        place = lax.rem(place + 2 * n, n)
        far = lax.div(place, hops)
        return (1 - far) * 2 * place + far * (2 * (n - 1 - place) + 1)

    ring = (at(p + 1), at(p - 1))
    sign = (1, -1)

    def remote(src, dst, send, recv, seq, head):
        return pltpu.make_async_remote_copy(
            src_ref=src,
            dst_ref=dst,
            send_sem=send,
            recv_sem=recv,
            device_id=(seq, head),
            device_id_type=MESH,
        )

    def drained(view, sem):
        remote(view, view, sem, sem, ring[0], h).wait_send()

    def landed(view, sem):
        remote(view, view, sem, sem, ring[0], h).wait_recv()

    barrier = pltpu.get_barrier_semaphore()
    for peer in ((ring[0], h), (ring[1], h), (s, pair), (s, cross)):
        pl.semaphore_signal(barrier, inc=1, device_id=peer, device_id_type=MESH)

    r.small[...] = jnp.zeros_like(r.small)
    r.small[0:2, :] = r.gains[...].astype(F32)
    r.small[2:5, :] = r.biases[...].astype(F32)
    r.small[5:6, :] = r.up_bias[...].astype(F32)

    first = s * rows
    row_at = lax.broadcasted_iota(jnp.int32, (rows, 128), 0)
    lane_at = lax.broadcasted_iota(jnp.int32, (rows, rows), 1)
    square = lax.broadcasted_iota(jnp.int32, (local, local), 0)
    square_lane = lax.broadcasted_iota(jnp.int32, (local, local), 1)
    same_head = (square // DH) == (square_lane // DH)
    diagonal = square == square_lane
    lane_head = lax.broadcasted_iota(jnp.int32, (rows, local), 1) // DH
    before_thr, after_thr = [], []

    def wide(value):
        return jnp.concatenate([value] * (local // 128), axis=1)

    def begin(offsets, place):
        value = 0
        for off in offsets:
            value = jnp.where(off <= place, off, value)
        return value

    def through(offsets, which):
        return jnp.where(
            begin(offsets, which * rows + rows - 1) < which * rows, 1.0, 0.0
        ).astype(F32)

    def crops(b):
        offsets, running = [], 0
        for i in range(r.lengths.shape[1]):
            offsets.append(running)
            running = running + r.lengths[b, i]
        start = jnp.zeros((rows, 128), jnp.int32)
        for off in offsets:
            start = jnp.where(off <= row_at + first, off, start)
        last = begin(offsets, first + rows - 1)
        r.mask[b] = jnp.where(
            (lane_at + first >= wide(start)) & (lane_at <= wide(row_at)), 1.0, 0.0
        ).astype(F32)
        r.car[b] = jnp.where(start < first, 1.0, 0.0).astype(F32)
        r.tail[b] = jnp.where(start == last, 1.0, 0.0).astype(F32)
        before_thr.append(through(offsets, lax.rem(s + n - 1, n)))
        after_thr.append(through(offsets, lax.rem(s + 1, n)))
        keep = r.pixel[b : b + 1, :].astype(F32)
        r.pmc[b] = dot_nn(
            jnp.where(diagonal, keep, 0.0).astype(BF), jnp.ones((rows, 128), BF)
        )

    crops(0)
    pl.semaphore_wait(barrier, 4)

    shards = (r.w_qkv, r.w_out, r.w_up, r.w_down, r.small)
    gathered = (r.wq, r.wo, r.wu, r.wd, r.smallg)

    def part_of(w, d, j):
        wide_part = r.wq.shape[2] if w == QKV else shards[w].shape[1]
        if j < hops - 1 or w == SMALL:
            return pl.ds(0, wide_part)
        return pl.ds(d * (wide_part // 2), wide_part // 2)

    def ag_shard(w, d, j):
        cols = part_of(w, d, j)
        if w == SMALL:
            return r.small
        return shards[w].at[:, :, cols] if w == QKV else shards[w].at[:, cols]

    def ag_full(w, owner, d, j):
        cols = part_of(w, d, j)
        if w == SMALL:
            return r.smallg.at[:, ds(owner * block, block)]
        if w == QKV:
            return r.wq.at[:, ds(owner * block, block), cols]
        return gathered[w].at[ds(owner * block, block), cols]

    def ways(w, j):
        return (0,) if w == SMALL and j == hops - 1 else (0, 1)

    def ag_send(w, j):
        for d in ways(w, j):
            owner = at(p - sign[d] * j)
            src = ag_shard(w, d, j) if j == 0 else ag_full(w, owner, d, j)
            remote(
                src, ag_full(w, owner, d, j), r.ag_s.at[w], r.ag_r.at[w, d, j], ring[d], h
            ).start()

    def ag_wait(w, j):
        for d in ways(w, j):
            landed(ag_full(w, at(p - sign[d] * (j + 1)), d, j), r.ag_r.at[w, d, j])

    def ag_pass(w, j):
        ag_wait(w, j)
        ag_send(w, j + 1)

    part_rows = own // 2

    def hg_view(k, c, who):
        if k < 2:
            return (r.xg, r.cg)[k].at[c, :, ds(who * local, local)]
        return (r.ntwo, r.gatt)[k - 2].at[ds(who * own + c * part_rows, part_rows), :]

    def hg_copy(k, c, i, src, who, to):
        return remote(src, hg_view(k, c, who), r.hg_s.at[k], r.hg_r.at[k % 2, c, i], s, to)

    def hg_start(k, c):
        src = (r.tok, r.cot)[k].at[c] if k < 2 else hg_view(k, c, h)
        hg_copy(k, c, 1, src, h, cross).start()
        hg_copy(k, c, 0, src, h, pair).start()

    def hg_forward(k, c):
        view = hg_view(k, c, cross)
        hg_copy(k, c, 1, view, cross, cross).wait_recv()
        hg_copy(k, c, 2, view, cross, pair).start()

    def hg_finish(k, c):
        view = hg_view(k, c, pair)
        hg_copy(k, c, 0, view, pair, pair).wait_recv()
        across = lax.rem(pair + 2, m)
        view = hg_view(k, c, across)
        hg_copy(k, c, 2, view, across, pair).wait_recv()

    tn = 256

    def hr_first(k, c, left, product):
        blocks = [2 * i + 1 - lo for i in (0, 1)] + [2 * i + lo for i in (0, 1)]
        where = [ds(who * own + c * part_rows, part_rows) for who in blocks]

        def some(i):
            cols = ds(i * tn, tn)
            v = product(left(where), cols)
            for q in (0, 1):
                r.h_s1[k, c, q, :, cols] = v[q * part_rows : (q + 1) * part_rows].astype(BF)
                r.h_acc[k, c, q, :, cols] = v[(q + 2) * part_rows : (q + 3) * part_rows]

        loop(width // tn, some)
        hr_copy(k, c, 0).start()

    def hr_copy(k, c, stage):
        if stage == 0:
            src, dst, to = r.h_s1.at[k, c], r.h_r1.at[k, c], pair
        else:
            src, dst, to = r.h_s2.at[k, c], r.h_r2.at[k, c], cross
        return remote(src, dst, r.hr_s.at[k, stage], r.hr_r.at[k // 2, c, stage], s, to)

    def hr_second(k, c):
        hr_copy(k, c, 0).wait_recv()

        def away(i):
            rw = ds(i * 32, 32)
            r.h_s2[k, c, rw, :] = (
                r.h_acc[k, c, 1 - hi, rw, :] + r.h_r1[k, c, 1 - hi, rw, :].astype(F32)
            ).astype(BF)

        loop(part_rows // 32, away)
        hr_copy(k, c, 1).start()

    def hr_wait(k, c):
        hr_copy(k, c, 1).wait_recv()

    def hr_value(k, c, rw):
        return (
            r.h_acc[k, c, hi, rw, :]
            + r.h_r1[k, c, hi, rw, :].astype(F32)
            + r.h_r2[k, c, rw, :].astype(F32)
        )

    def pick(ref):
        return lambda where: jnp.concatenate([ref[rw, :] for rw in where], axis=0)

    def product_nt(right):
        return lambda left, cols: dot_nt(left, right[cols, :])

    def rs_term(w, owner, piece):
        cols = ds(owner * block, block)
        if w == DOWN:
            left = r.cg[:, :, cols].reshape(tokens, block)
            half = hidden // 2
            return [dot_tn(left, r.activ[:, pl.ds(piece * half, half)])]
        if w == UP:
            half = hidden // 2
            return [dot_tn(r.ntwo[:, cols], r.g_hid[:, pl.ds(piece * half, half)])]
        half = local // 2
        if w == OUT:
            return [dot_tn(r.gatt[:, cols], r.mixed[:, pl.ds(piece * half, half)])]
        left = r.normed[:, cols]
        kinds = (0,) if w == QUERY else (1, 2)
        return [dot_tn(left, r.gproj[i, :, pl.ds(piece * half, half)]) for i in kinds]

    rs_send = (r.rq_s, r.ro_s, r.ru_s, r.rd_s, r.rx_s)
    rs_recv = (r.rq_r, r.ro_r, r.ru_r, r.rd_r, r.rx_r)

    def rs_half(w, piece):
        half = rs_send[w].shape[-1] // 2
        return pl.ds(piece * half, half)

    def rs_view(ref, w, d, step):
        if step > 0:
            return ref.at[d * hops + step]
        if w == QKV:
            return ref.at[d * hops, :, :, rs_half(w, d)]
        return ref.at[d * hops, :, rs_half(w, d)]

    def rs_arrived(w, d, step):
        landed(rs_view(rs_recv[w], w, d, step), r.ag_r.at[w, d, step])

    ahead = (r.pq, r.po, r.pu, r.pd, r.px)

    def rs_prepare(w, step):
        for d in (0, 1) if step < hops else (0,):
            owner = at(p + sign[d] * (hops - step)) if step < hops else s
            for piece in (0, 1) if step > 0 else (d,):
                cols = rs_half(w, piece)
                for i, v in enumerate(rs_term(w, owner, piece)):
                    lead = (i,) if w == QKV else ()
                    ahead[w][(d, *lead, slice(None), cols)] = v

    def rs_round(w, step):
        if step == 0:
            rs_prepare(w, 0)
        for d in (0, 1):
            slot = d * hops + step
            if step > 0:
                rs_arrived(w, d, step - 1)
            for piece in (0, 1) if step > 0 else (d,):
                cols = rs_half(w, piece)
                for i in range(2 if w == QKV else 1):
                    lead = (i,) if w == QKV else ()
                    v = ahead[w][(d, *lead, slice(None), cols)]
                    if step > 1 or (step == 1 and piece == d):
                        v = v + rs_recv[w][(slot - 1, *lead, slice(None), cols)].astype(F32)
                    rs_send[w][(slot, *lead, slice(None), cols)] = v.astype(BF)
            remote(
                rs_view(rs_send[w], w, d, step),
                rs_view(rs_recv[w], w, d, step),
                r.rs_s.at[w],
                r.ag_r.at[w, d, step],
                ring[d],
                h,
            ).start()
        rs_prepare(w, step + 1)

    finals = (r.gq_o.at[pl.ds(1, 2)], r.go_o, r.gu_o, r.gd_o, r.gq_o.at[0])
    local_copies = []

    def rs_final(w):
        for d in (0, 1):
            rs_arrived(w, d, hops - 1)
        for piece in (0, 1):
            cols = rs_half(w, piece)
            for i in range(2 if w == QKV else 1):
                lead = (i,) if w == QKV else ()
                v = ahead[w][(0, *lead, slice(None), cols)]
                for d in (0, 1):
                    v = v + rs_recv[w][(d * hops + hops - 1, *lead, slice(None), cols)].astype(F32)
                finals[w][(*lead, slice(None), cols)] = v

    def turn(k, src, dst):
        where = (hi, ds(lo * own, own))
        for i in range(1, m):
            to = lax.rem(h + i, m)
            remote(
                src.at[:, ds(to * local, local)],
                dst.at[where[0], where[1], :],
                r.aa_s.at[k],
                r.aa_r.at[k],
                s,
                to,
            ).start()
        copy = pltpu.make_async_copy(
            src.at[:, ds(h * local, local)], dst.at[where[0], where[1], :], r.lc.at[k]
        )
        copy.start()
        local_copies.append(copy)

    def turn_wait(k, src):
        landed(src.at[:, pl.ds(0, (m - 1) * local)], r.aa_r.at[k])

    ag_send(SMALL, 0)
    ag_send(QKV, 0)
    ag_send(OUT, 0)
    hg_start(0, 0)
    hg_start(0, 1)
    own_copies = [
        pltpu.make_async_copy(r.w_qkv, r.wq.at[:, ds(s * block, block), :], r.lc.at[4]),
        pltpu.make_async_copy(r.w_out, r.wo.at[ds(s * block, block), :], r.lc.at[5]),
        pltpu.make_async_copy(r.w_up, r.wu.at[ds(s * block, block), :], r.lc.at[6]),
        pltpu.make_async_copy(r.w_down, r.wd.at[ds(s * block, block), :], r.lc.at[7]),
        pltpu.make_async_copy(r.tok, r.xg.at[:, :, ds(h * local, local)], r.lc.at[2]),
        pltpu.make_async_copy(r.cot, r.cg.at[:, :, ds(h * local, local)], r.lc.at[3]),
    ]
    for copy in own_copies:
        copy.start()
    hg_start(1, 0)
    hg_start(1, 1)

    def ag_step(j):
        ag_pass(SMALL, j)
        ag_pass(QKV, j)
        ag_pass(OUT, j)

    hg_forward(0, 0)
    ag_step(0)
    hg_forward(0, 1)
    for copy in own_copies:
        copy.wait()
    r.smallg[:, ds(s * block, block)] = r.small[...]

    def unit(values):
        mean = jnp.mean(values, axis=1, keepdims=True)
        centered = values - mean
        inverse = lax.rsqrt(jnp.mean(centered * centered, axis=1, keepdims=True) + epsilon)
        return centered * inverse, inverse

    tile = 32

    def unit_one(b):
        def some(i):
            u, _ = unit(r.xg[b, ds(i * tile, tile), :].astype(F32))
            r.gelu_d[ds(b * rows + i * tile, tile), :] = u

        loop(rows // tile, some)

    def norm_one(i):
        rw = ds(i * tile, tile)
        r.normed[rw, :] = (r.gelu_d[rw, :] * gain_one + shift_one).astype(BF)

    for c in (0, 1):
        hg_finish(0, c)
    unit_one(0)
    ag_step(1)
    unit_one(1)
    crops(1)
    ag_step(2)
    ag_send(UP, 0)
    for c in (0, 1):
        hg_forward(1, c)
    ag_wait(SMALL, 3)
    gain_one, gain_two = r.smallg[0:1, :], r.smallg[1:2, :]
    shift_one, shift_two, shift_out = r.smallg[2:3, :], r.smallg[3:4, :], r.smallg[4:5, :]
    loop(tokens // tile, norm_one)
    ag_wait(QKV, 3)
    ag_wait(OUT, 3)

    tm = 128

    def project(i):
        rw = ds(i * tm, tm)
        b = lax.div(i, rows // tm)
        rb = ds(lax.rem(i, rows // tm) * tm, tm)
        left = r.normed[rw, :]
        v = dot_nn(left, r.wq[1])
        low = jnp.exp(jnp.minimum(v, 0.0))
        f = jnp.where(v > 0.0, v + 1.0, low).astype(BF)
        r.phi_d[1, rw, :] = low
        r.kf[rw, :] = (f.astype(F32) * wide(r.pmc[b, rb, :])).astype(BF)
        r.vf[rw, :] = dot_nn(left, r.wq[2]).astype(BF)

    def project_query(i):
        rw = ds(i * tm, tm)
        v = dot_nn(r.normed[rw, :], r.wq[0])
        low = jnp.exp(jnp.minimum(v, 0.0))
        r.phi_d[0, rw, :] = low
        r.qf[rw, :] = jnp.where(v > 0.0, v + 1.0, low).astype(BF)

    loop(tokens // tm, project)

    def fold(ref, parts):
        row = lax.broadcasted_iota(jnp.int32, (16, local), 0)
        sums = jnp.zeros((16, local), F32)
        for b, (matrix, total) in enumerate(parts):
            kept = jnp.where(same_head, matrix, 0.0)
            acc = kept[0:DH]
            for i in range(1, heads):
                acc = acc + kept[i * DH : (i + 1) * DH]
            ref[b * DH : (b + 1) * DH, :] = acc.astype(BF)
            sums = jnp.where(row == b, total, sums)
        ref[batches * DH :, :] = sums.astype(BF)

    def unfold(ref, i, b):
        acc = ref[i, b * DH : (b + 1) * DH, :].astype(F32)
        return jnp.where(same_head, jnp.concatenate([acc] * heads, axis=0), 0.0).astype(BF)

    def unfold_sum(ref, i, b):
        return ref[i, batches * DH :, :].astype(F32)[b : b + 1]

    def state_send(k, ref, dest, step):
        for i in (0, 1):
            to = lax.rem(s + n + step * (i + 1), n)
            remote(ref, dest.at[i], r.st_s.at[k], r.st_r.at[k], to, h).start()

    def state_wait(k, dest):
        landed(dest, r.st_r.at[k])

    def rows_of(b):
        return pl.ds(b * rows, rows)

    def by_head(value):
        return jnp.concatenate(
            [jnp.where(lane_head == hd, value.astype(F32), 0.0).astype(BF) for hd in range(heads)],
            axis=0,
        )

    parts = []
    for b in range(batches):
        k = r.kf[rows_of(b), :].astype(F32) * wide(r.tail[b])
        parts.append(
            (dot_tn(k.astype(BF), r.vf[rows_of(b), :]), jnp.sum(k, axis=0, keepdims=True))
        )
    fold(r.st_send, parts)
    state_send(0, r.st_send, r.st_recv, 1)
    loop(tokens // tm, project_query)

    for b in range(batches):
        q, k = r.qf[rows_of(b), :], r.kf[rows_of(b), :]
        acc = jnp.zeros((rows, local), F32)
        for hd in range(heads):
            sc = dot_nt(jnp.where(lane_head == hd, q.astype(F32), 0.0).astype(BF), k) * r.mask[b]
            r.low[b, :, hd * rows : (hd + 1) * rows] = sc.astype(BF)
            acc = acc + jnp.where(lane_head == hd, jnp.sum(sc, axis=1, keepdims=True), 0.0)
        r.denom[rows_of(b), :] = acc
        r.numer[rows_of(b), :] = dot_nn(r.low[b], by_head(r.vf[rows_of(b), :]))

    for c in (0, 1):
        hg_finish(1, c)
    ag_pass(UP, 0)
    ag_send(DOWN, 0)
    state_wait(0, r.st_recv)

    def both(b, value, thr):
        one = value.astype(F32) * wide(r.car[b])
        return jnp.concatenate([one.astype(BF), (one * thr).astype(BF)], axis=1)

    for b in range(batches):
        left = both(b, r.qf[rows_of(b), :], before_thr[b])
        states = jnp.concatenate([unfold(r.st_recv, i, b) for i in (0, 1)], axis=0)
        only = lax.broadcasted_iota(jnp.int32, (16, local), 0)
        sums = jnp.concatenate(
            [
                jnp.where(
                    same_head,
                    dot_tn(
                        jnp.where(
                            only == b, r.st_recv[i, batches * DH :, :].astype(F32), 0.0
                        ).astype(BF),
                        jnp.ones((16, local), BF),
                    ),
                    0.0,
                ).astype(BF)
                for i in (0, 1)
            ],
            axis=0,
        )
        top = r.numer[rows_of(b), :] + dot_nn(left, states)
        bottom = r.denom[rows_of(b), :] + dot_nn(left, sums)
        attn = top / jnp.maximum(bottom, 1.0)
        r.numer[rows_of(b), :] = attn
        r.denom[rows_of(b), :] = bottom
        r.mixed[rows_of(b), :] = attn.astype(BF)

    hr_first(0, 0, pick(r.mixed), product_nt(r.wo))
    hr_first(0, 1, pick(r.mixed), product_nt(r.wo))
    hr_second(0, 0)
    hr_second(0, 1)
    ag_pass(UP, 1)
    mine = h * own

    def x_rows(at_row):
        return r.xg[hi, ds(lo * own + at_row, tile), :].astype(F32)

    def c_rows(at_row):
        return r.cg[hi, ds(lo * own + at_row, tile), :].astype(F32)

    def norm_two(c):
        def some(i):
            at_row = c * part_rows + i * tile
            v = x_rows(at_row) + hr_value(0, c, ds(i * tile, tile))
            r.middle[ds(at_row, tile), :] = v
            u, _ = unit(v)
            r.ntwo[ds(mine + at_row, tile), :] = (u * gain_two + shift_two).astype(BF)

        loop(part_rows // tile, some)

    for c in (0, 1):
        hr_wait(0, c)
        norm_two(c)
        hg_start(2, c)
    ag_pass(DOWN, 0)
    hg_forward(2, 0)
    hg_forward(2, 1)
    ag_pass(UP, 2)
    hg_finish(2, 0)
    hg_finish(2, 1)
    ag_pass(DOWN, 1)
    ag_wait(UP, 3)

    tu = 256

    def up(i):
        rw = ds(lax.div(i, hidden // tn) * tu, tu)
        cols = ds(lax.rem(i, hidden // tn) * tn, tn)
        v = dot_nn(r.ntwo[rw, :], r.wu[:, cols]) + r.smallg[5:6, cols]
        square_of = v * v
        t = jnp.tanh(0.7978845608028654 * (v + 0.044715 * (square_of * v)))
        half = 0.5 * (1.0 + t)
        r.activ[rw, cols] = (v * half).astype(BF)
        r.gelu_d[rw, cols] = half + (0.5 * v) * (1.0 - t * t) * (
            0.7978845608028654 + (3.0 * 0.044715 * 0.7978845608028654) * square_of
        )

    loop((tokens // tu) * (hidden // tn), up)
    near = [ds(at(p + n + i) * block, block) for i in range(1 - hops, hops)]

    def back_near(i):
        cols = ds(i * tn, tn)
        right = jnp.concatenate([r.wd[rw, cols] for rw in near], axis=0)
        for b in range(batches):
            left = jnp.concatenate([r.cg[b, :, rw] for rw in near], axis=1)
            r.g_act[rows_of(b), cols] = dot_nn(left, right)

    rs_round(DOWN, 0)
    ag_pass(DOWN, 2)
    rs_round(DOWN, 1)
    loop(hidden // tn, back_near)
    ag_wait(DOWN, 3)

    far_block = ds(at(p + hops) * block, block)

    def back(i):
        cols = ds(i * tn, tn)
        for b in range(batches):
            rw = rows_of(b)
            g = r.g_act[rw, cols] + dot_nn(r.cg[b, :, far_block], r.wd[far_block, cols])
            r.g_hid[rw, cols] = (g * r.gelu_d[rw, cols]).astype(BF)

    loop(hidden // tn, back)
    rs_round(UP, 0)
    hr_first(2, 0, pick(r.g_hid), product_nt(r.wu))
    hr_first(2, 1, pick(r.g_hid), product_nt(r.wu))
    rs_round(DOWN, 2)
    hr_second(2, 0)
    hr_second(2, 1)

    r.hs_send[...] = jnp.zeros_like(r.hs_send)

    def back_norm(g, u, inverse, gain):
        scaled = g * gain
        centered = scaled - jnp.mean(scaled, axis=1, keepdims=True)
        return inverse * (centered - u * jnp.mean(scaled * u, axis=1, keepdims=True))

    def norm_two_back(c):
        def some(i):
            at_row = c * part_rows + i * tile
            rw = ds(at_row, tile)
            g = hr_value(2, c, ds(i * tile, tile))
            u, inverse = unit(r.middle[rw, :])
            out = c_rows(at_row)
            v = out + back_norm(g, u, inverse, gain_two)
            r.g_mid[rw, :] = v
            r.gatt[ds(mine + at_row, tile), :] = v.astype(BF)
            r.hs_send[1:2, :] += jnp.sum(g * u, axis=0, keepdims=True)
            r.hs_send[3:4, :] += jnp.sum(g, axis=0, keepdims=True)
            r.hs_send[4:5, :] += jnp.sum(out, axis=0, keepdims=True)

        loop(part_rows // tile, some)

    hr_wait(2, 0)
    norm_two_back(0)
    hg_start(3, 0)
    rs_round(UP, 1)
    hr_wait(2, 1)
    norm_two_back(1)
    hg_start(3, 1)
    hr_first(1, 0, pick(r.activ), product_nt(r.wd))
    hr_first(1, 1, pick(r.activ), product_nt(r.wd))
    rs_round(DOWN, 3)
    for c in (0, 1):
        hg_forward(3, c)
    for c in (0, 1):
        hr_second(1, c)
    for c in (0, 1):
        hg_finish(3, c)

    def mixed_back(i):
        rw = ds(i * tm, tm)
        g = dot_nn(r.gatt[rw, :], r.wo[...])
        attn, bottom = r.numer[rw, :], r.denom[rw, :]
        r.g_num[rw, :] = (g / jnp.maximum(bottom, 1.0)).astype(BF)
        prod = g * attn
        lh = lane_head[:tm]
        acc = jnp.zeros((tm, local), F32)
        for hd in range(heads):
            acc = acc + jnp.where(
                lh == hd,
                jnp.sum(jnp.where(lh == hd, prod, 0.0), axis=1, keepdims=True),
                0.0,
            )
        r.g_den[rw, :] = jnp.where(bottom > 1.0, -acc / jnp.maximum(bottom, 1.0), 0.0)

    loop(tokens // tm, mixed_back)

    parts = []
    for b in range(batches):
        q = r.qf[rows_of(b), :].astype(F32) * wide(r.car[b])
        parts.append(
            (
                dot_tn(q.astype(BF), r.g_num[rows_of(b), :]),
                jnp.sum(q * r.g_den[rows_of(b), :], axis=0, keepdims=True),
            )
        )
    fold(r.gs_send, parts)
    state_send(1, r.gs_send, r.gs_recv, -1)
    rs_round(UP, 2)

    def head_lanes(hd, value):
        return jnp.where(lane_head == hd, value.astype(F32), 0.0).astype(BF)

    for b in range(batches):
        rw = rows_of(b)
        gk = jnp.zeros((rows, local), F32)
        gv = jnp.zeros((rows, local), F32)
        gq = jnp.zeros((rows, local), F32)
        for hd in range(heads):
            gn = head_lanes(hd, r.g_num[rw, :])
            g = dot_nt(gn, r.vf[rw, :]) + r.g_den[rw, hd * DH : hd * DH + 1]
            g = (g * r.mask[b]).astype(BF)
            gq = gq + dot_nn(g, head_lanes(hd, r.kf[rw, :]))
            gk = gk + dot_tn(g, head_lanes(hd, r.qf[rw, :]))
            gv = gv + dot_tn(r.low[b, :, hd * rows : (hd + 1) * rows], gn)
        left = both(b, r.g_num[rw, :], before_thr[b])
        states = jnp.concatenate([unfold(r.st_recv, i, b) for i in (0, 1)], axis=1)
        totals = unfold_sum(r.st_recv, 0, b) + before_thr[b] * unfold_sum(r.st_recv, 1, b)
        gq = gq + dot_nt(left, states) + wide(r.car[b]) * r.g_den[rw, :] * totals
        r.gproj[0, rw, :] = (gq * r.phi_d[0, rw, :]).astype(BF)
        r.gk[rw, :] = gk
        r.gv[rw, :] = gv

    rs_round(OUT, 0)
    rs_round(QUERY, 0)
    state_wait(1, r.gs_recv)
    for b in range(batches):
        rw = rows_of(b)
        thr = after_thr[b]
        states = [unfold(r.gs_recv, i, b) for i in (0, 1)]
        totals = unfold_sum(r.gs_recv, 0, b) + thr * unfold_sum(r.gs_recv, 1, b)
        k = r.kf[rw, :].astype(F32) * wide(r.tail[b])
        v = r.vf[rw, :].astype(F32) * wide(r.tail[b])
        k2 = jnp.concatenate([k.astype(BF), (k * thr).astype(BF)], axis=1)
        v2 = jnp.concatenate([v.astype(BF), (v * thr).astype(BF)], axis=1)
        gk = r.gk[rw, :] + dot_nt(v2, jnp.concatenate(states, axis=1)) + wide(r.tail[b]) * totals
        gv = r.gv[rw, :] + dot_nn(k2, jnp.concatenate(states, axis=0))
        r.gproj[1, rw, :] = (gk * wide(r.pmc[b]) * r.phi_d[1, rw, :]).astype(BF)
        r.gproj[2, rw, :] = gv.astype(BF)

    rs_round(QKV, 0)

    def picks(where):
        return [
            jnp.concatenate([r.gproj[kind, rw, :] for rw in where], axis=0) for kind in range(3)
        ]

    def first_term(left, cols):
        v = dot_nt(left[0], r.wq[0, cols, :])
        for kind in (1, 2):
            v = v + dot_nt(left[kind], r.wq[kind, cols, :])
        return v

    hr_first(3, 0, picks, first_term)
    hr_first(3, 1, picks, first_term)
    hr_second(3, 0)
    hr_second(3, 1)
    rs_round(OUT, 1)
    rs_round(QUERY, 1)
    rs_round(QKV, 1)
    rs_round(UP, 3)

    def norm_one_back(c):
        def some(i):
            at_row = c * part_rows + i * tile
            rw = ds(at_row, tile)
            g = hr_value(3, c, ds(i * tile, tile))
            u, inverse = unit(x_rows(at_row))
            r.i_rows[rw, :] = r.g_mid[rw, :] + back_norm(g, u, inverse, gain_one)
            r.hs_send[0:1, :] += jnp.sum(g * u, axis=0, keepdims=True)
            r.hs_send[2:3, :] += jnp.sum(g, axis=0, keepdims=True)

        loop(part_rows // tile, some)

    for c in (0, 1):
        hr_wait(3, c)
        norm_one_back(c)
    turn(1, r.i_rows, r.ing_o)
    rs_round(OUT, 2)
    rs_round(QUERY, 2)
    rs_round(QKV, 2)

    def finish_rows(c):
        def some(i):
            rw = ds(c * part_rows + i * tile, tile)
            r.a_rows[rw, :] = r.middle[rw, :] + hr_value(1, c, ds(i * tile, tile)) + shift_out

        loop(part_rows // tile, some)

    for c in (0, 1):
        hr_wait(1, c)
        finish_rows(c)
    turn(0, r.a_rows, r.act_o)

    r.hs_recv[h] = r.hs_send[...]
    for i in range(1, m):
        remote(
            r.hs_send, r.hs_recv.at[h], r.hs_s.at[0], r.hs_r.at[0], s, lax.rem(h + i, m)
        ).start()
    r.upb[...] = jnp.zeros_like(r.upb)

    def column_sums(i):
        r.upb[...] += jnp.sum(r.g_hid[ds(i * tile, tile), :].astype(F32), axis=0, keepdims=True)

    loop(tokens // tile, column_sums)
    rs_round(OUT, 3)
    rs_round(QUERY, 3)
    rs_final(DOWN)
    rs_round(QKV, 3)
    landed(r.hs_recv.at[pl.ds(0, m - 1)], r.hs_r.at[0])
    acc = r.hs_recv[0]
    for i in range(1, m):
        acc = acc + r.hs_recv[i]
    r.sg[...] = acc
    r.sg[5:6, :] = r.upb[...]
    r.ss_recv[s] = r.sg[:, ds(s * block, block)]
    for i in range(1, n):
        to = lax.rem(s + i, n)
        remote(
            r.sg.at[:, ds(to * block, block)],
            r.ss_recv.at[s],
            r.ss_s.at[0],
            r.ss_r.at[0],
            to,
            h,
        ).start()
    rs_final(UP)
    rs_final(OUT)
    rs_final(QUERY)
    landed(r.ss_recv.at[pl.ds(0, n - 1)], r.ss_r.at[0])
    acc = r.ss_recv[0]
    for i in range(1, n):
        acc = acc + r.ss_recv[i]
    r.gg_o[...] = acc[0:2]
    r.gb_o[...] = acc[2:5]
    r.gup_o[...] = acc[5:6]
    turn_wait(0, r.a_rows)
    turn_wait(1, r.i_rows)

    far = pl.ds(0, (n - 1) * block)
    for w in range(5):
        views = (r.wq.at[:, far, :], r.wo.at[far], r.wu.at[far], r.wd.at[far], r.smallg.at[:, far])
        drained(views[w], r.ag_s.at[w])
    others = pl.ds(0, (m - 1) * local)
    rest = pl.ds(0, (m - 1) * own)
    for k in range(4):
        view = (r.xg, r.cg)[k].at[:, :, others] if k < 2 else (r.ntwo, r.gatt)[k - 2].at[rest]
        drained(view, r.hg_s.at[k])
        drained(r.h_s1.at[k], r.hr_s.at[k, 0])
        drained(r.h_s2.at[k], r.hr_s.at[k, 1])
    for k, dest in enumerate((r.st_recv, r.gs_recv)):
        drained(dest, r.st_s.at[k])
    drained(r.a_rows.at[:, others], r.aa_s.at[0])
    drained(r.i_rows.at[:, others], r.aa_s.at[1])
    drained(r.hs_recv.at[pl.ds(0, m - 1)], r.hs_s.at[0])
    drained(r.ss_recv.at[pl.ds(0, n - 1)], r.ss_s.at[0])
    rs_final(QKV)
    for w in range(5):
        drained(rs_send[w].at[pl.ds(0, n - 1)], r.rs_s.at[w])
    for copy in local_copies:
        copy.wait()


def settle(*refs):
    count = len(refs) // 2
    copies = [
        pltpu.make_async_copy(refs[i], refs[count + i], refs[-1].at[i]) for i in range(count)
    ]
    for copy in copies:
        copy.start()
    for copy in copies:
        copy.wait()


def whole_layer(n, m):
    def on_each(
        tokens, cotangent, w_qkv, w_out_t, w_up, w_down_t, gains, biases, up_bias, lengths, pixel_mask
    ):
        batches, rows, local = tokens.shape
        width = w_qkv.shape[0] * n
        hidden = w_up.shape[1]
        block = width // n
        vm, sems = layout(n, m, batches, rows, width, local, hidden)
        ins = ["tok", "cot", "w_qkv", "w_out", "w_up", "w_down", "gains", "biases", "up_bias", "lengths", "pixel"]
        outs = ["act_o", "ing_o", "gq_o", "go_o", "gu_o", "gd_o", "gg_o", "gb_o", "gup_o"]
        anywhere = pl.BlockSpec(memory_space=pl.ANY)
        in_vmem = pl.BlockSpec(memory_space=pltpu.VMEM)
        in_smem = pl.BlockSpec(memory_space=pltpu.SMEM)

        result = pl.pallas_call(
            functools.partial(body, n, m, ins + outs + list(vm) + list(sems)),
            name="layer",
            out_shape=(
                pltpu.VMEM((batches, rows, local), F32),
                pltpu.VMEM((batches, rows, local), F32),
                pltpu.VMEM((3, block, local), F32),
                pltpu.VMEM((block, local), F32),
                pltpu.VMEM((block, hidden), F32),
                pltpu.VMEM((block, hidden), F32),
                pltpu.VMEM((2, block), F32),
                pltpu.VMEM((3, block), F32),
                pltpu.VMEM((1, block), F32),
            ),
            in_specs=[anywhere] * 6 + [in_vmem] * 3 + [in_smem, in_vmem],
            out_specs=[in_vmem] * 9,
            scratch_shapes=[pltpu.VMEM(shape, kind) for shape, kind in vm.values()]
            + [pltpu.SemaphoreType.DMA(shape) for shape in sems.values()],
            compiler_params=pltpu.CompilerParams(
                collective_id=0, has_side_effects=True, vmem_limit_bytes=60_000_000
            ),
        )(
            tokens,
            cotangent,
            jnp.transpose(w_qkv, (1, 0, 2)),
            w_out_t,
            w_up,
            w_down_t,
            gains,
            biases,
            up_bias,
            lengths,
            pixel_mask,
        )
        result = pl.pallas_call(
            settle,
            name="settle",
            out_shape=[jax.ShapeDtypeStruct(a.shape, a.dtype) for a in result],
            in_specs=[in_vmem] * len(result),
            out_specs=[anywhere] * len(result),
            scratch_shapes=[pltpu.SemaphoreType.DMA((len(result),))],
        )(*[pltpu.with_memory_space_constraint(a, pltpu.VMEM) for a in result])
        return (*result[:2], jnp.transpose(result[2], (1, 0, 2)), *result[3:])

    return on_each


def solution(mesh):
    in_specs = (
        P(None, "seq", "head"),
        P(None, "seq", "head"),
        P("seq", None, "head"),
        P("seq", "head"),
        P("seq", "head"),
        P("seq", "head"),
        P(None, "seq"),
        P(None, "seq"),
        P("head", "seq"),
        P(),
        P(None, "seq"),
    )
    out_specs = (
        P(None, "seq", "head"),
        P(None, "seq", "head"),
        P("seq", None, "head"),
        P("seq", "head"),
        P("seq", "head"),
        P("seq", "head"),
        P(None, "seq"),
        P(None, "seq"),
        P("head", "seq"),
    )
    n, m = mesh.shape["seq"], mesh.shape["head"]
    fits = (n, m) == (8, 4)
    return jax.shard_map(
        whole_layer(n, m) if fits else on_device, mesh=mesh, in_specs=in_specs, out_specs=out_specs, check_vma=False
    )
```

```python
import functools

import jax
import jax.numpy as jnp
from jax import lax
from jax.experimental import pallas as pl
from jax.experimental.pallas import tpu as pltpu
from jax.sharding import PartitionSpec as P

DH = 64


highest = lax.Precision.HIGHEST
epsilon = 1e-05


def entering(array, axis, join, neutral):
    place = lax.axis_index(axis)
    gathered = jax.tree.map(
        lambda a, kind: lax.all_gather(a.astype(kind), axis),
        array,
        (jnp.bfloat16, jnp.bfloat16, jnp.bfloat16),
    )
    state = jax.tree.map(lambda a, e: jnp.zeros_like(a) + jnp.asarray(e, a.dtype), array, neutral)

    def one(hop, state):
        return join(
            state,
            jax.tree.map(
                lambda a, own: lax.dynamic_index_in_dim(a, hop, 0, False).astype(own.dtype),
                gathered,
                array,
            ),
        )

    return lax.fori_loop(0, place, one, state)


def entering_2(array, axis, combine, identity):
    length, place = (lax.axis_size(axis), lax.axis_index(axis))
    everything = jax.tree.map(
        lambda part, kind: lax.all_gather(part.astype(kind), axis),
        array,
        jax.tree.map(lambda a: jnp.bfloat16 if a.dtype == jnp.float32 else a.dtype, array),
    )
    start = jax.tree.map(
        lambda part, zero: jnp.broadcast_to(jnp.asarray(zero, part.dtype), part.shape),
        array,
        identity,
    )

    def hop(k, before):
        at = length - 1 - k
        reached = at > place
        new = combine(
            before, jax.tree.map(lambda part, own: part[at].astype(own.dtype), everything, array)
        )
        return jax.tree.map(lambda a, b: jnp.where(reached, a, b), new, before)

    return lax.fori_loop(0, length, hop, start)


def normalize(values, gain_vec, shift_vec):
    mean_val = jnp.mean(values, axis=-1, keepdims=True)
    centered = values - mean_val
    inverse = lax.rsqrt(jnp.mean(centered * centered, axis=-1, keepdims=True) + epsilon)
    unit_val = centered * inverse
    return (unit_val * gain_vec + shift_vec, unit_val, inverse)


def norm_back(grad_in, unit_val, inverse, gain_vec):
    scaled = grad_in * gain_vec
    centered = scaled - jnp.mean(scaled, axis=-1, keepdims=True)
    return inverse * (centered - unit_val * jnp.mean(scaled * unit_val, axis=-1, keepdims=True))


def features(values):
    return jax.nn.elu(values) + 1.0


def finish(numerator, denominator):
    return numerator / jnp.maximum(denominator, 1.0)[:, :, None]


def compose(earlier, later):
    return (
        later[0] + later[2] * earlier[0],
        later[1] + later[2] * earlier[1],
        later[2] * earlier[2],
    )


def item_numbers(lengths_row, first_place, number):
    offsets = jnp.cumsum(lengths_row) - lengths_row
    places = first_place + jnp.arange(number, dtype=jnp.int32)
    return jnp.sum((offsets[None, :] <= places[:, None]).astype(jnp.int32), axis=1) - 1


def on_device(
    tokens, cotangent, w_qkv, w_out_t, w_up, w_down_t, gains, biases, up_bias, lengths, pixel_mask
):
    batches, local_rows, columns = tokens.shape
    local_width = w_qkv.shape[2]
    heads_here = local_width // DH
    seq_index = lax.axis_index("seq")
    head_index = lax.axis_index("head")
    first_token = seq_index * local_rows
    position = jnp.arange(local_rows, dtype=jnp.int32)
    before = position[:, None] >= position[None, :]

    def own_columns(matrix):
        return lax.dynamic_slice_in_dim(matrix, head_index * columns, columns, 1)

    results = []
    input_grads = []
    shard_sums = None
    for batch_index in range(batches):
        full_qkv, full_out, full_up, full_down, full_gains, full_biases, full_upb = (
            lax.all_gather(w_qkv, "seq", axis=0, tiled=True),
            lax.all_gather(w_out_t, "seq", axis=0, tiled=True),
            lax.all_gather(w_up, "seq", axis=0, tiled=True),
            lax.all_gather(w_down_t, "seq", axis=0, tiled=True),
            lax.all_gather(gains, "seq", axis=1, tiled=True),
            lax.all_gather(biases, "seq", axis=1, tiled=True),
            lax.all_gather(up_bias, "seq", axis=1, tiled=True),
        )
        input_rows, grad_rows16 = (
            lax.all_gather(tokens[batch_index], "head", axis=1, tiled=True),
            lax.all_gather(cotangent[batch_index], "head", axis=1, tiled=True),
        )
        gains32 = full_gains.astype(jnp.float32)
        biases32 = full_biases.astype(jnp.float32)
        upb32 = full_upb.astype(jnp.float32).reshape(-1)
        inputs32 = input_rows.astype(jnp.float32)
        place_items = item_numbers(lengths[batch_index], first_token - 1, local_rows + 1)
        item_of = place_items[1:]
        carried = (item_of == place_items[0]).astype(jnp.float32)
        tail_mask = (item_of == item_of[local_rows - 1]).astype(jnp.float32)
        through = carried[local_rows - 1]
        same_item = ((item_of[:, None] == item_of[None, :]) & before).astype(jnp.float32)
        keep_half = pixel_mask[batch_index].astype(jnp.bfloat16)
        keep32 = pixel_mask[batch_index].astype(jnp.float32)
        lifted, unit_one, inverse_one = normalize(inputs32, gains32[0], biases32[0])
        normed = lifted.astype(jnp.bfloat16)
        projected = jnp.einsum("td,dsf->tsf", normed, full_qkv, preferred_element_type=jnp.float32)
        query_feat = (
            features(projected[:, 0]).astype(jnp.bfloat16).reshape(local_rows, heads_here, DH)
        )
        key_feat = (features(projected[:, 1]).astype(jnp.bfloat16) * keep_half[:, None]).reshape(
            local_rows, heads_here, DH
        )
        value_feat = projected[:, 2].astype(jnp.bfloat16).reshape(local_rows, heads_here, DH)
        tail_key = key_feat * tail_mask.astype(jnp.bfloat16)[:, None, None]
        state_loc = jnp.einsum(
            "jhd,jhe->hde", tail_key, value_feat, preferred_element_type=jnp.float32
        )
        total_loc = jnp.sum(tail_key.astype(jnp.float32), axis=0)
        identity = (jnp.zeros_like(state_loc), jnp.zeros_like(total_loc), jnp.ones((), jnp.float32))
        state_in, total_in, passed = entering(
            (state_loc, total_loc, through), "seq", compose, identity
        )
        query32 = query_feat.astype(jnp.float32)
        scores = (
            jnp.einsum("thd,jhd->htj", query_feat, key_feat, preferred_element_type=jnp.float32)
            * same_item[None]
        )
        scores_low = scores.astype(jnp.bfloat16)
        numerator = jnp.einsum(
            "htj,jhe->the", scores_low, value_feat, preferred_element_type=jnp.float32
        ) + carried[:, None, None] * jnp.einsum(
            "thd,hde->the", query32, state_in, precision=highest
        )
        denominator = jnp.sum(scores, axis=2).T + carried[:, None] * jnp.einsum(
            "thd,hd->th", query32, total_in, precision=highest
        )
        output, finish_back = jax.vjp(finish, numerator, denominator)
        mixed_out = output.reshape(local_rows, local_width).astype(jnp.bfloat16)
        attended = lax.psum(
            jnp.einsum("tf,df->td", mixed_out, full_out, preferred_element_type=jnp.float32).astype(
                jnp.bfloat16
            ),
            "head",
        ).astype(jnp.float32)
        middle = inputs32 + attended
        lifted_two, unit_two, inverse_two = normalize(middle, gains32[1], biases32[1])
        normed_two = lifted_two.astype(jnp.bfloat16)
        hidden = jnp.dot(normed_two, full_up, preferred_element_type=jnp.float32) + upb32
        activated32, gelu_back = jax.vjp(jax.nn.gelu, hidden)
        activated = activated32.astype(jnp.bfloat16)
        branch = lax.psum_scatter(
            jnp.einsum(
                "tf,df->td", activated, full_down, preferred_element_type=jnp.float32
            ).astype(jnp.bfloat16),
            "head",
            scatter_dimension=1,
            tiled=True,
        ).astype(jnp.float32)
        results.append(own_columns(middle) + branch + own_columns(biases32[2][None]))
        grad_out = grad_rows16.astype(jnp.float32)
        grad_down = jnp.einsum(
            "td,tf->df", grad_rows16, activated, preferred_element_type=jnp.float32
        )
        grad_act = jnp.einsum(
            "td,df->tf", grad_rows16, full_down, preferred_element_type=jnp.float32
        )
        grad_hidden = gelu_back(grad_act)[0].astype(jnp.bfloat16)
        grad_up = jnp.einsum(
            "td,tf->df", normed_two, grad_hidden, preferred_element_type=jnp.float32
        )
        grad_upb = jnp.sum(grad_hidden.astype(jnp.float32), axis=0).reshape(full_upb.shape)
        grad_two = lax.psum(
            jnp.einsum(
                "tf,df->td", grad_hidden, full_up, preferred_element_type=jnp.float32
            ).astype(jnp.bfloat16),
            "head",
        ).astype(jnp.float32)
        grad_middle = grad_out + norm_back(grad_two, unit_two, inverse_two, gains32[1])
        grad_attended = grad_middle.astype(jnp.bfloat16)
        grad_out_t = jnp.einsum(
            "td,tf->df", grad_attended, mixed_out, preferred_element_type=jnp.float32
        )
        grad_mixed = jnp.einsum(
            "td,df->tf", grad_attended, full_out, preferred_element_type=jnp.float32
        ).reshape(local_rows, heads_here, DH)
        grad_numer32, grad_denom = finish_back(grad_mixed)
        grad_numer = grad_numer32.astype(jnp.bfloat16)
        grad_numer_wide = grad_numer.astype(jnp.float32)
        grad_scores = (
            (
                jnp.einsum(
                    "the,jhe->htj", grad_numer, value_feat, preferred_element_type=jnp.float32
                )
                + grad_denom.T[:, :, None]
            )
            * same_item[None]
        ).astype(jnp.bfloat16)
        carried_query = query32 * carried[:, None, None]
        grad_query = jnp.einsum(
            "htj,jhd->thd", grad_scores, key_feat, preferred_element_type=jnp.float32
        ) + carried[:, None, None] * (
            jnp.einsum("hde,the->thd", state_in, grad_numer_wide, precision=highest)
            + grad_denom[:, :, None] * total_in[None]
        )
        grad_key = jnp.einsum(
            "htj,thd->jhd", grad_scores, query_feat, preferred_element_type=jnp.float32
        )
        grad_value = jnp.einsum(
            "htj,the->jhe", scores_low, grad_numer, preferred_element_type=jnp.float32
        )
        grad_state_in = jnp.einsum(
            "thd,the->hde", carried_query, grad_numer_wide, precision=highest
        )
        grad_total_in = jnp.einsum("thd,th->hd", carried_query, grad_denom, precision=highest)
        grad_state_loc, grad_total_loc, passed_back = entering_2(
            (grad_state_in, grad_total_in, through), "seq", compose, identity
        )
        tail_three = tail_mask[:, None, None]
        value_wide = value_feat.astype(jnp.float32)
        key_wide = key_feat.astype(jnp.float32)
        grad_key = grad_key + tail_three * (
            jnp.einsum("hde,jhe->jhd", grad_state_loc, value_wide, precision=highest)
            + grad_total_loc[None]
        )
        grad_value = grad_value + tail_three * jnp.einsum(
            "jhd,hde->jhe", key_wide, grad_state_loc, precision=highest
        )
        ignored, feature_back = jax.vjp(features, projected[:, :2])
        grad_features = jnp.stack(
            [
                grad_query.reshape(local_rows, local_width),
                grad_key.reshape(local_rows, local_width) * keep32[:, None],
            ],
            axis=1,
        )
        grad_pair = feature_back(grad_features)[0]
        grad_projected = jnp.concatenate(
            [grad_pair, grad_value.reshape(local_rows, 1, local_width)], axis=1
        ).astype(jnp.bfloat16)
        grad_qkv = jnp.einsum(
            "td,tsf->dsf", normed, grad_projected, preferred_element_type=jnp.float32
        )
        grad_one = lax.psum(
            jnp.einsum(
                "tsf,dsf->td", grad_projected, full_qkv, preferred_element_type=jnp.float32
            ).astype(jnp.bfloat16),
            "head",
        ).astype(jnp.float32)
        grad_inputs = grad_middle + norm_back(grad_one, unit_one, inverse_one, gains32[0])
        input_grads.append(own_columns(grad_inputs))
        grad_gains = jnp.stack(
            [jnp.sum(grad_one * unit_one, axis=0), jnp.sum(grad_two * unit_two, axis=0)]
        )
        grad_biases = jnp.stack(
            [jnp.sum(grad_one, axis=0), jnp.sum(grad_two, axis=0), jnp.sum(grad_out, axis=0)]
        )
        pieces = (
            lax.psum_scatter(grad_qkv, "seq", scatter_dimension=0, tiled=True),
            lax.psum_scatter(grad_out_t, "seq", scatter_dimension=0, tiled=True),
            lax.psum_scatter(grad_up, "seq", scatter_dimension=0, tiled=True),
            lax.psum_scatter(grad_down, "seq", scatter_dimension=0, tiled=True),
            lax.psum_scatter(grad_gains, "seq", scatter_dimension=1, tiled=True),
            lax.psum_scatter(grad_biases, "seq", scatter_dimension=1, tiled=True),
            lax.psum_scatter(grad_upb, "seq", scatter_dimension=1, tiled=True),
        )
        shard_sums = pieces if shard_sums is None else jax.tree.map(jnp.add, shard_sums, pieces)
    return (
        jnp.stack(results),
        jnp.stack(input_grads),
        shard_sums[0],
        shard_sums[1],
        shard_sums[2],
        shard_sums[3],
        shard_sums[4],
        shard_sums[5],
        shard_sums[6],
    )


MESH = pl.DeviceIdType.MESH
BF = jnp.bfloat16
F32 = jnp.float32
QKV, OUT, UP, DOWN, SMALL = range(5)
QUERY = 4


def dot_nn(a, b):
    return lax.dot_general(a, b, (((1,), (0,)), ((), ())), preferred_element_type=F32)


def dot_nt(a, b):
    return lax.dot_general(a, b, (((1,), (1,)), ((), ())), preferred_element_type=F32)


def dot_tn(a, b):
    return lax.dot_general(a, b, (((0,), (0,)), ((), ())), preferred_element_type=F32)


def ds(start, size):
    return pl.ds(pl.multiple_of(start, size), size)


def loop(count, body):
    def step(i, carry):
        body(i)
        return carry

    lax.fori_loop(0, count, step, 0)


def layout(n, m, batches, rows, width, local, hidden):
    tokens = batches * rows
    block = width // n
    own = tokens // m
    hops = n // 2
    heads = local // DH
    vm = {
        "xg": ((batches, rows, width), BF),
        "cg": ((batches, rows, width), BF),
        "wq": ((3, width, local), BF),
        "wo": ((width, local), BF),
        "wu": ((width, hidden), BF),
        "wd": ((width, hidden), BF),
        "small": ((8, block), F32),
        "smallg": ((8, width), F32),
        "normed": ((tokens, width), BF),
        "phi_d": ((2, tokens, local), F32),
        "qf": ((tokens, local), BF),
        "kf": ((tokens, local), BF),
        "vf": ((tokens, local), BF),
        "mask": ((batches, rows, rows), F32),
        "car": ((batches, rows, 128), F32),
        "tail": ((batches, rows, 128), F32),
        "pmc": ((batches, rows, 128), F32),
        "low": ((batches, rows, heads * rows), BF),
        "numer": ((tokens, local), F32),
        "denom": ((tokens, local), F32),
        "mixed": ((tokens, local), BF),
        "st_send": ((batches * DH + 16, local), BF),
        "st_recv": ((2, batches * DH + 16, local), BF),
        "gs_send": ((batches * DH + 16, local), BF),
        "gs_recv": ((2, batches * DH + 16, local), BF),
        "middle": ((own, width), F32),
        "ntwo": ((tokens, width), BF),
        "gelu_d": ((tokens, hidden), F32),
        "activ": ((tokens, hidden), BF),
        "g_hid": ((tokens, hidden), BF),
        "branch": ((own, width), F32),
        "total": ((own, width), F32),
        "g_mid": ((own, width), F32),
        "gatt": ((tokens, width), BF),
        "g_attn": ((tokens, local), F32),
        "g_num": ((tokens, local), BF),
        "g_den": ((tokens, local), F32),
        "gq": ((tokens, local), F32),
        "gk": ((tokens, local), F32),
        "gv": ((tokens, local), F32),
        "gproj": ((3, tokens, local), BF),
        "h_s1": ((4, 2, 2, own // 2, width), BF),
        "h_r1": ((4, 2, 2, own // 2, width), BF),
        "h_acc": ((4, 2, 2, own // 2, width), F32),
        "h_s2": ((4, 2, own // 2, width), BF),
        "h_r2": ((4, 2, own // 2, width), BF),
        "rq_s": ((n, 2, block, local), BF),
        "rq_r": ((n, 2, block, local), BF),
        "rx_s": ((n, block, local), BF),
        "rx_r": ((n, block, local), BF),
        "ro_s": ((n, block, local), BF),
        "ro_r": ((n, block, local), BF),
        "ru_s": ((n, block, hidden), BF),
        "ru_r": ((n, block, hidden), BF),
        "rd_s": ((n, block, hidden), BF),
        "rd_r": ((n, block, hidden), BF),
        "pq": ((2, 2, block, local), F32),
        "po": ((2, block, local), F32),
        "pu": ((2, block, hidden), F32),
        "pd": ((2, block, hidden), F32),
        "px": ((2, block, local), F32),
        "g_act": ((tokens, hidden), F32),
        "hs_recv": ((m, 8, width), F32),
        "hs_send": ((8, width), F32),
        "upb": ((1, hidden), F32),
        "sg": ((8, width), F32),
        "ss_recv": ((n, 8, block), F32),
        "a_rows": ((own, width), F32),
        "i_rows": ((own, width), F32),
    }
    sems = {
        "ag_s": (5,),
        "ag_r": (5, 2, hops),
        "rs_s": (5,),
        "hg_s": (4,),
        "hg_r": (2, 2, 3),
        "hr_s": (4, 2),
        "hr_r": (2, 2, 2),
        "st_s": (2,),
        "st_r": (2,),
        "aa_s": (2,),
        "aa_r": (2,),
        "hs_s": (1,),
        "hs_r": (1,),
        "ss_s": (1,),
        "ss_r": (1,),
        "lc": (8,),
    }
    return vm, sems


class Refs:
    pass


def body(n, m, names, *refs):
    r = Refs()
    for name, ref in zip(names, refs):
        setattr(r, name, ref)
    batches, rows, width = r.xg.shape
    tokens = batches * rows
    own = tokens // m
    block = width // n
    local = r.wo.shape[1]
    hidden = r.wu.shape[1]
    heads = local // DH
    hops = n // 2
    s = lax.axis_index("seq")
    h = lax.axis_index("head")
    odd = lax.rem(s, 2)
    p = (1 - odd) * lax.div(s, 2) + odd * (n - 1 - lax.div(s, 2))
    lo, hi = lax.rem(h, 2), lax.div(h, 2)
    pair = h + 1 - 2 * lo
    cross = lax.rem(h + 2, m)

    def at(place):
        place = lax.rem(place + 2 * n, n)
        far = lax.div(place, hops)
        return (1 - far) * 2 * place + far * (2 * (n - 1 - place) + 1)

    ring = (at(p + 1), at(p - 1))
    sign = (1, -1)

    def remote(src, dst, send, recv, seq, head):
        return pltpu.make_async_remote_copy(
            src_ref=src,
            dst_ref=dst,
            send_sem=send,
            recv_sem=recv,
            device_id=(seq, head),
            device_id_type=MESH,
        )

    def drained(view, sem):
        remote(view, view, sem, sem, ring[0], h).wait_send()

    def landed(view, sem):
        remote(view, view, sem, sem, ring[0], h).wait_recv()

    barrier = pltpu.get_barrier_semaphore()
    for peer in ((ring[0], h), (ring[1], h), (s, pair), (s, cross)):
        pl.semaphore_signal(barrier, inc=1, device_id=peer, device_id_type=MESH)

    r.small[...] = jnp.zeros_like(r.small)
    r.small[0:2, :] = r.gains[...].astype(F32)
    r.small[2:5, :] = r.biases[...].astype(F32)
    r.small[5:6, :] = r.up_bias[...].astype(F32)

    first = s * rows
    row_at = lax.broadcasted_iota(jnp.int32, (rows, 128), 0)
    lane_at = lax.broadcasted_iota(jnp.int32, (rows, rows), 1)
    square = lax.broadcasted_iota(jnp.int32, (local, local), 0)
    square_lane = lax.broadcasted_iota(jnp.int32, (local, local), 1)
    same_head = (square // DH) == (square_lane // DH)
    diagonal = square == square_lane
    lane_head = lax.broadcasted_iota(jnp.int32, (rows, local), 1) // DH
    before_thr, after_thr = [], []

    def wide(value):
        return jnp.concatenate([value] * (local // 128), axis=1)

    def begin(offsets, place):
        value = 0
        for off in offsets:
            value = jnp.where(off <= place, off, value)
        return value

    def through(offsets, which):
        return jnp.where(
            begin(offsets, which * rows + rows - 1) < which * rows, 1.0, 0.0
        ).astype(F32)

    def crops(b):
        offsets, running = [], 0
        for i in range(r.lengths.shape[1]):
            offsets.append(running)
            running = running + r.lengths[b, i]
        start = jnp.zeros((rows, 128), jnp.int32)
        for off in offsets:
            start = jnp.where(off <= row_at + first, off, start)
        last = begin(offsets, first + rows - 1)
        r.mask[b] = jnp.where(
            (lane_at + first >= wide(start)) & (lane_at <= wide(row_at)), 1.0, 0.0
        ).astype(F32)
        r.car[b] = jnp.where(start < first, 1.0, 0.0).astype(F32)
        r.tail[b] = jnp.where(start == last, 1.0, 0.0).astype(F32)
        before_thr.append(through(offsets, lax.rem(s + n - 1, n)))
        after_thr.append(through(offsets, lax.rem(s + 1, n)))
        keep = r.pixel[b : b + 1, :].astype(F32)
        r.pmc[b] = dot_nn(
            jnp.where(diagonal, keep, 0.0).astype(BF), jnp.ones((rows, 128), BF)
        )

    crops(0)
    pl.semaphore_wait(barrier, 4)

    shards = (r.w_qkv, r.w_out, r.w_up, r.w_down, r.small)
    gathered = (r.wq, r.wo, r.wu, r.wd, r.smallg)

    def part_of(w, d, j):
        wide_part = r.wq.shape[2] if w == QKV else shards[w].shape[1]
        if j < hops - 1 or w == SMALL:
            return pl.ds(0, wide_part)
        return pl.ds(d * (wide_part // 2), wide_part // 2)

    def ag_shard(w, d, j):
        cols = part_of(w, d, j)
        if w == SMALL:
            return r.small
        return shards[w].at[:, :, cols] if w == QKV else shards[w].at[:, cols]

    def ag_full(w, owner, d, j):
        cols = part_of(w, d, j)
        if w == SMALL:
            return r.smallg.at[:, ds(owner * block, block)]
        if w == QKV:
            return r.wq.at[:, ds(owner * block, block), cols]
        return gathered[w].at[ds(owner * block, block), cols]

    def ways(w, j):
        return (0,) if w == SMALL and j == hops - 1 else (0, 1)

    def ag_send(w, j):
        for d in ways(w, j):
            owner = at(p - sign[d] * j)
            src = ag_shard(w, d, j) if j == 0 else ag_full(w, owner, d, j)
            remote(
                src, ag_full(w, owner, d, j), r.ag_s.at[w], r.ag_r.at[w, d, j], ring[d], h
            ).start()

    def ag_wait(w, j):
        for d in ways(w, j):
            landed(ag_full(w, at(p - sign[d] * (j + 1)), d, j), r.ag_r.at[w, d, j])

    def ag_pass(w, j):
        ag_wait(w, j)
        ag_send(w, j + 1)

    part_rows = own // 2

    def hg_view(k, c, who):
        if k < 2:
            return (r.xg, r.cg)[k].at[c, :, ds(who * local, local)]
        return (r.ntwo, r.gatt)[k - 2].at[ds(who * own + c * part_rows, part_rows), :]

    def hg_copy(k, c, i, src, who, to):
        return remote(src, hg_view(k, c, who), r.hg_s.at[k], r.hg_r.at[k % 2, c, i], s, to)

    def hg_start(k, c):
        src = (r.tok, r.cot)[k].at[c] if k < 2 else hg_view(k, c, h)
        hg_copy(k, c, 1, src, h, cross).start()
        hg_copy(k, c, 0, src, h, pair).start()

    def hg_forward(k, c):
        view = hg_view(k, c, cross)
        hg_copy(k, c, 1, view, cross, cross).wait_recv()
        hg_copy(k, c, 2, view, cross, pair).start()

    def hg_finish(k, c):
        view = hg_view(k, c, pair)
        hg_copy(k, c, 0, view, pair, pair).wait_recv()
        across = lax.rem(pair + 2, m)
        view = hg_view(k, c, across)
        hg_copy(k, c, 2, view, across, pair).wait_recv()

    tn = 256

    def hr_first(k, c, left, product):
        blocks = [2 * i + 1 - lo for i in (0, 1)] + [2 * i + lo for i in (0, 1)]
        where = [ds(who * own + c * part_rows, part_rows) for who in blocks]

        def some(i):
            cols = ds(i * tn, tn)
            v = product(left(where), cols)
            for q in (0, 1):
                r.h_s1[k, c, q, :, cols] = v[q * part_rows : (q + 1) * part_rows].astype(BF)
                r.h_acc[k, c, q, :, cols] = v[(q + 2) * part_rows : (q + 3) * part_rows]

        loop(width // tn, some)
        hr_copy(k, c, 0).start()

    def hr_copy(k, c, stage):
        if stage == 0:
            src, dst, to = r.h_s1.at[k, c], r.h_r1.at[k, c], pair
        else:
            src, dst, to = r.h_s2.at[k, c], r.h_r2.at[k, c], cross
        return remote(src, dst, r.hr_s.at[k, stage], r.hr_r.at[k // 2, c, stage], s, to)

    def hr_second(k, c):
        hr_copy(k, c, 0).wait_recv()

        def away(i):
            rw = ds(i * 32, 32)
            r.h_s2[k, c, rw, :] = (
                r.h_acc[k, c, 1 - hi, rw, :] + r.h_r1[k, c, 1 - hi, rw, :].astype(F32)
            ).astype(BF)

        loop(part_rows // 32, away)
        hr_copy(k, c, 1).start()

    def hr_wait(k, c):
        hr_copy(k, c, 1).wait_recv()

    def hr_value(k, c, rw):
        return (
            r.h_acc[k, c, hi, rw, :]
            + r.h_r1[k, c, hi, rw, :].astype(F32)
            + r.h_r2[k, c, rw, :].astype(F32)
        )

    def pick(ref):
        return lambda where: jnp.concatenate([ref[rw, :] for rw in where], axis=0)

    def product_nt(right):
        return lambda left, cols: dot_nt(left, right[cols, :])

    def rs_term(w, owner, piece):
        cols = ds(owner * block, block)
        if w == DOWN:
            left = r.cg[:, :, cols].reshape(tokens, block)
            half = hidden // 2
            return [dot_tn(left, r.activ[:, pl.ds(piece * half, half)])]
        if w == UP:
            half = hidden // 2
            return [dot_tn(r.ntwo[:, cols], r.g_hid[:, pl.ds(piece * half, half)])]
        half = local // 2
        if w == OUT:
            return [dot_tn(r.gatt[:, cols], r.mixed[:, pl.ds(piece * half, half)])]
        left = r.normed[:, cols]
        kinds = (0,) if w == QUERY else (1, 2)
        return [dot_tn(left, r.gproj[i, :, pl.ds(piece * half, half)]) for i in kinds]

    rs_send = (r.rq_s, r.ro_s, r.ru_s, r.rd_s, r.rx_s)
    rs_recv = (r.rq_r, r.ro_r, r.ru_r, r.rd_r, r.rx_r)

    def rs_half(w, piece):
        half = rs_send[w].shape[-1] // 2
        return pl.ds(piece * half, half)

    def rs_view(ref, w, d, step):
        if step > 0:
            return ref.at[d * hops + step]
        if w == QKV:
            return ref.at[d * hops, :, :, rs_half(w, d)]
        return ref.at[d * hops, :, rs_half(w, d)]

    def rs_arrived(w, d, step):
        landed(rs_view(rs_recv[w], w, d, step), r.ag_r.at[w, d, step])

    ahead = (r.pq, r.po, r.pu, r.pd, r.px)

    def rs_prepare(w, step):
        for d in (0, 1) if step < hops else (0,):
            owner = at(p + sign[d] * (hops - step)) if step < hops else s
            for piece in (0, 1) if step > 0 else (d,):
                cols = rs_half(w, piece)
                for i, v in enumerate(rs_term(w, owner, piece)):
                    lead = (i,) if w == QKV else ()
                    ahead[w][(d, *lead, slice(None), cols)] = v

    def rs_round(w, step):
        if step == 0:
            rs_prepare(w, 0)
        for d in (0, 1):
            slot = d * hops + step
            if step > 0:
                rs_arrived(w, d, step - 1)
            for piece in (0, 1) if step > 0 else (d,):
                cols = rs_half(w, piece)
                for i in range(2 if w == QKV else 1):
                    lead = (i,) if w == QKV else ()
                    v = ahead[w][(d, *lead, slice(None), cols)]
                    if step > 1 or (step == 1 and piece == d):
                        v = v + rs_recv[w][(slot - 1, *lead, slice(None), cols)].astype(F32)
                    rs_send[w][(slot, *lead, slice(None), cols)] = v.astype(BF)
            remote(
                rs_view(rs_send[w], w, d, step),
                rs_view(rs_recv[w], w, d, step),
                r.rs_s.at[w],
                r.ag_r.at[w, d, step],
                ring[d],
                h,
            ).start()
        rs_prepare(w, step + 1)

    finals = (r.gq_o.at[pl.ds(1, 2)], r.go_o, r.gu_o, r.gd_o, r.gq_o.at[0])
    local_copies = []

    def rs_final(w):
        for d in (0, 1):
            rs_arrived(w, d, hops - 1)
        for piece in (0, 1):
            cols = rs_half(w, piece)
            for i in range(2 if w == QKV else 1):
                lead = (i,) if w == QKV else ()
                v = ahead[w][(0, *lead, slice(None), cols)]
                for d in (0, 1):
                    v = v + rs_recv[w][(d * hops + hops - 1, *lead, slice(None), cols)].astype(F32)
                finals[w][(*lead, slice(None), cols)] = v

    def turn(k, src, dst):
        where = (hi, ds(lo * own, own))
        for i in range(1, m):
            to = lax.rem(h + i, m)
            remote(
                src.at[:, ds(to * local, local)],
                dst.at[where[0], where[1], :],
                r.aa_s.at[k],
                r.aa_r.at[k],
                s,
                to,
            ).start()
        copy = pltpu.make_async_copy(
            src.at[:, ds(h * local, local)], dst.at[where[0], where[1], :], r.lc.at[k]
        )
        copy.start()
        local_copies.append(copy)

    def turn_wait(k, src):
        landed(src.at[:, pl.ds(0, (m - 1) * local)], r.aa_r.at[k])

    ag_send(SMALL, 0)
    ag_send(QKV, 0)
    ag_send(OUT, 0)
    hg_start(0, 0)
    hg_start(0, 1)
    own_copies = [
        pltpu.make_async_copy(r.w_qkv, r.wq.at[:, ds(s * block, block), :], r.lc.at[4]),
        pltpu.make_async_copy(r.w_out, r.wo.at[ds(s * block, block), :], r.lc.at[5]),
        pltpu.make_async_copy(r.w_up, r.wu.at[ds(s * block, block), :], r.lc.at[6]),
        pltpu.make_async_copy(r.w_down, r.wd.at[ds(s * block, block), :], r.lc.at[7]),
        pltpu.make_async_copy(r.tok, r.xg.at[:, :, ds(h * local, local)], r.lc.at[2]),
        pltpu.make_async_copy(r.cot, r.cg.at[:, :, ds(h * local, local)], r.lc.at[3]),
    ]
    for copy in own_copies:
        copy.start()
    hg_start(1, 0)
    hg_start(1, 1)

    def ag_step(j):
        ag_pass(SMALL, j)
        ag_pass(QKV, j)
        ag_pass(OUT, j)

    hg_forward(0, 0)
    ag_step(0)
    hg_forward(0, 1)
    for copy in own_copies:
        copy.wait()
    r.smallg[:, ds(s * block, block)] = r.small[...]

    def unit(values):
        mean = jnp.mean(values, axis=1, keepdims=True)
        centered = values - mean
        inverse = lax.rsqrt(jnp.mean(centered * centered, axis=1, keepdims=True) + epsilon)
        return centered * inverse, inverse

    tile = 32

    def unit_one(b):
        def some(i):
            u, _ = unit(r.xg[b, ds(i * tile, tile), :].astype(F32))
            r.gelu_d[ds(b * rows + i * tile, tile), :] = u

        loop(rows // tile, some)

    def norm_one(i):
        rw = ds(i * tile, tile)
        r.normed[rw, :] = (r.gelu_d[rw, :] * gain_one + shift_one).astype(BF)

    for c in (0, 1):
        hg_finish(0, c)
    unit_one(0)
    ag_step(1)
    unit_one(1)
    crops(1)
    ag_step(2)
    ag_send(UP, 0)
    for c in (0, 1):
        hg_forward(1, c)
    ag_wait(SMALL, 3)
    gain_one, gain_two = r.smallg[0:1, :], r.smallg[1:2, :]
    shift_one, shift_two, shift_out = r.smallg[2:3, :], r.smallg[3:4, :], r.smallg[4:5, :]
    loop(tokens // tile, norm_one)
    ag_wait(QKV, 3)
    ag_wait(OUT, 3)

    tm = 128

    def project(i):
        rw = ds(i * tm, tm)
        b = lax.div(i, rows // tm)
        rb = ds(lax.rem(i, rows // tm) * tm, tm)
        left = r.normed[rw, :]
        v = dot_nn(left, r.wq[1])
        low = jnp.exp(jnp.minimum(v, 0.0))
        f = jnp.where(v > 0.0, v + 1.0, low).astype(BF)
        r.phi_d[1, rw, :] = low
        r.kf[rw, :] = (f.astype(F32) * wide(r.pmc[b, rb, :])).astype(BF)
        r.vf[rw, :] = dot_nn(left, r.wq[2]).astype(BF)

    def project_query(i):
        rw = ds(i * tm, tm)
        v = dot_nn(r.normed[rw, :], r.wq[0])
        low = jnp.exp(jnp.minimum(v, 0.0))
        r.phi_d[0, rw, :] = low
        r.qf[rw, :] = jnp.where(v > 0.0, v + 1.0, low).astype(BF)

    loop(tokens // tm, project)

    def fold(ref, parts):
        row = lax.broadcasted_iota(jnp.int32, (16, local), 0)
        sums = jnp.zeros((16, local), F32)
        for b, (matrix, total) in enumerate(parts):
            kept = jnp.where(same_head, matrix, 0.0)
            acc = kept[0:DH]
            for i in range(1, heads):
                acc = acc + kept[i * DH : (i + 1) * DH]
            ref[b * DH : (b + 1) * DH, :] = acc.astype(BF)
            sums = jnp.where(row == b, total, sums)
        ref[batches * DH :, :] = sums.astype(BF)

    def unfold(ref, i, b):
        acc = ref[i, b * DH : (b + 1) * DH, :].astype(F32)
        return jnp.where(same_head, jnp.concatenate([acc] * heads, axis=0), 0.0).astype(BF)

    def unfold_sum(ref, i, b):
        return ref[i, batches * DH :, :].astype(F32)[b : b + 1]

    def state_send(k, ref, dest, step):
        for i in (0, 1):
            to = lax.rem(s + n + step * (i + 1), n)
            remote(ref, dest.at[i], r.st_s.at[k], r.st_r.at[k], to, h).start()

    def state_wait(k, dest):
        landed(dest, r.st_r.at[k])

    def rows_of(b):
        return pl.ds(b * rows, rows)

    def by_head(value):
        return jnp.concatenate(
            [jnp.where(lane_head == hd, value.astype(F32), 0.0).astype(BF) for hd in range(heads)],
            axis=0,
        )

    parts = []
    for b in range(batches):
        k = r.kf[rows_of(b), :].astype(F32) * wide(r.tail[b])
        parts.append(
            (dot_tn(k.astype(BF), r.vf[rows_of(b), :]), jnp.sum(k, axis=0, keepdims=True))
        )
    fold(r.st_send, parts)
    state_send(0, r.st_send, r.st_recv, 1)
    loop(tokens // tm, project_query)

    for b in range(batches):
        q, k = r.qf[rows_of(b), :], r.kf[rows_of(b), :]
        acc = jnp.zeros((rows, local), F32)
        for hd in range(heads):
            sc = dot_nt(jnp.where(lane_head == hd, q.astype(F32), 0.0).astype(BF), k) * r.mask[b]
            r.low[b, :, hd * rows : (hd + 1) * rows] = sc.astype(BF)
            acc = acc + jnp.where(lane_head == hd, jnp.sum(sc, axis=1, keepdims=True), 0.0)
        r.denom[rows_of(b), :] = acc
        r.numer[rows_of(b), :] = dot_nn(r.low[b], by_head(r.vf[rows_of(b), :]))

    for c in (0, 1):
        hg_finish(1, c)
    ag_pass(UP, 0)
    ag_send(DOWN, 0)
    state_wait(0, r.st_recv)

    def both(b, value, thr):
        one = value.astype(F32) * wide(r.car[b])
        return jnp.concatenate([one.astype(BF), (one * thr).astype(BF)], axis=1)

    for b in range(batches):
        left = both(b, r.qf[rows_of(b), :], before_thr[b])
        states = jnp.concatenate([unfold(r.st_recv, i, b) for i in (0, 1)], axis=0)
        only = lax.broadcasted_iota(jnp.int32, (16, local), 0)
        sums = jnp.concatenate(
            [
                jnp.where(
                    same_head,
                    dot_tn(
                        jnp.where(
                            only == b, r.st_recv[i, batches * DH :, :].astype(F32), 0.0
                        ).astype(BF),
                        jnp.ones((16, local), BF),
                    ),
                    0.0,
                ).astype(BF)
                for i in (0, 1)
            ],
            axis=0,
        )
        top = r.numer[rows_of(b), :] + dot_nn(left, states)
        bottom = r.denom[rows_of(b), :] + dot_nn(left, sums)
        attn = top / jnp.maximum(bottom, 1.0)
        r.numer[rows_of(b), :] = attn
        r.denom[rows_of(b), :] = bottom
        r.mixed[rows_of(b), :] = attn.astype(BF)

    hr_first(0, 0, pick(r.mixed), product_nt(r.wo))
    hr_first(0, 1, pick(r.mixed), product_nt(r.wo))
    hr_second(0, 0)
    hr_second(0, 1)
    ag_pass(UP, 1)
    mine = h * own

    def x_rows(at_row):
        return r.xg[hi, ds(lo * own + at_row, tile), :].astype(F32)

    def c_rows(at_row):
        return r.cg[hi, ds(lo * own + at_row, tile), :].astype(F32)

    def norm_two(c):
        def some(i):
            at_row = c * part_rows + i * tile
            v = x_rows(at_row) + hr_value(0, c, ds(i * tile, tile))
            r.middle[ds(at_row, tile), :] = v
            u, _ = unit(v)
            r.ntwo[ds(mine + at_row, tile), :] = (u * gain_two + shift_two).astype(BF)

        loop(part_rows // tile, some)

    for c in (0, 1):
        hr_wait(0, c)
        norm_two(c)
        hg_start(2, c)
    ag_pass(DOWN, 0)
    hg_forward(2, 0)
    hg_forward(2, 1)
    ag_pass(UP, 2)
    hg_finish(2, 0)
    hg_finish(2, 1)
    ag_pass(DOWN, 1)
    ag_wait(UP, 3)

    tu = 256

    def up(i):
        rw = ds(lax.div(i, hidden // tn) * tu, tu)
        cols = ds(lax.rem(i, hidden // tn) * tn, tn)
        v = dot_nn(r.ntwo[rw, :], r.wu[:, cols]) + r.smallg[5:6, cols]
        square_of = v * v
        t = jnp.tanh(0.7978845608028654 * (v + 0.044715 * (square_of * v)))
        half = 0.5 * (1.0 + t)
        r.activ[rw, cols] = (v * half).astype(BF)
        r.gelu_d[rw, cols] = half + (0.5 * v) * (1.0 - t * t) * (
            0.7978845608028654 + (3.0 * 0.044715 * 0.7978845608028654) * square_of
        )

    loop((tokens // tu) * (hidden // tn), up)
    near = [ds(at(p + n + i) * block, block) for i in range(1 - hops, hops)]

    def back_near(i):
        cols = ds(i * tn, tn)
        right = jnp.concatenate([r.wd[rw, cols] for rw in near], axis=0)
        for b in range(batches):
            left = jnp.concatenate([r.cg[b, :, rw] for rw in near], axis=1)
            r.g_act[rows_of(b), cols] = dot_nn(left, right)

    rs_round(DOWN, 0)
    ag_pass(DOWN, 2)
    rs_round(DOWN, 1)
    loop(hidden // tn, back_near)
    ag_wait(DOWN, 3)

    far_block = ds(at(p + hops) * block, block)

    def back(i):
        cols = ds(i * tn, tn)
        for b in range(batches):
            rw = rows_of(b)
            g = r.g_act[rw, cols] + dot_nn(r.cg[b, :, far_block], r.wd[far_block, cols])
            r.g_hid[rw, cols] = (g * r.gelu_d[rw, cols]).astype(BF)

    loop(hidden // tn, back)
    rs_round(UP, 0)
    hr_first(2, 0, pick(r.g_hid), product_nt(r.wu))
    hr_first(2, 1, pick(r.g_hid), product_nt(r.wu))
    rs_round(DOWN, 2)
    hr_second(2, 0)
    hr_second(2, 1)

    r.hs_send[...] = jnp.zeros_like(r.hs_send)

    def back_norm(g, u, inverse, gain):
        scaled = g * gain
        centered = scaled - jnp.mean(scaled, axis=1, keepdims=True)
        return inverse * (centered - u * jnp.mean(scaled * u, axis=1, keepdims=True))

    def norm_two_back(c):
        def some(i):
            at_row = c * part_rows + i * tile
            rw = ds(at_row, tile)
            g = hr_value(2, c, ds(i * tile, tile))
            u, inverse = unit(r.middle[rw, :])
            out = c_rows(at_row)
            v = out + back_norm(g, u, inverse, gain_two)
            r.g_mid[rw, :] = v
            r.gatt[ds(mine + at_row, tile), :] = v.astype(BF)
            r.hs_send[1:2, :] += jnp.sum(g * u, axis=0, keepdims=True)
            r.hs_send[3:4, :] += jnp.sum(g, axis=0, keepdims=True)
            r.hs_send[4:5, :] += jnp.sum(out, axis=0, keepdims=True)

        loop(part_rows // tile, some)

    hr_wait(2, 0)
    norm_two_back(0)
    hg_start(3, 0)
    rs_round(UP, 1)
    hr_wait(2, 1)
    norm_two_back(1)
    hg_start(3, 1)
    hr_first(1, 0, pick(r.activ), product_nt(r.wd))
    hr_first(1, 1, pick(r.activ), product_nt(r.wd))
    rs_round(DOWN, 3)
    r.upb[...] = jnp.zeros_like(r.upb)

    def column_sums(i):
        r.upb[...] += jnp.sum(r.g_hid[ds(i * tile, tile), :].astype(F32), axis=0, keepdims=True)

    loop(tokens // tile, column_sums)

    for c in (0, 1):
        hg_forward(3, c)
    for c in (0, 1):
        hr_second(1, c)
    for c in (0, 1):
        hg_finish(3, c)

    def mixed_back(i):
        rw = ds(i * tm, tm)
        g = dot_nn(r.gatt[rw, :], r.wo[...])
        attn, bottom = r.numer[rw, :], r.denom[rw, :]
        r.g_num[rw, :] = (g / jnp.maximum(bottom, 1.0)).astype(BF)
        prod = g * attn
        lh = lane_head[:tm]
        acc = jnp.zeros((tm, local), F32)
        for hd in range(heads):
            acc = acc + jnp.where(
                lh == hd,
                jnp.sum(jnp.where(lh == hd, prod, 0.0), axis=1, keepdims=True),
                0.0,
            )
        r.g_den[rw, :] = jnp.where(bottom > 1.0, -acc / jnp.maximum(bottom, 1.0), 0.0)

    loop(tokens // tm, mixed_back)

    parts = []
    for b in range(batches):
        q = r.qf[rows_of(b), :].astype(F32) * wide(r.car[b])
        parts.append(
            (
                dot_tn(q.astype(BF), r.g_num[rows_of(b), :]),
                jnp.sum(q * r.g_den[rows_of(b), :], axis=0, keepdims=True),
            )
        )
    fold(r.gs_send, parts)
    state_send(1, r.gs_send, r.gs_recv, -1)
    rs_round(UP, 2)

    def head_lanes(hd, value):
        return jnp.where(lane_head == hd, value.astype(F32), 0.0).astype(BF)

    for b in range(batches):
        rw = rows_of(b)
        gk = jnp.zeros((rows, local), F32)
        gv = jnp.zeros((rows, local), F32)
        gq = jnp.zeros((rows, local), F32)
        for hd in range(heads):
            gn = head_lanes(hd, r.g_num[rw, :])
            g = dot_nt(gn, r.vf[rw, :]) + r.g_den[rw, hd * DH : hd * DH + 1]
            g = (g * r.mask[b]).astype(BF)
            gq = gq + dot_nn(g, head_lanes(hd, r.kf[rw, :]))
            gk = gk + dot_tn(g, head_lanes(hd, r.qf[rw, :]))
            gv = gv + dot_tn(r.low[b, :, hd * rows : (hd + 1) * rows], gn)
        left = both(b, r.g_num[rw, :], before_thr[b])
        states = jnp.concatenate([unfold(r.st_recv, i, b) for i in (0, 1)], axis=1)
        totals = unfold_sum(r.st_recv, 0, b) + before_thr[b] * unfold_sum(r.st_recv, 1, b)
        gq = gq + dot_nt(left, states) + wide(r.car[b]) * r.g_den[rw, :] * totals
        r.gproj[0, rw, :] = (gq * r.phi_d[0, rw, :]).astype(BF)
        r.gk[rw, :] = gk
        r.gv[rw, :] = gv

    rs_round(OUT, 0)
    rs_round(QUERY, 0)
    state_wait(1, r.gs_recv)
    for b in range(batches):
        rw = rows_of(b)
        thr = after_thr[b]
        states = [unfold(r.gs_recv, i, b) for i in (0, 1)]
        totals = unfold_sum(r.gs_recv, 0, b) + thr * unfold_sum(r.gs_recv, 1, b)
        k = r.kf[rw, :].astype(F32) * wide(r.tail[b])
        v = r.vf[rw, :].astype(F32) * wide(r.tail[b])
        k2 = jnp.concatenate([k.astype(BF), (k * thr).astype(BF)], axis=1)
        v2 = jnp.concatenate([v.astype(BF), (v * thr).astype(BF)], axis=1)
        gk = r.gk[rw, :] + dot_nt(v2, jnp.concatenate(states, axis=1)) + wide(r.tail[b]) * totals
        gv = r.gv[rw, :] + dot_nn(k2, jnp.concatenate(states, axis=0))
        r.gproj[1, rw, :] = (gk * wide(r.pmc[b]) * r.phi_d[1, rw, :]).astype(BF)
        r.gproj[2, rw, :] = gv.astype(BF)

    rs_round(QKV, 0)

    def picks(where):
        return [
            jnp.concatenate([r.gproj[kind, rw, :] for rw in where], axis=0) for kind in range(3)
        ]

    def first_term(left, cols):
        v = dot_nt(left[0], r.wq[0, cols, :])
        for kind in (1, 2):
            v = v + dot_nt(left[kind], r.wq[kind, cols, :])
        return v

    hr_first(3, 0, picks, first_term)
    hr_first(3, 1, picks, first_term)
    hr_second(3, 0)
    hr_second(3, 1)
    rs_round(OUT, 1)
    rs_round(QUERY, 1)
    rs_round(QKV, 1)
    rs_round(UP, 3)

    def norm_one_back(c):
        def some(i):
            at_row = c * part_rows + i * tile
            rw = ds(at_row, tile)
            g = hr_value(3, c, ds(i * tile, tile))
            u, inverse = unit(x_rows(at_row))
            r.i_rows[rw, :] = r.g_mid[rw, :] + back_norm(g, u, inverse, gain_one)
            r.hs_send[0:1, :] += jnp.sum(g * u, axis=0, keepdims=True)
            r.hs_send[2:3, :] += jnp.sum(g, axis=0, keepdims=True)

        loop(part_rows // tile, some)

    for c in (0, 1):
        hr_wait(3, c)
        norm_one_back(c)
    turn(1, r.i_rows, r.ing_o)
    rs_round(OUT, 2)
    rs_round(QUERY, 2)
    rs_round(QKV, 2)

    def finish_rows(c):
        def some(i):
            rw = ds(c * part_rows + i * tile, tile)
            r.a_rows[rw, :] = r.middle[rw, :] + hr_value(1, c, ds(i * tile, tile)) + shift_out

        loop(part_rows // tile, some)

    for c in (0, 1):
        hr_wait(1, c)
        finish_rows(c)
    turn(0, r.a_rows, r.act_o)

    r.hs_recv[h] = r.hs_send[...]
    for i in range(1, m):
        remote(
            r.hs_send, r.hs_recv.at[h], r.hs_s.at[0], r.hs_r.at[0], s, lax.rem(h + i, m)
        ).start()
    rs_round(OUT, 3)
    rs_round(QUERY, 3)
    rs_final(DOWN)
    rs_round(QKV, 3)
    landed(r.hs_recv.at[pl.ds(0, m - 1)], r.hs_r.at[0])
    acc = r.hs_recv[0]
    for i in range(1, m):
        acc = acc + r.hs_recv[i]
    r.sg[...] = acc
    r.sg[5:6, :] = r.upb[...]
    r.ss_recv[s] = r.sg[:, ds(s * block, block)]
    for i in range(1, n):
        to = lax.rem(s + i, n)
        remote(
            r.sg.at[:, ds(to * block, block)],
            r.ss_recv.at[s],
            r.ss_s.at[0],
            r.ss_r.at[0],
            to,
            h,
        ).start()
    rs_final(UP)
    rs_final(OUT)
    rs_final(QUERY)
    landed(r.ss_recv.at[pl.ds(0, n - 1)], r.ss_r.at[0])
    acc = r.ss_recv[0]
    for i in range(1, n):
        acc = acc + r.ss_recv[i]
    r.gg_o[...] = acc[0:2]
    r.gb_o[...] = acc[2:5]
    r.gup_o[...] = acc[5:6]
    turn_wait(0, r.a_rows)
    turn_wait(1, r.i_rows)

    far = pl.ds(0, (n - 1) * block)
    for w in range(5):
        views = (r.wq.at[:, far, :], r.wo.at[far], r.wu.at[far], r.wd.at[far], r.smallg.at[:, far])
        drained(views[w], r.ag_s.at[w])
    others = pl.ds(0, (m - 1) * local)
    rest = pl.ds(0, (m - 1) * own)
    for k in range(4):
        view = (r.xg, r.cg)[k].at[:, :, others] if k < 2 else (r.ntwo, r.gatt)[k - 2].at[rest]
        drained(view, r.hg_s.at[k])
        drained(r.h_s1.at[k], r.hr_s.at[k, 0])
        drained(r.h_s2.at[k], r.hr_s.at[k, 1])
    for k, dest in enumerate((r.st_recv, r.gs_recv)):
        drained(dest, r.st_s.at[k])
    drained(r.a_rows.at[:, others], r.aa_s.at[0])
    drained(r.i_rows.at[:, others], r.aa_s.at[1])
    drained(r.hs_recv.at[pl.ds(0, m - 1)], r.hs_s.at[0])
    drained(r.ss_recv.at[pl.ds(0, n - 1)], r.ss_s.at[0])
    rs_final(QKV)
    for w in range(5):
        drained(rs_send[w].at[pl.ds(0, n - 1)], r.rs_s.at[w])
    for copy in local_copies:
        copy.wait()


def settle(*refs):
    count = len(refs) // 2
    copies = [
        pltpu.make_async_copy(refs[i], refs[count + i], refs[-1].at[i]) for i in range(count)
    ]
    for copy in copies:
        copy.start()
    for copy in copies:
        copy.wait()


def whole_layer(n, m):
    def on_each(
        tokens, cotangent, w_qkv, w_out_t, w_up, w_down_t, gains, biases, up_bias, lengths, pixel_mask
    ):
        batches, rows, local = tokens.shape
        width = w_qkv.shape[0] * n
        hidden = w_up.shape[1]
        block = width // n
        vm, sems = layout(n, m, batches, rows, width, local, hidden)
        ins = ["tok", "cot", "w_qkv", "w_out", "w_up", "w_down", "gains", "biases", "up_bias", "lengths", "pixel"]
        outs = ["act_o", "ing_o", "gq_o", "go_o", "gu_o", "gd_o", "gg_o", "gb_o", "gup_o"]
        anywhere = pl.BlockSpec(memory_space=pl.ANY)
        in_vmem = pl.BlockSpec(memory_space=pltpu.VMEM)
        in_smem = pl.BlockSpec(memory_space=pltpu.SMEM)

        result = pl.pallas_call(
            functools.partial(body, n, m, ins + outs + list(vm) + list(sems)),
            name="layer",
            out_shape=(
                pltpu.VMEM((batches, rows, local), F32),
                pltpu.VMEM((batches, rows, local), F32),
                pltpu.VMEM((3, block, local), F32),
                pltpu.VMEM((block, local), F32),
                pltpu.VMEM((block, hidden), F32),
                pltpu.VMEM((block, hidden), F32),
                pltpu.VMEM((2, block), F32),
                pltpu.VMEM((3, block), F32),
                pltpu.VMEM((1, block), F32),
            ),
            in_specs=[anywhere] * 6 + [in_vmem] * 3 + [in_smem, in_vmem],
            out_specs=[in_vmem] * 9,
            scratch_shapes=[pltpu.VMEM(shape, kind) for shape, kind in vm.values()]
            + [pltpu.SemaphoreType.DMA(shape) for shape in sems.values()],
            compiler_params=pltpu.CompilerParams(
                collective_id=0, has_side_effects=True, vmem_limit_bytes=60_000_000
            ),
        )(
            tokens,
            cotangent,
            jnp.transpose(w_qkv, (1, 0, 2)),
            w_out_t,
            w_up,
            w_down_t,
            gains,
            biases,
            up_bias,
            lengths,
            pixel_mask,
        )
        result = pl.pallas_call(
            settle,
            name="settle",
            out_shape=[jax.ShapeDtypeStruct(a.shape, a.dtype) for a in result],
            in_specs=[in_vmem] * len(result),
            out_specs=[anywhere] * len(result),
            scratch_shapes=[pltpu.SemaphoreType.DMA((len(result),))],
        )(*[pltpu.with_memory_space_constraint(a, pltpu.VMEM) for a in result])
        return (*result[:2], jnp.transpose(result[2], (1, 0, 2)), *result[3:])

    return on_each


def solution(mesh):
    in_specs = (
        P(None, "seq", "head"),
        P(None, "seq", "head"),
        P("seq", None, "head"),
        P("seq", "head"),
        P("seq", "head"),
        P("seq", "head"),
        P(None, "seq"),
        P(None, "seq"),
        P("head", "seq"),
        P(),
        P(None, "seq"),
    )
    out_specs = (
        P(None, "seq", "head"),
        P(None, "seq", "head"),
        P("seq", None, "head"),
        P("seq", "head"),
        P("seq", "head"),
        P("seq", "head"),
        P(None, "seq"),
        P(None, "seq"),
        P("head", "seq"),
    )
    n, m = mesh.shape["seq"], mesh.shape["head"]
    fits = (n, m) == (8, 4)
    return jax.shard_map(
        whole_layer(n, m) if fits else on_device, mesh=mesh, in_specs=in_specs, out_specs=out_specs, check_vma=False
    )
```
